32 devices in a mesh: dp: 4 (over y, x), ctx: 8 (over z, core).
Axes of the slice: x: 2, y: 2, z: 4, core: 2. Of those that a mesh axis runs over, the one named last changes fastest.
Arguments:
- tokens: bfloat16 [4, 2048, 1024], P('dp', 'ctx'), may hold values from -6 to 6
- norm1_gain: bfloat16 [1024], P('dp'), may hold values from 0.5 to 1.5
- qkv_weight: bfloat16 [1024, 3072], P('dp'), may hold values from -0.1875 to 0.1875
- attn_out_weight: bfloat16 [1024, 1024], P('dp'), may hold values from -6 to 6
- norm2_gain: bfloat16 [1024], P('dp'), may hold values from 0.5 to 1.5
- mlp_in_weight: bfloat16 [1024, 5248], P('dp'), may hold values from -0.1875 to 0.1875
- mlp_out_weight: bfloat16 [2624, 1024], P('dp'), may hold values from -0.125 to 0.125
- cotangent: bfloat16 [4, 2048, 1024], P('dp', 'ctx'), may hold values from -6 to 6
Outputs:
- layer_out: bfloat16 [4, 2048, 1024], P('dp', 'ctx')
- input_grad: bfloat16 [4, 2048, 1024], P('dp', 'ctx')
- norm1_grad: float32 [1024], P('dp')
- qkv_grad: float32 [1024, 3072], P('dp')
- attn_out_grad: float32 [1024, 1024], P('dp')
- norm2_grad: float32 [1024], P('dp')
- mlp_in_grad: float32 [1024, 5248], P('dp')
- mlp_out_grad: float32 [2624, 1024], P('dp')
The draws below stay inside these ranges and needn't reach their ends.
All inputs are finite; a program needn't handle non-finite values.
Results may differ from the reference program's by a relative error of at most 0.023.
Values may be sent and summed in bfloat16 or wider, within the bound.
A program may use at most 192 MiB of HBM per device.

```python
import jax
import jax.numpy as jnp
from jax import lax

D = 1024
HEADS = 16
HEAD = 64
FF = 2624
TOK_DEV = 256
LEN = 2048
SEQS = 4
N_CTX = 8


def shard_levels(stream_key, extent, split, low, largest):
    level, own = 1.0, jax.random.fold_in(stream_key, 6)
    for axis_at, parts in split:
        steps = jnp.exp(jax.random.uniform(jax.random.fold_in(own, axis_at), (parts,), jnp.float32, low / len(split), largest / len(split)))
        level = level * jnp.repeat(steps, extent[axis_at] // parts).reshape([-1 if axis == axis_at else 1 for axis in range(len(extent))])
    return level


def normal_values(stream_key, extent, spread, bound, shards=(), kind=jnp.bfloat16):
    factor_of = shard_levels(stream_key, extent, shards, -0.22, 0.18) if shards else 1.0
    entries = jax.random.normal(stream_key, extent, jnp.float32) * spread * factor_of
    return jnp.minimum(jnp.maximum(entries, -bound), bound).astype(kind)


def setup_inputs(seed: int = 0) -> dict:
    arg_keys = jax.random.split(jax.random.key(seed), 9)
    tokens = normal_values(arg_keys[0], (SEQS, LEN, D), 1.0, 6.0, ((0, 4), (1, 8)))
    norm1_gain = jnp.clip(1.0 + 0.1 * jax.random.normal(arg_keys[1], (D,), jnp.float32), 0.5, 1.5).astype(jnp.bfloat16)
    qkv_weight = normal_values(arg_keys[2], (D, 3 * D), D ** -0.5, 0.1875, ((0, 4),))
    attn_out_weight = normal_values(arg_keys[3], (D, D), (max(1, 3 * D // LEN)) ** -0.5, 6.0, ((0, 4),))
    norm2_gain = jnp.clip(1.0 + 0.1 * jax.random.normal(arg_keys[4], (D,), jnp.float32), 0.5, 1.5).astype(jnp.bfloat16)
    mlp_in_weight = normal_values(arg_keys[5], (D, 2 * FF), D ** -0.5, 0.1875, ((0, 4),))
    mlp_out_weight = normal_values(arg_keys[6], (FF, D), FF ** -0.5, 0.125, ((0, 4),))
    cotangent = normal_values(arg_keys[7], (SEQS, LEN, D), 1.0, 6.0, ((0, 4), (1, 8)))
    return {"tokens": tokens, "norm1_gain": norm1_gain, "qkv_weight": qkv_weight, "attn_out_weight": attn_out_weight, "norm2_gain": norm2_gain, "mlp_in_weight": mlp_in_weight, "mlp_out_weight": mlp_out_weight, "cotangent": cotangent}


norm_eps = 1e-05
rope_theta = 160000.0

def norm_rows(values, gain):
    row_mean = lax.optimization_barrier(jnp.mean(values, axis=-1, keepdims=True))
    centred = values - row_mean
    row_var = lax.optimization_barrier(jnp.mean(centred * centred, axis=-1, keepdims=True))
    return centred * lax.rsqrt(row_var + norm_eps) * gain

def gelu_exact(values):
    return 0.5 * values * (1.0 + lax.erf(values * 0.7071067811865476))

def gelu_slope(values):
    return 0.5 * (1.0 + lax.erf(values * 0.7071067811865476)) + values * jnp.exp(-0.5 * values * values) * 0.3989422804014327

def rope_tables(positions, width):
    half_width = width // 2
    frequency = rope_theta ** (-(jnp.arange(half_width, dtype=jnp.float32) * 2.0 / width))
    angles = positions.astype(jnp.float32)[:, None] * frequency[None, :]
    angles = jnp.concatenate([angles, angles], axis=1)
    return (jnp.cos(angles)[:, None, :], jnp.sin(angles)[:, None, :])

def rotate_half(values):
    half_width = values.shape[-1] // 2
    return jnp.concatenate([-values[..., half_width:], values[..., :half_width]], axis=-1)

def rotate_back(values):
    half_width = values.shape[-1] // 2
    return jnp.concatenate([values[..., half_width:], -values[..., :half_width]], axis=-1)

def one_sequence(inputs, upstream, gain_one, w_qkv, w_attn, gain_two, w_in, w_out):
    attn_scale = HEAD ** (-0.5)
    inputs_f = inputs.astype(jnp.float32)
    gain_onef = gain_one.astype(jnp.float32)
    gain_twof = gain_two.astype(jnp.float32)
    normed_one = norm_rows(inputs_f, gain_onef).astype(jnp.bfloat16)
    projected = jnp.dot(normed_one, w_qkv, preferred_element_type=jnp.float32).reshape(LEN, 3, HEADS, HEAD)
    cosine, sine = rope_tables(jnp.arange(LEN), HEAD)
    queries = (projected[:, 0] * cosine + rotate_half(projected[:, 0]) * sine).astype(jnp.bfloat16)
    keys_all = (projected[:, 1] * cosine + rotate_half(projected[:, 1]) * sine).astype(jnp.bfloat16)
    values_all = projected[:, 2].astype(jnp.bfloat16)
    keys_f = keys_all.astype(jnp.float32)
    values_f = values_all.astype(jnp.float32)
    query_blocks = queries.reshape(N_CTX, TOK_DEV, HEADS, HEAD)

    def attend(query_blk):
        scores = jnp.einsum('qhd,khd->hqk', query_blk.astype(jnp.float32), keys_f) * attn_scale
        log_sum = jax.nn.logsumexp(scores, axis=-1)
        probs = jnp.exp(scores - log_sum[..., None]).astype(jnp.bfloat16)
        return (jnp.einsum('hqk,khd->qhd', probs.astype(jnp.float32), values_f), log_sum)
    attended, log_sums = lax.map(attend, query_blocks)
    attended_b = attended.reshape(LEN, D).astype(jnp.bfloat16)
    attn_res = inputs_f + jnp.dot(attended_b, w_attn, preferred_element_type=jnp.float32)
    normed_two = norm_rows(attn_res, gain_twof).astype(jnp.bfloat16)
    lifted = jnp.dot(normed_two, w_in, preferred_element_type=jnp.float32)
    gelu_in = lifted[:, :FF]
    gate_in = lifted[:, FF:]
    activated = (gelu_exact(gelu_in) * gate_in).astype(jnp.bfloat16)
    layer_out = (attn_res + jnp.dot(activated, w_out, preferred_element_type=jnp.float32)).astype(jnp.bfloat16)
    grad_out = jnp.dot(activated.T, upstream, preferred_element_type=jnp.float32)
    grad_act = jnp.dot(upstream, w_out.T, preferred_element_type=jnp.float32)
    grad_lift = jnp.concatenate([grad_act * gate_in * gelu_slope(gelu_in), grad_act * gelu_exact(gelu_in)], axis=1).astype(jnp.bfloat16)
    grad_in = jnp.dot(normed_two.T, grad_lift, preferred_element_type=jnp.float32)
    grad_normed_two = jnp.dot(grad_lift, w_in.T, preferred_element_type=jnp.float32)
    unused_two, pull_two = jax.vjp(norm_rows, attn_res, gain_twof)
    grad_res_norm, grad_gain_two = pull_two(grad_normed_two)
    grad_res = upstream.astype(jnp.float32) + grad_res_norm
    grad_res_b = grad_res.astype(jnp.bfloat16)
    grad_attn = jnp.dot(attended_b.T, grad_res_b, preferred_element_type=jnp.float32)
    grad_heads = jnp.dot(grad_res_b, w_attn.T, preferred_element_type=jnp.float32).astype(jnp.bfloat16)
    grad_heads = grad_heads.reshape(N_CTX, TOK_DEV, HEADS, HEAD)
    deltas = lax.optimization_barrier(jnp.sum(grad_heads.astype(jnp.float32) * attended_b.reshape(N_CTX, TOK_DEV, HEADS, HEAD).astype(jnp.float32), axis=-1))
    deltas = jnp.transpose(deltas, (0, 2, 1))

    def back_block(carry, items):
        key_sum, value_sum = carry
        query_blk, grad_blk, log_sum, delta_blk = items
        query_f = query_blk.astype(jnp.float32)
        grad_f = grad_blk.astype(jnp.float32)
        scores = jnp.einsum('qhd,khd->hqk', query_f, keys_f) * attn_scale
        probs = jnp.exp(scores - log_sum[..., None])
        probs_b = probs.astype(jnp.bfloat16).astype(jnp.float32)
        value_part = jnp.einsum('hqk,qhd->khd', probs_b, grad_f)
        prob_grad = jnp.einsum('qhd,khd->hqk', grad_f, values_f)
        score_grad = (attn_scale * probs * (prob_grad - delta_blk[..., None])).astype(jnp.bfloat16).astype(jnp.float32)
        query_grad = jnp.einsum('hqk,khd->qhd', score_grad, keys_f)
        key_part = jnp.einsum('hqk,qhd->khd', score_grad, query_f)
        key_round = lax.optimization_barrier(key_part.astype(jnp.bfloat16))
        value_round = lax.optimization_barrier(value_part.astype(jnp.bfloat16))
        return ((key_sum + key_round.astype(jnp.float32), value_sum + value_round.astype(jnp.float32)), query_grad)
    start = (jnp.zeros((LEN, HEADS, HEAD), jnp.float32), jnp.zeros((LEN, HEADS, HEAD), jnp.float32))
    (key_grad, value_grad), query_grad = lax.scan(back_block, start, (query_blocks, grad_heads, log_sums, deltas))
    query_grad = query_grad.reshape(LEN, HEADS, HEAD)
    query_pre = query_grad * cosine + rotate_back(query_grad * sine)
    key_pre = key_grad * cosine + rotate_back(key_grad * sine)
    grad_proj = jnp.stack([query_pre, key_pre, value_grad], axis=1).reshape(LEN, 3 * D).astype(jnp.bfloat16)
    grad_qkv = jnp.dot(normed_one.T, grad_proj, preferred_element_type=jnp.float32)
    grad_normed_one = jnp.dot(grad_proj, w_qkv.T, preferred_element_type=jnp.float32)
    unused_one, pull_one = jax.vjp(norm_rows, inputs_f, gain_onef)
    grad_in_norm, grad_gain_one = pull_one(grad_normed_one)
    input_grad = (grad_res + grad_in_norm).astype(jnp.bfloat16)
    return (layer_out, input_grad, (grad_gain_one, grad_qkv, grad_attn, grad_gain_two, grad_in, grad_out))

def reference(tokens, norm1_gain, qkv_weight, attn_out_weight, norm2_gain, mlp_in_weight, mlp_out_weight, cotangent):
    start = (jnp.zeros((D,), jnp.float32), jnp.zeros((D, 3 * D), jnp.float32), jnp.zeros((D, D), jnp.float32), jnp.zeros((D,), jnp.float32), jnp.zeros((D, 2 * FF), jnp.float32), jnp.zeros((FF, D), jnp.float32))

    def per_sequence(carry, items):
        inputs, upstream = items
        layer_out, input_grad, grads = one_sequence(inputs, upstream, norm1_gain, qkv_weight, attn_out_weight, norm2_gain, mlp_in_weight, mlp_out_weight)
        return (tuple((total + part for total, part in zip(carry, grads))), (layer_out, input_grad))
    totals, (outputs, input_grads) = lax.scan(per_sequence, start, (tokens, cotangent))
    return (outputs, input_grads, totals[0], totals[1], totals[2], totals[3], totals[4], totals[5])
```

```python
import functools

import jax
import jax.numpy as jnp
from jax import lax
from jax.experimental import pallas as pl
from jax.experimental.pallas import tpu as pltpu
from jax.sharding import PartitionSpec as P

HEAD = 64
norm_eps = 1e-05
rope_theta = 160000.0
F32 = jnp.float32
BF16 = jnp.bfloat16
MESH = pl.DeviceIdType.MESH
LOG2E = 1.4426950408889634
VMEM_LIMIT = 64 * 1024 * 1024 - 65536
ANY = pl.BlockSpec(memory_space=pl.ANY)
VMEM = pl.BlockSpec(memory_space=pltpu.VMEM)
S = jax.ShapeDtypeStruct


def params(cid):
    return pltpu.CompilerParams(
        collective_id=cid, has_side_effects=True, vmem_limit_bytes=VMEM_LIMIT
    )


class Place:
    def __init__(self):
        self.nd = lax.axis_size("dp")
        self.nc = lax.axis_size("ctx")
        self.d = lax.axis_index("dp")
        self.c = lax.axis_index("ctx")
        self.nb = 2 if self.nd % 2 == 0 else 1
        self.na = self.nd // self.nb
        self.a = self.d // self.nb
        self.b = self.d % self.nb
        self.nz = self.nc // 2
        self.z = self.c // 2
        self.k = self.c % 2
        self.sibling = (self.d, self.z * 2 + 1 - self.k)

    def shard(self, da, db):
        return ((self.a + da) % self.na) * self.nb + (self.b + db) % self.nb

    def at(self, da, db):
        return (self.shard(da, db), self.c)


def barrier(pc, dp=True, ctx=True):
    sem = pltpu.get_barrier_semaphore()
    count = 0
    if dp:
        for t in range(1, pc.nd):
            pl.semaphore_signal(
                sem, inc=1, device_id=((pc.d + t) % pc.nd, pc.c), device_id_type=MESH
            )
            count += 1
    if ctx:
        for t in range(1, pc.nc):
            pl.semaphore_signal(
                sem, inc=1, device_id=(pc.d, (pc.c + t) % pc.nc), device_id_type=MESH
            )
            count += 1
    pl.semaphore_wait(sem, count)


def remote(src, dst, send, recv, target):
    return pltpu.make_async_remote_copy(
        src_ref=src,
        dst_ref=dst,
        send_sem=send,
        recv_sem=recv,
        device_id=target,
        device_id_type=MESH,
    )


class Gather:
    def __init__(self, pc, cut, own, send, recv):
        self.pc, self.cut, self.own, self.send, self.recv = pc, cut, own, send, recv

    @staticmethod
    def count(nd):
        nb = 2 if nd % 2 == 0 else 1
        na = nd // nb
        return 2 * ((na - 1) + (nb - 1) + 2 * (na - 1) * (nb - 1))

    def slots(self):
        pc = self.pc
        lines = [(da, 0) for da in range(1, pc.na)] + [(0, db) for db in range(1, pc.nb)]
        cross = [
            (da, db, part)
            for part in (0, 1)
            for da in range(1, pc.na)
            for db in range(1, pc.nb)
        ]
        return lines, cross

    def _copy(self, index, shard, part, target, own=False):
        src = (self.own if own else self.cut)(shard, self.pc.k, part)
        dst = self.cut(shard, self.pc.k, part)
        return remote(src, dst, self.send.at[index], self.recv.at[index], target)

    def _arrived(self, index, shard, core, part, wait=True):
        ref = self.cut(shard, core, part)
        return remote(ref, ref, self.send.at[index], self.recv.at[index], self.pc.sibling)

    def first(self):
        pc = self.pc
        lines, _ = self.slots()
        for i, (da, db) in enumerate(lines):
            self._copy(i, pc.d, None, pc.at(-da, -db), own=True).start()

    def relay(self):
        pc = self.pc
        lines, cross = self.slots()
        n = len(lines) + len(cross)
        for i, (da, db) in enumerate(lines):
            shard = pc.shard(da, db)
            self._arrived(i, shard, pc.k, None).wait_recv()
            for j, (xa, xb, part) in enumerate(cross):
                if part == 0 and db == 0 and xa == da:
                    self._copy(len(lines) + j, shard, part, pc.at(0, -xb)).start()
                if part == 1 and da == 0 and xb == db:
                    self._copy(len(lines) + j, shard, part, pc.at(-xa, 0)).start()
            self._copy(n + i, shard, None, pc.sibling).start()

    def cross(self):
        pc = self.pc
        lines, cross = self.slots()
        n = len(lines) + len(cross)
        for j, (xa, xb, part) in enumerate(cross):
            shard = pc.shard(xa, xb)
            self._arrived(len(lines) + j, shard, pc.k, part).wait_recv()
            self._copy(n + len(lines) + j, shard, part, pc.sibling).start()

    def finish(self):
        pc = self.pc
        lines, cross = self.slots()
        n = len(lines) + len(cross)
        for i, (da, db) in enumerate(lines):
            self._arrived(n + i, pc.shard(da, db), 1 - pc.k, None).wait_recv()
        for j, (xa, xb, part) in enumerate(cross):
            self._arrived(n + len(lines) + j, pc.shard(xa, xb), 1 - pc.k, part).wait_recv()

    def sent(self):
        pc = self.pc
        lines, cross = self.slots()
        n = len(lines) + len(cross)
        for i, _ in enumerate(lines):
            self._arrived(i, pc.d, pc.k, None).wait_send()
            self._arrived(n + i, pc.d, pc.k, None).wait_send()
        for j, (_, _, part) in enumerate(cross):
            self._arrived(len(lines) + j, pc.d, pc.k, part).wait_send()
            self._arrived(n + len(lines) + j, pc.d, pc.k, part).wait_send()


def row_cut(ref, rows, core, part, lead=0):
    start = core * (rows // 2) + (0 if part is None else part * (rows // 4))
    size = rows // 2 if part is None else rows // 4
    return ref.at[(slice(None),) * lead + (pl.ds(start, size),)]


def col_cut(ref, cols, core, part):
    start = core * (cols // 2) + (0 if part is None else part * (cols // 4))
    size = cols // 2 if part is None else cols // 4
    return ref.at[:, pl.ds(pl.multiple_of(start, 128), size)]


def project_kernel(
    x_ref, gains_ref, cos_ref, sin_ref, wqkv_ref, wattn_ref,
    h1_ref, gains_out, wqkv_out, wattn_out, heads_out,
    wbuf, abuf, gbuf, sendbuf,
    wsend, wrecv, asend, arecv, gsend, grecv, xsend, xrecv, local,
):
    pc = Place()
    nd, nc, nz = pc.nd, pc.nc, pc.nz
    rows = wqkv_ref.shape[0]
    width = wqkv_ref.shape[1] // 3
    tok = x_ref.shape[0]
    w = width // nc
    cw = 2 * w
    own_w = [
        pltpu.make_async_copy(
            wqkv_ref.at[:, pl.ds(g * width, width)], wbuf.at[g, pc.d], local.at[g]
        )
        for g in range(3)
    ]
    for cp in own_w:
        cp.start()
    own_a = pltpu.make_async_copy(wattn_ref, abuf, local.at[3])
    own_a.start()
    barrier(pc)
    for cp in own_w:
        cp.wait()

    def chip_of(j):
        return (pc.z + j + 1) % nz

    def chunk(j):
        col = pl.multiple_of(chip_of(j) * cw, cw)

        def cut(shard, core, part):
            return row_cut(wbuf.at[:, shard, :, pl.ds(col, cw)], rows, core, part, lead=1)

        return Gather(pc, cut, cut, wsend.at[j], wrecv.at[j])

    def attn_cut(shard, core, part):
        return row_cut(wattn_out.at[shard], rows, core, part)

    def attn_own(shard, core, part):
        return row_cut(wattn_ref, rows, core, part)

    attn = Gather(pc, attn_cut, attn_own, asend, arecv)

    gain_copies = []
    gbuf[pc.d] = gains_ref[...]
    for t in range(1, nd):
        gain_copies.append(
            remote(
                gains_ref, gbuf.at[pc.d], gsend.at[t], grecv.at[t], ((pc.d + t) % nd, pc.c)
            )
        )
        gain_copies[-1].start()
    chunk(0).first()
    if nz > 1:
        chunk(1).first()

    xf = x_ref[...].astype(F32)
    mean = jnp.mean(xf, axis=-1, keepdims=True)
    cen = xf - mean
    var = jnp.mean(cen * cen, axis=-1, keepdims=True)
    hat = cen * lax.rsqrt(var + norm_eps)
    for t in range(1, nd):
        src = gbuf.at[(pc.d + nd - t) % nd]
        remote(src, src, gsend.at[t], grecv.at[t], pc.sibling).wait_recv()
    for s in range(nd):
        cols = slice(s * rows, (s + 1) * rows)
        h1_ref[:, cols] = (hat[:, cols] * gbuf[s, 0:1, :]).astype(BF16)
    gains_out[...] = gbuf[...]
    own_a.wait()
    own_a2 = pltpu.make_async_copy(abuf, wattn_out.at[pc.d], local.at[3])
    own_a2.start()

    lane = lax.broadcasted_iota(jnp.int32, (1, cw), 1)
    low = (lane % HEAD) < HEAD // 2

    def out_copy(j):
        cols = pl.ds(pl.multiple_of(chip_of(j) * cw, cw), cw)
        return pltpu.make_async_copy(
            wbuf.at[:, :, :, cols], wqkv_out.at[:, :, :, cols], local.at[4 + j]
        )

    def place(ref):
        return ref.at[:, pl.ds(pl.multiple_of(pc.c * tok, tok), tok), :]

    def exchange(j, kk):
        return remote(
            sendbuf.at[j, kk], place(heads_out), xsend.at[j, kk], xrecv.at[j, pc.k],
            (pc.d, chip_of(j) * 2 + kk),
        )

    def step(j, _):
        g = chunk(j)
        g.relay()

        @pl.when(j + 2 < nz)
        def _():
            chunk(j + 2).first()

        @pl.when(j + 2 == nz)
        def _():
            attn.first()

        g.cross()
        g.finish()
        out_copy(j).start()
        cols = pl.ds(pl.multiple_of(chip_of(j) * cw, cw), cw)
        for part in range(3):
            weight = wbuf[part, :, :, cols].reshape(nd * rows, cw)
            proj = jnp.dot(h1_ref[...], weight, preferred_element_type=F32)
            if part < 2:
                up = pltpu.roll(proj, cw - HEAD // 2, 1)
                down = pltpu.roll(proj, HEAD // 2, 1)
                proj = proj * cos_ref[...] + jnp.where(low, up, down) * sin_ref[...]
            proj = proj.astype(BF16)
            for kk in range(2):
                sendbuf[j, kk, part] = proj[:, kk * w : (kk + 1) * w]

        @pl.when(j < nz - 1)
        def _():
            exchange(j, 0).start()
            exchange(j, 1).start()

        return 0

    lax.fori_loop(0, nz, step, 0)
    last = nz - 1
    remote(
        sendbuf.at[last, 1 - pc.k], place(heads_out), xsend.at[last, 1 - pc.k],
        xrecv.at[last, pc.k], pc.sibling,
    ).start()
    own_x = pltpu.make_async_copy(
        sendbuf.at[last, pc.k], place(heads_out), local.at[4 + nz]
    )
    own_x.start()
    attn.relay()
    attn.cross()
    attn.finish()

    def arrival(j, kk):
        ref = sendbuf.at[j, kk]
        return remote(ref, ref, xsend.at[j, kk], xrecv.at[j, kk], pc.sibling)

    def drain(j, _):
        arrival(j, 0).wait_recv()
        arrival(j, 1).wait_recv()
        arrival(j, 0).wait_send()
        arrival(j, 1).wait_send()
        chunk(j).sent()
        out_copy(j).wait()
        return 0

    lax.fori_loop(0, nz - 1, drain, 0)
    arrival(last, 1 - pc.k).wait_recv()
    arrival(last, 1 - pc.k).wait_send()
    chunk(last).sent()
    out_copy(last).wait()
    own_x.wait()
    own_a2.wait()
    attn.sent()
    for cp in gain_copies:
        cp.wait_send()


def project(x, gains, cosine, sine, wqkv, wattn):
    nd, nc = lax.axis_size("dp"), lax.axis_size("ctx")
    nz = nc // 2
    tok, width = x.shape
    rows = wqkv.shape[0]
    w = width // nc
    n = Gather.count(nd)
    dma = pltpu.SemaphoreType.DMA
    return pl.pallas_call(
        project_kernel,
        out_shape=[
            S((tok, width), BF16),
            S((nd, 8, rows), F32),
            S((3, nd, rows, width), BF16),
            S((nd, rows, width), BF16),
            S((3, nc * tok, w), BF16),
        ],
        in_specs=[VMEM, VMEM, VMEM, VMEM, ANY, ANY],
        out_specs=[VMEM, VMEM, ANY, ANY, ANY],
        scratch_shapes=[
            pltpu.VMEM((3, nd, rows, width), BF16),
            pltpu.VMEM((rows, width), BF16),
            pltpu.VMEM((nd, 8, rows), F32),
            pltpu.VMEM((nz, 2, 3, tok, w), BF16),
            dma((nz, n)), dma((nz, n)), dma((n,)), dma((n,)),
            dma((nd,)), dma((nd,)), dma((nz, 2)), dma((nz, 2)), dma((5 + nz,)),
        ],
        compiler_params=params(0),
        name="project",
    )(x, gains, cosine, sine, wqkv, wattn)


def attend_kernel(
    heads_ref, w1_ref, w2_ref, wout_ref,
    otok_out, o_ref, lse_ref, w1_out, w2_out, wout_out,
    qkv, vext, bounce1, bounce2, bounce3,
    s1, r1, s2, r2, s3, r3, xsend, xrecv, local,
):
    pc = Place()
    nd, nc = pc.nd, pc.nc
    keys, w = heads_ref.shape[1], heads_ref.shape[2]
    tok = keys // nc
    rows = w1_ref.shape[0]
    cols = wout_ref.shape[1]
    load = pltpu.make_async_copy(heads_ref, qkv, local.at[0])
    load.start()
    pairs = [(w1_ref, bounce1, w1_out), (w2_ref, bounce2, w2_out), (wout_ref, bounce3, wout_out)]
    for i, (src, mid, _) in enumerate(pairs):
        pltpu.make_async_copy(src, mid, local.at[1 + i]).start()
    barrier(pc)
    items = [
        Gather(
            pc,
            lambda s, k, p: row_cut(w1_out.at[s], rows, k, p),
            lambda s, k, p: row_cut(w1_ref, rows, k, p),
            s1, r1,
        ),
        Gather(
            pc,
            lambda s, k, p: row_cut(w2_out.at[s], rows, k, p),
            lambda s, k, p: row_cut(w2_ref, rows, k, p),
            s2, r2,
        ),
        Gather(
            pc,
            lambda s, k, p: col_cut(wout_out.at[s], cols, k, p),
            lambda s, k, p: col_cut(wout_ref, cols, k, p),
            s3, r3,
        ),
    ]
    items[0].first()
    items[1].first()
    load.wait()
    for i, (src, mid, _) in enumerate(pairs):
        pltpu.make_async_copy(src, mid, local.at[1 + i]).wait()
    for i, (_, mid, dst) in enumerate(pairs):
        pltpu.make_async_copy(mid, dst.at[pc.d], local.at[1 + i]).start()
    nh = w // HEAD
    for h in range(nh):
        vext[h, :, :HEAD] = qkv[2, :, h * HEAD : (h + 1) * HEAD]
        vext[h, :, HEAD:] = jnp.ones((keys, HEAD), BF16)
    scale = HEAD ** (-0.5) * LOG2E

    def block_copy(i):
        to = (pc.c + i + 1) % nc
        at = pl.ds(pl.multiple_of(to * tok, tok), tok)
        return remote(
            o_ref.at[at], otok_out.at[pc.c], xsend.at[i], xrecv.at[i], (pc.d, to)
        )

    def block(i, _):
        at = pl.ds(pl.multiple_of(((pc.c + i + 1) % nc) * tok, tok), tok)
        for h in range(nh):
            hs = slice(h * HEAD, (h + 1) * HEAD)
            s = lax.dot_general(
                qkv[0, at, hs], qkv[1, :, hs], (((1,), (1,)), ((), ())),
                preferred_element_type=F32,
            )
            m = jnp.max(s, axis=1, keepdims=True)
            p = jnp.exp2(s * scale - m * scale).astype(BF16)
            ol = jnp.dot(p, vext[h], preferred_element_type=F32)
            total = ol[:, HEAD:]
            o_ref[at, hs] = (ol[:, :HEAD] / total).astype(BF16)
            lse = m * scale + jnp.log2(total)
            lse_ref[h, :, at] = jnp.transpose(jnp.concatenate([lse, lse], axis=1))[:8]

        @pl.when(i < nc - 1)
        def _():
            block_copy(i).start()

        return 0

    lax.fori_loop(0, nc, block, 0)
    own = pltpu.make_async_copy(
        o_ref.at[pl.ds(pl.multiple_of(pc.c * tok, tok), tok)], otok_out.at[pc.c], local.at[0]
    )
    own.start()
    items[0].relay()
    items[2].first()
    items[1].relay()
    items[0].cross()
    items[2].relay()
    items[1].cross()
    items[2].cross()
    for it in items:
        it.finish()

    def drain(i, _):
        got = otok_out.at[(pc.c + nc - i - 1) % nc]
        remote(got, got, xsend.at[i], xrecv.at[i], pc.sibling).wait_recv()
        block_copy(i).wait_send()
        return 0

    lax.fori_loop(0, nc - 1, drain, 0)
    own.wait()
    for i, (_, mid, dst) in enumerate(pairs):
        pltpu.make_async_copy(mid, dst.at[pc.d], local.at[1 + i]).wait()
    for it in items:
        it.sent()


def attend(heads, w1, w2, wout):
    nd, nc = lax.axis_size("dp"), lax.axis_size("ctx")
    _, keys, w = heads.shape
    nh = w // HEAD
    n = Gather.count(nd)
    dma = pltpu.SemaphoreType.DMA
    return pl.pallas_call(
        attend_kernel,
        out_shape=[
            S((nc, keys // nc, w), BF16),
            S((keys, w), BF16),
            S((nh, 8, keys), F32),
            S((nd,) + w1.shape, BF16),
            S((nd,) + w2.shape, BF16),
            S((nd,) + wout.shape, BF16),
        ],
        in_specs=[ANY, ANY, ANY, ANY],
        out_specs=[ANY, VMEM, VMEM, ANY, ANY, ANY],
        scratch_shapes=[
            pltpu.VMEM((3, keys, w), BF16),
            pltpu.VMEM((nh, keys, 2 * HEAD), BF16),
            pltpu.VMEM(w1.shape, BF16),
            pltpu.VMEM(w2.shape, BF16),
            pltpu.VMEM(wout.shape, BF16),
            dma((n,)), dma((n,)), dma((n,)), dma((n,)), dma((n,)), dma((n,)),
            dma((nc,)), dma((nc,)), dma((4,)),
        ],
        compiler_params=params(1),
        name="attend",
    )(heads, w1, w2, wout)


def attend_back_kernel(
    heads_ref, o_ref, lse_ref, dout_ref, cos_ref, sin_ref,
    dtok_out,
    qkv, dout, delta, dq, sendbuf,
    dsend, drecv, xsend, xrecv, local,
):
    pc = Place()
    nc = pc.nc
    keys, w = heads_ref.shape[1], heads_ref.shape[2]
    tok = keys // nc
    nh = w // HEAD
    load = pltpu.make_async_copy(heads_ref, qkv, local.at[0])
    load.start()
    barrier(pc, dp=False)
    mine = pl.ds(pl.multiple_of(pc.c * tok, tok), tok)
    for i in range(nc - 1):
        to = (pc.c + i + 1) % nc
        remote(dout_ref.at[to], dout.at[mine], dsend.at[i], drecv.at[i], (pc.d, to)).start()
    own = pltpu.make_async_copy(dout_ref.at[pc.c], dout.at[mine], local.at[1])
    own.start()
    dq[...] = jnp.zeros_like(dq)
    load.wait()
    own.wait()
    for i in range(nc - 1):
        src = (pc.c + nc - i - 1) % nc
        got = dout.at[pl.ds(pl.multiple_of(src * tok, tok), tok)]
        remote(got, got, dsend.at[i], drecv.at[i], pc.sibling).wait_recv()

    def deltas(i, _):
        at = pl.ds(pl.multiple_of(i * tok, tok), tok)
        t = jnp.transpose(o_ref[at, :].astype(F32) * dout[at, :].astype(F32))
        for h in range(nh):
            row = jnp.sum(t[h * HEAD : (h + 1) * HEAD], axis=0, keepdims=True)
            delta[h, :, at] = jnp.broadcast_to(row, (8, tok))
        return 0

    lax.fori_loop(0, nc, deltas, 0)
    scale = HEAD ** (-0.5)
    lane = lax.broadcasted_iota(jnp.int32, (1, w), 1)
    low = (lane % HEAD) < HEAD // 2

    def unrotate(g, at):
        t = g * sin_ref[at, :]
        if w == HEAD:
            up = jnp.concatenate([t[:, HEAD // 2 :], t[:, : HEAD // 2]], axis=1)
            down = up
        else:
            up = pltpu.roll(t, w - HEAD // 2, 1)
            down = pltpu.roll(t, HEAD // 2, 1)
        return g * cos_ref[at, :] + jnp.where(low, up, -down)

    def kv_copy(i):
        to = (pc.c + i + 1) % nc
        return remote(
            sendbuf.at[to, pl.ds(1, 2)], dtok_out.at[pc.c, pl.ds(1, 2)],
            xsend.at[0, i], xrecv.at[0, i], (pc.d, to),
        )

    def q_copy(i):
        to = (pc.c + i + 1) % nc
        return remote(
            sendbuf.at[to, 0], dtok_out.at[pc.c, 0], xsend.at[1, i], xrecv.at[1, i], (pc.d, to)
        )

    def block(i, _):
        to = (pc.c + i + 1) % nc
        at = pl.ds(pl.multiple_of(to * tok, tok), tok)
        dks, dvs = [], []
        for h in range(nh):
            hs = slice(h * HEAD, (h + 1) * HEAD)
            kb, vb = qkv[1, at, hs], qkv[2, at, hs]
            q, do = qkv[0, :, hs], dout[:, hs]
            nt = (((1,), (1,)), ((), ()))
            st = lax.dot_general(kb, q, nt, preferred_element_type=F32)
            p = jnp.exp2(st * (scale * LOG2E) - lse_ref[h, 0:1, :])
            dvs.append(jnp.dot(p.astype(BF16), do, preferred_element_type=F32))
            dp = lax.dot_general(vb, do, nt, preferred_element_type=F32)
            ds = (p * (dp - delta[h, 0:1, :])).astype(BF16)
            dks.append(jnp.dot(ds, q, preferred_element_type=F32))
            dq[:, hs] += lax.dot_general(
                ds, kb, (((0,), (0,)), ((), ())), preferred_element_type=F32
            )
        dk = jnp.concatenate(dks, axis=1) * scale
        sendbuf[to, 1] = unrotate(dk, at).astype(BF16)
        sendbuf[to, 2] = jnp.concatenate(dvs, axis=1).astype(BF16)

        @pl.when(i < nc - 1)
        def _():
            kv_copy(i).start()

        return 0

    lax.fori_loop(0, nc, block, 0)

    def q_block(i, _):
        to = (pc.c + i + 1) % nc
        at = pl.ds(pl.multiple_of(to * tok, tok), tok)
        sendbuf[to, 0] = unrotate(dq[at, :] * scale, at).astype(BF16)

        @pl.when(i < nc - 1)
        def _():
            q_copy(i).start()

        return 0

    lax.fori_loop(0, nc, q_block, 0)
    keep = pltpu.make_async_copy(sendbuf.at[pc.c], dtok_out.at[pc.c], local.at[1])
    keep.start()

    def drain(i, _):
        got = dtok_out.at[(pc.c + nc - i - 1) % nc]
        remote(
            got.at[pl.ds(1, 2)], got.at[pl.ds(1, 2)], xsend.at[0, i], xrecv.at[0, i], pc.sibling
        ).wait_recv()
        remote(got.at[0], got.at[0], xsend.at[1, i], xrecv.at[1, i], pc.sibling).wait_recv()
        kv_copy(i).wait_send()
        q_copy(i).wait_send()
        to = (pc.c + i + 1) % nc
        remote(
            dout_ref.at[to], dout.at[mine], dsend.at[i], drecv.at[i], (pc.d, to)
        ).wait_send()
        return 0

    lax.fori_loop(0, nc - 1, drain, 0)
    keep.wait()


def attend_back(heads, o, lse, dout, cosine, sine):
    nc = lax.axis_size("ctx")
    _, keys, w = heads.shape
    nh = w // HEAD
    tok = keys // nc
    dma = pltpu.SemaphoreType.DMA
    return pl.pallas_call(
        attend_back_kernel,
        out_shape=S((nc, 3, tok, w), BF16),
        in_specs=[ANY, VMEM, VMEM, ANY, VMEM, VMEM],
        out_specs=ANY,
        scratch_shapes=[
            pltpu.VMEM((3, keys, w), BF16),
            pltpu.VMEM((keys, w), BF16),
            pltpu.VMEM((nh, 8, keys), F32),
            pltpu.VMEM((keys, w), F32),
            pltpu.VMEM((nc, 3, tok, w), BF16),
            dma((nc,)), dma((nc,)), dma((2, nc)), dma((2, nc)), dma((2,)),
        ],
        compiler_params=params(2),
        name="attend_back",
    )(heads, o, lse, dout, cosine, sine)


def norm_rows(values, gain):
    row_mean = jnp.mean(values, axis=-1, keepdims=True)
    centred = values - row_mean
    row_var = jnp.mean(centred * centred, axis=-1, keepdims=True)
    return centred * lax.rsqrt(row_var + norm_eps) * gain


def gelu_exact(values):
    return 0.5 * values * (1.0 + lax.erf(values * 0.7071067811865476))


def gelu_slope(values):
    return (
        0.5 * (1.0 + lax.erf(values * 0.7071067811865476))
        + values * jnp.exp(-0.5 * values * values) * 0.3989422804014327
    )


def rope_angles(positions, lanes):
    half = HEAD // 2
    freq = rope_theta ** (-(jnp.arange(half, dtype=F32) * 2.0 / HEAD))
    freq = jnp.tile(freq, lanes // half)
    return positions.astype(F32)[:, None] * freq[None, :]


def on_device(
    tokens,
    norm1_gain,
    qkv_weight,
    attn_out_weight,
    norm2_gain,
    mlp_in_weight,
    mlp_out_weight,
    cotangent,
):
    _, tok, width = tokens.shape
    nc, nd = lax.axis_size("ctx"), lax.axis_size("dp")
    keys = tok * nc
    w = width // nc
    ff = mlp_in_weight.shape[1] // 2
    rows = norm1_gain.shape[0]
    x = tokens.reshape(tok, width)
    upstream = cotangent.reshape(tok, width)
    gains = jnp.concatenate(
        [
            norm1_gain.astype(F32)[None],
            norm2_gain.astype(F32)[None],
            jnp.zeros((6, rows), F32),
        ]
    )
    ang = rope_angles(lax.axis_index("ctx") * tok + jnp.arange(tok, dtype=jnp.int32), 2 * w)
    sign = jnp.where(jnp.arange(2 * w) % HEAD < HEAD // 2, -1.0, 1.0).astype(F32)
    h1, gains_all, wqkv, wattn, heads = project(
        x, gains, jnp.cos(ang), jnp.sin(ang) * sign[None], qkv_weight, attn_out_weight
    )
    w1s, w2s = mlp_in_weight[:, :ff], mlp_in_weight[:, ff:]
    otok, o_heads, lse, w1, w2, wout = attend(heads, w1s, w2s, mlp_out_weight)
    wattn = wattn.reshape(width, width)
    w1 = w1.reshape(width, ff)
    w2 = w2.reshape(width, ff)
    wout = wout.reshape(ff, width)
    gain_one = gains_all[:, 0].reshape(width)
    gain_two = gains_all[:, 1].reshape(width)

    attended_b = jnp.transpose(otok, (1, 0, 2)).reshape(tok, width)
    inputs_f = x.astype(F32)
    attn_res = inputs_f + jnp.dot(attended_b, wattn, preferred_element_type=F32)
    normed_two = norm_rows(attn_res, gain_two).astype(BF16)
    gelu_in = jnp.dot(normed_two, w1, preferred_element_type=F32)
    gate_in = jnp.dot(normed_two, w2, preferred_element_type=F32)
    activated = (gelu_exact(gelu_in) * gate_in).astype(BF16)
    layer_out = (attn_res + jnp.dot(activated, wout, preferred_element_type=F32)).astype(BF16)
    grad_out = jnp.einsum("nf,nd->fd", activated, upstream, preferred_element_type=F32)
    grad_act = jnp.dot(upstream, wout.T, preferred_element_type=F32)
    dl1 = (grad_act * gate_in * gelu_slope(gelu_in)).astype(BF16)
    dl2 = (grad_act * gelu_exact(gelu_in)).astype(BF16)
    grad_in = jnp.concatenate(
        [
            jnp.einsum("nd,ne->de", normed_two, dl1, preferred_element_type=F32),
            jnp.einsum("nd,ne->de", normed_two, dl2, preferred_element_type=F32),
        ],
        axis=1,
    )
    grad_normed_two = jnp.dot(dl1, w1.T, preferred_element_type=F32) + jnp.dot(
        dl2, w2.T, preferred_element_type=F32
    )
    _, pull_two = jax.vjp(norm_rows, attn_res, gain_two)
    grad_res_norm, grad_gain_two = pull_two(grad_normed_two)
    grad_res = upstream.astype(F32) + grad_res_norm
    grad_res_b = grad_res.astype(BF16)
    grad_attn = jnp.einsum("nd,ne->de", attended_b, grad_res_b, preferred_element_type=F32)
    dout = jnp.dot(grad_res_b, wattn.T, preferred_element_type=F32).astype(BF16)
    dout = jnp.transpose(dout.reshape(tok, nc, w), (1, 0, 2))

    ang_all = rope_angles(jnp.arange(keys, dtype=jnp.int32), w)
    dtok = attend_back(heads, o_heads, lse, dout, jnp.cos(ang_all), jnp.sin(ang_all))
    grad_proj = jnp.transpose(dtok, (2, 1, 0, 3)).reshape(tok, 3 * width)
    wqkv = wqkv.reshape(3, width, width)
    grad_qkv = jnp.einsum("nd,ne->de", h1, grad_proj, preferred_element_type=F32)
    grad_normed_one = jnp.einsum(
        "ngc,gdc->nd", grad_proj.reshape(tok, 3, width), wqkv, preferred_element_type=F32
    )
    _, pull_one = jax.vjp(norm_rows, inputs_f, gain_one)
    grad_in_norm, grad_gain_one = pull_one(grad_normed_one)
    input_grad = (grad_res + grad_in_norm).astype(BF16)

    def total(part):
        part = lax.psum_scatter(part.astype(BF16), "dp", scatter_dimension=0, tiled=True)
        return lax.psum(part, "ctx").astype(F32)

    return (
        layer_out.reshape(1, tok, width),
        input_grad.reshape(1, tok, width),
        total(grad_gain_one.reshape(nd, rows)).reshape(rows),
        total(grad_qkv),
        total(grad_attn),
        total(grad_gain_two.reshape(nd, rows)).reshape(rows),
        total(grad_in),
        total(grad_out),
    )


def solution(mesh):
    in_specs = (
        P("dp", "ctx", None),
        P("dp"),
        P("dp", None),
        P("dp", None),
        P("dp"),
        P("dp", None),
        P("dp", None),
        P("dp", "ctx", None),
    )
    out_specs = (
        P("dp", "ctx", None),
        P("dp", "ctx", None),
        P("dp"),
        P("dp", None),
        P("dp", None),
        P("dp"),
        P("dp", None),
        P("dp", None),
    )
    return jax.shard_map(
        on_device, mesh=mesh, in_specs=in_specs, out_specs=out_specs, check_vma=False
    )
```

```python
import functools

import jax
import jax.numpy as jnp
from jax import lax
from jax.experimental import pallas as pl
from jax.experimental.pallas import tpu as pltpu
from jax.sharding import PartitionSpec as P

HEAD = 64
norm_eps = 1e-05
rope_theta = 160000.0
F32 = jnp.float32
BF16 = jnp.bfloat16
MESH = pl.DeviceIdType.MESH
LOG2E = 1.4426950408889634
VMEM_LIMIT = 64 * 1024 * 1024 - 65536
ANY = pl.BlockSpec(memory_space=pl.ANY)
VMEM = pl.BlockSpec(memory_space=pltpu.VMEM)
S = jax.ShapeDtypeStruct


def params(cid):
    return pltpu.CompilerParams(
        collective_id=cid, has_side_effects=True, vmem_limit_bytes=VMEM_LIMIT
    )


class Place:
    def __init__(self):
        self.nd = lax.axis_size("dp")
        self.nc = lax.axis_size("ctx")
        self.d = lax.axis_index("dp")
        self.c = lax.axis_index("ctx")
        self.nb = 2 if self.nd % 2 == 0 else 1
        self.na = self.nd // self.nb
        self.a = self.d // self.nb
        self.b = self.d % self.nb
        self.nz = self.nc // 2
        self.z = self.c // 2
        self.k = self.c % 2
        self.sibling = (self.d, self.z * 2 + 1 - self.k)

    def shard(self, da, db):
        return ((self.a + da) % self.na) * self.nb + (self.b + db) % self.nb

    def at(self, da, db):
        return (self.shard(da, db), self.c)


def barrier(pc, dp=True, ctx=True):
    sem = pltpu.get_barrier_semaphore()
    count = 0
    if dp:
        for t in range(1, pc.nd):
            pl.semaphore_signal(
                sem, inc=1, device_id=((pc.d + t) % pc.nd, pc.c), device_id_type=MESH
            )
            count += 1
    if ctx:
        for t in range(1, pc.nc):
            pl.semaphore_signal(
                sem, inc=1, device_id=(pc.d, (pc.c + t) % pc.nc), device_id_type=MESH
            )
            count += 1
    pl.semaphore_wait(sem, count)


def remote(src, dst, send, recv, target):
    return pltpu.make_async_remote_copy(
        src_ref=src,
        dst_ref=dst,
        send_sem=send,
        recv_sem=recv,
        device_id=target,
        device_id_type=MESH,
    )


class Gather:
    def __init__(self, pc, cut, own, send, recv):
        self.pc, self.cut, self.own, self.send, self.recv = pc, cut, own, send, recv

    @staticmethod
    def count(nd):
        nb = 2 if nd % 2 == 0 else 1
        na = nd // nb
        return 2 * ((na - 1) + (nb - 1) + 2 * (na - 1) * (nb - 1))

    def slots(self):
        pc = self.pc
        lines = [(da, 0) for da in range(1, pc.na)] + [(0, db) for db in range(1, pc.nb)]
        cross = [
            (da, db, part)
            for part in (0, 1)
            for da in range(1, pc.na)
            for db in range(1, pc.nb)
        ]
        return lines, cross

    def _copy(self, index, shard, part, target, own=False):
        src = (self.own if own else self.cut)(shard, self.pc.k, part)
        dst = self.cut(shard, self.pc.k, part)
        return remote(src, dst, self.send.at[index], self.recv.at[index], target)

    def _arrived(self, index, shard, core, part, wait=True):
        ref = self.cut(shard, core, part)
        return remote(ref, ref, self.send.at[index], self.recv.at[index], self.pc.sibling)

    def first(self):
        pc = self.pc
        lines, _ = self.slots()
        for i, (da, db) in enumerate(lines):
            self._copy(i, pc.d, None, pc.at(-da, -db), own=True).start()

    def relay(self):
        pc = self.pc
        lines, cross = self.slots()
        n = len(lines) + len(cross)
        for i, (da, db) in enumerate(lines):
            shard = pc.shard(da, db)
            self._arrived(i, shard, pc.k, None).wait_recv()
            for j, (xa, xb, part) in enumerate(cross):
                if part == 0 and db == 0 and xa == da:
                    self._copy(len(lines) + j, shard, part, pc.at(0, -xb)).start()
                if part == 1 and da == 0 and xb == db:
                    self._copy(len(lines) + j, shard, part, pc.at(-xa, 0)).start()
            self._copy(n + i, shard, None, pc.sibling).start()

    def cross(self):
        pc = self.pc
        lines, cross = self.slots()
        n = len(lines) + len(cross)
        for j, (xa, xb, part) in enumerate(cross):
            shard = pc.shard(xa, xb)
            self._arrived(len(lines) + j, shard, pc.k, part).wait_recv()
            self._copy(n + len(lines) + j, shard, part, pc.sibling).start()

    def finish(self):
        pc = self.pc
        lines, cross = self.slots()
        n = len(lines) + len(cross)
        for i, (da, db) in enumerate(lines):
            self._arrived(n + i, pc.shard(da, db), 1 - pc.k, None).wait_recv()
        for j, (xa, xb, part) in enumerate(cross):
            self._arrived(n + len(lines) + j, pc.shard(xa, xb), 1 - pc.k, part).wait_recv()

    def sent(self):
        pc = self.pc
        lines, cross = self.slots()
        n = len(lines) + len(cross)
        for i, _ in enumerate(lines):
            self._arrived(i, pc.d, pc.k, None).wait_send()
            self._arrived(n + i, pc.d, pc.k, None).wait_send()
        for j, (_, _, part) in enumerate(cross):
            self._arrived(len(lines) + j, pc.d, pc.k, part).wait_send()
            self._arrived(n + len(lines) + j, pc.d, pc.k, part).wait_send()


def row_cut(ref, rows, core, part, lead=0):
    start = core * (rows // 2) + (0 if part is None else part * (rows // 4))
    size = rows // 2 if part is None else rows // 4
    return ref.at[(slice(None),) * lead + (pl.ds(start, size),)]


def col_cut(ref, cols, core, part):
    start = core * (cols // 2) + (0 if part is None else part * (cols // 4))
    size = cols // 2 if part is None else cols // 4
    return ref.at[:, pl.ds(pl.multiple_of(start, 128), size)]


class Reduce:
    def __init__(self, pc, g, bufs, send, recv, by_rows):
        self.pc, self.g, self.send, self.recv, self.by_rows = pc, g, send, recv, by_rows
        self.r1a, self.r1b, self.r2a, self.r2b = bufs

    @staticmethod
    def count(nd):
        nb = 2 if nd % 2 == 0 else 1
        return 2 * (nd // nb - 1 + nb - 1)

    @staticmethod
    def scratch(nd, rows, cols, by_rows):
        nb = 2 if nd % 2 == 0 else 1
        na = nd // nb
        r, c = (rows // 2, cols) if by_rows else (rows, cols // 2)
        return [
            pltpu.VMEM((na, nb, rows, cols), BF16),
            pltpu.VMEM((na - 1, nb, r, c), BF16),
            pltpu.VMEM((nb - 1, na, r, c), BF16),
            pltpu.VMEM((nb - 1, r, c), BF16),
            pltpu.VMEM((na - 1, r, c), BF16),
        ]

    def part(self, ref, p):
        lead = (slice(None),) * (len(ref.shape) - 2)
        rows, cols = ref.shape[-2:]
        if self.by_rows:
            return ref.at[lead + (pl.ds(p * (rows // 2), rows // 2),)]
        return ref.at[lead + (slice(None), pl.ds(p * (cols // 2), cols // 2))]

    def copies(self, step):
        pc = self.pc
        na, nb = pc.na, pc.nb
        out = []
        base = 0 if step == 1 else na - 1 + nb - 1
        for da in range(1, na):
            a = (pc.a + na - da) % na
            i = base + da - 1
            if step == 1:
                src, dst = self.part(self.g.at[a], 0), self.r1a.at[da - 1]
            else:
                src, dst = self.part(self.g.at[a, pc.b], 1), self.r2b.at[da - 1]
            out.append(remote(src, dst, self.send.at[i], self.recv.at[i], pc.at(-da, 0)))
        for db in range(1, nb):
            b = (pc.b + nb - db) % nb
            i = base + na - 1 + db - 1
            if step == 1:
                src, dst = self.part(self.g.at[:, b], 1), self.r1b.at[db - 1]
            else:
                src, dst = self.part(self.g.at[pc.a, b], 0), self.r2a.at[db - 1]
            out.append(remote(src, dst, self.send.at[i], self.recv.at[i], pc.at(0, -db)))
        return out

    def start(self):
        for cp in self.copies(1):
            cp.start()

    def middle(self):
        pc = self.pc
        for cp in self.copies(1):
            cp.wait_recv()
        for b in range(pc.nb):
            at = self.part(self.g.at[pc.a, b], 0)
            add(at, [self.r1a.at[i, b] for i in range(pc.na - 1)])
        for a in range(pc.na):
            at = self.part(self.g.at[a, pc.b], 1)
            add(at, [self.r1b.at[i, a] for i in range(pc.nb - 1)])
        for cp in self.copies(2):
            cp.start()

    def finish(self, total):
        pc = self.pc
        for cp in self.copies(2):
            cp.wait_recv()
        own = self.g.at[pc.a, pc.b]
        add(self.part(own, 0), [self.r2a.at[i] for i in range(pc.nb - 1)], self.part(total, 0))
        add(self.part(own, 1), [self.r2b.at[i] for i in range(pc.na - 1)], self.part(total, 1))

    def sent(self):
        for cp in self.copies(1) + self.copies(2):
            cp.wait_send()


def add(ref, others, into=None):
    total = ref[...].astype(F32)
    for o in others:
        total = total + o[...].astype(F32)
    into = ref if into is None else into
    into[...] = total.astype(BF16)


class Chain:
    def __init__(self, pc, t, bufs, send, recv, part):
        self.pc, self.t, self.part = pc, t, part
        self.outer, self.swap, self.total, self.other = bufs
        self.send, self.recv = send, recv
        half = pc.nz // 2
        self.low = pc.z < half
        self.end = (pc.z == 0) | (pc.z == pc.nz - 1)
        self.mid = (pc.z == half - 1) | (pc.z == half)
        step = 1 - 2 * (pc.z // half)
        self.inner_id = (pc.d, ((pc.z + step + pc.nz) % pc.nz) * 2 + pc.k)
        self.outer_id = (pc.d, ((pc.z - step + pc.nz) % pc.nz) * 2 + pc.k)

    def up_copy(self, p):
        return remote(
            self.part(self.t, p), self.part(self.outer, p), self.send.at[0, p], self.recv.at[0, p],
            self.inner_id,
        )

    def swap_copy(self, p):
        return remote(
            self.part(self.t, p), self.part(self.swap, p), self.send.at[1, p], self.recv.at[1, p],
            self.inner_id,
        )

    def down_copy(self, p):
        at = self.part(self.total, p)
        return remote(at, at, self.send.at[2, p], self.recv.at[2, p], self.outer_id)

    def side_copy(self, p):
        return remote(
            self.part(self.total, p), self.part(self.other, p), self.send.at[3, p],
            self.recv.at[3, p], self.pc.sibling,
        )

    def open(self, p):
        @pl.when(self.end)
        def _():
            @pl.when(self.mid)
            def _():
                self.swap_copy(p).start()

            @pl.when(jnp.logical_not(self.mid))
            def _():
                self.up_copy(p).start()

    def up(self, p):
        @pl.when(jnp.logical_not(self.end))
        def _():
            self.up_copy(p).wait_recv()
            add(self.part(self.t, p), [self.part(self.outer, p)])

            @pl.when(self.mid)
            def _():
                self.swap_copy(p).start()

            @pl.when(jnp.logical_not(self.mid))
            def _():
                self.up_copy(p).start()

    def turn(self, p):
        @pl.when(self.mid)
        def _():
            self.swap_copy(p).wait_recv()
            add(self.part(self.t, p), [self.part(self.swap, p)], self.part(self.total, p))

        @pl.when(jnp.logical_not(self.mid))
        def _():
            self.down_copy(p).wait_recv()

        @pl.when(jnp.logical_not(self.end))
        def _():
            self.down_copy(p).start()

        self.side_copy(p).start()

    def sent(self, p):
        @pl.when(self.mid)
        def _():
            self.swap_copy(p).wait_send()

        @pl.when(jnp.logical_not(self.mid))
        def _():
            self.up_copy(p).wait_send()

        @pl.when(jnp.logical_not(self.end))
        def _():
            self.down_copy(p).wait_send()

        self.side_copy(p).wait_send()


def half_rows(pc, ref, core):
    rows = ref.shape[0] // pc.nd
    h = rows // 2
    return [ref.at[pl.ds(pl.multiple_of(s * rows + core * h, h), h)] for s in range(pc.nd)]


def project_kernel(
    x_ref, gains_ref, cos_ref, sin_ref, wqkv_ref, wattn_ref, win_ref,
    h1t_ref, gains_out, w1_out, w2_out, wqkv_out, wattn_out, heads_out,
    wbuf, abuf, ibuf, h1_ref, gbuf, sendbuf,
    wsend, wrecv, asend, arecv, gsend, grecv, xsend, xrecv, local,
):
    pc = Place()
    nd, nc, nz = pc.nd, pc.nc, pc.nz
    rows = wqkv_ref.shape[0]
    width = wqkv_ref.shape[1] // 3
    tok = x_ref.shape[0]
    w = width // nc
    cw = 2 * w
    own_w = [
        pltpu.make_async_copy(
            wqkv_ref.at[:, pl.ds(g * width, width)], wbuf.at[g, pc.d], local.at[g]
        )
        for g in range(3)
    ]
    for cp in own_w:
        cp.start()
    own_a = pltpu.make_async_copy(wattn_ref, abuf, local.at[3])
    own_a.start()
    own_i = pltpu.make_async_copy(win_ref, ibuf, local.at[5 + nz])
    own_i.start()
    barrier(pc)
    for cp in own_w:
        cp.wait()

    def chip_of(j):
        return (pc.z + j + 1) % nz

    def chunk(j):
        col = pl.multiple_of(chip_of(j) * cw, cw)

        def cut(shard, core, part):
            return row_cut(wbuf.at[:, shard, :, pl.ds(col, cw)], rows, core, part, lead=1)

        return Gather(pc, cut, cut, wsend.at[j], wrecv.at[j])

    def attn_cut(shard, core, part):
        return row_cut(wattn_out.at[shard], rows, core, part)

    def attn_own(shard, core, part):
        return row_cut(wattn_ref, rows, core, part)

    attn = Gather(pc, attn_cut, attn_own, asend, arecv)

    gain_copies = []
    gbuf[pc.d] = gains_ref[...]
    for t in range(1, nd):
        gain_copies.append(
            remote(
                gains_ref, gbuf.at[pc.d], gsend.at[t], grecv.at[t], ((pc.d + t) % nd, pc.c)
            )
        )
        gain_copies[-1].start()
    chunk(0).first()
    if nz > 1:
        chunk(1).first()

    xf = x_ref[...].astype(F32)
    mean = jnp.mean(xf, axis=-1, keepdims=True)
    cen = xf - mean
    var = jnp.mean(cen * cen, axis=-1, keepdims=True)
    hat = cen * lax.rsqrt(var + norm_eps)
    for t in range(1, nd):
        src = gbuf.at[(pc.d + nd - t) % nd]
        remote(src, src, gsend.at[t], grecv.at[t], pc.sibling).wait_recv()
    for s in range(nd):
        cols = slice(s * rows, (s + 1) * rows)
        h1_ref[:, cols] = (hat[:, cols] * gbuf[s, 0:1, :]).astype(BF16)
    gains_out[...] = gbuf[...]
    own_a.wait()
    own_a2 = pltpu.make_async_copy(abuf, wattn_out.at[pc.d], local.at[3])
    own_a2.start()
    own_i.wait()
    ff = w1_out.shape[1]
    w1_out[...] = ibuf[:, :ff]
    w2_out[...] = ibuf[:, ff:]
    h1t_ref[...] = jnp.transpose(h1_ref[...])

    lane = lax.broadcasted_iota(jnp.int32, (1, cw), 1)
    low = (lane % HEAD) < HEAD // 2

    def out_copy(j):
        cols = pl.ds(pl.multiple_of(chip_of(j) * cw, cw), cw)
        return pltpu.make_async_copy(
            wbuf.at[:, :, :, cols], wqkv_out.at[:, :, :, cols], local.at[4 + j]
        )

    def place(ref):
        return ref.at[:, pl.ds(pl.multiple_of(pc.c * tok, tok), tok), :]

    def exchange(j, kk):
        return remote(
            sendbuf.at[j, kk], place(heads_out), xsend.at[j, kk], xrecv.at[j, pc.k],
            (pc.d, chip_of(j) * 2 + kk),
        )

    def step(j, _):
        g = chunk(j)
        g.relay()

        @pl.when(j + 2 < nz)
        def _():
            chunk(j + 2).first()

        @pl.when(j + 2 == nz)
        def _():
            attn.first()

        g.cross()
        g.finish()
        out_copy(j).start()
        cols = pl.ds(pl.multiple_of(chip_of(j) * cw, cw), cw)
        for part in range(3):
            weight = wbuf[part, :, :, cols].reshape(nd * rows, cw)
            proj = jnp.dot(h1_ref[...], weight, preferred_element_type=F32)
            if part < 2:
                up = pltpu.roll(proj, cw - HEAD // 2, 1)
                down = pltpu.roll(proj, HEAD // 2, 1)
                proj = proj * cos_ref[...] + jnp.where(low, up, down) * sin_ref[...]
            proj = proj.astype(BF16)
            for kk in range(2):
                sendbuf[j, kk, part] = proj[:, kk * w : (kk + 1) * w]

        @pl.when(j < nz - 1)
        def _():
            exchange(j, 0).start()
            exchange(j, 1).start()

        return 0

    lax.fori_loop(0, nz, step, 0)
    last = nz - 1
    remote(
        sendbuf.at[last, 1 - pc.k], place(heads_out), xsend.at[last, 1 - pc.k],
        xrecv.at[last, pc.k], pc.sibling,
    ).start()
    own_x = pltpu.make_async_copy(
        sendbuf.at[last, pc.k], place(heads_out), local.at[4 + nz]
    )
    own_x.start()
    attn.relay()
    attn.cross()
    attn.finish()

    def arrival(j, kk):
        ref = sendbuf.at[j, kk]
        return remote(ref, ref, xsend.at[j, kk], xrecv.at[j, kk], pc.sibling)

    def drain(j, _):
        arrival(j, 0).wait_recv()
        arrival(j, 1).wait_recv()
        arrival(j, 0).wait_send()
        arrival(j, 1).wait_send()
        chunk(j).sent()
        out_copy(j).wait()
        return 0

    lax.fori_loop(0, nz - 1, drain, 0)
    arrival(last, 1 - pc.k).wait_recv()
    arrival(last, 1 - pc.k).wait_send()
    chunk(last).sent()
    out_copy(last).wait()
    own_x.wait()
    own_a2.wait()
    attn.sent()
    for cp in gain_copies:
        cp.wait_send()


def project(x, gains, cosine, sine, wqkv, wattn, win):
    nd, nc = lax.axis_size("dp"), lax.axis_size("ctx")
    nz = nc // 2
    tok, width = x.shape
    rows = wqkv.shape[0]
    w = width // nc
    n = Gather.count(nd)
    dma = pltpu.SemaphoreType.DMA
    return pl.pallas_call(
        project_kernel,
        out_shape=[
            S((width, tok), BF16),
            S((nd, 8, rows), F32),
            S((rows, win.shape[1] // 2), BF16),
            S((rows, win.shape[1] // 2), BF16),
            S((3, nd, rows, width), BF16),
            S((nd, rows, width), BF16),
            S((3, nc * tok, w), BF16),
        ],
        in_specs=[VMEM, VMEM, VMEM, VMEM, ANY, ANY, ANY],
        out_specs=[VMEM, VMEM, VMEM, VMEM, ANY, ANY, ANY],
        scratch_shapes=[
            pltpu.VMEM((3, nd, rows, width), BF16),
            pltpu.VMEM((rows, width), BF16),
            pltpu.VMEM(win.shape, BF16),
            pltpu.VMEM((tok, width), BF16),
            pltpu.VMEM((nd, 8, rows), F32),
            pltpu.VMEM((nz, 2, 3, tok, w), BF16),
            dma((nz, n)), dma((nz, n)), dma((n,)), dma((n,)),
            dma((nd,)), dma((nd,)), dma((nz, 2)), dma((nz, 2)), dma((6 + nz,)),
        ],
        compiler_params=params(0),
        name="project",
    )(x, gains, cosine, sine, wqkv, wattn, win)


def attend_kernel(
    heads_ref, w1_ref, w2_ref, wout_ref,
    otok_out, o_ref, lse_ref, w1_out, w2_out, wout_out,
    qkv, vext, bounce1, bounce2, bounce3,
    s1, r1, s2, r2, s3, r3, xsend, xrecv, local,
):
    pc = Place()
    nd, nc = pc.nd, pc.nc
    keys, w = heads_ref.shape[1], heads_ref.shape[2]
    tok = keys // nc
    rows = w1_ref.shape[0]
    cols = wout_ref.shape[1]
    load = pltpu.make_async_copy(heads_ref, qkv, local.at[0])
    load.start()
    pairs = [(w1_ref, bounce1, w1_out), (w2_ref, bounce2, w2_out), (wout_ref, bounce3, wout_out)]
    for i, (src, mid, _) in enumerate(pairs):
        pltpu.make_async_copy(src, mid, local.at[1 + i]).start()
    barrier(pc)
    items = [
        Gather(
            pc,
            lambda s, k, p: row_cut(w1_out.at[s], rows, k, p),
            lambda s, k, p: row_cut(w1_ref, rows, k, p),
            s1, r1,
        ),
        Gather(
            pc,
            lambda s, k, p: row_cut(w2_out.at[s], rows, k, p),
            lambda s, k, p: row_cut(w2_ref, rows, k, p),
            s2, r2,
        ),
        Gather(
            pc,
            lambda s, k, p: col_cut(wout_out.at[s], cols, k, p),
            lambda s, k, p: col_cut(wout_ref, cols, k, p),
            s3, r3,
        ),
    ]
    items[0].first()
    items[1].first()
    load.wait()
    for i, (src, mid, _) in enumerate(pairs):
        pltpu.make_async_copy(src, mid, local.at[1 + i]).wait()
    for i, (_, mid, dst) in enumerate(pairs):
        pltpu.make_async_copy(mid, dst.at[pc.d], local.at[1 + i]).start()
    nh = w // HEAD
    for h in range(nh):
        vext[h, :, :HEAD] = qkv[2, :, h * HEAD : (h + 1) * HEAD]
        vext[h, :, HEAD:] = jnp.ones((keys, HEAD), BF16)
    scale = HEAD ** (-0.5) * LOG2E

    def block_copy(i):
        to = (pc.c + i + 1) % nc
        at = pl.ds(pl.multiple_of(to * tok, tok), tok)
        return remote(
            o_ref.at[at], otok_out.at[pc.c], xsend.at[i], xrecv.at[i], (pc.d, to)
        )

    def block(i, _):
        at = pl.ds(pl.multiple_of(((pc.c + i + 1) % nc) * tok, tok), tok)
        for h in range(nh):
            hs = slice(h * HEAD, (h + 1) * HEAD)
            s = lax.dot_general(
                qkv[0, at, hs], qkv[1, :, hs], (((1,), (1,)), ((), ())),
                preferred_element_type=F32,
            )
            m = jnp.max(s, axis=1, keepdims=True)
            p = jnp.exp2(s * scale - m * scale).astype(BF16)
            ol = jnp.dot(p, vext[h], preferred_element_type=F32)
            total = ol[:, HEAD:]
            o_ref[at, hs] = (ol[:, :HEAD] / total).astype(BF16)
            lse = m * scale + jnp.log2(total)
            lse_ref[h, :, at] = jnp.transpose(jnp.concatenate([lse, lse], axis=1))[:8]

        @pl.when(i < nc - 1)
        def _():
            block_copy(i).start()

        return 0

    lax.fori_loop(0, nc, block, 0)
    own = pltpu.make_async_copy(
        o_ref.at[pl.ds(pl.multiple_of(pc.c * tok, tok), tok)], otok_out.at[pc.c], local.at[0]
    )
    own.start()
    items[0].relay()
    items[2].first()
    items[1].relay()
    items[0].cross()
    items[2].relay()
    items[1].cross()
    items[2].cross()
    for it in items:
        it.finish()

    def drain(i, _):
        got = otok_out.at[(pc.c + nc - i - 1) % nc]
        remote(got, got, xsend.at[i], xrecv.at[i], pc.sibling).wait_recv()
        block_copy(i).wait_send()
        return 0

    lax.fori_loop(0, nc - 1, drain, 0)
    own.wait()
    for i, (_, mid, dst) in enumerate(pairs):
        pltpu.make_async_copy(mid, dst.at[pc.d], local.at[1 + i]).wait()
    for it in items:
        it.sent()


def attend(heads, w1, w2, wout):
    nd, nc = lax.axis_size("dp"), lax.axis_size("ctx")
    _, keys, w = heads.shape
    nh = w // HEAD
    n = Gather.count(nd)
    dma = pltpu.SemaphoreType.DMA
    return pl.pallas_call(
        attend_kernel,
        out_shape=[
            S((nc, keys // nc, w), BF16),
            S((keys, w), BF16),
            S((nh, 8, keys), F32),
            S((nd,) + w1.shape, BF16),
            S((nd,) + w2.shape, BF16),
            S((nd,) + wout.shape, BF16),
        ],
        in_specs=[ANY, ANY, ANY, ANY],
        out_specs=[ANY, VMEM, VMEM, ANY, ANY, ANY],
        scratch_shapes=[
            pltpu.VMEM((3, keys, w), BF16),
            pltpu.VMEM((nh, keys, 2 * HEAD), BF16),
            pltpu.VMEM(w1.shape, BF16),
            pltpu.VMEM(w2.shape, BF16),
            pltpu.VMEM(wout.shape, BF16),
            dma((n,)), dma((n,)), dma((n,)), dma((n,)), dma((n,)), dma((n,)),
            dma((nc,)), dma((nc,)), dma((4,)),
        ],
        compiler_params=params(1),
        name="attend",
    )(heads, w1, w2, wout)


def attend_back_kernel(
    heads_ref, o_ref, lse_ref, dout_ref, cos_ref, sin_ref, h2t_ref, dl1_ref, dl2_ref,
    dtok_out, t1_ref, t2_ref,
    qkv, dout, delta, dq, sendbuf, h2t, dl,
    ga, ra0, ra1, ra2, ra3, gb, rb0, rb1, rb2, rb3,
    dsend, drecv, xsend, xrecv, ssend, srecv, asend, arecv, bsend, brecv, local,
):
    pc = Place()
    nd = pc.nd
    nc = pc.nc
    keys, w = heads_ref.shape[1], heads_ref.shape[2]
    tok = keys // nc
    nh = w // HEAD
    load = pltpu.make_async_copy(heads_ref, qkv, local.at[0])
    load.start()
    mine_t = half_rows(pc, h2t_ref, pc.k)
    hers_t = half_rows(pc, h2t_ref, 1 - pc.k)
    fetch = [pltpu.make_async_copy(mine_t[s], h2t.at[0, s], local.at[2 + s]) for s in range(nd)]
    fetch.append(pltpu.make_async_copy(dl1_ref, dl.at[0, 0], local.at[2 + nd]))
    fetch.append(pltpu.make_async_copy(dl2_ref, dl.at[1, 0], local.at[3 + nd]))
    for cp in fetch:
        cp.start()
    barrier(pc)
    swap = [
        remote(hers_t[s], h2t.at[1, s], ssend.at[s], srecv.at[s], pc.sibling) for s in range(nd)
    ]
    swap.append(remote(dl1_ref, dl.at[0, 1], ssend.at[nd], srecv.at[nd], pc.sibling))
    swap.append(remote(dl2_ref, dl.at[1, 1], ssend.at[nd + 1], srecv.at[nd + 1], pc.sibling))
    for cp in swap:
        cp.start()
    mine = pl.ds(pl.multiple_of(pc.c * tok, tok), tok)
    for i in range(nc - 1):
        to = (pc.c + i + 1) % nc
        remote(dout_ref.at[to], dout.at[mine], dsend.at[i], drecv.at[i], (pc.d, to)).start()
    own = pltpu.make_async_copy(dout_ref.at[pc.c], dout.at[mine], local.at[1])
    own.start()
    ra = Reduce(pc, ga, (ra0, ra1, ra2, ra3), asend, arecv, True)
    rb = Reduce(pc, gb, (rb0, rb1, rb2, rb3), bsend, brecv, True)
    for cp in fetch:
        cp.wait()
    for cp in swap[: nd + 1]:
        cp.wait_recv()
    weight_grad(pc, ga, h2t, dl.at[0])
    ra.start()
    swap[nd + 1].wait_recv()
    weight_grad(pc, gb, h2t, dl.at[1])
    rb.start()
    dq[...] = jnp.zeros_like(dq)
    load.wait()
    own.wait()
    for i in range(nc - 1):
        src = (pc.c + nc - i - 1) % nc
        got = dout.at[pl.ds(pl.multiple_of(src * tok, tok), tok)]
        remote(got, got, dsend.at[i], drecv.at[i], pc.sibling).wait_recv()

    def deltas(i, _):
        at = pl.ds(pl.multiple_of(i * tok, tok), tok)
        t = jnp.transpose(o_ref[at, :].astype(F32) * dout[at, :].astype(F32))
        for h in range(nh):
            row = jnp.sum(t[h * HEAD : (h + 1) * HEAD], axis=0, keepdims=True)
            delta[h, :, at] = jnp.broadcast_to(row, (8, tok))
        return 0

    lax.fori_loop(0, nc, deltas, 0)
    scale = HEAD ** (-0.5)
    lane = lax.broadcasted_iota(jnp.int32, (1, w), 1)
    low = (lane % HEAD) < HEAD // 2

    def unrotate(g, at):
        t = g * sin_ref[at, :]
        if w == HEAD:
            up = jnp.concatenate([t[:, HEAD // 2 :], t[:, : HEAD // 2]], axis=1)
            down = up
        else:
            up = pltpu.roll(t, w - HEAD // 2, 1)
            down = pltpu.roll(t, HEAD // 2, 1)
        return g * cos_ref[at, :] + jnp.where(low, up, -down)

    def kv_copy(i):
        to = (pc.c + i + 1) % nc
        return remote(
            sendbuf.at[to, pl.ds(1, 2)], dtok_out.at[pc.c, pl.ds(1, 2)],
            xsend.at[0, i], xrecv.at[0, i], (pc.d, to),
        )

    def q_copy(i):
        to = (pc.c + i + 1) % nc
        return remote(
            sendbuf.at[to, 0], dtok_out.at[pc.c, 0], xsend.at[1, i], xrecv.at[1, i], (pc.d, to)
        )

    def block(i, _):
        to = (pc.c + i + 1) % nc
        at = pl.ds(pl.multiple_of(to * tok, tok), tok)
        dks, dvs = [], []
        for h in range(nh):
            hs = slice(h * HEAD, (h + 1) * HEAD)
            kb, vb = qkv[1, at, hs], qkv[2, at, hs]
            q, do = qkv[0, :, hs], dout[:, hs]
            nt = (((1,), (1,)), ((), ()))
            st = lax.dot_general(kb, q, nt, preferred_element_type=F32)
            p = jnp.exp2(st * (scale * LOG2E) - lse_ref[h, 0:1, :])
            dvs.append(jnp.dot(p.astype(BF16), do, preferred_element_type=F32))
            dp = lax.dot_general(vb, do, nt, preferred_element_type=F32)
            ds = (p * (dp - delta[h, 0:1, :])).astype(BF16)
            dks.append(jnp.dot(ds, q, preferred_element_type=F32))
            dq[:, hs] += lax.dot_general(
                ds, kb, (((0,), (0,)), ((), ())), preferred_element_type=F32
            )
        dk = jnp.concatenate(dks, axis=1) * scale
        sendbuf[to, 1] = unrotate(dk, at).astype(BF16)
        sendbuf[to, 2] = jnp.concatenate(dvs, axis=1).astype(BF16)

        @pl.when(i < nc - 1)
        def _():
            kv_copy(i).start()

        @pl.when(i == (nc * 3) // 8)
        def _():
            ra.middle()

        @pl.when(i == (nc * 7) // 8)
        def _():
            rb.middle()

        return 0

    lax.fori_loop(0, nc, block, 0)

    def q_block(i, _):
        to = (pc.c + i + 1) % nc
        at = pl.ds(pl.multiple_of(to * tok, tok), tok)
        sendbuf[to, 0] = unrotate(dq[at, :] * scale, at).astype(BF16)

        @pl.when(i < nc - 1)
        def _():
            q_copy(i).start()

        return 0

    lax.fori_loop(0, nc, q_block, 0)
    keep = pltpu.make_async_copy(sendbuf.at[pc.c], dtok_out.at[pc.c], local.at[1])
    keep.start()
    ra.finish(t1_ref)
    rb.finish(t2_ref)

    def drain(i, _):
        got = dtok_out.at[(pc.c + nc - i - 1) % nc]
        remote(
            got.at[pl.ds(1, 2)], got.at[pl.ds(1, 2)], xsend.at[0, i], xrecv.at[0, i], pc.sibling
        ).wait_recv()
        remote(got.at[0], got.at[0], xsend.at[1, i], xrecv.at[1, i], pc.sibling).wait_recv()
        kv_copy(i).wait_send()
        q_copy(i).wait_send()
        to = (pc.c + i + 1) % nc
        remote(
            dout_ref.at[to], dout.at[mine], dsend.at[i], drecv.at[i], (pc.d, to)
        ).wait_send()
        return 0

    lax.fori_loop(0, nc - 1, drain, 0)
    keep.wait()
    for cp in swap:
        cp.wait_send()
    ra.sent()
    rb.sent()


def weight_grad(pc, g, lhs, rhs):
    def shard(s, _):
        total = jnp.dot(lhs[0, s], rhs[0], preferred_element_type=F32)
        total = total + jnp.dot(lhs[1, s], rhs[1], preferred_element_type=F32)
        g[s // pc.nb, s % pc.nb] = total.astype(BF16)
        return 0

    lax.fori_loop(0, pc.nd, shard, 0)


def attend_back(heads, o, lse, dout, cosine, sine, h2t, dl1, dl2):
    nc, nd = lax.axis_size("ctx"), lax.axis_size("dp")
    ff = dl1.shape[1]
    hr = h2t.shape[0] // nd // 2
    n = Reduce.count(nd)
    _, keys, w = heads.shape
    nh = w // HEAD
    tok = keys // nc
    dma = pltpu.SemaphoreType.DMA
    return pl.pallas_call(
        attend_back_kernel,
        out_shape=[S((nc, 3, tok, w), BF16), S((hr, ff), BF16), S((hr, ff), BF16)],
        in_specs=[ANY, VMEM, VMEM, ANY, VMEM, VMEM, ANY, ANY, ANY],
        out_specs=[ANY, VMEM, VMEM],
        scratch_shapes=[
            pltpu.VMEM((3, keys, w), BF16),
            pltpu.VMEM((keys, w), BF16),
            pltpu.VMEM((nh, 8, keys), F32),
            pltpu.VMEM((keys, w), F32),
            pltpu.VMEM((nc, 3, tok, w), BF16),
            pltpu.VMEM((2, nd, hr, tok), BF16),
            pltpu.VMEM((2, 2, tok, ff), BF16),
            *Reduce.scratch(nd, hr, ff, True),
            *Reduce.scratch(nd, hr, ff, True),
            dma((nc,)), dma((nc,)), dma((2, nc)), dma((2, nc)), dma((nd + 2,)), dma((nd + 2,)),
            dma((n,)), dma((n,)), dma((n,)), dma((n,)), dma((4 + nd,)),
        ],
        compiler_params=params(2),
        name="attend_back",
    )(heads, o, lse, dout, cosine, sine, h2t, dl1, dl2)


def close_kernel(
    dtok_ref, h1t_ref, wqkv_ref, x_ref, gain_ref, dres_ref, dres_b_ref, part_ref,
    actt_ref, c_ref, ot_ref, t1_ref, t2_ref,
    dx_ref, gain_out, tot1, oth1, tot2, oth2, totq, othq, toto, otho, tota, otha,
    dtok, dproj, h1t, wqkv, actt, cot, ot, dres,
    gq, q0, q1, q2, q3, go, o0, o1, o2, o3, ga, a0, a1, a2, a3,
    tq, to, ta, u1, s1, u2, s2, uq, sq, uo, so, ua, sa,
    gmine, gctx, gdp,
    ssend, srecv, qsend, qrecv, osend, orecv, asend, arecv, csend, crecv, gsend, grecv, local,
):
    pc = Place()
    nd, nc = pc.nd, pc.nc
    _, _, tok, w = dtok_ref.shape
    width = nc * w
    ns = ssend.shape[0]
    load = [
        pltpu.make_async_copy(dtok_ref, dtok, local.at[0]),
        pltpu.make_async_copy(wqkv_ref, wqkv, local.at[1]),
        pltpu.make_async_copy(actt_ref, actt.at[0], local.at[2]),
        pltpu.make_async_copy(dres_b_ref, dres.at[0], local.at[3]),
    ]
    half = cot.shape[2]
    col = lambda core: pl.ds(pl.multiple_of(core * half, half), half)
    load.append(pltpu.make_async_copy(c_ref.at[:, col(pc.k)], cot.at[0], local.at[4]))
    h1_mine, h1_hers = half_rows(pc, h1t_ref, pc.k), half_rows(pc, h1t_ref, 1 - pc.k)
    o_mine, o_hers = half_rows(pc, ot_ref, pc.k), half_rows(pc, ot_ref, 1 - pc.k)
    for s in range(nd):
        load.append(pltpu.make_async_copy(h1_mine[s], h1t.at[0, s], local.at[5 + s]))
        load.append(pltpu.make_async_copy(o_mine[s], ot.at[0, s], local.at[5 + nd + s]))
    for cp in load:
        cp.start()
    barrier(pc)
    pairs = [(actt_ref, actt.at[1]), (c_ref.at[:, col(1 - pc.k)], cot.at[1])]
    pairs += [(dres_b_ref, dres.at[1])]
    pairs += [(h1_hers[s], h1t.at[1, s]) for s in range(nd)]
    pairs += [(o_hers[s], ot.at[1, s]) for s in range(nd)]
    pairs += [(dproj.at[0], dproj.at[1])]
    swap = [
        remote(src, dst, ssend.at[i], srecv.at[i], pc.sibling) for i, (src, dst) in enumerate(pairs)
    ]
    rq = Reduce(pc, gq, (q0, q1, q2, q3), qsend, qrecv, True)
    ro = Reduce(pc, go, (o0, o1, o2, o3), osend, orecv, False)
    ra = Reduce(pc, ga, (a0, a1, a2, a3), asend, arecv, True)
    chains = [
        Chain(pc, t, bufs, csend.at[i], crecv.at[i], part)
        for i, (t, bufs, part) in enumerate(
            [
                (t1_ref, (u1, s1, tot1, oth1), rq.part),
                (t2_ref, (u2, s2, tot2, oth2), rq.part),
                (tq, (uq, sq, totq, othq), rq.part),
                (to, (uo, so, toto, otho), ro.part),
                (ta, (ua, sa, tota, otha), ra.part),
            ]
        )
    ]
    c1, c2, cq, co, ca = chains
    for c in (c1, c2):
        c.open(0)
        c.open(1)
    for cp in load:
        cp.wait()
    for g in range(3):
        for i in range(nc):
            dproj[0, :, g * width + i * w : g * width + (i + 1) * w] = dtok[i, g]
    for cp in swap[3:3 + nd] + swap[-1:] + swap[:3] + swap[3 + nd : 3 + 2 * nd]:
        cp.start()
    nt = (((1,), (1,)), ((), ()))
    dh1 = jnp.zeros((tok, width), F32)
    for g in range(3):
        dh1 = dh1 + lax.dot_general(
            dproj[0, :, g * width : (g + 1) * width], wqkv[g].reshape(width, width), nt,
            preferred_element_type=F32,
        )
    for i in list(range(3, 3 + nd)) + [ns - 1]:
        swap[i].wait_recv()
    weight_grad(pc, gq, h1t, dproj)
    rq.start()
    for i in (0, 1):
        swap[i].wait_recv()
    nr = go.shape[2]
    for s in range(nd):
        at = pl.ds(s * nr, nr)
        total = jnp.dot(actt[0, at], cot[0], preferred_element_type=F32)
        total = total + jnp.dot(actt[1, at], cot[1], preferred_element_type=F32)
        go[s // pc.nb, s % pc.nb] = total.astype(BF16)
    ro.start()
    for i in [2] + list(range(3 + nd, 3 + 2 * nd)):
        swap[i].wait_recv()
    weight_grad(pc, ga, ot, dres)

    xf = x_ref[...].astype(F32)
    mean = jnp.mean(xf, axis=-1, keepdims=True)
    cen = xf - mean
    inv = lax.rsqrt(jnp.mean(cen * cen, axis=-1, keepdims=True) + norm_eps)
    hat = cen * inv
    dhat = dh1 * gain_ref[0:1, :]
    m1 = jnp.mean(dhat, axis=-1, keepdims=True)
    m2 = jnp.mean(dhat * hat, axis=-1, keepdims=True)
    dx_ref[...] = (dres_ref[...] + inv * (dhat - m1 - hat * m2)).astype(BF16)
    row = lax.broadcasted_iota(jnp.int32, (8, 1), 0)
    gmine[...] = jnp.where(row == 0, jnp.sum(dh1 * hat, axis=0, keepdims=True), part_ref[...])
    gcopies = []
    for t in range(1, nc):
        gcopies.append(
            remote(
                gmine, gctx.at[t], gsend.at[t], grecv.at[t], (pc.d, (pc.c + t) % nc)
            )
        )
        gcopies[-1].start()

    for c in (c1, c2):
        c.up(0)
        c.up(1)
    rq.middle()
    ra.start()
    for c in (c1, c2):
        c.turn(0)
        c.turn(1)
    for cp in gcopies:
        cp.wait_recv()
    total = gmine[...]
    for t in range(1, nc):
        total = total + gctx[t]
    for cp in gcopies:
        cp.wait_send()
    gmine[...] = total
    dcopies = []
    rows = gain_out.shape[1]
    for t in range(1, nd):
        to_d = (pc.d + t) % nd
        dcopies.append(
            remote(
                gmine.at[:, pl.ds(pl.multiple_of(to_d * rows, 128), rows)], gdp.at[t],
                gsend.at[nc + t], grecv.at[nc + t], (to_d, pc.c),
            )
        )
        dcopies[-1].start()
    ro.middle()
    rq.finish(tq)
    cq.open(0)
    cq.open(1)
    ra.middle()
    for cp in dcopies:
        cp.wait_recv()
    total = gmine[:, pl.ds(pl.multiple_of(pc.d * rows, 128), rows)]
    for t in range(1, nd):
        total = total + gdp[t]
    gain_out[...] = total
    ro.finish(to)
    co.open(0)
    co.open(1)
    cq.up(0)
    cq.up(1)
    ra.finish(ta)
    ca.open(0)
    ca.open(1)
    cq.turn(0)
    co.up(0)
    cq.turn(1)
    co.up(1)
    ca.up(0)
    ca.up(1)
    for c in (co, ca):
        c.turn(0)
        c.turn(1)
    for c in chains:
        for p in (0, 1):
            c.side_copy(p).wait_recv()
    for cp in swap + dcopies:
        cp.wait_send()
    for r in (rq, ro, ra):
        r.sent()
    for c in chains:
        c.sent(0)
        c.sent(1)


def close(dtok, h1t, wqkv, x, gain, dres, dres_b, part, actt, cot, ot, t1, t2):
    nd, nc = lax.axis_size("dp"), lax.axis_size("ctx")
    tok, width = x.shape
    ff = actt.shape[0]
    rows = width // nd
    hr = rows // 2
    nq, na = Reduce.count(nd), 3 + 2 * nd + 1
    dma = pltpu.SemaphoreType.DMA
    sizes = [(hr, ff), (hr, ff), (hr, 3 * width), (ff // nd, width // 2), (hr, width)]
    n = len(sizes)
    vm = lambda *shape: pltpu.VMEM(shape, BF16)
    return pl.pallas_call(
        close_kernel,
        out_shape=[S((tok, width), BF16), S((8, rows), F32)]
        + [S(size, BF16) for size in sizes for _ in range(2)],
        in_specs=[ANY, ANY, ANY, VMEM, VMEM, VMEM, ANY, VMEM, ANY, ANY, ANY, VMEM, VMEM],
        out_specs=[VMEM] * (2 + 2 * n),
        scratch_shapes=[
            vm(*dtok.shape), vm(2, tok, 3 * width), vm(2, nd, hr, tok), vm(*wqkv.shape),
            vm(2, ff, tok), vm(2, tok, width // 2), vm(2, nd, hr, tok), vm(2, tok, width),
            *Reduce.scratch(nd, hr, 3 * width, True),
            *Reduce.scratch(nd, ff // nd, width // 2, False),
            *Reduce.scratch(nd, hr, width, True),
            vm(*sizes[2]), vm(*sizes[3]), vm(*sizes[4]),
            *[vm(*size) for size in sizes for _ in range(2)],
            pltpu.VMEM((8, width), F32), pltpu.VMEM((nc, 8, width), F32),
            pltpu.VMEM((nd, 8, rows), F32),
            dma((na,)), dma((na,)), dma((nq,)), dma((nq,)), dma((nq,)), dma((nq,)),
            dma((nq,)), dma((nq,)), dma((n, 4, 2)), dma((n, 4, 2)),
            dma((nc + nd,)), dma((nc + nd,)), dma((5 + 2 * nd,)),
        ],
        compiler_params=params(3),
        name="close",
    )(dtok, h1t, wqkv, x, gain, dres, dres_b, part, actt, cot, ot, t1, t2)


def norm_rows(values, gain):
    row_mean = jnp.mean(values, axis=-1, keepdims=True)
    centred = values - row_mean
    row_var = jnp.mean(centred * centred, axis=-1, keepdims=True)
    return centred * lax.rsqrt(row_var + norm_eps) * gain


def gelu_exact(values):
    return 0.5 * values * (1.0 + lax.erf(values * 0.7071067811865476))


def gelu_slope(values):
    return (
        0.5 * (1.0 + lax.erf(values * 0.7071067811865476))
        + values * jnp.exp(-0.5 * values * values) * 0.3989422804014327
    )


def rope_angles(positions, lanes):
    half = HEAD // 2
    freq = rope_theta ** (-(jnp.arange(half, dtype=F32) * 2.0 / HEAD))
    freq = jnp.tile(freq, lanes // half)
    return positions.astype(F32)[:, None] * freq[None, :]


def on_device(
    tokens,
    norm1_gain,
    qkv_weight,
    attn_out_weight,
    norm2_gain,
    mlp_in_weight,
    mlp_out_weight,
    cotangent,
):
    _, tok, width = tokens.shape
    nc, nd = lax.axis_size("ctx"), lax.axis_size("dp")
    keys = tok * nc
    w = width // nc
    ff = mlp_in_weight.shape[1] // 2
    rows = norm1_gain.shape[0]
    x = tokens.reshape(tok, width)
    upstream = cotangent.reshape(tok, width)
    gains = jnp.concatenate(
        [
            norm1_gain.astype(F32)[None],
            norm2_gain.astype(F32)[None],
            jnp.zeros((6, rows), F32),
        ]
    )
    ang = rope_angles(lax.axis_index("ctx") * tok + jnp.arange(tok, dtype=jnp.int32), 2 * w)
    sign = jnp.where(jnp.arange(2 * w) % HEAD < HEAD // 2, -1.0, 1.0).astype(F32)
    h1t, gains_all, w1s, w2s, wqkv, wattn, heads = project(
        x, gains, jnp.cos(ang), jnp.sin(ang) * sign[None], qkv_weight, attn_out_weight,
        mlp_in_weight,
    )
    otok, o_heads, lse, w1, w2, wout = attend(heads, w1s, w2s, mlp_out_weight)
    wattn = wattn.reshape(width, width)
    w1 = w1.reshape(width, ff)
    w2 = w2.reshape(width, ff)
    wout = wout.reshape(ff, width)
    gain_one = gains_all[:, 0].reshape(width)
    gain_two = gains_all[:, 1].reshape(width)

    attended_b = jnp.transpose(otok, (1, 0, 2)).reshape(tok, width)
    inputs_f = x.astype(F32)
    attn_res = inputs_f + jnp.dot(attended_b, wattn, preferred_element_type=F32)
    normed_two = norm_rows(attn_res, gain_two).astype(BF16)
    gelu_in = jnp.dot(normed_two, w1, preferred_element_type=F32)
    gate_in = jnp.dot(normed_two, w2, preferred_element_type=F32)
    activated = (gelu_exact(gelu_in) * gate_in).astype(BF16)
    layer_out = (attn_res + jnp.dot(activated, wout, preferred_element_type=F32)).astype(BF16)
    grad_act = jnp.dot(upstream, wout.T, preferred_element_type=F32)
    dl1 = (grad_act * gate_in * gelu_slope(gelu_in)).astype(BF16)
    dl2 = (grad_act * gelu_exact(gelu_in)).astype(BF16)
    grad_normed_two = jnp.dot(dl1, w1.T, preferred_element_type=F32) + jnp.dot(
        dl2, w2.T, preferred_element_type=F32
    )
    _, pull_two = jax.vjp(norm_rows, attn_res, gain_two)
    grad_res_norm, grad_gain_two = pull_two(grad_normed_two)
    grad_res = upstream.astype(F32) + grad_res_norm
    grad_res_b = grad_res.astype(BF16)
    dout = jnp.dot(grad_res_b, wattn.T, preferred_element_type=F32).astype(BF16)
    dout = jnp.transpose(dout.reshape(tok, nc, w), (1, 0, 2))

    ang_all = rope_angles(jnp.arange(keys, dtype=jnp.int32), w)
    dtok, t1, t2 = attend_back(
        heads, o_heads, lse, dout, jnp.cos(ang_all), jnp.sin(ang_all), normed_two.T, dl1, dl2
    )
    part = jnp.concatenate(
        [jnp.zeros((1, width), F32), grad_gain_two[None], jnp.zeros((6, width), F32)]
    )
    input_grad, gain_grads, *halves = close(
        dtok, h1t, wqkv, x, jnp.broadcast_to(gain_one[None], (8, width)), grad_res, grad_res_b,
        part, activated.T, upstream, attended_b.T, t1, t2,
    )
    first = lax.axis_index("ctx") % 2 == 0

    def join(i, axis):
        mine, hers = halves[2 * i], halves[2 * i + 1]
        low, high = jnp.where(first, mine, hers), jnp.where(first, hers, mine)
        return jnp.concatenate([low, high], axis=axis).astype(F32)

    return (
        layer_out.reshape(1, tok, width),
        input_grad.reshape(1, tok, width),
        gain_grads[0],
        join(2, 0),
        join(4, 0),
        gain_grads[1],
        jnp.concatenate([join(0, 0), join(1, 0)], axis=1),
        join(3, 1),
    )


def solution(mesh):
    in_specs = (
        P("dp", "ctx", None),
        P("dp"),
        P("dp", None),
        P("dp", None),
        P("dp"),
        P("dp", None),
        P("dp", None),
        P("dp", "ctx", None),
    )
    out_specs = (
        P("dp", "ctx", None),
        P("dp", "ctx", None),
        P("dp"),
        P("dp", None),
        P("dp", None),
        P("dp"),
        P("dp", None),
        P("dp", None),
    )
    return jax.shard_map(
        on_device, mesh=mesh, in_specs=in_specs, out_specs=out_specs, check_vma=False
    )
```

```python
import functools

import jax
import jax.numpy as jnp
from jax import lax
from jax.experimental import pallas as pl
from jax.experimental.pallas import tpu as pltpu
from jax.sharding import PartitionSpec as P

HEAD = 64
norm_eps = 1e-05
rope_theta = 160000.0
F32 = jnp.float32
BF16 = jnp.bfloat16
MESH = pl.DeviceIdType.MESH
LOG2E = 1.4426950408889634
VMEM_LIMIT = 64 * 1024 * 1024 - 65536
ANY = pl.BlockSpec(memory_space=pl.ANY)
VMEM = pl.BlockSpec(memory_space=pltpu.VMEM)
S = jax.ShapeDtypeStruct


def params(cid):
    return pltpu.CompilerParams(
        collective_id=cid, has_side_effects=True, vmem_limit_bytes=VMEM_LIMIT
    )


class Place:
    def __init__(self):
        self.nd = lax.axis_size("dp")
        self.nc = lax.axis_size("ctx")
        self.d = lax.axis_index("dp")
        self.c = lax.axis_index("ctx")
        self.nb = 2 if self.nd % 2 == 0 else 1
        self.na = self.nd // self.nb
        self.a = self.d // self.nb
        self.b = self.d % self.nb
        self.nz = self.nc // 2
        self.z = self.c // 2
        self.k = self.c % 2
        self.sibling = (self.d, self.z * 2 + 1 - self.k)

    def shard(self, da, db):
        return ((self.a + da) % self.na) * self.nb + (self.b + db) % self.nb

    def at(self, da, db):
        return (self.shard(da, db), self.c)


def barrier(pc, dp=True, ctx=True):
    sem = pltpu.get_barrier_semaphore()
    count = 0
    if dp:
        for t in range(1, pc.nd):
            pl.semaphore_signal(
                sem, inc=1, device_id=((pc.d + t) % pc.nd, pc.c), device_id_type=MESH
            )
            count += 1
    if ctx:
        for t in range(1, pc.nc):
            pl.semaphore_signal(
                sem, inc=1, device_id=(pc.d, (pc.c + t) % pc.nc), device_id_type=MESH
            )
            count += 1
    pl.semaphore_wait(sem, count)


def remote(src, dst, send, recv, target):
    return pltpu.make_async_remote_copy(
        src_ref=src,
        dst_ref=dst,
        send_sem=send,
        recv_sem=recv,
        device_id=target,
        device_id_type=MESH,
    )


class Gather:
    def __init__(self, pc, cut, own, send, recv):
        self.pc, self.cut, self.own, self.send, self.recv = pc, cut, own, send, recv

    @staticmethod
    def count(nd):
        nb = 2 if nd % 2 == 0 else 1
        na = nd // nb
        return 2 * ((na - 1) + (nb - 1) + 2 * (na - 1) * (nb - 1))

    def slots(self):
        pc = self.pc
        lines = [(da, 0) for da in range(1, pc.na)] + [(0, db) for db in range(1, pc.nb)]
        cross = [
            (da, db, part)
            for part in (0, 1)
            for da in range(1, pc.na)
            for db in range(1, pc.nb)
        ]
        return lines, cross

    def _copy(self, index, shard, part, target, own=False):
        src = (self.own if own else self.cut)(shard, self.pc.k, part)
        dst = self.cut(shard, self.pc.k, part)
        return remote(src, dst, self.send.at[index], self.recv.at[index], target)

    def _arrived(self, index, shard, core, part, wait=True):
        ref = self.cut(shard, core, part)
        return remote(ref, ref, self.send.at[index], self.recv.at[index], self.pc.sibling)

    def first(self):
        pc = self.pc
        lines, _ = self.slots()
        for i, (da, db) in enumerate(lines):
            self._copy(i, pc.d, None, pc.at(-da, -db), own=True).start()

    def relay(self):
        pc = self.pc
        lines, cross = self.slots()
        n = len(lines) + len(cross)
        for i, (da, db) in enumerate(lines):
            shard = pc.shard(da, db)
            self._arrived(i, shard, pc.k, None).wait_recv()
            for j, (xa, xb, part) in enumerate(cross):
                if part == 0 and db == 0 and xa == da:
                    self._copy(len(lines) + j, shard, part, pc.at(0, -xb)).start()
                if part == 1 and da == 0 and xb == db:
                    self._copy(len(lines) + j, shard, part, pc.at(-xa, 0)).start()
            self._copy(n + i, shard, None, pc.sibling).start()

    def cross(self):
        pc = self.pc
        lines, cross = self.slots()
        n = len(lines) + len(cross)
        for j, (xa, xb, part) in enumerate(cross):
            shard = pc.shard(xa, xb)
            self._arrived(len(lines) + j, shard, pc.k, part).wait_recv()
            self._copy(n + len(lines) + j, shard, part, pc.sibling).start()

    def finish(self):
        pc = self.pc
        lines, cross = self.slots()
        n = len(lines) + len(cross)
        for i, (da, db) in enumerate(lines):
            self._arrived(n + i, pc.shard(da, db), 1 - pc.k, None).wait_recv()
        for j, (xa, xb, part) in enumerate(cross):
            self._arrived(n + len(lines) + j, pc.shard(xa, xb), 1 - pc.k, part).wait_recv()

    def sent(self):
        pc = self.pc
        lines, cross = self.slots()
        n = len(lines) + len(cross)
        for i, _ in enumerate(lines):
            self._arrived(i, pc.d, pc.k, None).wait_send()
            self._arrived(n + i, pc.d, pc.k, None).wait_send()
        for j, (_, _, part) in enumerate(cross):
            self._arrived(len(lines) + j, pc.d, pc.k, part).wait_send()
            self._arrived(n + len(lines) + j, pc.d, pc.k, part).wait_send()


def row_cut(ref, rows, core, part, lead=0):
    start = core * (rows // 2) + (0 if part is None else part * (rows // 4))
    size = rows // 2 if part is None else rows // 4
    return ref.at[(slice(None),) * lead + (pl.ds(start, size),)]


def col_cut(ref, cols, core, part):
    start = core * (cols // 2) + (0 if part is None else part * (cols // 4))
    size = cols // 2 if part is None else cols // 4
    return ref.at[:, pl.ds(pl.multiple_of(start, 128), size)]


class Reduce:
    def __init__(self, pc, g, bufs, send, recv, by_rows):
        self.pc, self.g, self.send, self.recv, self.by_rows = pc, g, send, recv, by_rows
        self.r1a, self.r1b, self.r2a, self.r2b = bufs

    @staticmethod
    def count(nd):
        nb = 2 if nd % 2 == 0 else 1
        return 2 * (nd // nb - 1 + nb - 1)

    @staticmethod
    def scratch(nd, rows, cols, by_rows):
        nb = 2 if nd % 2 == 0 else 1
        na = nd // nb
        r, c = (rows // 2, cols) if by_rows else (rows, cols // 2)
        return [
            pltpu.VMEM((na, nb, rows, cols), BF16),
            pltpu.VMEM((na - 1, nb, r, c), BF16),
            pltpu.VMEM((nb - 1, na, r, c), BF16),
            pltpu.VMEM((nb - 1, r, c), BF16),
            pltpu.VMEM((na - 1, r, c), BF16),
        ]

    def part(self, ref, p):
        lead = (slice(None),) * (len(ref.shape) - 2)
        rows, cols = ref.shape[-2:]
        if self.by_rows:
            return ref.at[lead + (pl.ds(p * (rows // 2), rows // 2),)]
        return ref.at[lead + (slice(None), pl.ds(p * (cols // 2), cols // 2))]

    def copies(self, step):
        pc = self.pc
        na, nb = pc.na, pc.nb
        out = []
        base = 0 if step == 1 else na - 1 + nb - 1
        for da in range(1, na):
            a = (pc.a + na - da) % na
            i = base + da - 1
            if step == 1:
                src, dst = self.part(self.g.at[a], 0), self.r1a.at[da - 1]
            else:
                src, dst = self.part(self.g.at[a, pc.b], 1), self.r2b.at[da - 1]
            out.append(remote(src, dst, self.send.at[i], self.recv.at[i], pc.at(-da, 0)))
        for db in range(1, nb):
            b = (pc.b + nb - db) % nb
            i = base + na - 1 + db - 1
            if step == 1:
                src, dst = self.part(self.g.at[:, b], 1), self.r1b.at[db - 1]
            else:
                src, dst = self.part(self.g.at[pc.a, b], 0), self.r2a.at[db - 1]
            out.append(remote(src, dst, self.send.at[i], self.recv.at[i], pc.at(0, -db)))
        return out

    def start(self):
        for cp in self.copies(1):
            cp.start()

    def middle(self):
        pc = self.pc
        for cp in self.copies(1):
            cp.wait_recv()
        for b in range(pc.nb):
            at = self.part(self.g.at[pc.a, b], 0)
            add(at, [self.r1a.at[i, b] for i in range(pc.na - 1)])
        for a in range(pc.na):
            at = self.part(self.g.at[a, pc.b], 1)
            add(at, [self.r1b.at[i, a] for i in range(pc.nb - 1)])
        for cp in self.copies(2):
            cp.start()

    def finish(self, total):
        pc = self.pc
        for cp in self.copies(2):
            cp.wait_recv()
        own = self.g.at[pc.a, pc.b]
        add(self.part(own, 0), [self.r2a.at[i] for i in range(pc.nb - 1)], self.part(total, 0))
        add(self.part(own, 1), [self.r2b.at[i] for i in range(pc.na - 1)], self.part(total, 1))

    def sent(self):
        for cp in self.copies(1) + self.copies(2):
            cp.wait_send()


def add(ref, others, into=None):
    into = ref if into is None else into
    rows = ref.shape[0]
    chunk = next(n for n in (32, 16, rows) if rows % n == 0)

    def some(i, _):
        at = pl.ds(pl.multiple_of(i * chunk, chunk), chunk)
        total = ref[at, :].astype(F32)
        for o in others:
            total = total + o[at, :].astype(F32)
        into[at, :] = total.astype(BF16)
        return 0

    if rows == chunk:
        total = ref[...].astype(F32)
        for o in others:
            total = total + o[...].astype(F32)
        into[...] = total.astype(BF16)
    else:
        lax.fori_loop(0, rows // chunk, some, 0)


PARTS = 4


def chain_part(by_rows):
    def part(ref, p):
        rows, cols = ref.shape[-2:]
        if by_rows:
            n = rows // PARTS
            return ref.at[pl.ds(pl.multiple_of(p * n, n), n)]
        n = cols // PARTS
        return ref.at[:, pl.ds(pl.multiple_of(p * n, n), n)]

    return part


class Chain:
    def __init__(self, pc, t, bufs, send, recv, part):
        self.pc, self.t, self.part = pc, t, part
        self.outer, self.swap, total = bufs
        self.total, self.other = total.at[pc.k], total.at[1 - pc.k]
        self.all = total
        self.send, self.recv = send, recv
        half = pc.nz // 2
        self.low = pc.z < half
        self.end = (pc.z == 0) | (pc.z == pc.nz - 1)
        self.mid = (pc.z == half - 1) | (pc.z == half)
        step = 1 - 2 * (pc.z // half)
        self.inner_id = (pc.d, ((pc.z + step + pc.nz) % pc.nz) * 2 + pc.k)
        self.outer_id = (pc.d, ((pc.z - step + pc.nz) % pc.nz) * 2 + pc.k)

    def up_copy(self, p):
        return remote(
            self.part(self.t, p), self.part(self.outer, p), self.send.at[0, p], self.recv.at[0, p],
            self.inner_id,
        )

    def swap_copy(self, p):
        return remote(
            self.part(self.t, p), self.part(self.swap, p), self.send.at[1, p], self.recv.at[1, p],
            self.inner_id,
        )

    def down_copy(self, p):
        at = self.part(self.total, p)
        return remote(at, at, self.send.at[2, p], self.recv.at[2, p], self.outer_id)

    def side_copy(self, p):
        at = self.part(self.total, p)
        return remote(at, at, self.send.at[3, p], self.recv.at[3, p], self.pc.sibling)

    def side_wait(self, p):
        at = self.part(self.other, p)
        remote(at, at, self.send.at[3, p], self.recv.at[3, p], self.pc.sibling).wait_recv()

    def open(self, p):
        @pl.when(self.end)
        def _():
            @pl.when(self.mid)
            def _():
                self.swap_copy(p).start()

            @pl.when(jnp.logical_not(self.mid))
            def _():
                self.up_copy(p).start()

    def up(self, p):
        @pl.when(jnp.logical_not(self.end))
        def _():
            self.up_copy(p).wait_recv()
            add(self.part(self.t, p), [self.part(self.outer, p)])

            @pl.when(self.mid)
            def _():
                self.swap_copy(p).start()

            @pl.when(jnp.logical_not(self.mid))
            def _():
                self.up_copy(p).start()

    def turn(self, p):
        @pl.when(self.mid)
        def _():
            self.swap_copy(p).wait_recv()
            add(self.part(self.t, p), [self.part(self.swap, p)], self.part(self.total, p))

        @pl.when(jnp.logical_not(self.mid))
        def _():
            self.down_copy(p).wait_recv()

        @pl.when(jnp.logical_not(self.end))
        def _():
            self.down_copy(p).start()

        self.side_copy(p).start()

    def sent(self, p):
        @pl.when(self.mid)
        def _():
            self.swap_copy(p).wait_send()

        @pl.when(jnp.logical_not(self.mid))
        def _():
            self.up_copy(p).wait_send()

        @pl.when(jnp.logical_not(self.end))
        def _():
            self.down_copy(p).wait_send()

        self.side_copy(p).wait_send()


def half_rows(pc, ref, core):
    rows = ref.shape[0] // pc.nd
    h = rows // 2
    return [ref.at[pl.ds(pl.multiple_of(s * rows + core * h, h), h)] for s in range(pc.nd)]


def project_kernel(
    x_ref, gains_ref, cos_ref, sin_ref, wqkv_ref, wattn_ref, win_ref,
    h1t_ref, gains_out, w1_out, w2_out, wqkv_out, wattn_out, heads_out,
    wbuf, abuf, ibuf, h1_ref, gbuf, sendbuf,
    wsend, wrecv, asend, arecv, gsend, grecv, xsend, xrecv, local,
):
    pc = Place()
    nd, nc, nz = pc.nd, pc.nc, pc.nz
    rows = wqkv_ref.shape[0]
    width = wqkv_ref.shape[1] // 3
    tok = x_ref.shape[0]
    w = width // nc
    cw = 2 * w
    own_w = [
        pltpu.make_async_copy(
            wqkv_ref.at[:, pl.ds(g * width, width)], wbuf.at[g, pc.d], local.at[g]
        )
        for g in range(3)
    ]
    for cp in own_w:
        cp.start()
    own_a = pltpu.make_async_copy(wattn_ref, abuf, local.at[3])
    own_a.start()
    own_i = pltpu.make_async_copy(win_ref, ibuf, local.at[5 + nz])
    own_i.start()
    barrier(pc)
    for cp in own_w:
        cp.wait()

    def chip_of(j):
        return (pc.z + j + 1) % nz

    def chunk(j):
        col = pl.multiple_of(chip_of(j) * cw, cw)

        def cut(shard, core, part):
            return row_cut(wbuf.at[:, shard, :, pl.ds(col, cw)], rows, core, part, lead=1)

        return Gather(pc, cut, cut, wsend.at[j], wrecv.at[j])

    def attn_cut(shard, core, part):
        return row_cut(wattn_out.at[shard], rows, core, part)

    def attn_own(shard, core, part):
        return row_cut(wattn_ref, rows, core, part)

    attn = Gather(pc, attn_cut, attn_own, asend, arecv)

    gain_copies = []
    gbuf[pc.d] = gains_ref[...]
    for t in range(1, nd):
        gain_copies.append(
            remote(
                gains_ref, gbuf.at[pc.d], gsend.at[t], grecv.at[t], ((pc.d + t) % nd, pc.c)
            )
        )
        gain_copies[-1].start()
    chunk(0).first()
    if nz > 1:
        chunk(1).first()

    xf = x_ref[...].astype(F32)
    mean = jnp.mean(xf, axis=-1, keepdims=True)
    cen = xf - mean
    var = jnp.mean(cen * cen, axis=-1, keepdims=True)
    hat = cen * lax.rsqrt(var + norm_eps)
    for t in range(1, nd):
        src = gbuf.at[(pc.d + nd - t) % nd]
        remote(src, src, gsend.at[t], grecv.at[t], pc.sibling).wait_recv()
    for s in range(nd):
        cols = slice(s * rows, (s + 1) * rows)
        h1_ref[:, cols] = (hat[:, cols] * gbuf[s, 0:1, :]).astype(BF16)
    gains_out[...] = gbuf[...]
    own_a.wait()
    own_a2 = pltpu.make_async_copy(abuf, wattn_out.at[pc.d], local.at[3])
    own_a2.start()
    own_i.wait()
    ff = w1_out.shape[1]
    w1_out[...] = ibuf[:, :ff]
    w2_out[...] = ibuf[:, ff:]
    h1t_ref[...] = jnp.transpose(h1_ref[...])

    lane = lax.broadcasted_iota(jnp.int32, (1, cw), 1)
    low = (lane % HEAD) < HEAD // 2

    def out_copy(j):
        cols = pl.ds(pl.multiple_of(chip_of(j) * cw, cw), cw)
        return pltpu.make_async_copy(
            wbuf.at[:, :, :, cols], wqkv_out.at[:, :, :, cols], local.at[4 + j]
        )

    def place(ref):
        return ref.at[:, pl.ds(pl.multiple_of(pc.c * tok, tok), tok), :]

    def exchange(j, kk):
        return remote(
            sendbuf.at[j, kk], place(heads_out), xsend.at[j, kk], xrecv.at[j, pc.k],
            (pc.d, chip_of(j) * 2 + kk),
        )

    def step(j, _):
        g = chunk(j)
        g.relay()

        @pl.when(j + 2 < nz)
        def _():
            chunk(j + 2).first()

        @pl.when(j + 2 == nz)
        def _():
            attn.first()

        g.cross()
        g.finish()
        out_copy(j).start()
        cols = pl.ds(pl.multiple_of(chip_of(j) * cw, cw), cw)
        for part in range(3):
            weight = wbuf[part, :, :, cols].reshape(nd * rows, cw)
            proj = jnp.dot(h1_ref[...], weight, preferred_element_type=F32)
            if part < 2:
                up = pltpu.roll(proj, cw - HEAD // 2, 1)
                down = pltpu.roll(proj, HEAD // 2, 1)
                proj = proj * cos_ref[...] + jnp.where(low, up, down) * sin_ref[...]
            proj = proj.astype(BF16)
            for kk in range(2):
                sendbuf[j, kk, part] = proj[:, kk * w : (kk + 1) * w]

        @pl.when(j < nz - 1)
        def _():
            exchange(j, 0).start()
            exchange(j, 1).start()

        return 0

    lax.fori_loop(0, nz, step, 0)
    last = nz - 1
    remote(
        sendbuf.at[last, 1 - pc.k], place(heads_out), xsend.at[last, 1 - pc.k],
        xrecv.at[last, pc.k], pc.sibling,
    ).start()
    own_x = pltpu.make_async_copy(
        sendbuf.at[last, pc.k], place(heads_out), local.at[4 + nz]
    )
    own_x.start()
    attn.relay()
    attn.cross()
    attn.finish()

    def arrival(j, kk):
        ref = sendbuf.at[j, kk]
        return remote(ref, ref, xsend.at[j, kk], xrecv.at[j, kk], pc.sibling)

    def drain(j, _):
        arrival(j, 0).wait_recv()
        arrival(j, 1).wait_recv()
        arrival(j, 0).wait_send()
        arrival(j, 1).wait_send()
        chunk(j).sent()
        out_copy(j).wait()
        return 0

    lax.fori_loop(0, nz - 1, drain, 0)
    arrival(last, 1 - pc.k).wait_recv()
    arrival(last, 1 - pc.k).wait_send()
    chunk(last).sent()
    out_copy(last).wait()
    own_x.wait()
    own_a2.wait()
    attn.sent()
    for cp in gain_copies:
        cp.wait_send()


def project(x, gains, cosine, sine, wqkv, wattn, win):
    nd, nc = lax.axis_size("dp"), lax.axis_size("ctx")
    nz = nc // 2
    tok, width = x.shape
    rows = wqkv.shape[0]
    w = width // nc
    n = Gather.count(nd)
    dma = pltpu.SemaphoreType.DMA
    return pl.pallas_call(
        project_kernel,
        out_shape=[
            S((width, tok), BF16),
            S((nd, 8, rows), F32),
            S((rows, win.shape[1] // 2), BF16),
            S((rows, win.shape[1] // 2), BF16),
            S((3, nd, rows, width), BF16),
            S((nd, rows, width), BF16),
            S((3, nc * tok, w), BF16),
        ],
        in_specs=[VMEM, VMEM, VMEM, VMEM, ANY, ANY, ANY],
        out_specs=[VMEM, VMEM, VMEM, VMEM, ANY, ANY, ANY],
        scratch_shapes=[
            pltpu.VMEM((3, nd, rows, width), BF16),
            pltpu.VMEM((rows, width), BF16),
            pltpu.VMEM(win.shape, BF16),
            pltpu.VMEM((tok, width), BF16),
            pltpu.VMEM((nd, 8, rows), F32),
            pltpu.VMEM((nz, 2, 3, tok, w), BF16),
            dma((nz, n)), dma((nz, n)), dma((n,)), dma((n,)),
            dma((nd,)), dma((nd,)), dma((nz, 2)), dma((nz, 2)), dma((6 + nz,)),
        ],
        compiler_params=params(0),
        name="project",
    )(x, gains, cosine, sine, wqkv, wattn, win)


def attend_kernel(
    heads_ref, w1_ref, w2_ref, wout_ref,
    otok_out, o_ref, lse_ref, w1_out, w2_out, wout_out,
    qkv, vext, bounce1, bounce2, bounce3,
    s1, r1, s2, r2, s3, r3, xsend, xrecv, local,
):
    pc = Place()
    nd, nc = pc.nd, pc.nc
    keys, w = heads_ref.shape[1], heads_ref.shape[2]
    tok = keys // nc
    rows = w1_ref.shape[0]
    cols = wout_ref.shape[1]
    load = pltpu.make_async_copy(heads_ref, qkv, local.at[0])
    load.start()
    pairs = [(w1_ref, bounce1, w1_out), (w2_ref, bounce2, w2_out), (wout_ref, bounce3, wout_out)]
    for i, (src, mid, _) in enumerate(pairs):
        pltpu.make_async_copy(src, mid, local.at[1 + i]).start()
    barrier(pc)
    items = [
        Gather(
            pc,
            lambda s, k, p: row_cut(w1_out.at[s], rows, k, p),
            lambda s, k, p: row_cut(w1_ref, rows, k, p),
            s1, r1,
        ),
        Gather(
            pc,
            lambda s, k, p: row_cut(w2_out.at[s], rows, k, p),
            lambda s, k, p: row_cut(w2_ref, rows, k, p),
            s2, r2,
        ),
        Gather(
            pc,
            lambda s, k, p: col_cut(wout_out.at[s], cols, k, p),
            lambda s, k, p: col_cut(wout_ref, cols, k, p),
            s3, r3,
        ),
    ]
    items[0].first()
    items[1].first()
    load.wait()
    for i, (src, mid, _) in enumerate(pairs):
        pltpu.make_async_copy(src, mid, local.at[1 + i]).wait()
    for i, (_, mid, dst) in enumerate(pairs):
        pltpu.make_async_copy(mid, dst.at[pc.d], local.at[1 + i]).start()
    nh = w // HEAD
    for h in range(nh):
        vext[h, :, :HEAD] = qkv[2, :, h * HEAD : (h + 1) * HEAD]
        vext[h, :, HEAD:] = jnp.ones((keys, HEAD), BF16)
    scale = HEAD ** (-0.5) * LOG2E

    def block_copy(i):
        to = (pc.c + i + 1) % nc
        at = pl.ds(pl.multiple_of(to * tok, tok), tok)
        return remote(
            o_ref.at[at], otok_out.at[pc.c], xsend.at[i], xrecv.at[i], (pc.d, to)
        )

    def block(i, _):
        at = pl.ds(pl.multiple_of(((pc.c + i + 1) % nc) * tok, tok), tok)
        for h in range(nh):
            hs = slice(h * HEAD, (h + 1) * HEAD)
            s = lax.dot_general(
                qkv[0, at, hs], qkv[1, :, hs], (((1,), (1,)), ((), ())),
                preferred_element_type=F32,
            )
            m = jnp.max(s, axis=1, keepdims=True)
            p = jnp.exp2(s * scale - m * scale).astype(BF16)
            ol = jnp.dot(p, vext[h], preferred_element_type=F32)
            total = ol[:, HEAD:]
            o_ref[at, hs] = (ol[:, :HEAD] / total).astype(BF16)
            lse = m * scale + jnp.log2(total)
            lse_ref[h, :, at] = jnp.transpose(jnp.concatenate([lse, lse], axis=1))[:8]

        @pl.when(i < nc - 1)
        def _():
            block_copy(i).start()

        return 0

    lax.fori_loop(0, nc, block, 0)
    own = pltpu.make_async_copy(
        o_ref.at[pl.ds(pl.multiple_of(pc.c * tok, tok), tok)], otok_out.at[pc.c], local.at[0]
    )
    own.start()
    items[0].relay()
    items[2].first()
    items[1].relay()
    items[0].cross()
    items[2].relay()
    items[1].cross()
    items[2].cross()
    for it in items:
        it.finish()

    def drain(i, _):
        got = otok_out.at[(pc.c + nc - i - 1) % nc]
        remote(got, got, xsend.at[i], xrecv.at[i], pc.sibling).wait_recv()
        block_copy(i).wait_send()
        return 0

    lax.fori_loop(0, nc - 1, drain, 0)
    own.wait()
    for i, (_, mid, dst) in enumerate(pairs):
        pltpu.make_async_copy(mid, dst.at[pc.d], local.at[1 + i]).wait()
    for it in items:
        it.sent()


def attend(heads, w1, w2, wout):
    nd, nc = lax.axis_size("dp"), lax.axis_size("ctx")
    _, keys, w = heads.shape
    nh = w // HEAD
    n = Gather.count(nd)
    dma = pltpu.SemaphoreType.DMA
    return pl.pallas_call(
        attend_kernel,
        out_shape=[
            S((nc, keys // nc, w), BF16),
            S((keys, w), BF16),
            S((nh, 8, keys), F32),
            S((nd,) + w1.shape, BF16),
            S((nd,) + w2.shape, BF16),
            S((nd,) + wout.shape, BF16),
        ],
        in_specs=[ANY, ANY, ANY, ANY],
        out_specs=[ANY, VMEM, VMEM, ANY, ANY, ANY],
        scratch_shapes=[
            pltpu.VMEM((3, keys, w), BF16),
            pltpu.VMEM((nh, keys, 2 * HEAD), BF16),
            pltpu.VMEM(w1.shape, BF16),
            pltpu.VMEM(w2.shape, BF16),
            pltpu.VMEM(wout.shape, BF16),
            dma((n,)), dma((n,)), dma((n,)), dma((n,)), dma((n,)), dma((n,)),
            dma((nc,)), dma((nc,)), dma((4,)),
        ],
        compiler_params=params(1),
        name="attend",
    )(heads, w1, w2, wout)


def attend_back_kernel(
    heads_ref, o_ref, lse_ref, dout_ref, cos_ref, sin_ref, h2t_ref, dl1_ref, dl2_ref,
    dtok_out, t1_ref, t2_ref,
    qkv, dout, delta, dq, sendbuf, h2t, dl,
    ga, ra0, ra1, ra2, ra3, gb, rb0, rb1, rb2, rb3,
    dsend, drecv, xsend, xrecv, ssend, srecv, asend, arecv, bsend, brecv, local,
):
    pc = Place()
    nd = pc.nd
    nc = pc.nc
    keys, w = heads_ref.shape[1], heads_ref.shape[2]
    tok = keys // nc
    nh = w // HEAD
    load = pltpu.make_async_copy(heads_ref, qkv, local.at[0])
    load.start()
    mine_t = half_rows(pc, h2t_ref, pc.k)
    hers_t = half_rows(pc, h2t_ref, 1 - pc.k)
    fetch = [pltpu.make_async_copy(mine_t[s], h2t.at[0, s], local.at[2 + s]) for s in range(nd)]
    fetch.append(pltpu.make_async_copy(dl1_ref, dl.at[0, 0], local.at[2 + nd]))
    fetch.append(pltpu.make_async_copy(dl2_ref, dl.at[1, 0], local.at[3 + nd]))
    for cp in fetch:
        cp.start()
    barrier(pc)
    swap = [
        remote(hers_t[s], h2t.at[1, s], ssend.at[s], srecv.at[s], pc.sibling) for s in range(nd)
    ]
    swap.append(remote(dl1_ref, dl.at[0, 1], ssend.at[nd], srecv.at[nd], pc.sibling))
    swap.append(remote(dl2_ref, dl.at[1, 1], ssend.at[nd + 1], srecv.at[nd + 1], pc.sibling))
    for cp in swap:
        cp.start()
    mine = pl.ds(pl.multiple_of(pc.c * tok, tok), tok)
    for i in range(nc - 1):
        to = (pc.c + i + 1) % nc
        remote(dout_ref.at[to], dout.at[mine], dsend.at[i], drecv.at[i], (pc.d, to)).start()
    own = pltpu.make_async_copy(dout_ref.at[pc.c], dout.at[mine], local.at[1])
    own.start()
    ra = Reduce(pc, ga, (ra0, ra1, ra2, ra3), asend, arecv, True)
    rb = Reduce(pc, gb, (rb0, rb1, rb2, rb3), bsend, brecv, True)
    for cp in fetch:
        cp.wait()
    for cp in swap[: nd + 1]:
        cp.wait_recv()
    weight_grad(pc, ga, h2t, dl.at[0])
    ra.start()
    swap[nd + 1].wait_recv()
    weight_grad(pc, gb, h2t, dl.at[1])
    rb.start()
    dq[...] = jnp.zeros_like(dq)
    load.wait()
    own.wait()
    for i in range(nc - 1):
        src = (pc.c + nc - i - 1) % nc
        got = dout.at[pl.ds(pl.multiple_of(src * tok, tok), tok)]
        remote(got, got, dsend.at[i], drecv.at[i], pc.sibling).wait_recv()

    def deltas(i, _):
        at = pl.ds(pl.multiple_of(i * tok, tok), tok)
        t = jnp.transpose(o_ref[at, :].astype(F32) * dout[at, :].astype(F32))
        for h in range(nh):
            row = jnp.sum(t[h * HEAD : (h + 1) * HEAD], axis=0, keepdims=True)
            delta[h, :, at] = jnp.broadcast_to(row, (8, tok))
        return 0

    lax.fori_loop(0, nc, deltas, 0)
    scale = HEAD ** (-0.5)
    lane = lax.broadcasted_iota(jnp.int32, (1, w), 1)
    low = (lane % HEAD) < HEAD // 2

    def unrotate(g, at):
        t = g * sin_ref[at, :]
        if w == HEAD:
            up = jnp.concatenate([t[:, HEAD // 2 :], t[:, : HEAD // 2]], axis=1)
            down = up
        else:
            up = pltpu.roll(t, w - HEAD // 2, 1)
            down = pltpu.roll(t, HEAD // 2, 1)
        return g * cos_ref[at, :] + jnp.where(low, up, -down)

    def kv_copy(i):
        to = (pc.c + i + 1) % nc
        return remote(
            sendbuf.at[to, pl.ds(1, 2)], dtok_out.at[pc.c, pl.ds(1, 2)],
            xsend.at[0, i], xrecv.at[0, i], (pc.d, to),
        )

    def q_copy(i):
        to = (pc.c + i + 1) % nc
        return remote(
            sendbuf.at[to, 0], dtok_out.at[pc.c, 0], xsend.at[1, i], xrecv.at[1, i], (pc.d, to)
        )

    def block(i, _):
        to = (pc.c + i + 1) % nc
        at = pl.ds(pl.multiple_of(to * tok, tok), tok)
        dks, dvs = [], []
        for h in range(nh):
            hs = slice(h * HEAD, (h + 1) * HEAD)
            kb, vb = qkv[1, at, hs], qkv[2, at, hs]
            q, do = qkv[0, :, hs], dout[:, hs]
            nt = (((1,), (1,)), ((), ()))
            st = lax.dot_general(kb, q, nt, preferred_element_type=F32)
            p = jnp.exp2(st * (scale * LOG2E) - lse_ref[h, 0:1, :])
            dvs.append(jnp.dot(p.astype(BF16), do, preferred_element_type=F32))
            dp = lax.dot_general(vb, do, nt, preferred_element_type=F32)
            ds = (p * (dp - delta[h, 0:1, :])).astype(BF16)
            dks.append(jnp.dot(ds, q, preferred_element_type=F32))
            dq[:, hs] += lax.dot_general(
                ds, kb, (((0,), (0,)), ((), ())), preferred_element_type=F32
            )
        dk = jnp.concatenate(dks, axis=1) * scale
        sendbuf[to, 1] = unrotate(dk, at).astype(BF16)
        sendbuf[to, 2] = jnp.concatenate(dvs, axis=1).astype(BF16)

        @pl.when(i < nc - 1)
        def _():
            kv_copy(i).start()

        @pl.when(i == (nc * 3) // 8)
        def _():
            ra.middle()

        @pl.when(i == (nc * 7) // 8)
        def _():
            rb.middle()

        return 0

    lax.fori_loop(0, nc, block, 0)

    def q_block(i, _):
        to = (pc.c + i + 1) % nc
        at = pl.ds(pl.multiple_of(to * tok, tok), tok)
        sendbuf[to, 0] = unrotate(dq[at, :] * scale, at).astype(BF16)

        @pl.when(i < nc - 1)
        def _():
            q_copy(i).start()

        return 0

    lax.fori_loop(0, nc, q_block, 0)
    keep = pltpu.make_async_copy(sendbuf.at[pc.c], dtok_out.at[pc.c], local.at[1])
    keep.start()
    ra.finish(t1_ref)
    rb.finish(t2_ref)

    def drain(i, _):
        got = dtok_out.at[(pc.c + nc - i - 1) % nc]
        remote(
            got.at[pl.ds(1, 2)], got.at[pl.ds(1, 2)], xsend.at[0, i], xrecv.at[0, i], pc.sibling
        ).wait_recv()
        remote(got.at[0], got.at[0], xsend.at[1, i], xrecv.at[1, i], pc.sibling).wait_recv()
        kv_copy(i).wait_send()
        q_copy(i).wait_send()
        to = (pc.c + i + 1) % nc
        remote(
            dout_ref.at[to], dout.at[mine], dsend.at[i], drecv.at[i], (pc.d, to)
        ).wait_send()
        return 0

    lax.fori_loop(0, nc - 1, drain, 0)
    keep.wait()
    for cp in swap:
        cp.wait_send()
    ra.sent()
    rb.sent()


def weight_grad(pc, g, lhs, rhs):
    def shard(s, _):
        total = jnp.dot(lhs[0, s], rhs[0], preferred_element_type=F32)
        total = total + jnp.dot(lhs[1, s], rhs[1], preferred_element_type=F32)
        g[s // pc.nb, s % pc.nb] = total.astype(BF16)
        return 0

    lax.fori_loop(0, pc.nd, shard, 0)


def attend_back(heads, o, lse, dout, cosine, sine, h2t, dl1, dl2):
    nc, nd = lax.axis_size("ctx"), lax.axis_size("dp")
    ff = dl1.shape[1]
    hr = h2t.shape[0] // nd // 2
    n = Reduce.count(nd)
    _, keys, w = heads.shape
    nh = w // HEAD
    tok = keys // nc
    dma = pltpu.SemaphoreType.DMA
    return pl.pallas_call(
        attend_back_kernel,
        out_shape=[S((nc, 3, tok, w), BF16), S((hr, ff), BF16), S((hr, ff), BF16)],
        in_specs=[ANY, VMEM, VMEM, ANY, VMEM, VMEM, ANY, ANY, ANY],
        out_specs=[ANY, VMEM, VMEM],
        scratch_shapes=[
            pltpu.VMEM((3, keys, w), BF16),
            pltpu.VMEM((keys, w), BF16),
            pltpu.VMEM((nh, 8, keys), F32),
            pltpu.VMEM((keys, w), F32),
            pltpu.VMEM((nc, 3, tok, w), BF16),
            pltpu.VMEM((2, nd, hr, tok), BF16),
            pltpu.VMEM((2, 2, tok, ff), BF16),
            *Reduce.scratch(nd, hr, ff, True),
            *Reduce.scratch(nd, hr, ff, True),
            dma((nc,)), dma((nc,)), dma((2, nc)), dma((2, nc)), dma((nd + 2,)), dma((nd + 2,)),
            dma((n,)), dma((n,)), dma((n,)), dma((n,)), dma((4 + nd,)),
        ],
        compiler_params=params(2),
        name="attend_back",
    )(heads, o, lse, dout, cosine, sine, h2t, dl1, dl2)


def each(count, *calls):
    def body(p, _):
        for call in calls:
            call(p)
        return 0

    lax.fori_loop(0, count, body, 0)


def close_kernel(
    dtok_ref, h1t_ref, wqkv_ref, x_ref, gain_ref, dres_ref, dres_b_ref, part_ref,
    actt_ref, c_ref, ot_ref, t1_ref, t2_ref,
    dx_ref, gain_out, out1, out2, outq, outo, outa,
    dtok, dproj, h1t, wqkv, actt, cot, ot, dres,
    gq, q0, q1, q2, q3, go, o0, o1, o2, o3, ga, a0, a1, a2, a3,
    tq, to, ta, u1, s1, f1, u2, s2, f2, uq, sq, fq, uo, so, fo, ua, sa, fa,
    gmine, gctx, gdp,
    ssend, srecv, qsend, qrecv, osend, orecv, asend, arecv, csend, crecv, gsend, grecv, local,
    outsem,
):
    pc = Place()
    nd, nc = pc.nd, pc.nc
    _, _, tok, w = dtok_ref.shape
    width = nc * w
    half = cot.shape[2]
    nr = actt.shape[2]
    col = lambda core: pl.ds(pl.multiple_of(core * half, half), half)
    h1_mine, h1_hers = half_rows(pc, h1t_ref, pc.k), half_rows(pc, h1t_ref, 1 - pc.k)
    o_mine, o_hers = half_rows(pc, ot_ref, pc.k), half_rows(pc, ot_ref, 1 - pc.k)
    acts = [actt_ref.at[pl.ds(s * nr, nr)] for s in range(nd)]
    pairs = [(dtok_ref, dtok), (wqkv_ref, wqkv), (dres_b_ref, dres.at[0])]
    pairs += [(c_ref.at[:, col(pc.k)], cot.at[0])]
    pairs += [(h1_mine[s], h1t.at[0, s]) for s in range(nd)]
    pairs += [(o_mine[s], ot.at[0, s]) for s in range(nd)]
    pairs += [(acts[s], actt.at[0, s]) for s in range(nd)]
    load = [pltpu.make_async_copy(a, b, local.at[i]) for i, (a, b) in enumerate(pairs)]
    for cp in load:
        cp.start()
    barrier(pc)
    rq = Reduce(pc, gq, (q0, q1, q2, q3), qsend, qrecv, True)
    ro = Reduce(pc, go, (o0, o1, o2, o3), osend, orecv, False)
    ra = Reduce(pc, ga, (a0, a1, a2, a3), asend, arecv, True)
    rows_part, cols_part = chain_part(True), chain_part(False)
    chains = [
        Chain(pc, t, bufs, csend.at[i], crecv.at[i], part)
        for i, (t, bufs, part) in enumerate(
            [
                (t1_ref, (u1, s1, f1), rows_part),
                (t2_ref, (u2, s2, f2), rows_part),
                (tq, (uq, sq, fq), rows_part),
                (to, (uo, so, fo), cols_part),
                (ta, (ua, sa, fa), rows_part),
            ]
        )
    ]
    c1, c2, cq, co, ca = chains
    each(PARTS, c1.open)
    each(PARTS, c2.open)
    pairs = [(h1_hers[s], h1t.at[1, s]) for s in range(nd)] + [(dproj.at[0], dproj.at[1])]
    pairs += [(o_hers[s], ot.at[1, s]) for s in range(nd)] + [(dres_b_ref, dres.at[1])]
    pairs += [(acts[s], actt.at[1, s]) for s in range(nd)]
    pairs += [(c_ref.at[:, col(1 - pc.k)], cot.at[1])]
    swap = [
        remote(src, dst, ssend.at[i], srecv.at[i], pc.sibling) for i, (src, dst) in enumerate(pairs)
    ]
    for cp in swap[:nd]:
        cp.start()
    load[0].wait()
    for g in range(3):
        for i in range(nc):
            dproj[0, :, g * width + i * w : g * width + (i + 1) * w] = dtok[i, g]
    for cp in swap[nd:]:
        cp.start()
    for cp in load[1:]:
        cp.wait()
    nt = (((1,), (1,)), ((), ()))
    dh1 = jnp.zeros((tok, width), F32)
    for g in range(3):
        dh1 = dh1 + lax.dot_general(
            dproj[0, :, g * width : (g + 1) * width], wqkv[g].reshape(width, width), nt,
            preferred_element_type=F32,
        )
    for cp in swap[: nd + 1]:
        cp.wait_recv()
    weight_grad(pc, gq, h1t, dproj)
    rq.start()
    c1.up(0)
    c1.up(1)
    for cp in swap[nd + 1 : 2 * nd + 2]:
        cp.wait_recv()
    weight_grad(pc, ga, ot, dres)
    ra.start()
    c1.up(2)
    for cp in swap[2 * nd + 2 :]:
        cp.wait_recv()
    weight_grad(pc, go, actt, cot)
    c1.up(3)
    c1.turn(0)

    xf = x_ref[...].astype(F32)
    mean = jnp.mean(xf, axis=-1, keepdims=True)
    cen = xf - mean
    inv = lax.rsqrt(jnp.mean(cen * cen, axis=-1, keepdims=True) + norm_eps)
    hat = cen * inv
    gain = jnp.concatenate([gain_ref[s, 0:1, :] for s in range(nd)], axis=1)
    dhat = dh1 * gain
    m1 = jnp.mean(dhat, axis=-1, keepdims=True)
    m2 = jnp.mean(dhat * hat, axis=-1, keepdims=True)
    dx_ref[...] = (dres_ref[...] + inv * (dhat - m1 - hat * m2)).astype(BF16)
    row = lax.broadcasted_iota(jnp.int32, (8, 1), 0)
    gmine[...] = jnp.where(row == 0, jnp.sum(dh1 * hat, axis=0, keepdims=True), part_ref[...])
    gcopies = []
    for t in range(1, nc):
        gcopies.append(
            remote(gmine, gctx.at[t], gsend.at[t], grecv.at[t], (pc.d, (pc.c + t) % nc))
        )
        gcopies[-1].start()

    c2.up(0)
    c1.turn(1)
    c2.up(1)
    c1.turn(2)
    rq.middle()
    ro.start()
    c2.up(2)
    c1.turn(3)
    c2.up(3)
    c2.turn(0)
    for cp in gcopies:
        cp.wait_recv()
    total = gmine[...]
    for t in range(1, nc):
        total = total + gctx[t]
    for cp in gcopies:
        cp.wait_send()
    gmine[...] = total
    dcopies = []
    rows = gain_out.shape[1]
    for t in range(1, nd):
        to_d = (pc.d + t) % nd
        dcopies.append(
            remote(
                gmine.at[:, pl.ds(pl.multiple_of(to_d * rows, 128), rows)], gdp.at[t],
                gsend.at[nc + t], grecv.at[nc + t], (to_d, pc.c),
            )
        )
        dcopies[-1].start()
    c2.turn(1)
    ra.middle()
    c2.turn(2)
    c2.turn(3)
    rq.finish(tq)
    each(PARTS, cq.open)
    for cp in dcopies:
        cp.wait_recv()
    total = gmine[:, pl.ds(pl.multiple_of(pc.d * rows, 128), rows)]
    for t in range(1, nd):
        total = total + gdp[t]
    gain_out[...] = total
    outs = [
        pltpu.make_async_copy(c.all, out, outsem.at[i])
        for i, (c, out) in enumerate(zip(chains, (out1, out2, outq, outo, outa)))
    ]
    each(PARTS, c1.side_wait)
    outs[0].start()
    each(PARTS, c2.side_wait)
    outs[1].start()
    cq.up(0)
    cq.up(1)
    ro.middle()
    cq.turn(0)
    cq.up(2)
    ra.finish(ta)
    each(PARTS, ca.open)
    cq.turn(1)
    cq.up(3)
    cq.turn(2)
    ro.finish(to)
    each(PARTS, co.open)
    cq.turn(3)
    each(PARTS, ca.up)
    each(PARTS, cq.side_wait)
    outs[2].start()
    each(PARTS, ca.turn)
    co.up(0)
    each(PARTS - 1, lambda p: co.up(p + 1), co.turn)
    co.turn(PARTS - 1)
    each(PARTS, ca.side_wait)
    outs[4].start()
    each(PARTS, co.side_wait)
    outs[3].start()
    for cp in swap + dcopies:
        cp.wait_send()
    for r in (rq, ro, ra):
        r.sent()
    for c in chains:
        each(PARTS, c.sent)
    for cp in outs:
        cp.wait()


def close(dtok, h1t, wqkv, x, gains, dres, dres_b, part, actt, cot, ot, t1, t2):
    nd, nc = lax.axis_size("dp"), lax.axis_size("ctx")
    tok, width = x.shape
    ff = actt.shape[0]
    rows = width // nd
    hr = rows // 2
    nq, ns = Reduce.count(nd), 3 * nd + 3
    dma = pltpu.SemaphoreType.DMA
    sizes = [(hr, ff), (hr, ff), (hr, 3 * width), (ff // nd, width // 2), (hr, width)]
    n = len(sizes)
    vm = lambda *shape: pltpu.VMEM(shape, BF16)
    chain_bufs = [b for size in sizes for b in (vm(*size), vm(*size), vm(2, *size))]
    return pl.pallas_call(
        close_kernel,
        out_shape=[S((tok, width), BF16), S((8, rows), F32)]
        + [S((2,) + size, BF16) for size in sizes],
        in_specs=[ANY, ANY, ANY, VMEM, VMEM, VMEM, ANY, VMEM, ANY, ANY, ANY, VMEM, VMEM],
        out_specs=[VMEM] * 2 + [ANY] * n,
        scratch_shapes=[
            vm(*dtok.shape), vm(2, tok, 3 * width), vm(2, nd, hr, tok), vm(*wqkv.shape),
            vm(2, nd, ff // nd, tok), vm(2, tok, width // 2), vm(2, nd, hr, tok), vm(2, tok, width),
            *Reduce.scratch(nd, hr, 3 * width, True),
            *Reduce.scratch(nd, ff // nd, width // 2, False),
            *Reduce.scratch(nd, hr, width, True),
            vm(*sizes[2]), vm(*sizes[3]), vm(*sizes[4]),
            *chain_bufs,
            pltpu.VMEM((8, width), F32), pltpu.VMEM((nc, 8, width), F32),
            pltpu.VMEM((nd, 8, rows), F32),
            dma((ns,)), dma((ns,)), dma((nq,)), dma((nq,)), dma((nq,)), dma((nq,)),
            dma((nq,)), dma((nq,)), dma((n, 4, PARTS)), dma((n, 4, PARTS)),
            dma((nc + nd,)), dma((nc + nd,)), dma((4 + 3 * nd,)), dma((n,)),
        ],
        compiler_params=params(3),
        name="close",
    )(dtok, h1t, wqkv, x, gains, dres, dres_b, part, actt, cot, ot, t1, t2)


def norm_rows(values, gain):
    row_mean = jnp.mean(values, axis=-1, keepdims=True)
    centred = values - row_mean
    row_var = jnp.mean(centred * centred, axis=-1, keepdims=True)
    return centred * lax.rsqrt(row_var + norm_eps) * gain


def gelu_exact(values):
    return 0.5 * values * (1.0 + lax.erf(values * 0.7071067811865476))


def gelu_slope(values):
    return (
        0.5 * (1.0 + lax.erf(values * 0.7071067811865476))
        + values * jnp.exp(-0.5 * values * values) * 0.3989422804014327
    )


def rope_angles(positions, lanes):
    half = HEAD // 2
    freq = rope_theta ** (-(jnp.arange(half, dtype=F32) * 2.0 / HEAD))
    freq = jnp.tile(freq, lanes // half)
    return positions.astype(F32)[:, None] * freq[None, :]


def on_device(
    tokens,
    norm1_gain,
    qkv_weight,
    attn_out_weight,
    norm2_gain,
    mlp_in_weight,
    mlp_out_weight,
    cotangent,
):
    _, tok, width = tokens.shape
    nc, nd = lax.axis_size("ctx"), lax.axis_size("dp")
    keys = tok * nc
    w = width // nc
    ff = mlp_in_weight.shape[1] // 2
    rows = norm1_gain.shape[0]
    x = tokens.reshape(tok, width)
    upstream = cotangent.reshape(tok, width)
    gains = jnp.concatenate(
        [
            norm1_gain.astype(F32)[None],
            norm2_gain.astype(F32)[None],
            jnp.zeros((6, rows), F32),
        ]
    )
    ang = rope_angles(lax.axis_index("ctx") * tok + jnp.arange(tok, dtype=jnp.int32), 2 * w)
    sign = jnp.where(jnp.arange(2 * w) % HEAD < HEAD // 2, -1.0, 1.0).astype(F32)
    h1t, gains_all, w1s, w2s, wqkv, wattn, heads = project(
        x, gains, jnp.cos(ang), jnp.sin(ang) * sign[None], qkv_weight, attn_out_weight,
        mlp_in_weight,
    )
    otok, o_heads, lse, w1, w2, wout = attend(heads, w1s, w2s, mlp_out_weight)
    wattn = wattn.reshape(width, width)
    w1 = w1.reshape(width, ff)
    w2 = w2.reshape(width, ff)
    wout = wout.reshape(ff, width)
    gain_one = gains_all[:, 0].reshape(width)
    gain_two = gains_all[:, 1].reshape(width)

    attended_b = jnp.transpose(otok, (1, 0, 2)).reshape(tok, width)
    inputs_f = x.astype(F32)
    attn_res = inputs_f + jnp.dot(attended_b, wattn, preferred_element_type=F32)
    normed_two = norm_rows(attn_res, gain_two).astype(BF16)
    gelu_in = jnp.dot(normed_two, w1, preferred_element_type=F32)
    gate_in = jnp.dot(normed_two, w2, preferred_element_type=F32)
    activated = (gelu_exact(gelu_in) * gate_in).astype(BF16)
    layer_out = (attn_res + jnp.dot(activated, wout, preferred_element_type=F32)).astype(BF16)
    grad_act = jnp.dot(upstream, wout.T, preferred_element_type=F32)
    dl1 = (grad_act * gate_in * gelu_slope(gelu_in)).astype(BF16)
    dl2 = (grad_act * gelu_exact(gelu_in)).astype(BF16)
    grad_normed_two = jnp.dot(dl1, w1.T, preferred_element_type=F32) + jnp.dot(
        dl2, w2.T, preferred_element_type=F32
    )
    _, pull_two = jax.vjp(norm_rows, attn_res, gain_two)
    grad_res_norm, grad_gain_two = pull_two(grad_normed_two)
    grad_res = upstream.astype(F32) + grad_res_norm
    grad_res_b = grad_res.astype(BF16)
    dout = jnp.dot(grad_res_b, wattn.T, preferred_element_type=F32).astype(BF16)
    dout = jnp.transpose(dout.reshape(tok, nc, w), (1, 0, 2))

    near = rope_angles(jnp.arange(tok, dtype=jnp.int32), w)[None]
    far = rope_angles(jnp.arange(nc, dtype=jnp.int32) * tok, w)[:, None]
    cos_near, sin_near, cos_far, sin_far = lax.optimization_barrier(
        (jnp.cos(near), jnp.sin(near), jnp.cos(far), jnp.sin(far))
    )
    cos_all = (cos_far * cos_near - sin_far * sin_near).reshape(keys, w)
    sin_all = (sin_far * cos_near + cos_far * sin_near).reshape(keys, w)
    dtok, t1, t2 = attend_back(
        heads, o_heads, lse, dout, cos_all, sin_all, normed_two.T, dl1, dl2
    )
    input_grad, gain_grads, in1, in2, gqkv, gout, gattn = close(
        dtok, h1t, wqkv, x, gains_all, grad_res, grad_res_b, grad_gain_two.reshape(1, width),
        activated.T, upstream, attended_b.T, t1, t2,
    )
    grad_in = jnp.concatenate([in1.reshape(rows, ff), in2.reshape(rows, ff)], axis=1)
    return (
        layer_out.reshape(1, tok, width),
        input_grad.reshape(1, tok, width),
        gain_grads[0],
        gqkv.reshape(rows, 3 * width).astype(F32),
        gattn.reshape(rows, width).astype(F32),
        gain_grads[1],
        grad_in.astype(F32),
        jnp.concatenate([gout[0], gout[1]], axis=1).astype(F32),
    )


def solution(mesh):
    in_specs = (
        P("dp", "ctx", None),
        P("dp"),
        P("dp", None),
        P("dp", None),
        P("dp"),
        P("dp", None),
        P("dp", None),
        P("dp", "ctx", None),
    )
    out_specs = (
        P("dp", "ctx", None),
        P("dp", "ctx", None),
        P("dp"),
        P("dp", None),
        P("dp", None),
        P("dp"),
        P("dp", None),
        P("dp", None),
    )
    return jax.shard_map(
        on_device, mesh=mesh, in_specs=in_specs, out_specs=out_specs, check_vma=False
    )
```

```python
import functools

import jax
import jax.numpy as jnp
from jax import lax
from jax.experimental import pallas as pl
from jax.experimental.pallas import tpu as pltpu
from jax.sharding import PartitionSpec as P

HEAD = 64
norm_eps = 1e-05
rope_theta = 160000.0
F32 = jnp.float32
BF16 = jnp.bfloat16
MESH = pl.DeviceIdType.MESH
LOG2E = 1.4426950408889634
VMEM_LIMIT = 64 * 1024 * 1024 - 65536
ANY = pl.BlockSpec(memory_space=pl.ANY)
VMEM = pl.BlockSpec(memory_space=pltpu.VMEM)
S = jax.ShapeDtypeStruct


def params(cid):
    return pltpu.CompilerParams(
        collective_id=cid, has_side_effects=True, vmem_limit_bytes=VMEM_LIMIT
    )


class Place:
    def __init__(self):
        self.nd = lax.axis_size("dp")
        self.nc = lax.axis_size("ctx")
        self.d = lax.axis_index("dp")
        self.c = lax.axis_index("ctx")
        self.nb = 2 if self.nd % 2 == 0 else 1
        self.na = self.nd // self.nb
        self.a = self.d // self.nb
        self.b = self.d % self.nb
        self.nz = self.nc // 2
        self.z = self.c // 2
        self.k = self.c % 2
        self.sibling = (self.d, self.z * 2 + 1 - self.k)

    def shard(self, da, db):
        return ((self.a + da) % self.na) * self.nb + (self.b + db) % self.nb

    def at(self, da, db):
        return (self.shard(da, db), self.c)


def barrier(pc, dp=True, ctx=True):
    sem = pltpu.get_barrier_semaphore()
    count = 0
    if dp:
        for t in range(1, pc.nd):
            pl.semaphore_signal(
                sem, inc=1, device_id=((pc.d + t) % pc.nd, pc.c), device_id_type=MESH
            )
            count += 1
    if ctx:
        for t in range(1, pc.nc):
            pl.semaphore_signal(
                sem, inc=1, device_id=(pc.d, (pc.c + t) % pc.nc), device_id_type=MESH
            )
            count += 1
    pl.semaphore_wait(sem, count)


def remote(src, dst, send, recv, target):
    return pltpu.make_async_remote_copy(
        src_ref=src,
        dst_ref=dst,
        send_sem=send,
        recv_sem=recv,
        device_id=target,
        device_id_type=MESH,
    )


class Gather:
    def __init__(self, pc, cut, own, send, recv, deep=None):
        self.pc, self.cut, self.own, self.send, self.recv, self.deep = pc, cut, own, send, recv, deep
        self.lines = [(da, 0) for da in range(1, pc.na)] + [(0, db) for db in range(1, pc.nb)]
        self.cross_at = [
            (da, db, part)
            for part in (0, 1)
            for da in range(1, pc.na)
            for db in range(1, pc.nb)
        ]
        self.n = len(self.lines) + len(self.cross_at)
        self.pair = (pc.d, (pc.z + 1 - 2 * (pc.z % 2)) * 2 + pc.k)

    @staticmethod
    def count(nd):
        nb = 2 if nd % 2 == 0 else 1
        na = nd // nb
        return 2 * ((na - 1) + (nb - 1) + 2 * (na - 1) * (nb - 1)) + 2 * nd

    def _copy(self, index, shard, part, target, own=False):
        src = (self.own if own else self.cut)(shard, self.pc.k, part)
        dst = self.cut(shard, self.pc.k, part)
        return remote(src, dst, self.send.at[index], self.recv.at[index], target)

    def _arrived(self, index, shard, core, part):
        ref = self.cut(shard, core, part)
        return remote(ref, ref, self.send.at[index], self.recv.at[index], self.pc.sibling)

    def _deep(self, index, shard, core, mine, target):
        ref = self.deep(shard, core, mine)
        return remote(ref, ref, self.send.at[index], self.recv.at[index], target)

    def others(self):
        pc = self.pc
        return [(da, db) for da in range(pc.na) for db in range(pc.nb) if (da, db) != (0, 0)]

    def first(self):
        pc = self.pc
        for i, (da, db) in enumerate(self.lines):
            self._copy(i, pc.d, None, pc.at(-da, -db), own=True).start()

    def _down(self, da, db):
        if self.deep is not None:
            i = self.others().index((da, db))
            self._deep(2 * self.n + i, self.pc.shard(da, db), self.pc.k, True, self.pair).start()

    def relay(self):
        pc, nl = self.pc, len(self.lines)
        for i, (da, db) in enumerate(self.lines):
            shard = pc.shard(da, db)
            self._arrived(i, shard, pc.k, None).wait_recv()
            for j, (xa, xb, part) in enumerate(self.cross_at):
                if part == 0 and db == 0 and xa == da:
                    self._copy(nl + j, shard, part, pc.at(0, -xb)).start()
                if part == 1 and da == 0 and xb == db:
                    self._copy(nl + j, shard, part, pc.at(-xa, 0)).start()
            self._down(da, db)
            self._copy(self.n + i, shard, None, pc.sibling).start()

    def cross(self):
        pc, nl = self.pc, len(self.lines)
        for j, (xa, xb, part) in enumerate(self.cross_at):
            shard = pc.shard(xa, xb)
            self._arrived(nl + j, shard, pc.k, part).wait_recv()
            self._copy(self.n + nl + j, shard, part, pc.sibling).start()
            if part == 1:
                self._down(xa, xb)

    def across(self):
        pc = self.pc
        for i, (da, db) in enumerate(self.others()):
            shard = pc.shard(da, db)
            self._deep(2 * self.n + i, shard, pc.k, False, pc.sibling).wait_recv()
            self._deep(2 * self.n + pc.nd + i, shard, pc.k, False, pc.sibling).start()

    def finish(self):
        pc, nl = self.pc, len(self.lines)
        for i, (da, db) in enumerate(self.lines):
            self._arrived(self.n + i, pc.shard(da, db), 1 - pc.k, None).wait_recv()
        for j, (xa, xb, part) in enumerate(self.cross_at):
            self._arrived(self.n + nl + j, pc.shard(xa, xb), 1 - pc.k, part).wait_recv()
        if self.deep is not None:
            for i, (da, db) in enumerate(self.others()):
                shard = pc.shard(da, db)
                self._deep(2 * self.n + pc.nd + i, shard, 1 - pc.k, False, pc.sibling).wait_recv()

    def sent(self):
        pc, nl = self.pc, len(self.lines)
        for i, _ in enumerate(self.lines):
            self._arrived(i, pc.d, pc.k, None).wait_send()
            self._arrived(self.n + i, pc.d, pc.k, None).wait_send()
        for j, (_, _, part) in enumerate(self.cross_at):
            self._arrived(nl + j, pc.d, pc.k, part).wait_send()
            self._arrived(self.n + nl + j, pc.d, pc.k, part).wait_send()
        if self.deep is not None:
            for i, _ in enumerate(self.others()):
                self._deep(2 * self.n + i, pc.d, pc.k, True, pc.sibling).wait_send()
                self._deep(2 * self.n + pc.nd + i, pc.d, pc.k, False, pc.sibling).wait_send()


def row_cut(ref, rows, core, part, lead=0):
    start = core * (rows // 2) + (0 if part is None else part * (rows // 4))
    size = rows // 2 if part is None else rows // 4
    return ref.at[(slice(None),) * lead + (pl.ds(start, size),)]


def share_rows(pc, rows):
    q = rows // 8
    odd = pc.z % 2

    def cut(ref, core, part):
        start = core * (4 * q) + odd * q
        if part is None:
            return ref.at[pl.ds(start, 3 * q)]
        n = 3 * q // 2
        return ref.at[pl.ds(start + part * n, n)]

    def deep(ref, core, mine):
        at = odd * (3 * q) if mine else (1 - odd) * (3 * q)
        return ref.at[pl.ds(core * (4 * q) + at, q)]

    return cut, deep


def share_cols(pc, rows, cols):
    q = cols // 8
    odd = pc.z % 2
    n = rows // 2 // 16 * 16

    def cut(ref, core, part):
        start = pl.multiple_of(core * (4 * q) + odd * q, 128)
        at = slice(None) if part is None else pl.ds(0, n) if part == 0 else pl.ds(n, rows - n)
        return ref.at[at, pl.ds(start, 3 * q)]

    def deep(ref, core, mine):
        at = odd * (3 * q) if mine else (1 - odd) * (3 * q)
        return ref.at[:, pl.ds(pl.multiple_of(core * (4 * q) + at, 128), q)]

    return cut, deep


class Reduce:
    def __init__(self, pc, g, bufs, send, recv, by_rows):
        self.pc, self.g, self.send, self.recv, self.by_rows = pc, g, send, recv, by_rows
        self.r1a, self.r1b, self.r2a, self.r2b = bufs

    @staticmethod
    def count(nd):
        nb = 2 if nd % 2 == 0 else 1
        return 2 * (nd // nb - 1 + nb - 1)

    @staticmethod
    def scratch(nd, rows, cols, by_rows):
        nb = 2 if nd % 2 == 0 else 1
        na = nd // nb
        r, c = (rows // 2, cols) if by_rows else (rows, cols // 2)
        return [
            pltpu.VMEM((na, nb, rows, cols), BF16),
            pltpu.VMEM((na - 1, nb, r, c), BF16),
            pltpu.VMEM((nb - 1, na, r, c), BF16),
            pltpu.VMEM((nb - 1, r, c), BF16),
            pltpu.VMEM((na - 1, r, c), BF16),
        ]

    def part(self, ref, p):
        lead = (slice(None),) * (len(ref.shape) - 2)
        rows, cols = ref.shape[-2:]
        if self.by_rows:
            return ref.at[lead + (pl.ds(p * (rows // 2), rows // 2),)]
        return ref.at[lead + (slice(None), pl.ds(p * (cols // 2), cols // 2))]

    def copies(self, step):
        pc = self.pc
        na, nb = pc.na, pc.nb
        out = []
        base = 0 if step == 1 else na - 1 + nb - 1
        for da in range(1, na):
            a = (pc.a + na - da) % na
            i = base + da - 1
            if step == 1:
                src, dst = self.part(self.g.at[a], 0), self.r1a.at[da - 1]
            else:
                src, dst = self.part(self.g.at[a, pc.b], 1), self.r2b.at[da - 1]
            out.append(remote(src, dst, self.send.at[i], self.recv.at[i], pc.at(-da, 0)))
        for db in range(1, nb):
            b = (pc.b + nb - db) % nb
            i = base + na - 1 + db - 1
            if step == 1:
                src, dst = self.part(self.g.at[:, b], 1), self.r1b.at[db - 1]
            else:
                src, dst = self.part(self.g.at[pc.a, b], 0), self.r2a.at[db - 1]
            out.append(remote(src, dst, self.send.at[i], self.recv.at[i], pc.at(0, -db)))
        return out

    def start(self):
        for cp in self.copies(1):
            cp.start()

    def middle(self):
        pc = self.pc
        for cp in self.copies(1):
            cp.wait_recv()
        for b in range(pc.nb):
            at = self.part(self.g.at[pc.a, b], 0)
            add(at, [self.r1a.at[i, b] for i in range(pc.na - 1)])
        for a in range(pc.na):
            at = self.part(self.g.at[a, pc.b], 1)
            add(at, [self.r1b.at[i, a] for i in range(pc.nb - 1)])
        for cp in self.copies(2):
            cp.start()

    def finish(self, total):
        pc = self.pc
        for cp in self.copies(2):
            cp.wait_recv()
        own = self.g.at[pc.a, pc.b]
        add(self.part(own, 0), [self.r2a.at[i] for i in range(pc.nb - 1)], self.part(total, 0))
        add(self.part(own, 1), [self.r2b.at[i] for i in range(pc.na - 1)], self.part(total, 1))

    def sent(self):
        for cp in self.copies(1) + self.copies(2):
            cp.wait_send()


def add(ref, others, into=None):
    into = ref if into is None else into
    rows = ref.shape[0]
    chunk = next(n for n in (32, 16, rows) if rows % n == 0)

    def some(i, _):
        at = pl.ds(pl.multiple_of(i * chunk, chunk), chunk)
        total = ref[at, :].astype(F32)
        for o in others:
            total = total + o[at, :].astype(F32)
        into[at, :] = total.astype(BF16)
        return 0

    if rows == chunk:
        total = ref[...].astype(F32)
        for o in others:
            total = total + o[...].astype(F32)
        into[...] = total.astype(BF16)
    else:
        lax.fori_loop(0, rows // chunk, some, 0)


PARTS = 4


def chain_part(by_rows):
    def part(ref, p):
        rows, cols = ref.shape[-2:]
        if by_rows:
            n = rows // PARTS
            return ref.at[pl.ds(pl.multiple_of(p * n, n), n)]
        n = cols // PARTS
        return ref.at[:, pl.ds(pl.multiple_of(p * n, n), n)]

    return part


class Chain:
    def __init__(self, pc, t, bufs, send, recv, part):
        self.pc, self.t, self.part = pc, t, part
        self.outer, self.swap, total = bufs
        self.total, self.other = total.at[pc.k], total.at[1 - pc.k]
        self.all = total
        self.send, self.recv = send, recv
        half = pc.nz // 2
        self.low = pc.z < half
        self.end = (pc.z == 0) | (pc.z == pc.nz - 1)
        self.mid = (pc.z == half - 1) | (pc.z == half)
        step = 1 - 2 * (pc.z // half)
        self.inner_id = (pc.d, ((pc.z + step + pc.nz) % pc.nz) * 2 + pc.k)
        self.outer_id = (pc.d, ((pc.z - step + pc.nz) % pc.nz) * 2 + pc.k)

    def up_copy(self, p):
        return remote(
            self.part(self.t, p), self.part(self.outer, p), self.send.at[0, p], self.recv.at[0, p],
            self.inner_id,
        )

    def swap_copy(self, p):
        return remote(
            self.part(self.t, p), self.part(self.swap, p), self.send.at[1, p], self.recv.at[1, p],
            self.inner_id,
        )

    def down_copy(self, p):
        at = self.part(self.total, p)
        return remote(at, at, self.send.at[2, p], self.recv.at[2, p], self.outer_id)

    def side_copy(self, p):
        at = self.part(self.total, p)
        return remote(at, at, self.send.at[3, p], self.recv.at[3, p], self.pc.sibling)

    def side_wait(self, p):
        at = self.part(self.other, p)
        remote(at, at, self.send.at[3, p], self.recv.at[3, p], self.pc.sibling).wait_recv()

    def open(self, p):
        @pl.when(self.end)
        def _():
            @pl.when(self.mid)
            def _():
                self.swap_copy(p).start()

            @pl.when(jnp.logical_not(self.mid))
            def _():
                self.up_copy(p).start()

    def up(self, p):
        @pl.when(jnp.logical_not(self.end))
        def _():
            self.up_copy(p).wait_recv()
            add(self.part(self.t, p), [self.part(self.outer, p)])

            @pl.when(self.mid)
            def _():
                self.swap_copy(p).start()

            @pl.when(jnp.logical_not(self.mid))
            def _():
                self.up_copy(p).start()

    def turn(self, p):
        @pl.when(self.mid)
        def _():
            self.swap_copy(p).wait_recv()
            add(self.part(self.t, p), [self.part(self.swap, p)], self.part(self.total, p))

        @pl.when(jnp.logical_not(self.mid))
        def _():
            self.down_copy(p).wait_recv()

        @pl.when(jnp.logical_not(self.end))
        def _():
            self.down_copy(p).start()

        self.side_copy(p).start()

    def sent(self, p):
        @pl.when(self.mid)
        def _():
            self.swap_copy(p).wait_send()

        @pl.when(jnp.logical_not(self.mid))
        def _():
            self.up_copy(p).wait_send()

        @pl.when(jnp.logical_not(self.end))
        def _():
            self.down_copy(p).wait_send()

        self.side_copy(p).wait_send()


def half_rows(pc, ref, core):
    rows = ref.shape[0] // pc.nd
    h = rows // 2
    return [ref.at[pl.ds(pl.multiple_of(s * rows + core * h, h), h)] for s in range(pc.nd)]


def project_kernel(
    x_ref, gains_ref, cos_ref, sin_ref, wqkv_ref, wattn_ref, win_ref,
    h1t_ref, gains_out, w1_out, w2_out, wqkv_out, wattn_out, heads_out,
    wbuf, abuf, ibuf, h1_ref, gbuf, sendbuf,
    wsend, wrecv, asend, arecv, gsend, grecv, xsend, xrecv, local,
):
    pc = Place()
    nd, nc, nz = pc.nd, pc.nc, pc.nz
    rows = wqkv_ref.shape[0]
    width = wqkv_ref.shape[1] // 3
    tok = x_ref.shape[0]
    w = width // nc
    cw = 2 * w
    own_w = [
        pltpu.make_async_copy(
            wqkv_ref.at[:, pl.ds(g * width, width)], wbuf.at[g, pc.d], local.at[g]
        )
        for g in range(3)
    ]
    for cp in own_w:
        cp.start()
    own_a = pltpu.make_async_copy(wattn_ref, abuf, local.at[3])
    own_a.start()
    own_i = pltpu.make_async_copy(win_ref, ibuf, local.at[5 + nz])
    own_i.start()
    barrier(pc)
    for cp in own_w:
        cp.wait()

    def chip_of(j):
        return (pc.z + j + 1) % nz

    def chunk(j):
        col = pl.multiple_of(chip_of(j) * cw, cw)

        def cut(shard, core, part):
            return row_cut(wbuf.at[:, shard, :, pl.ds(col, cw)], rows, core, part, lead=1)

        return Gather(pc, cut, cut, wsend.at[j], wrecv.at[j])

    def attn_cut(shard, core, part):
        return row_cut(wattn_out.at[shard], rows, core, part)

    def attn_own(shard, core, part):
        return row_cut(wattn_ref, rows, core, part)

    attn = Gather(pc, attn_cut, attn_own, asend, arecv)

    gain_copies = []
    gbuf[pc.d] = gains_ref[...]
    for t in range(1, nd):
        gain_copies.append(
            remote(
                gains_ref, gbuf.at[pc.d], gsend.at[t], grecv.at[t], ((pc.d + t) % nd, pc.c)
            )
        )
        gain_copies[-1].start()
    chunk(0).first()

    xf = x_ref[...].astype(F32)
    mean = jnp.mean(xf, axis=-1, keepdims=True)
    cen = xf - mean
    var = jnp.mean(cen * cen, axis=-1, keepdims=True)
    hat = cen * lax.rsqrt(var + norm_eps)
    for t in range(1, nd):
        src = gbuf.at[(pc.d + nd - t) % nd]
        remote(src, src, gsend.at[t], grecv.at[t], pc.sibling).wait_recv()
    for s in range(nd):
        cols = slice(s * rows, (s + 1) * rows)
        h1_ref[:, cols] = (hat[:, cols] * gbuf[s, 0:1, :]).astype(BF16)
    gains_out[...] = gbuf[...]
    own_a.wait()
    own_a2 = pltpu.make_async_copy(abuf, wattn_out.at[pc.d], local.at[3])
    own_a2.start()
    own_i.wait()
    ff = w1_out.shape[1]
    w1_out[...] = ibuf[:, :ff]
    w2_out[...] = ibuf[:, ff:]
    h1t_ref[...] = jnp.transpose(h1_ref[...])

    lane = lax.broadcasted_iota(jnp.int32, (1, cw), 1)
    low = (lane % HEAD) < HEAD // 2

    def out_copy(j):
        cols = pl.ds(pl.multiple_of(chip_of(j) * cw, cw), cw)
        return pltpu.make_async_copy(
            wbuf.at[:, :, :, cols], wqkv_out.at[:, :, :, cols], local.at[4 + j]
        )

    def place(ref):
        return ref.at[:, pl.ds(pl.multiple_of(pc.c * tok, tok), tok), :]

    def exchange(j, kk):
        return remote(
            sendbuf.at[j, kk], place(heads_out), xsend.at[j, kk], xrecv.at[j, pc.k],
            (pc.d, chip_of(j) * 2 + kk),
        )

    def step(j, _):
        g = chunk(j)
        g.relay()

        @pl.when(j + 1 < nz)
        def _():
            chunk(j + 1).first()

        @pl.when(j + 1 == nz)
        def _():
            attn.first()

        g.cross()
        g.finish()
        out_copy(j).start()
        cols = pl.ds(pl.multiple_of(chip_of(j) * cw, cw), cw)
        for part in range(3):
            weight = wbuf[part, :, :, cols].reshape(nd * rows, cw)
            proj = jnp.dot(h1_ref[...], weight, preferred_element_type=F32)
            if part < 2:
                up = pltpu.roll(proj, cw - HEAD // 2, 1)
                down = pltpu.roll(proj, HEAD // 2, 1)
                proj = proj * cos_ref[...] + jnp.where(low, up, down) * sin_ref[...]
            proj = proj.astype(BF16)
            for kk in range(2):
                sendbuf[j, kk, part] = proj[:, kk * w : (kk + 1) * w]

        @pl.when(j < nz - 1)
        def _():
            exchange(j, 0).start()
            exchange(j, 1).start()

        return 0

    lax.fori_loop(0, nz, step, 0)
    last = nz - 1
    remote(
        sendbuf.at[last, 1 - pc.k], place(heads_out), xsend.at[last, 1 - pc.k],
        xrecv.at[last, pc.k], pc.sibling,
    ).start()
    own_x = pltpu.make_async_copy(
        sendbuf.at[last, pc.k], place(heads_out), local.at[4 + nz]
    )
    own_x.start()
    attn.relay()
    attn.cross()
    attn.finish()

    def arrival(j, kk):
        ref = sendbuf.at[j, kk]
        return remote(ref, ref, xsend.at[j, kk], xrecv.at[j, kk], pc.sibling)

    def drain(j, _):
        arrival(j, 0).wait_recv()
        arrival(j, 1).wait_recv()
        arrival(j, 0).wait_send()
        arrival(j, 1).wait_send()
        chunk(j).sent()
        out_copy(j).wait()
        return 0

    lax.fori_loop(0, nz - 1, drain, 0)
    arrival(last, 1 - pc.k).wait_recv()
    arrival(last, 1 - pc.k).wait_send()
    chunk(last).sent()
    out_copy(last).wait()
    own_x.wait()
    own_a2.wait()
    attn.sent()
    for cp in gain_copies:
        cp.wait_send()


def project(x, gains, cosine, sine, wqkv, wattn, win):
    nd, nc = lax.axis_size("dp"), lax.axis_size("ctx")
    nz = nc // 2
    tok, width = x.shape
    rows = wqkv.shape[0]
    w = width // nc
    n = Gather.count(nd)
    dma = pltpu.SemaphoreType.DMA
    return pl.pallas_call(
        project_kernel,
        out_shape=[
            S((width, tok), BF16),
            S((nd, 8, rows), F32),
            S((rows, win.shape[1] // 2), BF16),
            S((rows, win.shape[1] // 2), BF16),
            S((3, nd, rows, width), BF16),
            S((nd, rows, width), BF16),
            S((3, nc * tok, w), BF16),
        ],
        in_specs=[VMEM, VMEM, VMEM, VMEM, ANY, ANY, ANY],
        out_specs=[VMEM, VMEM, VMEM, VMEM, ANY, ANY, ANY],
        scratch_shapes=[
            pltpu.VMEM((3, nd, rows, width), BF16),
            pltpu.VMEM((rows, width), BF16),
            pltpu.VMEM(win.shape, BF16),
            pltpu.VMEM((tok, width), BF16),
            pltpu.VMEM((nd, 8, rows), F32),
            pltpu.VMEM((nz, 2, 3, tok, w), BF16),
            dma((nz, n)), dma((nz, n)), dma((n,)), dma((n,)),
            dma((nd,)), dma((nd,)), dma((nz, 2)), dma((nz, 2)), dma((6 + nz,)),
        ],
        compiler_params=params(0),
        name="project",
    )(x, gains, cosine, sine, wqkv, wattn, win)


def attend_kernel(
    heads_ref, w1_ref, w2_ref, wout_ref,
    otok_out, o_ref, lse_ref, w1_out, w2_out, wout_out,
    qkv, vext, bounce1, bounce2, bounce3,
    s1, r1, s2, r2, s3, r3, xsend, xrecv, local,
):
    pc = Place()
    nd, nc = pc.nd, pc.nc
    keys, w = heads_ref.shape[1], heads_ref.shape[2]
    tok = keys // nc
    rows = w1_ref.shape[0]
    load = pltpu.make_async_copy(heads_ref, qkv, local.at[0])
    load.start()
    pairs = [(w1_ref, bounce1, w1_out), (w2_ref, bounce2, w2_out), (wout_ref, bounce3, wout_out)]
    for i, (src, mid, _) in enumerate(pairs):
        pltpu.make_async_copy(src, mid, local.at[1 + i]).start()
    barrier(pc)
    cut_r, deep_r = share_rows(pc, rows)
    cut_c, deep_c = share_cols(pc, *wout_ref.shape)

    def item(ref, out, cut, deep, send, recv):
        return Gather(
            pc,
            lambda s, k, p: cut(out.at[s], k, p),
            lambda s, k, p: cut(ref, k, p),
            send,
            recv,
            lambda s, k, mine: deep(out.at[s], k, mine),
        )

    items = [
        item(w1_ref, w1_out, cut_r, deep_r, s1, r1),
        item(w2_ref, w2_out, cut_r, deep_r, s2, r2),
        item(wout_ref, wout_out, cut_c, deep_c, s3, r3),
    ]
    items[0].first()
    items[1].first()
    load.wait()
    for i, (src, mid, _) in enumerate(pairs):
        pltpu.make_async_copy(src, mid, local.at[1 + i]).wait()
    for i, (_, mid, dst) in enumerate(pairs):
        pltpu.make_async_copy(mid, dst.at[pc.d], local.at[1 + i]).start()
    nh = w // HEAD
    for h in range(nh):
        vext[h, :, :HEAD] = qkv[2, :, h * HEAD : (h + 1) * HEAD]
        vext[h, :, HEAD:] = jnp.ones((keys, HEAD), BF16)
    scale = HEAD ** (-0.5) * LOG2E

    def block_copy(i):
        to = (pc.c + i + 1) % nc
        at = pl.ds(pl.multiple_of(to * tok, tok), tok)
        return remote(
            o_ref.at[at], otok_out.at[pc.c], xsend.at[i], xrecv.at[i], (pc.d, to)
        )

    def block(i, _):
        at = pl.ds(pl.multiple_of(((pc.c + i + 1) % nc) * tok, tok), tok)
        for h in range(nh):
            hs = slice(h * HEAD, (h + 1) * HEAD)
            s = lax.dot_general(
                qkv[0, at, hs], qkv[1, :, hs], (((1,), (1,)), ((), ())),
                preferred_element_type=F32,
            )
            m = jnp.max(s, axis=1, keepdims=True)
            p = jnp.exp2(s * scale - m * scale).astype(BF16)
            ol = jnp.dot(p, vext[h], preferred_element_type=F32)
            total = ol[:, HEAD:]
            o_ref[at, hs] = (ol[:, :HEAD] / total).astype(BF16)
            lse = m * scale + jnp.log2(total)
            lse_ref[h, :, at] = jnp.transpose(jnp.concatenate([lse, lse], axis=1))[:8]

        @pl.when(i < nc - 1)
        def _():
            block_copy(i).start()

        @pl.when(i == nc // 2)
        def _():
            items[0].relay()
            items[2].first()

        return 0

    lax.fori_loop(0, nc, block, 0)
    own = pltpu.make_async_copy(
        o_ref.at[pl.ds(pl.multiple_of(pc.c * tok, tok), tok)], otok_out.at[pc.c], local.at[0]
    )
    own.start()
    items[1].relay()
    items[0].cross()
    items[2].relay()
    items[1].cross()
    items[0].across()
    items[2].cross()
    items[1].across()
    items[2].across()
    for it in items:
        it.finish()

    def drain(i, _):
        got = otok_out.at[(pc.c + nc - i - 1) % nc]
        remote(got, got, xsend.at[i], xrecv.at[i], pc.sibling).wait_recv()
        block_copy(i).wait_send()
        return 0

    lax.fori_loop(0, nc - 1, drain, 0)
    own.wait()
    for i, (_, mid, dst) in enumerate(pairs):
        pltpu.make_async_copy(mid, dst.at[pc.d], local.at[1 + i]).wait()
    for it in items:
        it.sent()


def attend(heads, w1, w2, wout):
    nd, nc = lax.axis_size("dp"), lax.axis_size("ctx")
    _, keys, w = heads.shape
    nh = w // HEAD
    n = Gather.count(nd)
    dma = pltpu.SemaphoreType.DMA
    return pl.pallas_call(
        attend_kernel,
        out_shape=[
            S((nc, keys // nc, w), BF16),
            S((keys, w), BF16),
            S((nh, 8, keys), F32),
            S((nd,) + w1.shape, BF16),
            S((nd,) + w2.shape, BF16),
            S((nd,) + wout.shape, BF16),
        ],
        in_specs=[ANY, ANY, ANY, ANY],
        out_specs=[ANY, VMEM, VMEM, ANY, ANY, ANY],
        scratch_shapes=[
            pltpu.VMEM((3, keys, w), BF16),
            pltpu.VMEM((nh, keys, 2 * HEAD), BF16),
            pltpu.VMEM(w1.shape, BF16),
            pltpu.VMEM(w2.shape, BF16),
            pltpu.VMEM(wout.shape, BF16),
            dma((n,)), dma((n,)), dma((n,)), dma((n,)), dma((n,)), dma((n,)),
            dma((nc,)), dma((nc,)), dma((4,)),
        ],
        compiler_params=params(1),
        name="attend",
    )(heads, w1, w2, wout)


def attend_back_kernel(
    heads_ref, o_ref, lse_ref, dout_ref, cos_ref, sin_ref, h2t_ref, dl1_ref, dl2_ref,
    dtok_out, t1_ref, t2_ref,
    qkv, dout, delta, dq, sendbuf, h2t, dl,
    ga, ra0, ra1, ra2, ra3, gb, rb0, rb1, rb2, rb3,
    dsend, drecv, xsend, xrecv, ssend, srecv, asend, arecv, bsend, brecv, local,
):
    pc = Place()
    nd = pc.nd
    nc = pc.nc
    keys, w = heads_ref.shape[1], heads_ref.shape[2]
    tok = keys // nc
    nh = w // HEAD
    load = pltpu.make_async_copy(heads_ref, qkv, local.at[0])
    load.start()
    mine_t = half_rows(pc, h2t_ref, pc.k)
    hers_t = half_rows(pc, h2t_ref, 1 - pc.k)
    fetch = [pltpu.make_async_copy(mine_t[s], h2t.at[0, s], local.at[2 + s]) for s in range(nd)]
    fetch.append(pltpu.make_async_copy(dl1_ref, dl.at[0, 0], local.at[2 + nd]))
    fetch.append(pltpu.make_async_copy(dl2_ref, dl.at[1, 0], local.at[3 + nd]))
    for cp in fetch:
        cp.start()
    barrier(pc)
    swap = [
        remote(hers_t[s], h2t.at[1, s], ssend.at[s], srecv.at[s], pc.sibling) for s in range(nd)
    ]
    swap.append(remote(dl1_ref, dl.at[0, 1], ssend.at[nd], srecv.at[nd], pc.sibling))
    swap.append(remote(dl2_ref, dl.at[1, 1], ssend.at[nd + 1], srecv.at[nd + 1], pc.sibling))
    for cp in swap:
        cp.start()
    mine = pl.ds(pl.multiple_of(pc.c * tok, tok), tok)
    for i in range(nc - 1):
        to = (pc.c + i + 1) % nc
        remote(dout_ref.at[to], dout.at[mine], dsend.at[i], drecv.at[i], (pc.d, to)).start()
    own = pltpu.make_async_copy(dout_ref.at[pc.c], dout.at[mine], local.at[1])
    own.start()
    ra = Reduce(pc, ga, (ra0, ra1, ra2, ra3), asend, arecv, True)
    rb = Reduce(pc, gb, (rb0, rb1, rb2, rb3), bsend, brecv, True)
    for cp in fetch:
        cp.wait()
    for cp in swap[: nd + 1]:
        cp.wait_recv()
    weight_grad(pc, ga, h2t, dl.at[0])
    ra.start()
    swap[nd + 1].wait_recv()
    weight_grad(pc, gb, h2t, dl.at[1])
    rb.start()
    dq[...] = jnp.zeros_like(dq)
    load.wait()
    own.wait()
    for i in range(nc - 1):
        src = (pc.c + nc - i - 1) % nc
        got = dout.at[pl.ds(pl.multiple_of(src * tok, tok), tok)]
        remote(got, got, dsend.at[i], drecv.at[i], pc.sibling).wait_recv()

    def deltas(i, _):
        at = pl.ds(pl.multiple_of(i * tok, tok), tok)
        t = jnp.transpose(o_ref[at, :].astype(F32) * dout[at, :].astype(F32))
        for h in range(nh):
            row = jnp.sum(t[h * HEAD : (h + 1) * HEAD], axis=0, keepdims=True)
            delta[h, :, at] = jnp.broadcast_to(row, (8, tok))
        return 0

    lax.fori_loop(0, nc, deltas, 0)
    scale = HEAD ** (-0.5)
    lane = lax.broadcasted_iota(jnp.int32, (1, w), 1)
    low = (lane % HEAD) < HEAD // 2

    def unrotate(g, at):
        t = g * sin_ref[at, :]
        if w == HEAD:
            up = jnp.concatenate([t[:, HEAD // 2 :], t[:, : HEAD // 2]], axis=1)
            down = up
        else:
            up = pltpu.roll(t, w - HEAD // 2, 1)
            down = pltpu.roll(t, HEAD // 2, 1)
        return g * cos_ref[at, :] + jnp.where(low, up, -down)

    def kv_copy(i):
        to = (pc.c + i + 1) % nc
        return remote(
            sendbuf.at[to, pl.ds(1, 2)], dtok_out.at[pc.c, pl.ds(1, 2)],
            xsend.at[0, i], xrecv.at[0, i], (pc.d, to),
        )

    def q_copy(i):
        to = (pc.c + i + 1) % nc
        return remote(
            sendbuf.at[to, 0], dtok_out.at[pc.c, 0], xsend.at[1, i], xrecv.at[1, i], (pc.d, to)
        )

    def block(i, _):
        to = (pc.c + i + 1) % nc
        at = pl.ds(pl.multiple_of(to * tok, tok), tok)
        dks, dvs = [], []
        for h in range(nh):
            hs = slice(h * HEAD, (h + 1) * HEAD)
            kb, vb = qkv[1, at, hs], qkv[2, at, hs]
            q, do = qkv[0, :, hs], dout[:, hs]
            nt = (((1,), (1,)), ((), ()))
            st = lax.dot_general(kb, q, nt, preferred_element_type=F32)
            p = jnp.exp2(st * (scale * LOG2E) - lse_ref[h, 0:1, :])
            dvs.append(jnp.dot(p.astype(BF16), do, preferred_element_type=F32))
            dp = lax.dot_general(vb, do, nt, preferred_element_type=F32)
            ds = (p * (dp - delta[h, 0:1, :])).astype(BF16)
            dks.append(jnp.dot(ds, q, preferred_element_type=F32))
            dq[:, hs] += lax.dot_general(
                ds, kb, (((0,), (0,)), ((), ())), preferred_element_type=F32
            )
        dk = jnp.concatenate(dks, axis=1) * scale
        sendbuf[to, 1] = unrotate(dk, at).astype(BF16)
        sendbuf[to, 2] = jnp.concatenate(dvs, axis=1).astype(BF16)

        @pl.when(i < nc - 1)
        def _():
            kv_copy(i).start()

        @pl.when(i == (nc * 3) // 8)
        def _():
            ra.middle()

        @pl.when(i == (nc * 7) // 8)
        def _():
            rb.middle()

        return 0

    lax.fori_loop(0, nc, block, 0)

    def q_block(i, _):
        to = (pc.c + i + 1) % nc
        at = pl.ds(pl.multiple_of(to * tok, tok), tok)
        sendbuf[to, 0] = unrotate(dq[at, :] * scale, at).astype(BF16)

        @pl.when(i < nc - 1)
        def _():
            q_copy(i).start()

        return 0

    lax.fori_loop(0, nc, q_block, 0)
    keep = pltpu.make_async_copy(sendbuf.at[pc.c], dtok_out.at[pc.c], local.at[1])
    keep.start()
    ra.finish(t1_ref)
    rb.finish(t2_ref)

    def drain(i, _):
        got = dtok_out.at[(pc.c + nc - i - 1) % nc]
        remote(
            got.at[pl.ds(1, 2)], got.at[pl.ds(1, 2)], xsend.at[0, i], xrecv.at[0, i], pc.sibling
        ).wait_recv()
        remote(got.at[0], got.at[0], xsend.at[1, i], xrecv.at[1, i], pc.sibling).wait_recv()
        kv_copy(i).wait_send()
        q_copy(i).wait_send()
        to = (pc.c + i + 1) % nc
        remote(
            dout_ref.at[to], dout.at[mine], dsend.at[i], drecv.at[i], (pc.d, to)
        ).wait_send()
        return 0

    lax.fori_loop(0, nc - 1, drain, 0)
    keep.wait()
    for cp in swap:
        cp.wait_send()
    ra.sent()
    rb.sent()


def weight_grad(pc, g, lhs, rhs):
    def shard(s, _):
        total = jnp.dot(lhs[0, s], rhs[0], preferred_element_type=F32)
        total = total + jnp.dot(lhs[1, s], rhs[1], preferred_element_type=F32)
        g[s // pc.nb, s % pc.nb] = total.astype(BF16)
        return 0

    lax.fori_loop(0, pc.nd, shard, 0)


def attend_back(heads, o, lse, dout, cosine, sine, h2t, dl1, dl2):
    nc, nd = lax.axis_size("ctx"), lax.axis_size("dp")
    ff = dl1.shape[1]
    hr = h2t.shape[0] // nd // 2
    n = Reduce.count(nd)
    _, keys, w = heads.shape
    nh = w // HEAD
    tok = keys // nc
    dma = pltpu.SemaphoreType.DMA
    return pl.pallas_call(
        attend_back_kernel,
        out_shape=[S((nc, 3, tok, w), BF16), S((hr, ff), BF16), S((hr, ff), BF16)],
        in_specs=[ANY, VMEM, VMEM, ANY, VMEM, VMEM, ANY, ANY, ANY],
        out_specs=[ANY, VMEM, VMEM],
        scratch_shapes=[
            pltpu.VMEM((3, keys, w), BF16),
            pltpu.VMEM((keys, w), BF16),
            pltpu.VMEM((nh, 8, keys), F32),
            pltpu.VMEM((keys, w), F32),
            pltpu.VMEM((nc, 3, tok, w), BF16),
            pltpu.VMEM((2, nd, hr, tok), BF16),
            pltpu.VMEM((2, 2, tok, ff), BF16),
            *Reduce.scratch(nd, hr, ff, True),
            *Reduce.scratch(nd, hr, ff, True),
            dma((nc,)), dma((nc,)), dma((2, nc)), dma((2, nc)), dma((nd + 2,)), dma((nd + 2,)),
            dma((n,)), dma((n,)), dma((n,)), dma((n,)), dma((4 + nd,)),
        ],
        compiler_params=params(2),
        name="attend_back",
    )(heads, o, lse, dout, cosine, sine, h2t, dl1, dl2)


def each(count, *calls):
    def body(p, _):
        for call in calls:
            call(p)
        return 0

    lax.fori_loop(0, count, body, 0)


def close_kernel(
    dtok_ref, h1t_ref, wqkv_ref, x_ref, gain_ref, dres_ref, dres_b_ref, part_ref,
    actt_ref, c_ref, ot_ref, t1_ref, t2_ref,
    dx_ref, gain_out, out1, out2, outq, outo, outa,
    dtok, dproj, h1t, wqkv, actt, cot, ot, dres,
    gq, q0, q1, q2, q3, go, o0, o1, o2, o3, ga, a0, a1, a2, a3,
    tq, to, ta, u1, s1, f1, u2, s2, f2, uq, sq, fq, uo, so, fo, ua, sa, fa,
    gmine, gctx, gdp,
    ssend, srecv, qsend, qrecv, osend, orecv, asend, arecv, csend, crecv, gsend, grecv, local,
    outsem,
):
    pc = Place()
    nd, nc = pc.nd, pc.nc
    _, _, tok, w = dtok_ref.shape
    width = nc * w
    half = cot.shape[2]
    nr = actt.shape[2]
    col = lambda core: pl.ds(pl.multiple_of(core * half, half), half)
    h1_mine, h1_hers = half_rows(pc, h1t_ref, pc.k), half_rows(pc, h1t_ref, 1 - pc.k)
    o_mine, o_hers = half_rows(pc, ot_ref, pc.k), half_rows(pc, ot_ref, 1 - pc.k)
    acts = [actt_ref.at[pl.ds(s * nr, nr)] for s in range(nd)]
    pairs = [(dtok_ref, dtok), (wqkv_ref, wqkv), (dres_b_ref, dres.at[0])]
    pairs += [(c_ref.at[:, col(pc.k)], cot.at[0])]
    pairs += [(h1_mine[s], h1t.at[0, s]) for s in range(nd)]
    pairs += [(o_mine[s], ot.at[0, s]) for s in range(nd)]
    pairs += [(acts[s], actt.at[0, s]) for s in range(nd)]
    load = [pltpu.make_async_copy(a, b, local.at[i]) for i, (a, b) in enumerate(pairs)]
    for cp in load:
        cp.start()
    barrier(pc)
    rq = Reduce(pc, gq, (q0, q1, q2, q3), qsend, qrecv, True)
    ro = Reduce(pc, go, (o0, o1, o2, o3), osend, orecv, False)
    ra = Reduce(pc, ga, (a0, a1, a2, a3), asend, arecv, True)
    rows_part, cols_part = chain_part(True), chain_part(False)
    chains = [
        Chain(pc, t, bufs, csend.at[i], crecv.at[i], part)
        for i, (t, bufs, part) in enumerate(
            [
                (t1_ref, (u1, s1, f1), rows_part),
                (t2_ref, (u2, s2, f2), rows_part),
                (tq, (uq, sq, fq), rows_part),
                (to, (uo, so, fo), cols_part),
                (ta, (ua, sa, fa), rows_part),
            ]
        )
    ]
    c1, c2, cq, co, ca = chains
    each(PARTS, c1.open)
    each(PARTS, c2.open)
    pairs = [(h1_hers[s], h1t.at[1, s]) for s in range(nd)] + [(dproj.at[0], dproj.at[1])]
    pairs += [(o_hers[s], ot.at[1, s]) for s in range(nd)] + [(dres_b_ref, dres.at[1])]
    pairs += [(acts[s], actt.at[1, s]) for s in range(nd)]
    pairs += [(c_ref.at[:, col(1 - pc.k)], cot.at[1])]
    swap = [
        remote(src, dst, ssend.at[i], srecv.at[i], pc.sibling) for i, (src, dst) in enumerate(pairs)
    ]
    for cp in swap[:nd]:
        cp.start()
    load[0].wait()
    for g in range(3):
        for i in range(nc):
            dproj[0, :, g * width + i * w : g * width + (i + 1) * w] = dtok[i, g]
    for cp in swap[nd:]:
        cp.start()
    for cp in load[1:]:
        cp.wait()
    nt = (((1,), (1,)), ((), ()))
    dh1 = jnp.zeros((tok, width), F32)
    for g in range(3):
        dh1 = dh1 + lax.dot_general(
            dproj[0, :, g * width : (g + 1) * width], wqkv[g].reshape(width, width), nt,
            preferred_element_type=F32,
        )
    for cp in swap[: nd + 1]:
        cp.wait_recv()
    weight_grad(pc, gq, h1t, dproj)
    rq.start()
    c1.up(0)
    c1.up(1)
    for cp in swap[nd + 1 : 2 * nd + 2]:
        cp.wait_recv()
    weight_grad(pc, ga, ot, dres)
    ra.start()
    c1.up(2)
    for cp in swap[2 * nd + 2 :]:
        cp.wait_recv()
    weight_grad(pc, go, actt, cot)
    c1.up(3)
    c1.turn(0)

    xf = x_ref[...].astype(F32)
    mean = jnp.mean(xf, axis=-1, keepdims=True)
    cen = xf - mean
    inv = lax.rsqrt(jnp.mean(cen * cen, axis=-1, keepdims=True) + norm_eps)
    hat = cen * inv
    gain = jnp.concatenate([gain_ref[s, 0:1, :] for s in range(nd)], axis=1)
    dhat = dh1 * gain
    m1 = jnp.mean(dhat, axis=-1, keepdims=True)
    m2 = jnp.mean(dhat * hat, axis=-1, keepdims=True)
    dx_ref[...] = (dres_ref[...] + inv * (dhat - m1 - hat * m2)).astype(BF16)
    row = lax.broadcasted_iota(jnp.int32, (8, 1), 0)
    gmine[...] = jnp.where(row == 0, jnp.sum(dh1 * hat, axis=0, keepdims=True), part_ref[...])
    gcopies = []
    for t in range(1, nc):
        gcopies.append(
            remote(gmine, gctx.at[t], gsend.at[t], grecv.at[t], (pc.d, (pc.c + t) % nc))
        )
        gcopies[-1].start()

    c2.up(0)
    c1.turn(1)
    c2.up(1)
    c1.turn(2)
    rq.middle()
    ro.start()
    c2.up(2)
    c1.turn(3)
    c2.up(3)
    c2.turn(0)
    for cp in gcopies:
        cp.wait_recv()
    total = gmine[...]
    for t in range(1, nc):
        total = total + gctx[t]
    for cp in gcopies:
        cp.wait_send()
    gmine[...] = total
    dcopies = []
    rows = gain_out.shape[1]
    for t in range(1, nd):
        to_d = (pc.d + t) % nd
        dcopies.append(
            remote(
                gmine.at[:, pl.ds(pl.multiple_of(to_d * rows, 128), rows)], gdp.at[t],
                gsend.at[nc + t], grecv.at[nc + t], (to_d, pc.c),
            )
        )
        dcopies[-1].start()
    c2.turn(1)
    ra.middle()
    c2.turn(2)
    c2.turn(3)
    rq.finish(tq)
    each(PARTS, cq.open)
    for cp in dcopies:
        cp.wait_recv()
    total = gmine[:, pl.ds(pl.multiple_of(pc.d * rows, 128), rows)]
    for t in range(1, nd):
        total = total + gdp[t]
    gain_out[...] = total
    outs = [
        pltpu.make_async_copy(c.all, out, outsem.at[i])
        for i, (c, out) in enumerate(zip(chains, (out1, out2, outq, outo, outa)))
    ]
    each(PARTS, c1.side_wait)
    outs[0].start()
    each(PARTS, c2.side_wait)
    outs[1].start()
    cq.up(0)
    cq.up(1)
    ro.middle()
    cq.turn(0)
    cq.up(2)
    ra.finish(ta)
    each(PARTS, ca.open)
    cq.turn(1)
    cq.up(3)
    cq.turn(2)
    ro.finish(to)
    each(PARTS, co.open)
    cq.turn(3)
    each(PARTS, ca.up)
    each(PARTS, cq.side_wait)
    outs[2].start()
    each(PARTS, ca.turn)
    co.up(0)
    each(PARTS - 1, lambda p: co.up(p + 1), co.turn)
    co.turn(PARTS - 1)
    each(PARTS, ca.side_wait)
    outs[4].start()
    each(PARTS, co.side_wait)
    outs[3].start()
    for cp in swap + dcopies:
        cp.wait_send()
    for r in (rq, ro, ra):
        r.sent()
    for c in chains:
        each(PARTS, c.sent)
    for cp in outs:
        cp.wait()


def close(dtok, h1t, wqkv, x, gains, dres, dres_b, part, actt, cot, ot, t1, t2):
    nd, nc = lax.axis_size("dp"), lax.axis_size("ctx")
    tok, width = x.shape
    ff = actt.shape[0]
    rows = width // nd
    hr = rows // 2
    nq, ns = Reduce.count(nd), 3 * nd + 3
    dma = pltpu.SemaphoreType.DMA
    sizes = [(hr, ff), (hr, ff), (hr, 3 * width), (ff // nd, width // 2), (hr, width)]
    n = len(sizes)
    vm = lambda *shape: pltpu.VMEM(shape, BF16)
    chain_bufs = [b for size in sizes for b in (vm(*size), vm(*size), vm(2, *size))]
    return pl.pallas_call(
        close_kernel,
        out_shape=[S((tok, width), BF16), S((8, rows), F32)]
        + [S((2,) + size, BF16) for size in sizes],
        in_specs=[ANY, ANY, ANY, VMEM, VMEM, VMEM, ANY, VMEM, ANY, ANY, ANY, VMEM, VMEM],
        out_specs=[VMEM] * 2 + [ANY] * n,
        scratch_shapes=[
            vm(*dtok.shape), vm(2, tok, 3 * width), vm(2, nd, hr, tok), vm(*wqkv.shape),
            vm(2, nd, ff // nd, tok), vm(2, tok, width // 2), vm(2, nd, hr, tok), vm(2, tok, width),
            *Reduce.scratch(nd, hr, 3 * width, True),
            *Reduce.scratch(nd, ff // nd, width // 2, False),
            *Reduce.scratch(nd, hr, width, True),
            vm(*sizes[2]), vm(*sizes[3]), vm(*sizes[4]),
            *chain_bufs,
            pltpu.VMEM((8, width), F32), pltpu.VMEM((nc, 8, width), F32),
            pltpu.VMEM((nd, 8, rows), F32),
            dma((ns,)), dma((ns,)), dma((nq,)), dma((nq,)), dma((nq,)), dma((nq,)),
            dma((nq,)), dma((nq,)), dma((n, 4, PARTS)), dma((n, 4, PARTS)),
            dma((nc + nd,)), dma((nc + nd,)), dma((4 + 3 * nd,)), dma((n,)),
        ],
        compiler_params=params(3),
        name="close",
    )(dtok, h1t, wqkv, x, gains, dres, dres_b, part, actt, cot, ot, t1, t2)


def norm_rows(values, gain):
    row_mean = jnp.mean(values, axis=-1, keepdims=True)
    centred = values - row_mean
    row_var = jnp.mean(centred * centred, axis=-1, keepdims=True)
    return centred * lax.rsqrt(row_var + norm_eps) * gain


def gelu_exact(values):
    return 0.5 * values * (1.0 + lax.erf(values * 0.7071067811865476))


def gelu_slope(values):
    return (
        0.5 * (1.0 + lax.erf(values * 0.7071067811865476))
        + values * jnp.exp(-0.5 * values * values) * 0.3989422804014327
    )


def rope_angles(positions, lanes):
    half = HEAD // 2
    freq = rope_theta ** (-(jnp.arange(half, dtype=F32) * 2.0 / HEAD))
    freq = jnp.tile(freq, lanes // half)
    return positions.astype(F32)[:, None] * freq[None, :]


def on_device(
    tokens,
    norm1_gain,
    qkv_weight,
    attn_out_weight,
    norm2_gain,
    mlp_in_weight,
    mlp_out_weight,
    cotangent,
):
    _, tok, width = tokens.shape
    nc, nd = lax.axis_size("ctx"), lax.axis_size("dp")
    keys = tok * nc
    w = width // nc
    ff = mlp_in_weight.shape[1] // 2
    rows = norm1_gain.shape[0]
    x = tokens.reshape(tok, width)
    upstream = cotangent.reshape(tok, width)
    gains = jnp.concatenate(
        [
            norm1_gain.astype(F32)[None],
            norm2_gain.astype(F32)[None],
            jnp.zeros((6, rows), F32),
        ]
    )
    ang = rope_angles(lax.axis_index("ctx") * tok + jnp.arange(tok, dtype=jnp.int32), 2 * w)
    sign = jnp.where(jnp.arange(2 * w) % HEAD < HEAD // 2, -1.0, 1.0).astype(F32)
    h1t, gains_all, w1s, w2s, wqkv, wattn, heads = project(
        x, gains, jnp.cos(ang), jnp.sin(ang) * sign[None], qkv_weight, attn_out_weight,
        mlp_in_weight,
    )
    otok, o_heads, lse, w1, w2, wout = attend(heads, w1s, w2s, mlp_out_weight)
    wattn = wattn.reshape(width, width)
    w1 = w1.reshape(width, ff)
    w2 = w2.reshape(width, ff)
    wout = wout.reshape(ff, width)
    gain_one = gains_all[:, 0].reshape(width)
    gain_two = gains_all[:, 1].reshape(width)

    attended_b = jnp.transpose(otok, (1, 0, 2)).reshape(tok, width)
    inputs_f = x.astype(F32)
    attn_res = inputs_f + jnp.dot(attended_b, wattn, preferred_element_type=F32)
    normed_two = norm_rows(attn_res, gain_two).astype(BF16)
    gelu_in = jnp.dot(normed_two, w1, preferred_element_type=F32)
    gate_in = jnp.dot(normed_two, w2, preferred_element_type=F32)
    activated = (gelu_exact(gelu_in) * gate_in).astype(BF16)
    layer_out = (attn_res + jnp.dot(activated, wout, preferred_element_type=F32)).astype(BF16)
    grad_act = jnp.dot(upstream, wout.T, preferred_element_type=F32)
    dl1 = (grad_act * gate_in * gelu_slope(gelu_in)).astype(BF16)
    dl2 = (grad_act * gelu_exact(gelu_in)).astype(BF16)
    grad_normed_two = jnp.dot(dl1, w1.T, preferred_element_type=F32) + jnp.dot(
        dl2, w2.T, preferred_element_type=F32
    )
    _, pull_two = jax.vjp(norm_rows, attn_res, gain_two)
    grad_res_norm, grad_gain_two = pull_two(grad_normed_two)
    grad_res = upstream.astype(F32) + grad_res_norm
    grad_res_b = grad_res.astype(BF16)
    dout = jnp.dot(grad_res_b, wattn.T, preferred_element_type=F32).astype(BF16)
    dout = jnp.transpose(dout.reshape(tok, nc, w), (1, 0, 2))

    near = rope_angles(jnp.arange(tok, dtype=jnp.int32), w)[None]
    far = rope_angles(jnp.arange(nc, dtype=jnp.int32) * tok, w)[:, None]
    cos_near, sin_near, cos_far, sin_far = lax.optimization_barrier(
        (jnp.cos(near), jnp.sin(near), jnp.cos(far), jnp.sin(far))
    )
    cos_all = (cos_far * cos_near - sin_far * sin_near).reshape(keys, w)
    sin_all = (sin_far * cos_near + cos_far * sin_near).reshape(keys, w)
    dtok, t1, t2 = attend_back(
        heads, o_heads, lse, dout, cos_all, sin_all, normed_two.T, dl1, dl2
    )
    input_grad, gain_grads, in1, in2, gqkv, gout, gattn = close(
        dtok, h1t, wqkv, x, gains_all, grad_res, grad_res_b, grad_gain_two.reshape(1, width),
        activated.T, upstream, attended_b.T, t1, t2,
    )
    grad_in = jnp.concatenate([in1.reshape(rows, ff), in2.reshape(rows, ff)], axis=1)
    return (
        layer_out.reshape(1, tok, width),
        input_grad.reshape(1, tok, width),
        gain_grads[0],
        gqkv.reshape(rows, 3 * width).astype(F32),
        gattn.reshape(rows, width).astype(F32),
        gain_grads[1],
        grad_in.astype(F32),
        jnp.concatenate([gout[0], gout[1]], axis=1).astype(F32),
    )


def solution(mesh):
    in_specs = (
        P("dp", "ctx", None),
        P("dp"),
        P("dp", None),
        P("dp", None),
        P("dp"),
        P("dp", None),
        P("dp", None),
        P("dp", "ctx", None),
    )
    out_specs = (
        P("dp", "ctx", None),
        P("dp", "ctx", None),
        P("dp"),
        P("dp", None),
        P("dp", None),
        P("dp"),
        P("dp", None),
        P("dp", None),
    )
    return jax.shard_map(
        on_device, mesh=mesh, in_specs=in_specs, out_specs=out_specs, check_vma=False
    )
```

```python
import functools

import jax
import jax.numpy as jnp
from jax import lax
from jax.experimental import pallas as pl
from jax.experimental.pallas import tpu as pltpu
from jax.sharding import PartitionSpec as P

HEAD = 64
norm_eps = 1e-05
rope_theta = 160000.0
F32 = jnp.float32
BF16 = jnp.bfloat16
MESH = pl.DeviceIdType.MESH
LOG2E = 1.4426950408889634
VMEM_LIMIT = 64 * 1024 * 1024 - 65536
ANY = pl.BlockSpec(memory_space=pl.ANY)
VMEM = pl.BlockSpec(memory_space=pltpu.VMEM)
S = jax.ShapeDtypeStruct


def params(cid):
    return pltpu.CompilerParams(
        collective_id=cid, has_side_effects=True, vmem_limit_bytes=VMEM_LIMIT
    )


class Place:
    def __init__(self):
        self.nd = lax.axis_size("dp")
        self.nc = lax.axis_size("ctx")
        self.d = lax.axis_index("dp")
        self.c = lax.axis_index("ctx")
        self.nb = 2 if self.nd % 2 == 0 else 1
        self.na = self.nd // self.nb
        self.a = self.d // self.nb
        self.b = self.d % self.nb
        self.nz = self.nc // 2
        self.z = self.c // 2
        self.k = self.c % 2
        self.sibling = (self.d, self.z * 2 + 1 - self.k)

    def shard(self, da, db):
        return ((self.a + da) % self.na) * self.nb + (self.b + db) % self.nb

    def at(self, da, db):
        return (self.shard(da, db), self.c)


def barrier(pc, dp=True, ctx=True):
    sem = pltpu.get_barrier_semaphore()
    count = 0
    if dp:
        for t in range(1, pc.nd):
            pl.semaphore_signal(
                sem, inc=1, device_id=((pc.d + t) % pc.nd, pc.c), device_id_type=MESH
            )
            count += 1
    if ctx:
        for t in range(1, pc.nc):
            pl.semaphore_signal(
                sem, inc=1, device_id=(pc.d, (pc.c + t) % pc.nc), device_id_type=MESH
            )
            count += 1
    pl.semaphore_wait(sem, count)


def remote(src, dst, send, recv, target):
    return pltpu.make_async_remote_copy(
        src_ref=src,
        dst_ref=dst,
        send_sem=send,
        recv_sem=recv,
        device_id=target,
        device_id_type=MESH,
    )


class Gather:
    def __init__(self, pc, cut, own, send, recv, deep=None):
        self.pc, self.cut, self.own, self.send, self.recv, self.deep = pc, cut, own, send, recv, deep
        self.lines = [(da, 0) for da in range(1, pc.na)] + [(0, db) for db in range(1, pc.nb)]
        self.cross_at = [
            (da, db, part)
            for part in (0, 1)
            for da in range(1, pc.na)
            for db in range(1, pc.nb)
        ]
        self.n = len(self.lines) + len(self.cross_at)
        self.pair = (pc.d, (pc.z + 1 - 2 * (pc.z % 2)) * 2 + pc.k)

    @staticmethod
    def count(nd):
        nb = 2 if nd % 2 == 0 else 1
        na = nd // nb
        return 2 * ((na - 1) + (nb - 1) + 2 * (na - 1) * (nb - 1)) + 2 * nd

    def _copy(self, index, shard, part, target, own=False):
        src = (self.own if own else self.cut)(shard, self.pc.k, part)
        dst = self.cut(shard, self.pc.k, part)
        return remote(src, dst, self.send.at[index], self.recv.at[index], target)

    def _arrived(self, index, shard, core, part):
        ref = self.cut(shard, core, part)
        return remote(ref, ref, self.send.at[index], self.recv.at[index], self.pc.sibling)

    def _deep(self, index, shard, core, mine, target):
        ref = self.deep(shard, core, mine)
        return remote(ref, ref, self.send.at[index], self.recv.at[index], target)

    def others(self):
        pc = self.pc
        return [(da, db) for da in range(pc.na) for db in range(pc.nb) if (da, db) != (0, 0)]

    def first(self):
        pc = self.pc
        for i, (da, db) in enumerate(self.lines):
            self._copy(i, pc.d, None, pc.at(-da, -db), own=True).start()

    def _down(self, da, db):
        if self.deep is not None:
            i = self.others().index((da, db))
            self._deep(2 * self.n + i, self.pc.shard(da, db), self.pc.k, True, self.pair).start()

    def relay(self):
        pc, nl = self.pc, len(self.lines)
        for i, (da, db) in enumerate(self.lines):
            shard = pc.shard(da, db)
            self._arrived(i, shard, pc.k, None).wait_recv()
            for j, (xa, xb, part) in enumerate(self.cross_at):
                if part == 0 and db == 0 and xa == da:
                    self._copy(nl + j, shard, part, pc.at(0, -xb)).start()
                if part == 1 and da == 0 and xb == db:
                    self._copy(nl + j, shard, part, pc.at(-xa, 0)).start()
            self._down(da, db)
            self._copy(self.n + i, shard, None, pc.sibling).start()

    def cross(self):
        pc, nl = self.pc, len(self.lines)
        for j, (xa, xb, part) in enumerate(self.cross_at):
            shard = pc.shard(xa, xb)
            self._arrived(nl + j, shard, pc.k, part).wait_recv()
            self._copy(self.n + nl + j, shard, part, pc.sibling).start()
            if part == 1:
                self._down(xa, xb)

    def across(self):
        pc = self.pc
        for i, (da, db) in enumerate(self.others()):
            shard = pc.shard(da, db)
            self._deep(2 * self.n + i, shard, pc.k, False, pc.sibling).wait_recv()
            self._deep(2 * self.n + pc.nd + i, shard, pc.k, False, pc.sibling).start()

    def finish(self):
        pc, nl = self.pc, len(self.lines)
        for i, (da, db) in enumerate(self.lines):
            self._arrived(self.n + i, pc.shard(da, db), 1 - pc.k, None).wait_recv()
        for j, (xa, xb, part) in enumerate(self.cross_at):
            self._arrived(self.n + nl + j, pc.shard(xa, xb), 1 - pc.k, part).wait_recv()
        if self.deep is not None:
            for i, (da, db) in enumerate(self.others()):
                shard = pc.shard(da, db)
                self._deep(2 * self.n + pc.nd + i, shard, 1 - pc.k, False, pc.sibling).wait_recv()

    def sent(self):
        pc, nl = self.pc, len(self.lines)
        for i, _ in enumerate(self.lines):
            self._arrived(i, pc.d, pc.k, None).wait_send()
            self._arrived(self.n + i, pc.d, pc.k, None).wait_send()
        for j, (_, _, part) in enumerate(self.cross_at):
            self._arrived(nl + j, pc.d, pc.k, part).wait_send()
            self._arrived(self.n + nl + j, pc.d, pc.k, part).wait_send()
        if self.deep is not None:
            for i, _ in enumerate(self.others()):
                self._deep(2 * self.n + i, pc.d, pc.k, True, pc.sibling).wait_send()
                self._deep(2 * self.n + pc.nd + i, pc.d, pc.k, False, pc.sibling).wait_send()


def row_cut(ref, rows, core, part, lead=0):
    start = core * (rows // 2) + (0 if part is None else part * (rows // 4))
    size = rows // 2 if part is None else rows // 4
    return ref.at[(slice(None),) * lead + (pl.ds(start, size),)]


def share_rows(pc, rows):
    q = rows // 8
    odd = pc.z % 2

    def cut(ref, core, part):
        start = core * (4 * q) + odd * q
        if part is None:
            return ref.at[pl.ds(start, 3 * q)]
        n = 3 * q // 2
        return ref.at[pl.ds(start + part * n, n)]

    def deep(ref, core, mine):
        at = odd * (3 * q) if mine else (1 - odd) * (3 * q)
        return ref.at[pl.ds(core * (4 * q) + at, q)]

    return cut, deep


def share_cols(pc, rows, cols):
    q = cols // 8
    odd = pc.z % 2
    n = rows // 2 // 16 * 16

    def cut(ref, core, part):
        start = pl.multiple_of(core * (4 * q) + odd * q, 128)
        at = slice(None) if part is None else pl.ds(0, n) if part == 0 else pl.ds(n, rows - n)
        return ref.at[at, pl.ds(start, 3 * q)]

    def deep(ref, core, mine):
        at = odd * (3 * q) if mine else (1 - odd) * (3 * q)
        return ref.at[:, pl.ds(pl.multiple_of(core * (4 * q) + at, 128), q)]

    return cut, deep


class Reduce:
    def __init__(self, pc, g, bufs, send, recv, by_rows):
        self.pc, self.g, self.send, self.recv, self.by_rows = pc, g, send, recv, by_rows
        self.r1a, self.r1b, self.r2a, self.r2b = bufs

    @staticmethod
    def count(nd):
        nb = 2 if nd % 2 == 0 else 1
        return 2 * (nd // nb - 1 + nb - 1)

    @staticmethod
    def scratch(nd, rows, cols, by_rows):
        nb = 2 if nd % 2 == 0 else 1
        na = nd // nb
        r, c = (rows // 2, cols) if by_rows else (rows, cols // 2)
        return [
            pltpu.VMEM((na, nb, rows, cols), BF16),
            pltpu.VMEM((na - 1, nb, r, c), BF16),
            pltpu.VMEM((nb - 1, na, r, c), BF16),
            pltpu.VMEM((nb - 1, r, c), BF16),
            pltpu.VMEM((na - 1, r, c), BF16),
        ]

    def part(self, ref, p):
        lead = (slice(None),) * (len(ref.shape) - 2)
        rows, cols = ref.shape[-2:]
        if self.by_rows:
            return ref.at[lead + (pl.ds(p * (rows // 2), rows // 2),)]
        return ref.at[lead + (slice(None), pl.ds(p * (cols // 2), cols // 2))]

    def copies(self, step):
        pc = self.pc
        na, nb = pc.na, pc.nb
        out = []
        base = 0 if step == 1 else na - 1 + nb - 1
        for da in range(1, na):
            a = (pc.a + na - da) % na
            i = base + da - 1
            if step == 1:
                src, dst = self.part(self.g.at[a], 0), self.r1a.at[da - 1]
            else:
                src, dst = self.part(self.g.at[a, pc.b], 1), self.r2b.at[da - 1]
            out.append(remote(src, dst, self.send.at[i], self.recv.at[i], pc.at(-da, 0)))
        for db in range(1, nb):
            b = (pc.b + nb - db) % nb
            i = base + na - 1 + db - 1
            if step == 1:
                src, dst = self.part(self.g.at[:, b], 1), self.r1b.at[db - 1]
            else:
                src, dst = self.part(self.g.at[pc.a, b], 0), self.r2a.at[db - 1]
            out.append(remote(src, dst, self.send.at[i], self.recv.at[i], pc.at(0, -db)))
        return out

    def start(self):
        for cp in self.copies(1):
            cp.start()

    def middle(self):
        pc = self.pc
        for cp in self.copies(1):
            cp.wait_recv()
        for b in range(pc.nb):
            at = self.part(self.g.at[pc.a, b], 0)
            add(at, [self.r1a.at[i, b] for i in range(pc.na - 1)])
        for a in range(pc.na):
            at = self.part(self.g.at[a, pc.b], 1)
            add(at, [self.r1b.at[i, a] for i in range(pc.nb - 1)])
        for cp in self.copies(2):
            cp.start()

    def finish(self, total):
        pc = self.pc
        for cp in self.copies(2):
            cp.wait_recv()
        own = self.g.at[pc.a, pc.b]
        add(self.part(own, 0), [self.r2a.at[i] for i in range(pc.nb - 1)], self.part(total, 0))
        add(self.part(own, 1), [self.r2b.at[i] for i in range(pc.na - 1)], self.part(total, 1))

    def sent(self):
        for cp in self.copies(1) + self.copies(2):
            cp.wait_send()


def add(ref, others, into=None):
    into = ref if into is None else into
    rows = ref.shape[0]
    chunk = next(n for n in (32, 16, rows) if rows % n == 0)

    def some(i, _):
        at = pl.ds(pl.multiple_of(i * chunk, chunk), chunk)
        total = ref[at, :].astype(F32)
        for o in others:
            total = total + o[at, :].astype(F32)
        into[at, :] = total.astype(BF16)
        return 0

    if rows == chunk:
        total = ref[...].astype(F32)
        for o in others:
            total = total + o[...].astype(F32)
        into[...] = total.astype(BF16)
    else:
        lax.fori_loop(0, rows // chunk, some, 0)


PARTS = 4


def chain_part(by_rows, parts):
    def part(ref, p):
        rows, cols = ref.shape[-2:]
        if by_rows:
            n = rows // parts
            return ref.at[pl.ds(pl.multiple_of(p * n, n), n)]
        n = cols // parts
        return ref.at[:, pl.ds(pl.multiple_of(p * n, n), n)]

    return part


class Chain:
    def __init__(self, pc, t, bufs, send, recv, by_rows, parts):
        self.pc, self.t, self.n = pc, t, parts
        self.part = chain_part(by_rows, parts)
        self.outer, self.swap, total = bufs
        self.total, self.other = total.at[pc.k], total.at[1 - pc.k]
        self.all = total
        self.send, self.recv = send, recv
        half = pc.nz // 2
        self.low = pc.z < half
        self.end = (pc.z == 0) | (pc.z == pc.nz - 1)
        self.mid = (pc.z == half - 1) | (pc.z == half)
        step = 1 - 2 * (pc.z // half)
        self.inner_id = (pc.d, ((pc.z + step + pc.nz) % pc.nz) * 2 + pc.k)
        self.outer_id = (pc.d, ((pc.z - step + pc.nz) % pc.nz) * 2 + pc.k)

    def up_copy(self, p):
        return remote(
            self.part(self.t, p), self.part(self.outer, p), self.send.at[0, p], self.recv.at[0, p],
            self.inner_id,
        )

    def swap_copy(self, p):
        return remote(
            self.part(self.t, p), self.part(self.swap, p), self.send.at[1, p], self.recv.at[1, p],
            self.inner_id,
        )

    def down_copy(self, p):
        at = self.part(self.total, p)
        return remote(at, at, self.send.at[2, p], self.recv.at[2, p], self.outer_id)

    def side_copy(self, p):
        at = self.part(self.total, p)
        return remote(at, at, self.send.at[3, p], self.recv.at[3, p], self.pc.sibling)

    def side_wait(self, p):
        at = self.part(self.other, p)
        remote(at, at, self.send.at[3, p], self.recv.at[3, p], self.pc.sibling).wait_recv()

    def open(self, p):
        @pl.when(self.end)
        def _():
            @pl.when(self.mid)
            def _():
                self.swap_copy(p).start()

            @pl.when(jnp.logical_not(self.mid))
            def _():
                self.up_copy(p).start()

    def up(self, p):
        @pl.when(jnp.logical_not(self.end))
        def _():
            self.up_copy(p).wait_recv()
            add(self.part(self.t, p), [self.part(self.outer, p)])

            @pl.when(self.mid)
            def _():
                self.swap_copy(p).start()

            @pl.when(jnp.logical_not(self.mid))
            def _():
                self.up_copy(p).start()

    def turn_in(self, p):
        @pl.when(self.mid)
        def _():
            self.swap_copy(p).wait_recv()
            add(self.part(self.t, p), [self.part(self.swap, p)], self.part(self.total, p))

            @pl.when(jnp.logical_not(self.end))
            def _():
                self.down_copy(p).start()

            self.side_copy(p).start()

    def turn_out(self, p):
        @pl.when(jnp.logical_not(self.mid))
        def _():
            self.down_copy(p).wait_recv()

            @pl.when(jnp.logical_not(self.end))
            def _():
                self.down_copy(p).start()

            self.side_copy(p).start()

    def both(self, p):
        self.up(p)
        self.turn_in(p - 1)

    def sent(self, p):
        @pl.when(self.mid)
        def _():
            self.swap_copy(p).wait_send()

        @pl.when(jnp.logical_not(self.mid))
        def _():
            self.up_copy(p).wait_send()

        @pl.when(jnp.logical_not(self.end))
        def _():
            self.down_copy(p).wait_send()

        self.side_copy(p).wait_send()


def half_rows(pc, ref, core):
    rows = ref.shape[0] // pc.nd
    h = rows // 2
    return [ref.at[pl.ds(pl.multiple_of(s * rows + core * h, h), h)] for s in range(pc.nd)]


def project_kernel(
    x_ref, gains_ref, cos_ref, sin_ref, wqkv_ref, wattn_ref, win_ref,
    h1t_ref, gains_out, w1_out, w2_out, wqkv_out, wattn_out, heads_out,
    wbuf, abuf, ibuf, h1_ref, gbuf, sendbuf,
    wsend, wrecv, asend, arecv, gsend, grecv, xsend, xrecv, local,
):
    pc = Place()
    nd, nc, nz = pc.nd, pc.nc, pc.nz
    rows = wqkv_ref.shape[0]
    width = wqkv_ref.shape[1] // 3
    tok = x_ref.shape[0]
    w = width // nc
    cw = 2 * w
    own_w = [
        pltpu.make_async_copy(
            wqkv_ref.at[:, pl.ds(g * width, width)], wbuf.at[g, pc.d], local.at[g]
        )
        for g in range(3)
    ]
    for cp in own_w:
        cp.start()
    own_a = pltpu.make_async_copy(wattn_ref, abuf, local.at[3])
    own_a.start()
    own_i = pltpu.make_async_copy(win_ref, ibuf, local.at[5 + nz])
    own_i.start()
    barrier(pc)
    for cp in own_w:
        cp.wait()

    def chip_of(j):
        return (pc.z + j + 1) % nz

    def chunk(j):
        col = pl.multiple_of(chip_of(j) * cw, cw)

        def cut(shard, core, part):
            return row_cut(wbuf.at[:, shard, :, pl.ds(col, cw)], rows, core, part, lead=1)

        return Gather(pc, cut, cut, wsend.at[j], wrecv.at[j])

    def attn_cut(shard, core, part):
        return row_cut(wattn_out.at[shard], rows, core, part)

    def attn_own(shard, core, part):
        return row_cut(wattn_ref, rows, core, part)

    attn = Gather(pc, attn_cut, attn_own, asend, arecv)

    gain_copies = []
    gbuf[pc.d] = gains_ref[...]
    for t in range(1, nd):
        gain_copies.append(
            remote(
                gains_ref, gbuf.at[pc.d], gsend.at[t], grecv.at[t], ((pc.d + t) % nd, pc.c)
            )
        )
        gain_copies[-1].start()
    chunk(0).first()

    xf = x_ref[...].astype(F32)
    mean = jnp.mean(xf, axis=-1, keepdims=True)
    cen = xf - mean
    var = jnp.mean(cen * cen, axis=-1, keepdims=True)
    hat = cen * lax.rsqrt(var + norm_eps)
    for t in range(1, nd):
        src = gbuf.at[(pc.d + nd - t) % nd]
        remote(src, src, gsend.at[t], grecv.at[t], pc.sibling).wait_recv()
    for s in range(nd):
        cols = slice(s * rows, (s + 1) * rows)
        h1_ref[:, cols] = (hat[:, cols] * gbuf[s, 0:1, :]).astype(BF16)
    gains_out[...] = gbuf[...]
    own_a.wait()
    own_a2 = pltpu.make_async_copy(abuf, wattn_out.at[pc.d], local.at[3])
    own_a2.start()
    own_i.wait()
    ff = w1_out.shape[1]
    w1_out[...] = ibuf[:, :ff]
    w2_out[...] = ibuf[:, ff:]
    h1t_ref[...] = jnp.transpose(h1_ref[...])

    lane = lax.broadcasted_iota(jnp.int32, (1, cw), 1)
    low = (lane % HEAD) < HEAD // 2

    def out_copy(j):
        cols = pl.ds(pl.multiple_of(chip_of(j) * cw, cw), cw)
        return pltpu.make_async_copy(
            wbuf.at[:, :, :, cols], wqkv_out.at[:, :, :, cols], local.at[4 + j]
        )

    def place(ref):
        return ref.at[:, pl.ds(pl.multiple_of(pc.c * tok, tok), tok), :]

    def exchange(j, kk):
        return remote(
            sendbuf.at[j, kk], place(heads_out), xsend.at[j, kk], xrecv.at[j, pc.k],
            (pc.d, chip_of(j) * 2 + kk),
        )

    def step(j, _):
        g = chunk(j)
        g.relay()

        @pl.when(j + 1 < nz)
        def _():
            chunk(j + 1).first()

        @pl.when(j + 1 == nz)
        def _():
            attn.first()

        g.cross()
        g.finish()
        out_copy(j).start()
        cols = pl.ds(pl.multiple_of(chip_of(j) * cw, cw), cw)
        for part in range(3):
            weight = wbuf[part, :, :, cols].reshape(nd * rows, cw)
            proj = jnp.dot(h1_ref[...], weight, preferred_element_type=F32)
            if part < 2:
                up = pltpu.roll(proj, cw - HEAD // 2, 1)
                down = pltpu.roll(proj, HEAD // 2, 1)
                proj = proj * cos_ref[...] + jnp.where(low, up, down) * sin_ref[...]
            proj = proj.astype(BF16)
            for kk in range(2):
                sendbuf[j, kk, part] = proj[:, kk * w : (kk + 1) * w]

        @pl.when(j < nz - 1)
        def _():
            exchange(j, 0).start()
            exchange(j, 1).start()

        return 0

    lax.fori_loop(0, nz, step, 0)
    last = nz - 1
    remote(
        sendbuf.at[last, 1 - pc.k], place(heads_out), xsend.at[last, 1 - pc.k],
        xrecv.at[last, pc.k], pc.sibling,
    ).start()
    own_x = pltpu.make_async_copy(
        sendbuf.at[last, pc.k], place(heads_out), local.at[4 + nz]
    )
    own_x.start()
    attn.relay()
    attn.cross()
    attn.finish()

    def arrival(j, kk):
        ref = sendbuf.at[j, kk]
        return remote(ref, ref, xsend.at[j, kk], xrecv.at[j, kk], pc.sibling)

    def drain(j, _):
        arrival(j, 0).wait_recv()
        arrival(j, 1).wait_recv()
        arrival(j, 0).wait_send()
        arrival(j, 1).wait_send()
        chunk(j).sent()
        out_copy(j).wait()
        return 0

    lax.fori_loop(0, nz - 1, drain, 0)
    arrival(last, 1 - pc.k).wait_recv()
    arrival(last, 1 - pc.k).wait_send()
    chunk(last).sent()
    out_copy(last).wait()
    own_x.wait()
    own_a2.wait()
    attn.sent()
    for cp in gain_copies:
        cp.wait_send()


def project(x, gains, cosine, sine, wqkv, wattn, win):
    nd, nc = lax.axis_size("dp"), lax.axis_size("ctx")
    nz = nc // 2
    tok, width = x.shape
    rows = wqkv.shape[0]
    w = width // nc
    n = Gather.count(nd)
    dma = pltpu.SemaphoreType.DMA
    return pl.pallas_call(
        project_kernel,
        out_shape=[
            S((width, tok), BF16),
            S((nd, 8, rows), F32),
            S((rows, win.shape[1] // 2), BF16),
            S((rows, win.shape[1] // 2), BF16),
            S((3, nd, rows, width), BF16),
            S((nd, rows, width), BF16),
            S((3, nc * tok, w), BF16),
        ],
        in_specs=[VMEM, VMEM, VMEM, VMEM, ANY, ANY, ANY],
        out_specs=[VMEM, VMEM, VMEM, VMEM, ANY, ANY, ANY],
        scratch_shapes=[
            pltpu.VMEM((3, nd, rows, width), BF16),
            pltpu.VMEM((rows, width), BF16),
            pltpu.VMEM(win.shape, BF16),
            pltpu.VMEM((tok, width), BF16),
            pltpu.VMEM((nd, 8, rows), F32),
            pltpu.VMEM((nz, 2, 3, tok, w), BF16),
            dma((nz, n)), dma((nz, n)), dma((n,)), dma((n,)),
            dma((nd,)), dma((nd,)), dma((nz, 2)), dma((nz, 2)), dma((6 + nz,)),
        ],
        compiler_params=params(0),
        name="project",
    )(x, gains, cosine, sine, wqkv, wattn, win)


def attend_kernel(
    heads_ref, w1_ref, w2_ref, wout_ref,
    otok_out, o_ref, lse_ref, w1_out, w2_out, wout_out,
    qkv, vext, bounce1, bounce2, bounce3,
    s1, r1, s2, r2, s3, r3, xsend, xrecv, local,
):
    pc = Place()
    nd, nc = pc.nd, pc.nc
    keys, w = heads_ref.shape[1], heads_ref.shape[2]
    tok = keys // nc
    rows = w1_ref.shape[0]
    load = pltpu.make_async_copy(heads_ref, qkv, local.at[0])
    load.start()
    pairs = [(w1_ref, bounce1, w1_out), (w2_ref, bounce2, w2_out), (wout_ref, bounce3, wout_out)]
    for i, (src, mid, _) in enumerate(pairs):
        pltpu.make_async_copy(src, mid, local.at[1 + i]).start()
    barrier(pc)
    cut_r, deep_r = share_rows(pc, rows)
    cut_c, deep_c = share_cols(pc, *wout_ref.shape)

    def item(ref, out, cut, deep, send, recv):
        return Gather(
            pc,
            lambda s, k, p: cut(out.at[s], k, p),
            lambda s, k, p: cut(ref, k, p),
            send,
            recv,
            lambda s, k, mine: deep(out.at[s], k, mine),
        )

    items = [
        item(w1_ref, w1_out, cut_r, deep_r, s1, r1),
        item(w2_ref, w2_out, cut_r, deep_r, s2, r2),
        item(wout_ref, wout_out, cut_c, deep_c, s3, r3),
    ]
    items[0].first()
    items[1].first()
    load.wait()
    for i, (src, mid, _) in enumerate(pairs):
        pltpu.make_async_copy(src, mid, local.at[1 + i]).wait()
    for i, (_, mid, dst) in enumerate(pairs):
        pltpu.make_async_copy(mid, dst.at[pc.d], local.at[1 + i]).start()
    nh = w // HEAD
    for h in range(nh):
        vext[h, :, :HEAD] = qkv[2, :, h * HEAD : (h + 1) * HEAD]
        vext[h, :, HEAD:] = jnp.ones((keys, HEAD), BF16)
    scale = HEAD ** (-0.5) * LOG2E

    def block_copy(i):
        to = (pc.c + i + 1) % nc
        at = pl.ds(pl.multiple_of(to * tok, tok), tok)
        return remote(
            o_ref.at[at], otok_out.at[pc.c], xsend.at[i], xrecv.at[i], (pc.d, to)
        )

    def block(i, _):
        at = pl.ds(pl.multiple_of(((pc.c + i + 1) % nc) * tok, tok), tok)
        for h in range(nh):
            hs = slice(h * HEAD, (h + 1) * HEAD)
            s = lax.dot_general(
                qkv[0, at, hs], qkv[1, :, hs], (((1,), (1,)), ((), ())),
                preferred_element_type=F32,
            )
            m = jnp.max(s, axis=1, keepdims=True)
            p = jnp.exp2(s * scale - m * scale).astype(BF16)
            ol = jnp.dot(p, vext[h], preferred_element_type=F32)
            total = ol[:, HEAD:]
            o_ref[at, hs] = (ol[:, :HEAD] / total).astype(BF16)
            lse = m * scale + jnp.log2(total)
            lse_ref[h, :, at] = jnp.transpose(jnp.concatenate([lse, lse], axis=1))[:8]

        @pl.when(i < nc - 1)
        def _():
            block_copy(i).start()

        @pl.when(i == nc // 2)
        def _():
            items[0].relay()
            items[2].first()

        return 0

    lax.fori_loop(0, nc, block, 0)
    own = pltpu.make_async_copy(
        o_ref.at[pl.ds(pl.multiple_of(pc.c * tok, tok), tok)], otok_out.at[pc.c], local.at[0]
    )
    own.start()
    items[1].relay()
    items[0].cross()
    items[2].relay()
    items[1].cross()
    items[0].across()
    items[2].cross()
    items[1].across()
    items[2].across()
    for it in items:
        it.finish()

    def drain(i, _):
        got = otok_out.at[(pc.c + nc - i - 1) % nc]
        remote(got, got, xsend.at[i], xrecv.at[i], pc.sibling).wait_recv()
        block_copy(i).wait_send()
        return 0

    lax.fori_loop(0, nc - 1, drain, 0)
    own.wait()
    for i, (_, mid, dst) in enumerate(pairs):
        pltpu.make_async_copy(mid, dst.at[pc.d], local.at[1 + i]).wait()
    for it in items:
        it.sent()


def attend(heads, w1, w2, wout):
    nd, nc = lax.axis_size("dp"), lax.axis_size("ctx")
    _, keys, w = heads.shape
    nh = w // HEAD
    n = Gather.count(nd)
    dma = pltpu.SemaphoreType.DMA
    return pl.pallas_call(
        attend_kernel,
        out_shape=[
            S((nc, keys // nc, w), BF16),
            S((keys, w), BF16),
            S((nh, 8, keys), F32),
            S((nd,) + w1.shape, BF16),
            S((nd,) + w2.shape, BF16),
            S((nd,) + wout.shape, BF16),
        ],
        in_specs=[ANY, ANY, ANY, ANY],
        out_specs=[ANY, VMEM, VMEM, ANY, ANY, ANY],
        scratch_shapes=[
            pltpu.VMEM((3, keys, w), BF16),
            pltpu.VMEM((nh, keys, 2 * HEAD), BF16),
            pltpu.VMEM(w1.shape, BF16),
            pltpu.VMEM(w2.shape, BF16),
            pltpu.VMEM(wout.shape, BF16),
            dma((n,)), dma((n,)), dma((n,)), dma((n,)), dma((n,)), dma((n,)),
            dma((nc,)), dma((nc,)), dma((4,)),
        ],
        compiler_params=params(1),
        name="attend",
    )(heads, w1, w2, wout)


def attend_back_kernel(
    heads_ref, o_ref, lse_ref, dout_ref, near_ref, far_ref, h2t_ref, dl1_ref, dl2_ref,
    actt_ref, c_ref, ot_ref, dres_ref,
    dtok_out, t_ref, gout_out, gattn_out,
    qkv, dout, delta, dq, sendbuf, h2t, dl, actt, cot, ot, dres, gout, gattn,
    ga, ra0, ra1, ra2, ra3, gb, rb0, rb1, rb2, rb3,
    dsend, drecv, xsend, xrecv, ssend, srecv, asend, arecv, bsend, brecv, local,
):
    pc = Place()
    nd = pc.nd
    nc = pc.nc
    keys, w = heads_ref.shape[1], heads_ref.shape[2]
    tok = keys // nc
    nh = w // HEAD
    load = pltpu.make_async_copy(heads_ref, qkv, local.at[0])
    load.start()
    mine_t = half_rows(pc, h2t_ref, pc.k)
    hers_t = half_rows(pc, h2t_ref, 1 - pc.k)
    fetch = [pltpu.make_async_copy(mine_t[s], h2t.at[0, s], local.at[2 + s]) for s in range(nd)]
    fetch.append(pltpu.make_async_copy(dl1_ref, dl.at[0, 0], local.at[2 + nd]))
    fetch.append(pltpu.make_async_copy(dl2_ref, dl.at[1, 0], local.at[3 + nd]))
    half = cot.shape[2]
    nr = actt.shape[2]
    col = lambda core: pl.ds(pl.multiple_of(core * half, half), half)
    o_mine, o_hers = half_rows(pc, ot_ref, pc.k), half_rows(pc, ot_ref, 1 - pc.k)
    acts = [actt_ref.at[pl.ds(s * nr, nr)] for s in range(nd)]
    more = [(acts[s], actt.at[0, s]) for s in range(nd)] + [(o_mine[s], ot.at[0, s]) for s in range(nd)]
    more += [(c_ref.at[:, col(pc.k)], cot.at[0]), (dres_ref, dres.at[0])]
    first = len(fetch)
    fetch += [pltpu.make_async_copy(a, b, local.at[4 + nd + i]) for i, (a, b) in enumerate(more)]
    for cp in fetch:
        cp.start()
    barrier(pc)
    swap = [
        remote(hers_t[s], h2t.at[1, s], ssend.at[s], srecv.at[s], pc.sibling) for s in range(nd)
    ]
    more = [(acts[s], actt.at[1, s]) for s in range(nd)] + [(o_hers[s], ot.at[1, s]) for s in range(nd)]
    more += [(c_ref.at[:, col(1 - pc.k)], cot.at[1]), (dres_ref, dres.at[1])]
    late = [
        remote(a, b, ssend.at[nd + 2 + i], srecv.at[nd + 2 + i], pc.sibling)
        for i, (a, b) in enumerate(more)
    ]
    swap.append(remote(dl1_ref, dl.at[0, 1], ssend.at[nd], srecv.at[nd], pc.sibling))
    swap.append(remote(dl2_ref, dl.at[1, 1], ssend.at[nd + 1], srecv.at[nd + 1], pc.sibling))
    for cp in swap:
        cp.start()
    mine = pl.ds(pl.multiple_of(pc.c * tok, tok), tok)
    for i in range(nc - 1):
        to = (pc.c + i + 1) % nc
        remote(dout_ref.at[to], dout.at[mine], dsend.at[i], drecv.at[i], (pc.d, to)).start()
    own = pltpu.make_async_copy(dout_ref.at[pc.c], dout.at[mine], local.at[1])
    own.start()
    ra = Reduce(pc, ga, (ra0, ra1, ra2, ra3), asend, arecv, True)
    rb = Reduce(pc, gb, (rb0, rb1, rb2, rb3), bsend, brecv, True)
    for cp in late:
        cp.start()
    for cp in fetch[:first]:
        cp.wait()
    for cp in swap[: nd + 1]:
        cp.wait_recv()
    weight_grad(pc, ga, h2t, dl.at[0], True)
    ra.start()
    swap[nd + 1].wait_recv()
    weight_grad(pc, gb, h2t, dl.at[1], True)
    rb.start()
    for cp in fetch[first:]:
        cp.wait()
    for cp in late:
        cp.wait_recv()
    weight_grad(pc, gout, actt, cot)
    weight_grad(pc, gattn, ot, dres)
    keep_g = [
        pltpu.make_async_copy(gout, gout_out, local.at[2]),
        pltpu.make_async_copy(gattn, gattn_out, local.at[3]),
    ]
    for cp in keep_g:
        cp.start()
    dq[...] = jnp.zeros_like(dq)
    load.wait()
    own.wait()
    for i in range(nc - 1):
        src = (pc.c + nc - i - 1) % nc
        got = dout.at[pl.ds(pl.multiple_of(src * tok, tok), tok)]
        remote(got, got, dsend.at[i], drecv.at[i], pc.sibling).wait_recv()

    def deltas(i, _):
        at = pl.ds(pl.multiple_of(i * tok, tok), tok)
        t = jnp.transpose(o_ref[at, :].astype(F32) * dout[at, :].astype(F32))
        for h in range(nh):
            row = jnp.sum(t[h * HEAD : (h + 1) * HEAD], axis=0, keepdims=True)
            delta[h, :, at] = jnp.broadcast_to(row, (8, tok))
        return 0

    lax.fori_loop(0, nc, deltas, 0)
    scale = HEAD ** (-0.5)
    lane = lax.broadcasted_iota(jnp.int32, (1, w), 1)
    low = (lane % HEAD) < HEAD // 2

    def unrotate(g, to):
        cos_n, sin_n, cos_f, sin_f = near_ref[0], near_ref[1], far_ref[0, to], far_ref[1, to]
        t = g * (sin_f * cos_n + cos_f * sin_n)
        if w == HEAD:
            up = jnp.concatenate([t[:, HEAD // 2 :], t[:, : HEAD // 2]], axis=1)
            down = up
        else:
            up = pltpu.roll(t, w - HEAD // 2, 1)
            down = pltpu.roll(t, HEAD // 2, 1)
        return g * (cos_f * cos_n - sin_f * sin_n) + jnp.where(low, up, -down)

    def kv_copy(i):
        to = (pc.c + i + 1) % nc
        return remote(
            sendbuf.at[to, pl.ds(1, 2)], dtok_out.at[pc.c, pl.ds(1, 2)],
            xsend.at[0, i], xrecv.at[0, i], (pc.d, to),
        )

    def q_copy(i):
        to = (pc.c + i + 1) % nc
        return remote(
            sendbuf.at[to, 0], dtok_out.at[pc.c, 0], xsend.at[1, i], xrecv.at[1, i], (pc.d, to)
        )

    def block(i, _):
        to = (pc.c + i + 1) % nc
        at = pl.ds(pl.multiple_of(to * tok, tok), tok)
        dks, dvs = [], []
        for h in range(nh):
            hs = slice(h * HEAD, (h + 1) * HEAD)
            kb, vb = qkv[1, at, hs], qkv[2, at, hs]
            q, do = qkv[0, :, hs], dout[:, hs]
            nt = (((1,), (1,)), ((), ()))
            st = lax.dot_general(kb, q, nt, preferred_element_type=F32)
            p = jnp.exp2(st * (scale * LOG2E) - lse_ref[h, 0:1, :])
            dvs.append(jnp.dot(p.astype(BF16), do, preferred_element_type=F32))
            dp = lax.dot_general(vb, do, nt, preferred_element_type=F32)
            ds = (p * (dp - delta[h, 0:1, :])).astype(BF16)
            dks.append(jnp.dot(ds, q, preferred_element_type=F32))
            dq[:, hs] += lax.dot_general(
                ds, kb, (((0,), (0,)), ((), ())), preferred_element_type=F32
            )
        dk = jnp.concatenate(dks, axis=1) * scale
        sendbuf[to, 1] = unrotate(dk, to).astype(BF16)
        sendbuf[to, 2] = jnp.concatenate(dvs, axis=1).astype(BF16)

        @pl.when(i < nc - 1)
        def _():
            kv_copy(i).start()

        @pl.when(i == (nc * 3) // 8)
        def _():
            ra.middle()

        @pl.when(i == (nc * 7) // 8)
        def _():
            rb.middle()

        return 0

    lax.fori_loop(0, nc, block, 0)

    def q_block(i, _):
        to = (pc.c + i + 1) % nc
        at = pl.ds(pl.multiple_of(to * tok, tok), tok)
        sendbuf[to, 0] = unrotate(dq[at, :] * scale, to).astype(BF16)

        @pl.when(i < nc - 1)
        def _():
            q_copy(i).start()

        return 0

    lax.fori_loop(0, nc, q_block, 0)
    keep = pltpu.make_async_copy(sendbuf.at[pc.c], dtok_out.at[pc.c], local.at[1])
    keep.start()
    hr = ga.shape[2]
    ra.finish(t_ref.at[pl.ds(0, hr)])
    rb.finish(t_ref.at[pl.ds(hr, hr)])

    def drain(i, _):
        got = dtok_out.at[(pc.c + nc - i - 1) % nc]
        remote(
            got.at[pl.ds(1, 2)], got.at[pl.ds(1, 2)], xsend.at[0, i], xrecv.at[0, i], pc.sibling
        ).wait_recv()
        remote(got.at[0], got.at[0], xsend.at[1, i], xrecv.at[1, i], pc.sibling).wait_recv()
        kv_copy(i).wait_send()
        q_copy(i).wait_send()
        to = (pc.c + i + 1) % nc
        remote(
            dout_ref.at[to], dout.at[mine], dsend.at[i], drecv.at[i], (pc.d, to)
        ).wait_send()
        return 0

    lax.fori_loop(0, nc - 1, drain, 0)
    keep.wait()
    for cp in keep_g:
        cp.wait()
    for cp in swap + late:
        cp.wait_send()
    ra.sent()
    rb.sent()


def weight_grad(pc, g, lhs, rhs, flipped=False):
    dims = (((1,), (1 if flipped else 0,)), ((), ()))

    def shard(s, _):
        total = lax.dot_general(lhs[0, s], rhs[0], dims, preferred_element_type=F32)
        total = total + lax.dot_general(lhs[1, s], rhs[1], dims, preferred_element_type=F32)
        g[s // pc.nb, s % pc.nb] = total.astype(BF16)
        return 0

    lax.fori_loop(0, pc.nd, shard, 0)


def attend_back(heads, o, lse, dout, near, far, h2t, dl1, dl2, actt, cot, ot, dres):
    nc, nd = lax.axis_size("ctx"), lax.axis_size("dp")
    ff = dl1.shape[0]
    hr = h2t.shape[0] // nd // 2
    n = Reduce.count(nd)
    _, keys, w = heads.shape
    nh = w // HEAD
    tok = keys // nc
    width = w * nc
    nb = 2 if nd % 2 == 0 else 1
    vm = lambda *shape: pltpu.VMEM(shape, BF16)
    gout, gattn = (nd // nb, nb, ff // nd, width // 2), (nd // nb, nb, hr, width)
    ns = 3 * nd + 4
    dma = pltpu.SemaphoreType.DMA
    return pl.pallas_call(
        attend_back_kernel,
        out_shape=[
            S((nc, 3, tok, w), BF16), S((2 * hr, ff), BF16), S(gout, BF16), S(gattn, BF16)
        ],
        in_specs=[ANY, VMEM, VMEM, ANY, VMEM, VMEM] + [ANY] * 7,
        out_specs=[ANY, VMEM, ANY, ANY],
        scratch_shapes=[
            pltpu.VMEM((3, keys, w), BF16),
            pltpu.VMEM((keys, w), BF16),
            pltpu.VMEM((nh, 8, keys), F32),
            pltpu.VMEM((keys, w), F32),
            pltpu.VMEM((nc, 3, tok, w), BF16),
            pltpu.VMEM((2, nd, hr, tok), BF16),
            pltpu.VMEM((2, 2, ff, tok), BF16),
            vm(2, nd, ff // nd, tok), vm(2, tok, width // 2), vm(2, nd, hr, tok), vm(2, tok, width),
            vm(*gout), vm(*gattn),
            *Reduce.scratch(nd, hr, ff, True),
            *Reduce.scratch(nd, hr, ff, True),
            dma((nc,)), dma((nc,)), dma((2, nc)), dma((2, nc)), dma((ns,)), dma((ns,)),
            dma((n,)), dma((n,)), dma((n,)), dma((n,)), dma((6 + 3 * nd,)),
        ],
        compiler_params=params(2),
        name="attend_back",
    )(heads, o, lse, dout, near, far, h2t, dl1, dl2, actt, cot, ot, dres)


def each(count, *calls):
    def body(p, _):
        for call in calls:
            call(p)
        return 0

    lax.fori_loop(0, count, body, 0)


def close_kernel(
    dtok_ref, h1t_ref, wqkv_ref, x_ref, gain_ref, dres_ref, part_ref, gout_ref, gattn_ref, t_ref,
    dx_ref, gain_out, outi, outq, outo, outa,
    dtok, dproj, h1t, wqkv, dh1,
    *refs,
):
    pc = Place()
    nd, nc = pc.nd, pc.nc
    _, _, tok, w = dtok_ref.shape
    width = nc * w
    reds, refs = [refs[5 * i : 5 * i + 5] for i in range(5)], refs[25:]
    sums, refs = refs[:5], refs[5:]
    bufs, refs = [refs[3 * i : 3 * i + 3] for i in range(6)], refs[18:]
    gmine, gtotal, gctx, gdp, ssend, srecv, rsend, rrecv, isend, irecv, csend, crecv = refs[:12]
    gsend, grecv, local, outsem = refs[12:]
    third = lambda g: pl.ds(pl.multiple_of(g * width, width), width)
    h1_mine, h1_hers = half_rows(pc, h1t_ref, pc.k), half_rows(pc, h1t_ref, 1 - pc.k)
    pairs = [(dtok_ref, dtok), (gout_ref, reds[0][0])]
    pairs += [(h1_mine[s], h1t.at[0, s]) for s in range(nd)]
    pairs += [(gattn_ref, reds[4][0]), (wqkv_ref, wqkv)]
    load = [pltpu.make_async_copy(a, b, local.at[i]) for i, (a, b) in enumerate(pairs)]
    for cp in load:
        cp.start()
    barrier(pc)
    pairs = [(h1_hers[s], h1t.at[1, s]) for s in range(nd)]
    pairs += [(dproj.at[0, :, third(g)], dproj.at[1, :, third(g)]) for g in range(3)]
    swap = [
        remote(src, dst, ssend.at[i], srecv.at[i], pc.sibling) for i, (src, dst) in enumerate(pairs)
    ]
    ro, *rq, ra = [
        Reduce(pc, bs[0], bs[1:], rsend.at[i], rrecv.at[i], i > 0) for i, bs in enumerate(reds)
    ]
    to, *tq, ta = sums
    ci = Chain(pc, t_ref, bufs[0], isend, irecv, True, 2 * PARTS)
    co, *cq, ca = [
        Chain(pc, t, bs, csend.at[i], crecv.at[i], i > 0, PARTS)
        for i, (t, bs) in enumerate(zip(sums, bufs[1:]))
    ]
    for cp in swap[:nd]:
        cp.start()
    each(ci.n, ci.open)
    load[1].wait()
    ro.start()
    load[0].wait()
    for g in range(3):
        for i in range(nc):
            dproj[0, :, g * width + i * w : g * width + (i + 1) * w] = dtok[i, g]
        swap[nd + g].start()
    for cp in load[2:]:
        cp.wait()
    for cp in swap[: nd + 1]:
        cp.wait_recv()
    weight_grad(pc, reds[1][0], h1t, dproj.at[:, :, third(0)])
    rq[0].start()
    ci.up(0)
    for g in (1, 2):
        swap[nd + g].wait_recv()
        weight_grad(pc, reds[1 + g][0], h1t, dproj.at[:, :, third(g)])
    dh1[...] = jnp.zeros_like(dh1)

    def back(g, _):
        dh1[...] += lax.dot_general(
            dproj[0, :, third(g)], wqkv[g].reshape(width, width), (((1,), (1,)), ((), ())),
            preferred_element_type=F32,
        )
        ci.both(1 + g)
        return 0

    lax.fori_loop(0, 3, back, 0)
    ci.turn_out(0)
    ro.middle()
    rq[1].start()
    gain = jnp.concatenate([gain_ref[s, 0:1, :] for s in range(nd)], axis=1)
    gtotal[...] = jnp.zeros_like(gtotal)
    chunk = 32

    def norm_back(i, _):
        at = pl.ds(pl.multiple_of(i * chunk, chunk), chunk)
        xf = x_ref[at, :].astype(F32)
        mean = jnp.mean(xf, axis=-1, keepdims=True)
        cen = xf - mean
        inv = lax.rsqrt(jnp.mean(cen * cen, axis=-1, keepdims=True) + norm_eps)
        hat = cen * inv
        d = dh1[at, :]
        dhat = d * gain
        m1 = jnp.mean(dhat, axis=-1, keepdims=True)
        m2 = jnp.mean(dhat * hat, axis=-1, keepdims=True)
        dx_ref[at, :] = (dres_ref[at, :] + inv * (dhat - m1 - hat * m2)).astype(BF16)
        gtotal[...] += jnp.sum((d * hat).reshape(chunk // 8, 8, width), axis=0)
        return 0

    lax.fori_loop(0, tok // chunk, norm_back, 0)
    row = lax.broadcasted_iota(jnp.int32, (8, 1), 0)
    gmine[...] = jnp.where(row == 0, jnp.sum(gtotal[...], axis=0, keepdims=True), part_ref[...])
    rows = gain_out.shape[1]
    here = lambda d: pl.ds(pl.multiple_of(d * rows, 128), rows)
    dcopies = []
    for t in range(1, nd):
        to_d = (pc.d + t) % nd
        dcopies.append(
            remote(
                gmine.at[:, here(to_d)], gdp.at[t], gsend.at[nc + t], grecv.at[nc + t], (to_d, pc.c)
            )
        )
        dcopies[-1].start()
    ci.both(4)
    ci.turn_out(1)
    rq[0].middle()
    rq[2].start()
    ci.both(5)
    ci.turn_out(2)
    for cp in dcopies:
        cp.wait_recv()
    total = gmine[:, here(pc.d)]
    for t in range(1, nd):
        total = total + gdp[t]
    gdp[0] = total
    gcopies = []
    for t in range(1, nc):
        gcopies.append(
            remote(gdp.at[0], gctx.at[t], gsend.at[t], grecv.at[t], (pc.d, (pc.c + t) % nc))
        )
        gcopies[-1].start()
    ci.both(6)
    ci.turn_out(3)
    ro.finish(to)
    each(PARTS, co.open)
    ci.both(7)
    ci.turn_in(7)
    ci.turn_out(4)
    rq[1].middle()
    ra.start()
    ci.turn_out(5)
    co.up(0)
    rq[0].finish(tq[0])
    each(PARTS, cq[0].open)
    ci.turn_out(6)
    co.both(1)
    ci.turn_out(7)
    outs = [
        pltpu.make_async_copy(c.all, out, outsem.at[i])
        for i, (c, out) in enumerate(
            [(ci, outi), (co, outo)]
            + [(cq[g], outq.at[:, :, third(g)]) for g in range(3)]
            + [(ca, outa)]
        )
    ]
    for cp in gcopies:
        cp.wait_recv()
    total = gdp[0]
    for t in range(1, nc):
        total = total + gctx[t]
    gain_out[...] = total
    rq[2].middle()
    co.both(2)
    co.turn_out(0)
    rq[1].finish(tq[1])
    each(PARTS, cq[1].open)
    co.both(3)
    cq[0].up(0)
    co.turn_in(3)
    co.turn_out(1)
    ra.middle()
    each(PARTS - 1, lambda p: cq[0].both(p + 1))
    co.turn_out(2)
    rq[2].finish(tq[2])
    each(PARTS, cq[2].open)
    co.turn_out(3)
    cq[1].up(0)
    cq[0].turn_in(3)
    ra.finish(ta)
    each(PARTS, ca.open)
    each(PARTS - 1, lambda p: cq[1].both(p + 1), cq[0].turn_out)
    cq[2].up(0)
    cq[1].turn_in(3)
    cq[0].turn_out(3)
    each(PARTS - 1, lambda p: cq[2].both(p + 1), cq[1].turn_out)
    ca.up(0)
    cq[2].turn_in(3)
    cq[1].turn_out(3)
    each(PARTS - 1, lambda p: ca.both(p + 1), cq[2].turn_out)
    ca.turn_in(3)
    cq[2].turn_out(3)
    each(ci.n, ci.side_wait)
    outs[0].start()
    each(PARTS, co.side_wait)
    outs[1].start()
    each(PARTS, ca.turn_out)
    for i, c in enumerate(cq + [ca]):
        each(PARTS, c.side_wait)
        outs[2 + i].start()
    for cp in swap + dcopies + gcopies:
        cp.wait_send()
    for r in [ro] + rq + [ra]:
        r.sent()
    for c in [ci, co] + cq + [ca]:
        each(c.n, c.sent)
    for cp in outs:
        cp.wait()


def close(dtok, h1t, wqkv, x, gains, dres, part, gout, gattn, totals):
    nd, nc = lax.axis_size("dp"), lax.axis_size("ctx")
    tok, width = x.shape
    rows = width // nd
    hr = rows // 2
    nq, ns = Reduce.count(nd), nd + 3
    dma = pltpu.SemaphoreType.DMA
    mine = [gout.shape[2:]] + [(hr, width)] * 4
    sizes = [totals.shape] + mine
    vm = lambda *shape: pltpu.VMEM(shape, BF16)
    chain_bufs = [b for size in sizes for b in (vm(*size), vm(*size), vm(2, *size))]
    reduce_bufs = [b for i, size in enumerate(mine) for b in Reduce.scratch(nd, *size, i > 0)]
    return pl.pallas_call(
        close_kernel,
        out_shape=[S((tok, width), BF16), S((8, rows), F32)]
        + [S((2,) + size, BF16) for size in (sizes[0], (hr, 3 * width), mine[0], mine[4])],
        in_specs=[ANY, ANY, ANY, VMEM, VMEM, VMEM, VMEM, ANY, ANY, VMEM],
        out_specs=[VMEM] * 2 + [ANY] * 4,
        scratch_shapes=[
            vm(*dtok.shape), vm(2, tok, 3 * width), vm(2, nd, hr, tok), vm(*wqkv.shape),
            pltpu.VMEM((tok, width), F32),
            *reduce_bufs, *[vm(*size) for size in mine], *chain_bufs,
            pltpu.VMEM((8, width), F32), pltpu.VMEM((8, width), F32),
            pltpu.VMEM((nc, 8, rows), F32), pltpu.VMEM((nd, 8, rows), F32),
            dma((ns,)), dma((ns,)), dma((5, nq)), dma((5, nq)),
            dma((4, 2 * PARTS)), dma((4, 2 * PARTS)), dma((5, 4, PARTS)), dma((5, 4, PARTS)),
            dma((nc + nd,)), dma((nc + nd,)), dma((4 + nd,)), dma((6,)),
        ],
        compiler_params=params(3),
        name="close",
    )(dtok, h1t, wqkv, x, gains, dres, part, gout, gattn, totals)


def norm_rows(values, gain):
    row_mean = jnp.mean(values, axis=-1, keepdims=True)
    centred = values - row_mean
    row_var = jnp.mean(centred * centred, axis=-1, keepdims=True)
    return centred * lax.rsqrt(row_var + norm_eps) * gain


def gelu_exact(values):
    return 0.5 * values * (1.0 + lax.erf(values * 0.7071067811865476))


def gelu_slope(values):
    return (
        0.5 * (1.0 + lax.erf(values * 0.7071067811865476))
        + values * jnp.exp(-0.5 * values * values) * 0.3989422804014327
    )


def rope_angles(positions, lanes):
    half = HEAD // 2
    freq = rope_theta ** (-(jnp.arange(half, dtype=F32) * 2.0 / HEAD))
    freq = jnp.tile(freq, lanes // half)
    return positions.astype(F32)[:, None] * freq[None, :]


def on_device(
    tokens,
    norm1_gain,
    qkv_weight,
    attn_out_weight,
    norm2_gain,
    mlp_in_weight,
    mlp_out_weight,
    cotangent,
):
    _, tok, width = tokens.shape
    nc, nd = lax.axis_size("ctx"), lax.axis_size("dp")
    keys = tok * nc
    w = width // nc
    ff = mlp_in_weight.shape[1] // 2
    rows = norm1_gain.shape[0]
    x = tokens.reshape(tok, width)
    upstream = cotangent.reshape(tok, width)
    gains = jnp.concatenate(
        [
            norm1_gain.astype(F32)[None],
            norm2_gain.astype(F32)[None],
            jnp.zeros((6, rows), F32),
        ]
    )
    ang = rope_angles(lax.axis_index("ctx") * tok + jnp.arange(tok, dtype=jnp.int32), 2 * w)
    sign = jnp.where(jnp.arange(2 * w) % HEAD < HEAD // 2, -1.0, 1.0).astype(F32)
    h1t, gains_all, w1s, w2s, wqkv, wattn, heads = project(
        x, gains, jnp.cos(ang), jnp.sin(ang) * sign[None], qkv_weight, attn_out_weight,
        mlp_in_weight,
    )
    otok, o_heads, lse, w1, w2, wout = attend(heads, w1s, w2s, mlp_out_weight)
    wattn = wattn.reshape(width, width)
    w1 = w1.reshape(width, ff)
    w2 = w2.reshape(width, ff)
    wout = wout.reshape(ff, width)
    gain_one = gains_all[:, 0].reshape(width)
    gain_two = gains_all[:, 1].reshape(width)

    attended_b = jnp.transpose(otok, (1, 0, 2)).reshape(tok, width)
    inputs_f = x.astype(F32)
    attn_res = inputs_f + jnp.dot(attended_b, wattn, preferred_element_type=F32)
    normed_two = norm_rows(attn_res, gain_two).astype(BF16)
    gelu_in = jnp.dot(normed_two, w1, preferred_element_type=F32)
    gate_in = jnp.dot(normed_two, w2, preferred_element_type=F32)
    activated = (gelu_exact(gelu_in) * gate_in).astype(BF16)
    layer_out = (attn_res + jnp.dot(activated, wout, preferred_element_type=F32)).astype(BF16)
    grad_act = jnp.dot(upstream, wout.T, preferred_element_type=F32)
    dl1 = (grad_act * gate_in * gelu_slope(gelu_in)).astype(BF16)
    dl2 = (grad_act * gelu_exact(gelu_in)).astype(BF16)
    dl1, dl2 = lax.optimization_barrier((dl1, dl2))
    grad_normed_two = jnp.dot(dl1, w1.T, preferred_element_type=F32) + jnp.dot(
        dl2, w2.T, preferred_element_type=F32
    )
    _, pull_two = jax.vjp(norm_rows, attn_res, gain_two)
    grad_res_norm, grad_gain_two = pull_two(grad_normed_two)
    grad_res = upstream.astype(F32) + grad_res_norm
    grad_res_b = grad_res.astype(BF16)
    dout = jnp.dot(grad_res_b, wattn.T, preferred_element_type=F32).astype(BF16)
    dout = jnp.transpose(dout.reshape(tok, nc, w), (1, 0, 2))

    near = rope_angles(jnp.arange(tok, dtype=jnp.int32), w)
    far = rope_angles(jnp.arange(nc, dtype=jnp.int32) * tok, w)[:, None]
    near, far = [jnp.stack([jnp.cos(ang), jnp.sin(ang)]) for ang in (near, far)]
    dtok, totals, gout, gattn = attend_back(
        heads, o_heads, lse, dout, near, far, normed_two.T, dl1.T, dl2.T,
        activated.T, upstream, attended_b.T, grad_res_b,
    )
    input_grad, gain_grads, gin, gqkv, gout, gattn = close(
        dtok, h1t, wqkv, x, gains_all, grad_res, grad_gain_two.reshape(1, width), gout, gattn, totals
    )
    gin = gin.reshape(2, 2, rows // 2, ff)
    grad_in = jnp.concatenate([gin[:, i].reshape(rows, ff) for i in range(2)], axis=1)
    return (
        layer_out.reshape(1, tok, width),
        input_grad.reshape(1, tok, width),
        gain_grads[0],
        gqkv.reshape(rows, 3 * width).astype(F32),
        gattn.reshape(rows, width).astype(F32),
        gain_grads[1],
        grad_in.astype(F32),
        jnp.concatenate([gout[0], gout[1]], axis=1).astype(F32),
    )


def solution(mesh):
    in_specs = (
        P("dp", "ctx", None),
        P("dp"),
        P("dp", None),
        P("dp", None),
        P("dp"),
        P("dp", None),
        P("dp", None),
        P("dp", "ctx", None),
    )
    out_specs = (
        P("dp", "ctx", None),
        P("dp", "ctx", None),
        P("dp"),
        P("dp", None),
        P("dp", None),
        P("dp"),
        P("dp", None),
        P("dp", None),
    )
    return jax.shard_map(
        on_device, mesh=mesh, in_specs=in_specs, out_specs=out_specs, check_vma=False
    )
```

```python
import functools

import jax
import jax.numpy as jnp
from jax import lax
from jax.experimental import pallas as pl
from jax.experimental.pallas import tpu as pltpu
from jax.sharding import PartitionSpec as P

HEAD = 64
norm_eps = 1e-05
rope_theta = 160000.0
F32 = jnp.float32
BF16 = jnp.bfloat16
MESH = pl.DeviceIdType.MESH
LOG2E = 1.4426950408889634
VMEM_LIMIT = 64 * 1024 * 1024 - 65536
ANY = pl.BlockSpec(memory_space=pl.ANY)
VMEM = pl.BlockSpec(memory_space=pltpu.VMEM)
S = jax.ShapeDtypeStruct


def params(cid):
    return pltpu.CompilerParams(
        collective_id=cid, has_side_effects=True, vmem_limit_bytes=VMEM_LIMIT
    )


class Place:
    def __init__(self):
        self.nd = lax.axis_size("dp")
        self.nc = lax.axis_size("ctx")
        self.d = lax.axis_index("dp")
        self.c = lax.axis_index("ctx")
        self.nb = 2 if self.nd % 2 == 0 else 1
        self.na = self.nd // self.nb
        self.a = self.d // self.nb
        self.b = self.d % self.nb
        self.nz = self.nc // 2
        self.z = self.c // 2
        self.k = self.c % 2
        self.sibling = (self.d, self.z * 2 + 1 - self.k)

    def shard(self, da, db):
        return ((self.a + da) % self.na) * self.nb + (self.b + db) % self.nb

    def at(self, da, db):
        return (self.shard(da, db), self.c)


def barrier(pc, dp=True, ctx=True):
    sem = pltpu.get_barrier_semaphore()
    count = 0
    if dp:
        for t in range(1, pc.nd):
            pl.semaphore_signal(
                sem, inc=1, device_id=((pc.d + t) % pc.nd, pc.c), device_id_type=MESH
            )
            count += 1
    if ctx:
        for t in range(1, pc.nc):
            pl.semaphore_signal(
                sem, inc=1, device_id=(pc.d, (pc.c + t) % pc.nc), device_id_type=MESH
            )
            count += 1
    pl.semaphore_wait(sem, count)


def remote(src, dst, send, recv, target):
    return pltpu.make_async_remote_copy(
        src_ref=src,
        dst_ref=dst,
        send_sem=send,
        recv_sem=recv,
        device_id=target,
        device_id_type=MESH,
    )


class Gather:
    def __init__(self, pc, cut, own, send, recv, deep=None):
        self.pc, self.cut, self.own, self.send, self.recv, self.deep = pc, cut, own, send, recv, deep
        self.lines = [(da, 0) for da in range(1, pc.na)] + [(0, db) for db in range(1, pc.nb)]
        self.cross_at = [
            (da, db, part)
            for part in (0, 1)
            for da in range(1, pc.na)
            for db in range(1, pc.nb)
        ]
        self.n = len(self.lines) + len(self.cross_at)
        self.pair = (pc.d, (pc.z + 1 - 2 * (pc.z % 2)) * 2 + pc.k)

    @staticmethod
    def count(nd):
        nb = 2 if nd % 2 == 0 else 1
        na = nd // nb
        return 2 * ((na - 1) + (nb - 1) + 2 * (na - 1) * (nb - 1)) + 2 * nd

    def _copy(self, index, shard, part, target, own=False):
        src = (self.own if own else self.cut)(shard, self.pc.k, part)
        dst = self.cut(shard, self.pc.k, part)
        return remote(src, dst, self.send.at[index], self.recv.at[index], target)

    def _arrived(self, index, shard, core, part):
        ref = self.cut(shard, core, part)
        return remote(ref, ref, self.send.at[index], self.recv.at[index], self.pc.sibling)

    def _deep(self, index, shard, core, mine, target):
        ref = self.deep(shard, core, mine)
        return remote(ref, ref, self.send.at[index], self.recv.at[index], target)

    def others(self):
        pc = self.pc
        return [(da, db) for da in range(pc.na) for db in range(pc.nb) if (da, db) != (0, 0)]

    def first(self):
        pc = self.pc
        for i, (da, db) in enumerate(self.lines):
            self._copy(i, pc.d, None, pc.at(-da, -db), own=True).start()

    def _down(self, da, db):
        if self.deep is not None:
            i = self.others().index((da, db))
            self._deep(2 * self.n + i, self.pc.shard(da, db), self.pc.k, True, self.pair).start()

    def relay(self):
        pc, nl = self.pc, len(self.lines)
        for i, (da, db) in enumerate(self.lines):
            shard = pc.shard(da, db)
            self._arrived(i, shard, pc.k, None).wait_recv()
            for j, (xa, xb, part) in enumerate(self.cross_at):
                if part == 0 and db == 0 and xa == da:
                    self._copy(nl + j, shard, part, pc.at(0, -xb)).start()
                if part == 1 and da == 0 and xb == db:
                    self._copy(nl + j, shard, part, pc.at(-xa, 0)).start()
            self._down(da, db)
            self._copy(self.n + i, shard, None, pc.sibling).start()

    def cross(self):
        pc, nl = self.pc, len(self.lines)
        for j, (xa, xb, part) in enumerate(self.cross_at):
            shard = pc.shard(xa, xb)
            self._arrived(nl + j, shard, pc.k, part).wait_recv()
            self._copy(self.n + nl + j, shard, part, pc.sibling).start()
            if part == 1:
                self._down(xa, xb)

    def across(self):
        pc = self.pc
        for i, (da, db) in enumerate(self.others()):
            shard = pc.shard(da, db)
            self._deep(2 * self.n + i, shard, pc.k, False, pc.sibling).wait_recv()
            self._deep(2 * self.n + pc.nd + i, shard, pc.k, False, pc.sibling).start()

    def finish(self):
        pc, nl = self.pc, len(self.lines)
        for i, (da, db) in enumerate(self.lines):
            self._arrived(self.n + i, pc.shard(da, db), 1 - pc.k, None).wait_recv()
        for j, (xa, xb, part) in enumerate(self.cross_at):
            self._arrived(self.n + nl + j, pc.shard(xa, xb), 1 - pc.k, part).wait_recv()
        if self.deep is not None:
            for i, (da, db) in enumerate(self.others()):
                shard = pc.shard(da, db)
                self._deep(2 * self.n + pc.nd + i, shard, 1 - pc.k, False, pc.sibling).wait_recv()

    def sent(self):
        pc, nl = self.pc, len(self.lines)
        for i, _ in enumerate(self.lines):
            self._arrived(i, pc.d, pc.k, None).wait_send()
            self._arrived(self.n + i, pc.d, pc.k, None).wait_send()
        for j, (_, _, part) in enumerate(self.cross_at):
            self._arrived(nl + j, pc.d, pc.k, part).wait_send()
            self._arrived(self.n + nl + j, pc.d, pc.k, part).wait_send()
        if self.deep is not None:
            for i, _ in enumerate(self.others()):
                self._deep(2 * self.n + i, pc.d, pc.k, True, pc.sibling).wait_send()
                self._deep(2 * self.n + pc.nd + i, pc.d, pc.k, False, pc.sibling).wait_send()


def row_cut(ref, rows, core, part, lead=0):
    start = core * (rows // 2) + (0 if part is None else part * (rows // 4))
    size = rows // 2 if part is None else rows // 4
    return ref.at[(slice(None),) * lead + (pl.ds(start, size),)]


def share_rows(pc, rows):
    q = rows // 8
    odd = pc.z % 2

    def cut(ref, core, part):
        start = core * (4 * q) + odd * q
        if part is None:
            return ref.at[pl.ds(start, 3 * q)]
        n = 3 * q // 2
        return ref.at[pl.ds(start + part * n, n)]

    def deep(ref, core, mine):
        at = odd * (3 * q) if mine else (1 - odd) * (3 * q)
        return ref.at[pl.ds(core * (4 * q) + at, q)]

    return cut, deep


def share_cols(pc, rows, cols):
    q = cols // 8
    odd = pc.z % 2
    n = rows // 2 // 16 * 16

    def cut(ref, core, part):
        start = pl.multiple_of(core * (4 * q) + odd * q, 128)
        at = slice(None) if part is None else pl.ds(0, n) if part == 0 else pl.ds(n, rows - n)
        return ref.at[at, pl.ds(start, 3 * q)]

    def deep(ref, core, mine):
        at = odd * (3 * q) if mine else (1 - odd) * (3 * q)
        return ref.at[:, pl.ds(pl.multiple_of(core * (4 * q) + at, 128), q)]

    return cut, deep


def early_rows(rows):
    return rows // 2 if rows % 256 == 0 else 0


class Reduce:
    def __init__(self, pc, g, bufs, send, recv, by_rows):
        self.pc, self.g, self.send, self.recv, self.by_rows = pc, g, send, recv, by_rows
        self.r1a, self.r1b, self.r2a, self.r2b = bufs

    @staticmethod
    def count(nd):
        nb = 2 if nd % 2 == 0 else 1
        return 2 * (nd // nb - 1 + nb - 1)

    @staticmethod
    def scratch(nd, rows, cols, by_rows):
        nb = 2 if nd % 2 == 0 else 1
        na = nd // nb
        r, c = (rows // 2, cols) if by_rows else (rows, cols // 2)
        return [
            pltpu.VMEM((na, nb, rows, cols), BF16),
            pltpu.VMEM((na - 1, nb, r, c), BF16),
            pltpu.VMEM((nb - 1, na, r, c), BF16),
            pltpu.VMEM((nb - 1, r, c), BF16),
            pltpu.VMEM((na - 1, r, c), BF16),
        ]

    def part(self, ref, p):
        lead = (slice(None),) * (len(ref.shape) - 2)
        rows, cols = ref.shape[-2:]
        if self.by_rows:
            return ref.at[lead + (pl.ds(p * (rows // 2), rows // 2),)]
        return ref.at[lead + (slice(None), pl.ds(p * (cols // 2), cols // 2))]

    def copies(self, step):
        pc = self.pc
        na, nb = pc.na, pc.nb
        out = []
        base = 0 if step == 1 else na - 1 + nb - 1
        for da in range(1, na):
            a = (pc.a + na - da) % na
            i = base + da - 1
            if step == 1:
                src, dst = self.part(self.g.at[a], 0), self.r1a.at[da - 1]
            else:
                src, dst = self.part(self.g.at[a, pc.b], 1), self.r2b.at[da - 1]
            out.append(remote(src, dst, self.send.at[i], self.recv.at[i], pc.at(-da, 0)))
        for db in range(1, nb):
            b = (pc.b + nb - db) % nb
            i = base + na - 1 + db - 1
            if step == 1:
                src, dst = self.part(self.g.at[:, b], 1), self.r1b.at[db - 1]
            else:
                src, dst = self.part(self.g.at[pc.a, b], 0), self.r2a.at[db - 1]
            out.append(remote(src, dst, self.send.at[i], self.recv.at[i], pc.at(0, -db)))
        return out

    def start(self):
        for cp in self.copies(1):
            cp.start()

    def middle(self):
        pc = self.pc
        for cp in self.copies(1):
            cp.wait_recv()
        for b in range(pc.nb):
            at = self.part(self.g.at[pc.a, b], 0)
            add(at, [self.r1a.at[i, b] for i in range(pc.na - 1)])
        for a in range(pc.na):
            at = self.part(self.g.at[a, pc.b], 1)
            add(at, [self.r1b.at[i, a] for i in range(pc.nb - 1)])
        for cp in self.copies(2):
            cp.start()

    def finish(self, total):
        pc = self.pc
        for cp in self.copies(2):
            cp.wait_recv()
        own = self.g.at[pc.a, pc.b]
        add(self.part(own, 0), [self.r2a.at[i] for i in range(pc.nb - 1)], self.part(total, 0))
        add(self.part(own, 1), [self.r2b.at[i] for i in range(pc.na - 1)], self.part(total, 1))

    def sent(self):
        for cp in self.copies(1) + self.copies(2):
            cp.wait_send()


def add(ref, others, into=None):
    into = ref if into is None else into
    rows = ref.shape[0]
    chunk = next(n for n in (32, 16, rows) if rows % n == 0)

    def some(i, _):
        at = pl.ds(pl.multiple_of(i * chunk, chunk), chunk)
        total = ref[at, :].astype(F32)
        for o in others:
            total = total + o[at, :].astype(F32)
        into[at, :] = total.astype(BF16)
        return 0

    if rows == chunk:
        total = ref[...].astype(F32)
        for o in others:
            total = total + o[...].astype(F32)
        into[...] = total.astype(BF16)
    else:
        lax.fori_loop(0, rows // chunk, some, 0)


PARTS = 4


def chain_part(by_rows, parts):
    def part(ref, p):
        rows, cols = ref.shape[-2:]
        if by_rows:
            n = rows // parts
            return ref.at[pl.ds(pl.multiple_of(p * n, n), n)]
        n = cols // parts
        return ref.at[:, pl.ds(pl.multiple_of(p * n, n), n)]

    return part


class Chain:
    def __init__(self, pc, t, bufs, send, recv, by_rows, parts):
        self.pc, self.t, self.n = pc, t, parts
        self.part = chain_part(by_rows, parts)
        self.outer, self.swap, total = bufs
        self.total, self.other = total.at[pc.k], total.at[1 - pc.k]
        self.all = total
        self.send, self.recv = send, recv
        half = pc.nz // 2
        self.low = pc.z < half
        self.end = (pc.z == 0) | (pc.z == pc.nz - 1)
        self.mid = (pc.z == half - 1) | (pc.z == half)
        step = 1 - 2 * (pc.z // half)
        self.inner_id = (pc.d, ((pc.z + step + pc.nz) % pc.nz) * 2 + pc.k)
        self.outer_id = (pc.d, ((pc.z - step + pc.nz) % pc.nz) * 2 + pc.k)

    def up_copy(self, p):
        return remote(
            self.part(self.t, p), self.part(self.outer, p), self.send.at[0, p], self.recv.at[0, p],
            self.inner_id,
        )

    def swap_copy(self, p):
        return remote(
            self.part(self.t, p), self.part(self.swap, p), self.send.at[1, p], self.recv.at[1, p],
            self.inner_id,
        )

    def down_copy(self, p):
        at = self.part(self.total, p)
        return remote(at, at, self.send.at[2, p], self.recv.at[2, p], self.outer_id)

    def side_copy(self, p):
        at = self.part(self.total, p)
        return remote(at, at, self.send.at[3, p], self.recv.at[3, p], self.pc.sibling)

    def side_wait(self, p):
        at = self.part(self.other, p)
        remote(at, at, self.send.at[3, p], self.recv.at[3, p], self.pc.sibling).wait_recv()

    def open(self, p):
        @pl.when(self.end)
        def _():
            @pl.when(self.mid)
            def _():
                self.swap_copy(p).start()

            @pl.when(jnp.logical_not(self.mid))
            def _():
                self.up_copy(p).start()

    def up(self, p):
        @pl.when(jnp.logical_not(self.end))
        def _():
            self.up_copy(p).wait_recv()
            add(self.part(self.t, p), [self.part(self.outer, p)])

            @pl.when(self.mid)
            def _():
                self.swap_copy(p).start()

            @pl.when(jnp.logical_not(self.mid))
            def _():
                self.up_copy(p).start()

    def turn_in(self, p):
        @pl.when(self.mid)
        def _():
            self.swap_copy(p).wait_recv()
            add(self.part(self.t, p), [self.part(self.swap, p)], self.part(self.total, p))

            @pl.when(jnp.logical_not(self.end))
            def _():
                self.down_copy(p).start()

            self.side_copy(p).start()

    def turn_out(self, p):
        @pl.when(jnp.logical_not(self.mid))
        def _():
            self.down_copy(p).wait_recv()

            @pl.when(jnp.logical_not(self.end))
            def _():
                self.down_copy(p).start()

            self.side_copy(p).start()

    def both(self, p):
        self.up(p)
        self.turn_in(p - 1)

    def sent(self, p):
        @pl.when(self.mid)
        def _():
            self.swap_copy(p).wait_send()

        @pl.when(jnp.logical_not(self.mid))
        def _():
            self.up_copy(p).wait_send()

        @pl.when(jnp.logical_not(self.end))
        def _():
            self.down_copy(p).wait_send()

        self.side_copy(p).wait_send()


def half_rows(pc, ref, core):
    rows = ref.shape[0] // pc.nd
    h = rows // 2
    return [ref.at[pl.ds(pl.multiple_of(s * rows + core * h, h), h)] for s in range(pc.nd)]


def project_kernel(
    x_ref, gains_ref, cos_ref, sin_ref, wqkv_ref, wattn_ref, win_ref,
    h1t_ref, gains_out, w1_out, w2_out, wqkv_out, wattn_out, heads_out, w1_all,
    wbuf, abuf, ibuf, h1_ref, gbuf, sendbuf,
    wsend, wrecv, asend, arecv, esend, erecv, gsend, grecv, xsend, xrecv, local,
):
    pc = Place()
    nd, nc, nz = pc.nd, pc.nc, pc.nz
    rows = wqkv_ref.shape[0]
    width = wqkv_ref.shape[1] // 3
    tok = x_ref.shape[0]
    w = width // nc
    cw = 2 * w
    own_w = [
        pltpu.make_async_copy(
            wqkv_ref.at[:, pl.ds(g * width, width)], wbuf.at[g, pc.d], local.at[g]
        )
        for g in range(3)
    ]
    for cp in own_w:
        cp.start()
    own_a = pltpu.make_async_copy(wattn_ref, abuf, local.at[3])
    own_a.start()
    own_i = pltpu.make_async_copy(win_ref, ibuf, local.at[5 + nz])
    own_i.start()
    barrier(pc)
    for cp in own_w:
        cp.wait()

    def chip_of(j):
        return (pc.z + j + 1) % nz

    def chunk(j):
        col = pl.multiple_of(chip_of(j) * cw, cw)

        def cut(shard, core, part):
            return row_cut(wbuf.at[:, shard, :, pl.ds(col, cw)], rows, core, part, lead=1)

        return Gather(pc, cut, cut, wsend.at[j], wrecv.at[j])

    def attn_cut(shard, core, part):
        return row_cut(wattn_out.at[shard], rows, core, part)

    def attn_own(shard, core, part):
        return row_cut(wattn_ref, rows, core, part)

    attn = Gather(pc, attn_cut, attn_own, asend, arecv)

    def early_cut(shard, core, part):
        return row_cut(w1_all.at[shard], e, core, part)

    def early_own(shard, core, part):
        return row_cut(w1_out, e, core, part)

    early = Gather(pc, early_cut, early_own, esend, erecv)
    e = early_rows(rows)
    extra = [attn] + [early] * (e > 0)

    gain_copies = []
    gbuf[pc.d] = gains_ref[...]
    for t in range(1, nd):
        gain_copies.append(
            remote(
                gains_ref, gbuf.at[pc.d], gsend.at[t], grecv.at[t], ((pc.d + t) % nd, pc.c)
            )
        )
        gain_copies[-1].start()
    for j in range(min(2, nz)):
        chunk(j).first()

    xf = x_ref[...].astype(F32)
    mean = jnp.mean(xf, axis=-1, keepdims=True)
    cen = xf - mean
    var = jnp.mean(cen * cen, axis=-1, keepdims=True)
    hat = cen * lax.rsqrt(var + norm_eps)
    for t in range(1, nd):
        src = gbuf.at[(pc.d + nd - t) % nd]
        remote(src, src, gsend.at[t], grecv.at[t], pc.sibling).wait_recv()
    for s in range(nd):
        cols = slice(s * rows, (s + 1) * rows)
        h1_ref[:, cols] = (hat[:, cols] * gbuf[s, 0:1, :]).astype(BF16)
    gains_out[...] = gbuf[...]
    own_a.wait()
    own_a2 = pltpu.make_async_copy(abuf, wattn_out.at[pc.d], local.at[3])
    own_a2.start()
    own_i.wait()
    ff = w1_out.shape[1]
    w1_out[...] = ibuf[:, :ff]
    w2_out[...] = ibuf[:, ff:]
    h1t_ref[...] = jnp.transpose(h1_ref[...])

    lane = lax.broadcasted_iota(jnp.int32, (1, cw), 1)
    low = (lane % HEAD) < HEAD // 2

    def out_copy(j):
        cols = pl.ds(pl.multiple_of(chip_of(j) * cw, cw), cw)
        return pltpu.make_async_copy(
            wbuf.at[:, :, :, cols], wqkv_out.at[:, :, :, cols], local.at[4 + j]
        )

    def place(ref):
        return ref.at[:, pl.ds(pl.multiple_of(pc.c * tok, tok), tok), :]

    def exchange(j, kk):
        return remote(
            sendbuf.at[j, kk], place(heads_out), xsend.at[j, kk], xrecv.at[j, pc.k],
            (pc.d, chip_of(j) * 2 + kk),
        )

    def step(j, _):
        g = chunk(j)
        g.relay()

        @pl.when(j + 2 < nz)
        def _():
            chunk(j + 2).first()

        @pl.when(j == max(nz - 2, 0))
        def _():
            attn.first()

        @pl.when(j == nz - 1)
        def _():
            for it in extra[1:]:
                it.first()

        g.cross()
        g.finish()
        out_copy(j).start()
        cols = pl.ds(pl.multiple_of(chip_of(j) * cw, cw), cw)
        for part in range(3):
            weight = wbuf[part, :, :, cols].reshape(nd * rows, cw)
            proj = jnp.dot(h1_ref[...], weight, preferred_element_type=F32)
            if part < 2:
                up = pltpu.roll(proj, cw - HEAD // 2, 1)
                down = pltpu.roll(proj, HEAD // 2, 1)
                proj = proj * cos_ref[...] + jnp.where(low, up, down) * sin_ref[...]
            proj = proj.astype(BF16)
            for kk in range(2):
                sendbuf[j, kk, part] = proj[:, kk * w : (kk + 1) * w]

        @pl.when(j < nz - 1)
        def _():
            exchange(j, 0).start()
            exchange(j, 1).start()

        return 0

    lax.fori_loop(0, nz, step, 0)
    last = nz - 1
    remote(
        sendbuf.at[last, 1 - pc.k], place(heads_out), xsend.at[last, 1 - pc.k],
        xrecv.at[last, pc.k], pc.sibling,
    ).start()
    own_x = pltpu.make_async_copy(
        sendbuf.at[last, pc.k], place(heads_out), local.at[4 + nz]
    )
    own_x.start()
    for it in extra:
        it.relay()
    for it in extra:
        it.cross()
    for it in extra:
        it.finish()

    def arrival(j, kk):
        ref = sendbuf.at[j, kk]
        return remote(ref, ref, xsend.at[j, kk], xrecv.at[j, kk], pc.sibling)

    def drain(j, _):
        arrival(j, 0).wait_recv()
        arrival(j, 1).wait_recv()
        arrival(j, 0).wait_send()
        arrival(j, 1).wait_send()
        chunk(j).sent()
        out_copy(j).wait()
        return 0

    lax.fori_loop(0, nz - 1, drain, 0)
    arrival(last, 1 - pc.k).wait_recv()
    arrival(last, 1 - pc.k).wait_send()
    chunk(last).sent()
    out_copy(last).wait()
    own_x.wait()
    own_a2.wait()
    for it in extra:
        it.sent()
    for cp in gain_copies:
        cp.wait_send()


def project(x, gains, cosine, sine, wqkv, wattn, win):
    nd, nc = lax.axis_size("dp"), lax.axis_size("ctx")
    nz = nc // 2
    tok, width = x.shape
    rows = wqkv.shape[0]
    w = width // nc
    n = Gather.count(nd)
    dma = pltpu.SemaphoreType.DMA
    return pl.pallas_call(
        project_kernel,
        out_shape=[
            S((width, tok), BF16),
            S((nd, 8, rows), F32),
            S((rows, win.shape[1] // 2), BF16),
            S((rows, win.shape[1] // 2), BF16),
            S((3, nd, rows, width), BF16),
            S((nd, rows, width), BF16),
            S((3, nc * tok, w), BF16),
            S((nd, rows, win.shape[1] // 2), BF16),
        ],
        in_specs=[VMEM, VMEM, VMEM, VMEM, ANY, ANY, ANY],
        out_specs=[VMEM, VMEM, VMEM, VMEM, ANY, ANY, ANY, ANY],
        scratch_shapes=[
            pltpu.VMEM((3, nd, rows, width), BF16),
            pltpu.VMEM((rows, width), BF16),
            pltpu.VMEM(win.shape, BF16),
            pltpu.VMEM((tok, width), BF16),
            pltpu.VMEM((nd, 8, rows), F32),
            pltpu.VMEM((nz, 2, 3, tok, w), BF16),
            dma((nz, n)), dma((nz, n)), dma((n,)), dma((n,)), dma((n,)), dma((n,)),
            dma((nd,)), dma((nd,)), dma((nz, 2)), dma((nz, 2)), dma((6 + nz,)),
        ],
        compiler_params=params(0),
        name="project",
    )(x, gains, cosine, sine, wqkv, wattn, win)


def attend_kernel(
    heads_ref, w1_ref, w2_ref, wout_ref, w1_early,
    otok_out, o_ref, lse_ref, w1_out, w2_out, wout_out,
    qkv, vext, bounce1, bounce2, bounce3,
    s1, r1, s2, r2, s3, r3, xsend, xrecv, local,
):
    pc = Place()
    nd, nc = pc.nd, pc.nc
    keys, w = heads_ref.shape[1], heads_ref.shape[2]
    tok = keys // nc
    rows = w1_ref.shape[0]
    load = pltpu.make_async_copy(heads_ref, qkv, local.at[0])
    load.start()
    pairs = [(w1_ref, bounce1, w1_out), (w2_ref, bounce2, w2_out), (wout_ref, bounce3, wout_out)]
    for i, (src, mid, _) in enumerate(pairs):
        pltpu.make_async_copy(src, mid, local.at[1 + i]).start()
    barrier(pc)
    e = early_rows(rows)
    lower = lambda ref: ref.at[pl.ds(e, rows - e)]
    cut_h, deep_h = share_rows(pc, rows - e)
    cut_r, deep_r = share_rows(pc, rows)
    cut_c, deep_c = share_cols(pc, *wout_ref.shape)

    def item(ref, out, cut, deep, send, recv):
        return Gather(
            pc,
            lambda s, k, p: cut(out.at[s], k, p),
            lambda s, k, p: cut(ref, k, p),
            send,
            recv,
            lambda s, k, mine: deep(out.at[s], k, mine),
        )

    items = [
        item(wout_ref, wout_out, cut_c, deep_c, s3, r3),
        item(w2_ref, w2_out, cut_r, deep_r, s2, r2),
        Gather(
            pc,
            lambda s, k, p: cut_h(lower(w1_out.at[s]), k, p),
            lambda s, k, p: cut_h(lower(w1_ref), k, p),
            s1,
            r1,
            lambda s, k, mine: deep_h(lower(w1_out.at[s]), k, mine),
        ),
    ]
    items[0].first()
    items[1].first()
    load.wait()
    for i, (src, mid, _) in enumerate(pairs):
        pltpu.make_async_copy(src, mid, local.at[1 + i]).wait()
    for i, (_, mid, dst) in enumerate(pairs):
        pltpu.make_async_copy(mid, dst.at[pc.d], local.at[1 + i]).start()
    nh = w // HEAD
    for h in range(nh):
        vext[h, :, :HEAD] = qkv[2, :, h * HEAD : (h + 1) * HEAD]
        vext[h, :, HEAD:] = jnp.ones((keys, HEAD), BF16)
    scale = HEAD ** (-0.5) * LOG2E

    def block_copy(i):
        to = (pc.c + i + 1) % nc
        at = pl.ds(pl.multiple_of(to * tok, tok), tok)
        return remote(
            o_ref.at[at], otok_out.at[pc.c], xsend.at[i], xrecv.at[i], (pc.d, to)
        )

    def block(i, _):
        at = pl.ds(pl.multiple_of(((pc.c + i + 1) % nc) * tok, tok), tok)
        for h in range(nh):
            hs = slice(h * HEAD, (h + 1) * HEAD)
            s = lax.dot_general(
                qkv[0, at, hs], qkv[1, :, hs], (((1,), (1,)), ((), ())),
                preferred_element_type=F32,
            )
            m = jnp.max(s, axis=1, keepdims=True)
            p = jnp.exp2(s * scale - m * scale).astype(BF16)
            ol = jnp.dot(p, vext[h], preferred_element_type=F32)
            total = ol[:, HEAD:]
            o_ref[at, hs] = (ol[:, :HEAD] / total).astype(BF16)
            lse = m * scale + jnp.log2(total)
            lse_ref[h, :, at] = jnp.transpose(jnp.concatenate([lse, lse], axis=1))[:8]

        @pl.when(i < nc - 1)
        def _():
            block_copy(i).start()

        @pl.when(i == nc // 2)
        def _():
            items[0].relay()
            items[2].first()

        return 0

    lax.fori_loop(0, nc, block, 0)
    own = pltpu.make_async_copy(
        o_ref.at[pl.ds(pl.multiple_of(pc.c * tok, tok), tok)], otok_out.at[pc.c], local.at[0]
    )
    own.start()
    items[1].relay()
    items[0].cross()
    items[2].relay()
    items[1].cross()
    items[0].across()
    items[2].cross()
    items[1].across()
    items[2].across()
    for it in items:
        it.finish()

    def drain(i, _):
        got = otok_out.at[(pc.c + nc - i - 1) % nc]
        remote(got, got, xsend.at[i], xrecv.at[i], pc.sibling).wait_recv()
        block_copy(i).wait_send()
        return 0

    lax.fori_loop(0, nc - 1, drain, 0)
    own.wait()
    for i, (_, mid, dst) in enumerate(pairs):
        pltpu.make_async_copy(mid, dst.at[pc.d], local.at[1 + i]).wait()
    for it in items:
        it.sent()


def attend(heads, w1, w2, wout, w1_early):
    nd, nc = lax.axis_size("dp"), lax.axis_size("ctx")
    _, keys, w = heads.shape
    nh = w // HEAD
    n = Gather.count(nd)
    dma = pltpu.SemaphoreType.DMA
    return pl.pallas_call(
        attend_kernel,
        out_shape=[
            S((nc, keys // nc, w), BF16),
            S((keys, w), BF16),
            S((nh, 8, keys), F32),
            S((nd,) + w1.shape, BF16),
            S((nd,) + w2.shape, BF16),
            S((nd,) + wout.shape, BF16),
        ],
        in_specs=[ANY] * 5,
        out_specs=[ANY, VMEM, VMEM, ANY, ANY, ANY],
        input_output_aliases={4: 3},
        scratch_shapes=[
            pltpu.VMEM((3, keys, w), BF16),
            pltpu.VMEM((nh, keys, 2 * HEAD), BF16),
            pltpu.VMEM(w1.shape, BF16),
            pltpu.VMEM(w2.shape, BF16),
            pltpu.VMEM(wout.shape, BF16),
            dma((n,)), dma((n,)), dma((n,)), dma((n,)), dma((n,)), dma((n,)),
            dma((nc,)), dma((nc,)), dma((4,)),
        ],
        compiler_params=params(1),
        name="attend",
    )(heads, w1, w2, wout, w1_early)


def attend_back_kernel(
    heads_ref, o_ref, lse_ref, dout_ref, near_ref, far_ref, h2t_ref, dl1_ref, dl2_ref,
    actt_ref, c_ref, ot_ref, dres_ref,
    dtok_out, t_ref, gout_out, gattn_out,
    qkv, dout, delta, dq, sendbuf, h2t, dl, actt, cot, ot, dres, gout, gattn,
    ga, ra0, ra1, ra2, ra3, gb, rb0, rb1, rb2, rb3,
    dsend, drecv, xsend, xrecv, ssend, srecv, asend, arecv, bsend, brecv, local,
):
    pc = Place()
    nd = pc.nd
    nc = pc.nc
    keys, w = heads_ref.shape[1], heads_ref.shape[2]
    tok = keys // nc
    nh = w // HEAD
    load = pltpu.make_async_copy(heads_ref, qkv, local.at[0])
    load.start()
    mine_t = half_rows(pc, h2t_ref, pc.k)
    hers_t = half_rows(pc, h2t_ref, 1 - pc.k)
    fetch = [pltpu.make_async_copy(mine_t[s], h2t.at[0, s], local.at[2 + s]) for s in range(nd)]
    fetch.append(pltpu.make_async_copy(dl1_ref, dl.at[0, 0], local.at[2 + nd]))
    fetch.append(pltpu.make_async_copy(dl2_ref, dl.at[1, 0], local.at[3 + nd]))
    half = cot.shape[2]
    nr = actt.shape[2]
    col = lambda core: pl.ds(pl.multiple_of(core * half, half), half)
    o_mine, o_hers = half_rows(pc, ot_ref, pc.k), half_rows(pc, ot_ref, 1 - pc.k)
    acts = [actt_ref.at[pl.ds(s * nr, nr)] for s in range(nd)]
    more = [(acts[s], actt.at[0, s]) for s in range(nd)] + [(o_mine[s], ot.at[0, s]) for s in range(nd)]
    more += [(c_ref.at[:, col(pc.k)], cot.at[0]), (dres_ref, dres.at[0])]
    first = len(fetch)
    fetch += [pltpu.make_async_copy(a, b, local.at[4 + nd + i]) for i, (a, b) in enumerate(more)]
    for cp in fetch:
        cp.start()
    barrier(pc)
    swap = [
        remote(hers_t[s], h2t.at[1, s], ssend.at[s], srecv.at[s], pc.sibling) for s in range(nd)
    ]
    more = [(acts[s], actt.at[1, s]) for s in range(nd)] + [(o_hers[s], ot.at[1, s]) for s in range(nd)]
    more += [(c_ref.at[:, col(1 - pc.k)], cot.at[1]), (dres_ref, dres.at[1])]
    late = [
        remote(a, b, ssend.at[nd + 2 + i], srecv.at[nd + 2 + i], pc.sibling)
        for i, (a, b) in enumerate(more)
    ]
    swap.append(remote(dl1_ref, dl.at[0, 1], ssend.at[nd], srecv.at[nd], pc.sibling))
    swap.append(remote(dl2_ref, dl.at[1, 1], ssend.at[nd + 1], srecv.at[nd + 1], pc.sibling))
    for cp in swap:
        cp.start()
    mine = pl.ds(pl.multiple_of(pc.c * tok, tok), tok)
    for i in range(nc - 1):
        to = (pc.c + i + 1) % nc
        remote(dout_ref.at[to], dout.at[mine], dsend.at[i], drecv.at[i], (pc.d, to)).start()
    own = pltpu.make_async_copy(dout_ref.at[pc.c], dout.at[mine], local.at[1])
    own.start()
    ra = Reduce(pc, ga, (ra0, ra1, ra2, ra3), asend, arecv, True)
    rb = Reduce(pc, gb, (rb0, rb1, rb2, rb3), bsend, brecv, True)
    for cp in late:
        cp.start()
    for cp in fetch[:first]:
        cp.wait()
    for cp in swap[: nd + 1]:
        cp.wait_recv()
    weight_grad(pc, ga, h2t, dl.at[0], True)
    ra.start()
    swap[nd + 1].wait_recv()
    weight_grad(pc, gb, h2t, dl.at[1], True)
    rb.start()
    for cp in fetch[first:]:
        cp.wait()
    for cp in late:
        cp.wait_recv()
    weight_grad(pc, gout, actt, cot)
    weight_grad(pc, gattn, ot, dres)
    keep_g = [
        pltpu.make_async_copy(gout, gout_out, local.at[2]),
        pltpu.make_async_copy(gattn, gattn_out, local.at[3]),
    ]
    for cp in keep_g:
        cp.start()
    dq[...] = jnp.zeros_like(dq)
    load.wait()
    own.wait()
    for i in range(nc - 1):
        src = (pc.c + nc - i - 1) % nc
        got = dout.at[pl.ds(pl.multiple_of(src * tok, tok), tok)]
        remote(got, got, dsend.at[i], drecv.at[i], pc.sibling).wait_recv()

    def deltas(i, _):
        at = pl.ds(pl.multiple_of(i * tok, tok), tok)
        t = jnp.transpose(o_ref[at, :].astype(F32) * dout[at, :].astype(F32))
        for h in range(nh):
            row = jnp.sum(t[h * HEAD : (h + 1) * HEAD], axis=0, keepdims=True)
            delta[h, :, at] = jnp.broadcast_to(row, (8, tok))
        return 0

    lax.fori_loop(0, nc, deltas, 0)
    scale = HEAD ** (-0.5)
    lane = lax.broadcasted_iota(jnp.int32, (1, w), 1)
    low = (lane % HEAD) < HEAD // 2

    def unrotate(g, to):
        cos_n, sin_n, cos_f, sin_f = near_ref[0], near_ref[1], far_ref[0, to], far_ref[1, to]
        t = g * (sin_f * cos_n + cos_f * sin_n)
        if w == HEAD:
            up = jnp.concatenate([t[:, HEAD // 2 :], t[:, : HEAD // 2]], axis=1)
            down = up
        else:
            up = pltpu.roll(t, w - HEAD // 2, 1)
            down = pltpu.roll(t, HEAD // 2, 1)
        return g * (cos_f * cos_n - sin_f * sin_n) + jnp.where(low, up, -down)

    def kv_copy(i):
        to = (pc.c + i + 1) % nc
        return remote(
            sendbuf.at[to, pl.ds(1, 2)], dtok_out.at[pc.c, pl.ds(1, 2)],
            xsend.at[0, i], xrecv.at[0, i], (pc.d, to),
        )

    def q_copy(i):
        to = (pc.c + i + 1) % nc
        return remote(
            sendbuf.at[to, 0], dtok_out.at[pc.c, 0], xsend.at[1, i], xrecv.at[1, i], (pc.d, to)
        )

    def block(i, _):
        to = (pc.c + i + 1) % nc
        at = pl.ds(pl.multiple_of(to * tok, tok), tok)
        dks, dvs = [], []
        for h in range(nh):
            hs = slice(h * HEAD, (h + 1) * HEAD)
            kb, vb = qkv[1, at, hs], qkv[2, at, hs]
            q, do = qkv[0, :, hs], dout[:, hs]
            nt = (((1,), (1,)), ((), ()))
            st = lax.dot_general(kb, q, nt, preferred_element_type=F32)
            p = jnp.exp2(st * (scale * LOG2E) - lse_ref[h, 0:1, :])
            dvs.append(jnp.dot(p.astype(BF16), do, preferred_element_type=F32))
            dp = lax.dot_general(vb, do, nt, preferred_element_type=F32)
            ds = (p * (dp - delta[h, 0:1, :])).astype(BF16)
            dks.append(jnp.dot(ds, q, preferred_element_type=F32))
            dq[:, hs] += lax.dot_general(
                ds, kb, (((0,), (0,)), ((), ())), preferred_element_type=F32
            )
        dk = jnp.concatenate(dks, axis=1) * scale
        sendbuf[to, 1] = unrotate(dk, to).astype(BF16)
        sendbuf[to, 2] = jnp.concatenate(dvs, axis=1).astype(BF16)

        @pl.when(i < nc - 1)
        def _():
            kv_copy(i).start()

        @pl.when(i == (nc * 3) // 8)
        def _():
            ra.middle()

        @pl.when(i == (nc * 7) // 8)
        def _():
            rb.middle()

        return 0

    lax.fori_loop(0, nc, block, 0)

    def q_block(i, _):
        to = (pc.c + i + 1) % nc
        at = pl.ds(pl.multiple_of(to * tok, tok), tok)
        sendbuf[to, 0] = unrotate(dq[at, :] * scale, to).astype(BF16)

        @pl.when(i < nc - 1)
        def _():
            q_copy(i).start()

        return 0

    lax.fori_loop(0, nc, q_block, 0)
    keep = pltpu.make_async_copy(sendbuf.at[pc.c], dtok_out.at[pc.c], local.at[1])
    keep.start()
    hr = ga.shape[2]
    ra.finish(t_ref.at[pl.ds(0, hr)])
    rb.finish(t_ref.at[pl.ds(hr, hr)])

    def drain(i, _):
        got = dtok_out.at[(pc.c + nc - i - 1) % nc]
        remote(
            got.at[pl.ds(1, 2)], got.at[pl.ds(1, 2)], xsend.at[0, i], xrecv.at[0, i], pc.sibling
        ).wait_recv()
        remote(got.at[0], got.at[0], xsend.at[1, i], xrecv.at[1, i], pc.sibling).wait_recv()
        kv_copy(i).wait_send()
        q_copy(i).wait_send()
        to = (pc.c + i + 1) % nc
        remote(
            dout_ref.at[to], dout.at[mine], dsend.at[i], drecv.at[i], (pc.d, to)
        ).wait_send()
        return 0

    lax.fori_loop(0, nc - 1, drain, 0)
    keep.wait()
    for cp in keep_g:
        cp.wait()
    for cp in swap + late:
        cp.wait_send()
    ra.sent()
    rb.sent()


def weight_grad(pc, g, lhs, rhs, flipped=False):
    dims = (((1,), (1 if flipped else 0,)), ((), ()))

    def shard(s, _):
        total = lax.dot_general(lhs[0, s], rhs[0], dims, preferred_element_type=F32)
        total = total + lax.dot_general(lhs[1, s], rhs[1], dims, preferred_element_type=F32)
        g[s // pc.nb, s % pc.nb] = total.astype(BF16)
        return 0

    lax.fori_loop(0, pc.nd, shard, 0)


def attend_back(heads, o, lse, dout, near, far, h2t, dl1, dl2, actt, cot, ot, dres):
    nc, nd = lax.axis_size("ctx"), lax.axis_size("dp")
    ff = dl1.shape[0]
    hr = h2t.shape[0] // nd // 2
    n = Reduce.count(nd)
    _, keys, w = heads.shape
    nh = w // HEAD
    tok = keys // nc
    width = w * nc
    nb = 2 if nd % 2 == 0 else 1
    vm = lambda *shape: pltpu.VMEM(shape, BF16)
    gout, gattn = (nd // nb, nb, ff // nd, width // 2), (nd // nb, nb, hr, width)
    ns = 3 * nd + 4
    dma = pltpu.SemaphoreType.DMA
    return pl.pallas_call(
        attend_back_kernel,
        out_shape=[
            S((nc, 3, tok, w), BF16), S((2 * hr, ff), BF16), S(gout, BF16), S(gattn, BF16)
        ],
        in_specs=[ANY, VMEM, VMEM, ANY, VMEM, VMEM] + [ANY] * 7,
        out_specs=[ANY, VMEM, ANY, ANY],
        scratch_shapes=[
            pltpu.VMEM((3, keys, w), BF16),
            pltpu.VMEM((keys, w), BF16),
            pltpu.VMEM((nh, 8, keys), F32),
            pltpu.VMEM((keys, w), F32),
            pltpu.VMEM((nc, 3, tok, w), BF16),
            pltpu.VMEM((2, nd, hr, tok), BF16),
            pltpu.VMEM((2, 2, ff, tok), BF16),
            vm(2, nd, ff // nd, tok), vm(2, tok, width // 2), vm(2, nd, hr, tok), vm(2, tok, width),
            vm(*gout), vm(*gattn),
            *Reduce.scratch(nd, hr, ff, True),
            *Reduce.scratch(nd, hr, ff, True),
            dma((nc,)), dma((nc,)), dma((2, nc)), dma((2, nc)), dma((ns,)), dma((ns,)),
            dma((n,)), dma((n,)), dma((n,)), dma((n,)), dma((6 + 3 * nd,)),
        ],
        compiler_params=params(2),
        name="attend_back",
    )(heads, o, lse, dout, near, far, h2t, dl1, dl2, actt, cot, ot, dres)


def each(count, *calls):
    def body(p, _):
        for call in calls:
            call(p)
        return 0

    lax.fori_loop(0, count, body, 0)


def close_kernel(
    dtok_ref, h1t_ref, wqkv_ref, x_ref, gain_ref, dres_ref, part_ref, gout_ref, gattn_ref, t_ref,
    dx_ref, gain_out, outi, outq, outo, outa,
    dtok, dproj, h1t, wqkv, dh1,
    *refs,
):
    pc = Place()
    nd, nc = pc.nd, pc.nc
    _, _, tok, w = dtok_ref.shape
    width = nc * w
    reds, refs = [refs[5 * i : 5 * i + 5] for i in range(5)], refs[25:]
    sums, refs = refs[:5], refs[5:]
    bufs, refs = [refs[3 * i : 3 * i + 3] for i in range(6)], refs[18:]
    gmine, gtotal, gctx, gdp, ssend, srecv, rsend, rrecv, isend, irecv, csend, crecv = refs[:12]
    gsend, grecv, local, outsem = refs[12:]
    third = lambda g: pl.ds(pl.multiple_of(g * width, width), width)
    h1_mine, h1_hers = half_rows(pc, h1t_ref, pc.k), half_rows(pc, h1t_ref, 1 - pc.k)
    pairs = [(dtok_ref, dtok), (gout_ref, reds[0][0])]
    pairs += [(h1_mine[s], h1t.at[0, s]) for s in range(nd)]
    pairs += [(gattn_ref, reds[4][0]), (wqkv_ref, wqkv)]
    load = [pltpu.make_async_copy(a, b, local.at[i]) for i, (a, b) in enumerate(pairs)]
    for cp in load:
        cp.start()
    barrier(pc)
    pairs = [(h1_hers[s], h1t.at[1, s]) for s in range(nd)]
    pairs += [(dproj.at[0, :, third(g)], dproj.at[1, :, third(g)]) for g in range(3)]
    swap = [
        remote(src, dst, ssend.at[i], srecv.at[i], pc.sibling) for i, (src, dst) in enumerate(pairs)
    ]
    ro, *rq, ra = [
        Reduce(pc, bs[0], bs[1:], rsend.at[i], rrecv.at[i], i > 0) for i, bs in enumerate(reds)
    ]
    to, *tq, ta = sums
    ci = Chain(pc, t_ref, bufs[0], isend, irecv, True, 2 * PARTS)
    co, *cq, ca = [
        Chain(pc, t, bs, csend.at[i], crecv.at[i], i > 0, PARTS)
        for i, (t, bs) in enumerate(zip(sums, bufs[1:]))
    ]
    for cp in swap[:nd]:
        cp.start()
    each(ci.n, ci.open)
    load[1].wait()
    ro.start()
    load[0].wait()
    for g in range(3):
        for i in range(nc):
            dproj[0, :, g * width + i * w : g * width + (i + 1) * w] = dtok[i, g]
        swap[nd + g].start()
    for cp in load[2:]:
        cp.wait()
    for cp in swap[: nd + 1]:
        cp.wait_recv()
    weight_grad(pc, reds[1][0], h1t, dproj.at[:, :, third(0)])
    rq[0].start()
    ci.up(0)
    for g in (1, 2):
        swap[nd + g].wait_recv()
        weight_grad(pc, reds[1 + g][0], h1t, dproj.at[:, :, third(g)])
    dh1[...] = jnp.zeros_like(dh1)

    def back(g, _):
        dh1[...] += lax.dot_general(
            dproj[0, :, third(g)], wqkv[g].reshape(width, width), (((1,), (1,)), ((), ())),
            preferred_element_type=F32,
        )
        ci.both(1 + g)
        return 0

    lax.fori_loop(0, 3, back, 0)
    ci.turn_out(0)
    ro.middle()
    rq[1].start()
    gain = jnp.concatenate([gain_ref[s, 0:1, :] for s in range(nd)], axis=1)
    gtotal[...] = jnp.zeros_like(gtotal)
    chunk = 32

    def norm_back(i, _):
        at = pl.ds(pl.multiple_of(i * chunk, chunk), chunk)
        xf = x_ref[at, :].astype(F32)
        mean = jnp.mean(xf, axis=-1, keepdims=True)
        cen = xf - mean
        inv = lax.rsqrt(jnp.mean(cen * cen, axis=-1, keepdims=True) + norm_eps)
        hat = cen * inv
        d = dh1[at, :]
        dhat = d * gain
        m1 = jnp.mean(dhat, axis=-1, keepdims=True)
        m2 = jnp.mean(dhat * hat, axis=-1, keepdims=True)
        dx_ref[at, :] = (dres_ref[at, :] + inv * (dhat - m1 - hat * m2)).astype(BF16)
        gtotal[...] += jnp.sum((d * hat).reshape(chunk // 8, 8, width), axis=0)
        return 0

    lax.fori_loop(0, tok // chunk, norm_back, 0)
    row = lax.broadcasted_iota(jnp.int32, (8, 1), 0)
    gmine[...] = jnp.where(row == 0, jnp.sum(gtotal[...], axis=0, keepdims=True), part_ref[...])
    rows = gain_out.shape[1]
    here = lambda d: pl.ds(pl.multiple_of(d * rows, 128), rows)
    dcopies = []
    for t in range(1, nd):
        to_d = (pc.d + t) % nd
        dcopies.append(
            remote(
                gmine.at[:, here(to_d)], gdp.at[t], gsend.at[nc + t], grecv.at[nc + t], (to_d, pc.c)
            )
        )
        dcopies[-1].start()
    ci.both(4)
    ci.turn_out(1)
    rq[0].middle()
    rq[2].start()
    ci.both(5)
    ci.turn_out(2)
    for cp in dcopies:
        cp.wait_recv()
    total = gmine[:, here(pc.d)]
    for t in range(1, nd):
        total = total + gdp[t]
    gdp[0] = total
    gcopies = []
    for t in range(1, nc):
        gcopies.append(
            remote(gdp.at[0], gctx.at[t], gsend.at[t], grecv.at[t], (pc.d, (pc.c + t) % nc))
        )
        gcopies[-1].start()
    ci.both(6)
    ci.turn_out(3)
    ro.finish(to)
    each(PARTS, co.open)
    ci.both(7)
    ci.turn_in(7)
    ci.turn_out(4)
    rq[1].middle()
    ra.start()
    ci.turn_out(5)
    co.up(0)
    rq[0].finish(tq[0])
    each(PARTS, cq[0].open)
    ci.turn_out(6)
    co.both(1)
    ci.turn_out(7)
    outs = [
        pltpu.make_async_copy(c.all, out, outsem.at[i])
        for i, (c, out) in enumerate(
            [(ci, outi), (co, outo)]
            + [(cq[g], outq.at[:, :, third(g)]) for g in range(3)]
            + [(ca, outa)]
        )
    ]
    for cp in gcopies:
        cp.wait_recv()
    total = gdp[0]
    for t in range(1, nc):
        total = total + gctx[t]
    gain_out[...] = total
    rq[2].middle()
    co.both(2)
    co.turn_out(0)
    rq[1].finish(tq[1])
    each(PARTS, cq[1].open)
    co.both(3)
    cq[0].up(0)
    co.turn_in(3)
    co.turn_out(1)
    ra.middle()
    each(PARTS - 1, lambda p: cq[0].both(p + 1))
    co.turn_out(2)
    rq[2].finish(tq[2])
    each(PARTS, cq[2].open)
    co.turn_out(3)
    cq[1].up(0)
    cq[0].turn_in(3)
    ra.finish(ta)
    each(PARTS, ca.open)
    each(PARTS - 1, lambda p: cq[1].both(p + 1), cq[0].turn_out)
    cq[2].up(0)
    cq[1].turn_in(3)
    cq[0].turn_out(3)
    each(PARTS - 1, lambda p: cq[2].both(p + 1), cq[1].turn_out)
    ca.up(0)
    cq[2].turn_in(3)
    cq[1].turn_out(3)
    each(PARTS - 1, lambda p: ca.both(p + 1), cq[2].turn_out)
    ca.turn_in(3)
    cq[2].turn_out(3)
    each(ci.n, ci.side_wait)
    outs[0].start()
    each(PARTS, co.side_wait)
    outs[1].start()
    each(PARTS, ca.turn_out)
    for i, c in enumerate(cq + [ca]):
        each(PARTS, c.side_wait)
        outs[2 + i].start()
    for cp in swap + dcopies + gcopies:
        cp.wait_send()
    for r in [ro] + rq + [ra]:
        r.sent()
    for c in [ci, co] + cq + [ca]:
        each(c.n, c.sent)
    for cp in outs:
        cp.wait()


def close(dtok, h1t, wqkv, x, gains, dres, part, gout, gattn, totals):
    nd, nc = lax.axis_size("dp"), lax.axis_size("ctx")
    tok, width = x.shape
    rows = width // nd
    hr = rows // 2
    nq, ns = Reduce.count(nd), nd + 3
    dma = pltpu.SemaphoreType.DMA
    mine = [gout.shape[2:]] + [(hr, width)] * 4
    sizes = [totals.shape] + mine
    vm = lambda *shape: pltpu.VMEM(shape, BF16)
    chain_bufs = [b for size in sizes for b in (vm(*size), vm(*size), vm(2, *size))]
    reduce_bufs = [b for i, size in enumerate(mine) for b in Reduce.scratch(nd, *size, i > 0)]
    return pl.pallas_call(
        close_kernel,
        out_shape=[S((tok, width), BF16), S((8, rows), F32)]
        + [S((2,) + size, BF16) for size in (sizes[0], (hr, 3 * width), mine[0], mine[4])],
        in_specs=[ANY, ANY, ANY, VMEM, VMEM, VMEM, VMEM, ANY, ANY, VMEM],
        out_specs=[VMEM] * 2 + [ANY] * 4,
        scratch_shapes=[
            vm(*dtok.shape), vm(2, tok, 3 * width), vm(2, nd, hr, tok), vm(*wqkv.shape),
            pltpu.VMEM((tok, width), F32),
            *reduce_bufs, *[vm(*size) for size in mine], *chain_bufs,
            pltpu.VMEM((8, width), F32), pltpu.VMEM((8, width), F32),
            pltpu.VMEM((nc, 8, rows), F32), pltpu.VMEM((nd, 8, rows), F32),
            dma((ns,)), dma((ns,)), dma((5, nq)), dma((5, nq)),
            dma((4, 2 * PARTS)), dma((4, 2 * PARTS)), dma((5, 4, PARTS)), dma((5, 4, PARTS)),
            dma((nc + nd,)), dma((nc + nd,)), dma((4 + nd,)), dma((6,)),
        ],
        compiler_params=params(3),
        name="close",
    )(dtok, h1t, wqkv, x, gains, dres, part, gout, gattn, totals)


def norm_rows(values, gain):
    row_mean = jnp.mean(values, axis=-1, keepdims=True)
    centred = values - row_mean
    row_var = jnp.mean(centred * centred, axis=-1, keepdims=True)
    return centred * lax.rsqrt(row_var + norm_eps) * gain


def gelu_exact(values):
    return 0.5 * values * (1.0 + lax.erf(values * 0.7071067811865476))


def gelu_slope(values):
    return (
        0.5 * (1.0 + lax.erf(values * 0.7071067811865476))
        + values * jnp.exp(-0.5 * values * values) * 0.3989422804014327
    )


def rope_angles(positions, lanes):
    half = HEAD // 2
    freq = rope_theta ** (-(jnp.arange(half, dtype=F32) * 2.0 / HEAD))
    freq = jnp.tile(freq, lanes // half)
    return positions.astype(F32)[:, None] * freq[None, :]


def on_device(
    tokens,
    norm1_gain,
    qkv_weight,
    attn_out_weight,
    norm2_gain,
    mlp_in_weight,
    mlp_out_weight,
    cotangent,
):
    _, tok, width = tokens.shape
    nc, nd = lax.axis_size("ctx"), lax.axis_size("dp")
    keys = tok * nc
    w = width // nc
    ff = mlp_in_weight.shape[1] // 2
    rows = norm1_gain.shape[0]
    x = tokens.reshape(tok, width)
    upstream = cotangent.reshape(tok, width)
    gains = jnp.concatenate(
        [
            norm1_gain.astype(F32)[None],
            norm2_gain.astype(F32)[None],
            jnp.zeros((6, rows), F32),
        ]
    )
    ang = rope_angles(lax.axis_index("ctx") * tok + jnp.arange(tok, dtype=jnp.int32), 2 * w)
    sign = jnp.where(jnp.arange(2 * w) % HEAD < HEAD // 2, -1.0, 1.0).astype(F32)
    h1t, gains_all, w1s, w2s, wqkv, wattn, heads, w1_early = project(
        x, gains, jnp.cos(ang), jnp.sin(ang) * sign[None], qkv_weight, attn_out_weight,
        mlp_in_weight,
    )
    otok, o_heads, lse, w1, w2, wout = attend(
        heads, w1s, w2s, mlp_out_weight, w1_early
    )
    wattn = wattn.reshape(width, width)
    w1 = w1.reshape(width, ff)
    w2 = w2.reshape(width, ff)
    wout = wout.reshape(ff, width)
    gain_one = gains_all[:, 0].reshape(width)
    gain_two = gains_all[:, 1].reshape(width)

    attended_b = jnp.transpose(otok, (1, 0, 2)).reshape(tok, width)
    inputs_f = x.astype(F32)
    attn_res = inputs_f + jnp.dot(attended_b, wattn, preferred_element_type=F32)
    normed_two = norm_rows(attn_res, gain_two).astype(BF16)
    gelu_in = jnp.dot(normed_two, w1, preferred_element_type=F32)
    gate_in = jnp.dot(normed_two, w2, preferred_element_type=F32)
    activated = (gelu_exact(gelu_in) * gate_in).astype(BF16)
    layer_out = (attn_res + jnp.dot(activated, wout, preferred_element_type=F32)).astype(BF16)
    grad_act = jnp.dot(upstream, wout.T, preferred_element_type=F32)
    dl1 = (grad_act * gate_in * gelu_slope(gelu_in)).astype(BF16)
    dl2 = (grad_act * gelu_exact(gelu_in)).astype(BF16)
    dl1, dl2 = lax.optimization_barrier((dl1, dl2))
    grad_normed_two = jnp.dot(dl1, w1.T, preferred_element_type=F32) + jnp.dot(
        dl2, w2.T, preferred_element_type=F32
    )
    _, pull_two = jax.vjp(norm_rows, attn_res, gain_two)
    grad_res_norm, grad_gain_two = pull_two(grad_normed_two)
    grad_res = upstream.astype(F32) + grad_res_norm
    grad_res_b = grad_res.astype(BF16)
    dout = jnp.dot(grad_res_b, wattn.T, preferred_element_type=F32).astype(BF16)
    dout = jnp.transpose(dout.reshape(tok, nc, w), (1, 0, 2))

    near = rope_angles(jnp.arange(tok, dtype=jnp.int32), w)
    far = rope_angles(jnp.arange(nc, dtype=jnp.int32) * tok, w)[:, None]
    near, far = [jnp.stack([jnp.cos(ang), jnp.sin(ang)]) for ang in (near, far)]
    dtok, totals, gout, gattn = attend_back(
        heads, o_heads, lse, dout, near, far, normed_two.T, dl1.T, dl2.T,
        activated.T, upstream, attended_b.T, grad_res_b,
    )
    input_grad, gain_grads, gin, gqkv, gout, gattn = close(
        dtok, h1t, wqkv, x, gains_all, grad_res, grad_gain_two.reshape(1, width), gout, gattn, totals
    )
    gin = gin.reshape(2, 2, rows // 2, ff)
    grad_in = jnp.concatenate([gin[:, i].reshape(rows, ff) for i in range(2)], axis=1)
    return (
        layer_out.reshape(1, tok, width),
        input_grad.reshape(1, tok, width),
        gain_grads[0],
        gqkv.reshape(rows, 3 * width).astype(F32),
        gattn.reshape(rows, width).astype(F32),
        gain_grads[1],
        grad_in.astype(F32),
        jnp.concatenate([gout[0], gout[1]], axis=1).astype(F32),
    )


def solution(mesh):
    in_specs = (
        P("dp", "ctx", None),
        P("dp"),
        P("dp", None),
        P("dp", None),
        P("dp"),
        P("dp", None),
        P("dp", None),
        P("dp", "ctx", None),
    )
    out_specs = (
        P("dp", "ctx", None),
        P("dp", "ctx", None),
        P("dp"),
        P("dp", None),
        P("dp", None),
        P("dp"),
        P("dp", None),
        P("dp", None),
    )
    return jax.shard_map(
        on_device, mesh=mesh, in_specs=in_specs, out_specs=out_specs, check_vma=False
    )
```

```python
import functools

import jax
import jax.numpy as jnp
from jax import lax
from jax.experimental import pallas as pl
from jax.experimental.pallas import tpu as pltpu
from jax.sharding import PartitionSpec as P

HEAD = 64
norm_eps = 1e-05
rope_theta = 160000.0
F32 = jnp.float32
BF16 = jnp.bfloat16
MESH = pl.DeviceIdType.MESH
LOG2E = 1.4426950408889634
VMEM_LIMIT = 64 * 1024 * 1024 - 65536
ANY = pl.BlockSpec(memory_space=pl.ANY)
VMEM = pl.BlockSpec(memory_space=pltpu.VMEM)
S = jax.ShapeDtypeStruct


def params(cid):
    return pltpu.CompilerParams(
        collective_id=cid, has_side_effects=True, vmem_limit_bytes=VMEM_LIMIT
    )


class Place:
    def __init__(self):
        self.nd = lax.axis_size("dp")
        self.nc = lax.axis_size("ctx")
        self.d = lax.axis_index("dp")
        self.c = lax.axis_index("ctx")
        self.nb = 2 if self.nd % 2 == 0 else 1
        self.na = self.nd // self.nb
        self.a = self.d // self.nb
        self.b = self.d % self.nb
        self.nz = self.nc // 2
        self.z = self.c // 2
        self.k = self.c % 2
        self.sibling = (self.d, self.z * 2 + 1 - self.k)

    def shard(self, da, db):
        return ((self.a + da) % self.na) * self.nb + (self.b + db) % self.nb

    def at(self, da, db):
        return (self.shard(da, db), self.c)


def barrier(pc, dp=True, ctx=True):
    sem = pltpu.get_barrier_semaphore()
    count = 0
    if dp:
        for t in range(1, pc.nd):
            pl.semaphore_signal(
                sem, inc=1, device_id=((pc.d + t) % pc.nd, pc.c), device_id_type=MESH
            )
            count += 1
    if ctx:
        for t in range(1, pc.nc):
            pl.semaphore_signal(
                sem, inc=1, device_id=(pc.d, (pc.c + t) % pc.nc), device_id_type=MESH
            )
            count += 1
    pl.semaphore_wait(sem, count)


def remote(src, dst, send, recv, target):
    return pltpu.make_async_remote_copy(
        src_ref=src,
        dst_ref=dst,
        send_sem=send,
        recv_sem=recv,
        device_id=target,
        device_id_type=MESH,
    )


class Gather:
    def __init__(self, pc, cut, own, send, recv, deep=None):
        self.pc, self.cut, self.own, self.send, self.recv, self.deep = pc, cut, own, send, recv, deep
        self.lines = [(da, 0) for da in range(1, pc.na)] + [(0, db) for db in range(1, pc.nb)]
        self.cross_at = [
            (da, db, part)
            for part in (0, 1)
            for da in range(1, pc.na)
            for db in range(1, pc.nb)
        ]
        self.n = len(self.lines) + len(self.cross_at)
        self.pair = (pc.d, (pc.z + 1 - 2 * (pc.z % 2)) * 2 + pc.k)

    @staticmethod
    def count(nd):
        nb = 2 if nd % 2 == 0 else 1
        na = nd // nb
        return 2 * ((na - 1) + (nb - 1) + 2 * (na - 1) * (nb - 1)) + 2 * nd

    def _copy(self, index, shard, part, target, own=False):
        src = (self.own if own else self.cut)(shard, self.pc.k, part)
        dst = self.cut(shard, self.pc.k, part)
        return remote(src, dst, self.send.at[index], self.recv.at[index], target)

    def _arrived(self, index, shard, core, part):
        ref = self.cut(shard, core, part)
        return remote(ref, ref, self.send.at[index], self.recv.at[index], self.pc.sibling)

    def _deep(self, index, shard, core, mine, target):
        ref = self.deep(shard, core, mine)
        return remote(ref, ref, self.send.at[index], self.recv.at[index], target)

    def others(self):
        pc = self.pc
        return [(da, db) for da in range(pc.na) for db in range(pc.nb) if (da, db) != (0, 0)]

    def first(self):
        pc = self.pc
        for i, (da, db) in enumerate(self.lines):
            self._copy(i, pc.d, None, pc.at(-da, -db), own=True).start()

    def _down(self, da, db):
        if self.deep is not None:
            i = self.others().index((da, db))
            self._deep(2 * self.n + i, self.pc.shard(da, db), self.pc.k, True, self.pair).start()

    def relay(self):
        pc, nl = self.pc, len(self.lines)
        for i, (da, db) in enumerate(self.lines):
            shard = pc.shard(da, db)
            self._arrived(i, shard, pc.k, None).wait_recv()
            for j, (xa, xb, part) in enumerate(self.cross_at):
                if part == 0 and db == 0 and xa == da:
                    self._copy(nl + j, shard, part, pc.at(0, -xb)).start()
                if part == 1 and da == 0 and xb == db:
                    self._copy(nl + j, shard, part, pc.at(-xa, 0)).start()
            self._down(da, db)
            self._copy(self.n + i, shard, None, pc.sibling).start()

    def cross(self):
        pc, nl = self.pc, len(self.lines)
        for j, (xa, xb, part) in enumerate(self.cross_at):
            shard = pc.shard(xa, xb)
            self._arrived(nl + j, shard, pc.k, part).wait_recv()
            self._copy(self.n + nl + j, shard, part, pc.sibling).start()
            if part == 1:
                self._down(xa, xb)

    def across(self):
        pc = self.pc
        for i, (da, db) in enumerate(self.others()):
            shard = pc.shard(da, db)
            self._deep(2 * self.n + i, shard, pc.k, False, pc.sibling).wait_recv()
            self._deep(2 * self.n + pc.nd + i, shard, pc.k, False, pc.sibling).start()

    def finish(self):
        pc, nl = self.pc, len(self.lines)
        for i, (da, db) in enumerate(self.lines):
            self._arrived(self.n + i, pc.shard(da, db), 1 - pc.k, None).wait_recv()
        for j, (xa, xb, part) in enumerate(self.cross_at):
            self._arrived(self.n + nl + j, pc.shard(xa, xb), 1 - pc.k, part).wait_recv()
        if self.deep is not None:
            for i, (da, db) in enumerate(self.others()):
                shard = pc.shard(da, db)
                self._deep(2 * self.n + pc.nd + i, shard, 1 - pc.k, False, pc.sibling).wait_recv()

    def sent(self):
        pc, nl = self.pc, len(self.lines)
        for i, _ in enumerate(self.lines):
            self._arrived(i, pc.d, pc.k, None).wait_send()
            self._arrived(self.n + i, pc.d, pc.k, None).wait_send()
        for j, (_, _, part) in enumerate(self.cross_at):
            self._arrived(nl + j, pc.d, pc.k, part).wait_send()
            self._arrived(self.n + nl + j, pc.d, pc.k, part).wait_send()
        if self.deep is not None:
            for i, _ in enumerate(self.others()):
                self._deep(2 * self.n + i, pc.d, pc.k, True, pc.sibling).wait_send()
                self._deep(2 * self.n + pc.nd + i, pc.d, pc.k, False, pc.sibling).wait_send()


def row_cut(ref, rows, core, part, lead=0):
    start = core * (rows // 2) + (0 if part is None else part * (rows // 4))
    size = rows // 2 if part is None else rows // 4
    return ref.at[(slice(None),) * lead + (pl.ds(start, size),)]


def share_rows(pc, rows):
    q = rows // 8
    odd = pc.z % 2

    def cut(ref, core, part):
        start = core * (4 * q) + odd * q
        if part is None:
            return ref.at[pl.ds(start, 3 * q)]
        n = 3 * q // 2
        return ref.at[pl.ds(start + part * n, n)]

    def deep(ref, core, mine):
        at = odd * (3 * q) if mine else (1 - odd) * (3 * q)
        return ref.at[pl.ds(core * (4 * q) + at, q)]

    return cut, deep


def share_cols(pc, rows, cols):
    q = cols // 8
    odd = pc.z % 2
    n = rows // 2 // 16 * 16

    def cut(ref, core, part):
        start = pl.multiple_of(core * (4 * q) + odd * q, 128)
        at = slice(None) if part is None else pl.ds(0, n) if part == 0 else pl.ds(n, rows - n)
        return ref.at[at, pl.ds(start, 3 * q)]

    def deep(ref, core, mine):
        at = odd * (3 * q) if mine else (1 - odd) * (3 * q)
        return ref.at[:, pl.ds(pl.multiple_of(core * (4 * q) + at, 128), q)]

    return cut, deep


def early_rows(rows):
    return rows // 2 if rows % 256 == 0 else 0


class Reduce:
    def __init__(self, pc, g, bufs, send, recv, by_rows):
        self.pc, self.g, self.send, self.recv, self.by_rows = pc, g, send, recv, by_rows
        self.r1a, self.r1b, self.r2a, self.r2b = bufs

    @staticmethod
    def count(nd):
        nb = 2 if nd % 2 == 0 else 1
        return 2 * (nd // nb - 1 + nb - 1)

    @staticmethod
    def scratch(nd, rows, cols, by_rows):
        nb = 2 if nd % 2 == 0 else 1
        na = nd // nb
        r, c = (rows // 2, cols) if by_rows else (rows, cols // 2)
        return [
            pltpu.VMEM((na, nb, rows, cols), BF16),
            pltpu.VMEM((na - 1, nb, r, c), BF16),
            pltpu.VMEM((nb - 1, na, r, c), BF16),
            pltpu.VMEM((nb - 1, r, c), BF16),
            pltpu.VMEM((na - 1, r, c), BF16),
        ]

    def part(self, ref, p):
        lead = (slice(None),) * (len(ref.shape) - 2)
        rows, cols = ref.shape[-2:]
        if self.by_rows:
            return ref.at[lead + (pl.ds(p * (rows // 2), rows // 2),)]
        return ref.at[lead + (slice(None), pl.ds(p * (cols // 2), cols // 2))]

    def copies(self, step):
        pc = self.pc
        na, nb = pc.na, pc.nb
        out = []
        base = 0 if step == 1 else na - 1 + nb - 1
        for da in range(1, na):
            a = (pc.a + na - da) % na
            i = base + da - 1
            if step == 1:
                src, dst = self.part(self.g.at[a], 0), self.r1a.at[da - 1]
            else:
                src, dst = self.part(self.g.at[a, pc.b], 1), self.r2b.at[da - 1]
            out.append(remote(src, dst, self.send.at[i], self.recv.at[i], pc.at(-da, 0)))
        for db in range(1, nb):
            b = (pc.b + nb - db) % nb
            i = base + na - 1 + db - 1
            if step == 1:
                src, dst = self.part(self.g.at[:, b], 1), self.r1b.at[db - 1]
            else:
                src, dst = self.part(self.g.at[pc.a, b], 0), self.r2a.at[db - 1]
            out.append(remote(src, dst, self.send.at[i], self.recv.at[i], pc.at(0, -db)))
        return out

    def start(self):
        for cp in self.copies(1):
            cp.start()

    def middle(self):
        pc = self.pc
        for cp in self.copies(1):
            cp.wait_recv()
        for b in range(pc.nb):
            at = self.part(self.g.at[pc.a, b], 0)
            add(at, [self.r1a.at[i, b] for i in range(pc.na - 1)])
        for a in range(pc.na):
            at = self.part(self.g.at[a, pc.b], 1)
            add(at, [self.r1b.at[i, a] for i in range(pc.nb - 1)])
        for cp in self.copies(2):
            cp.start()

    def finish(self, total):
        pc = self.pc
        for cp in self.copies(2):
            cp.wait_recv()
        own = self.g.at[pc.a, pc.b]
        add(self.part(own, 0), [self.r2a.at[i] for i in range(pc.nb - 1)], self.part(total, 0))
        add(self.part(own, 1), [self.r2b.at[i] for i in range(pc.na - 1)], self.part(total, 1))

    def sent(self):
        for cp in self.copies(1) + self.copies(2):
            cp.wait_send()


def add(ref, others, into=None):
    into = ref if into is None else into
    rows = ref.shape[0]
    chunk = next(n for n in (32, 16, rows) if rows % n == 0)

    def some(i, _):
        at = pl.ds(pl.multiple_of(i * chunk, chunk), chunk)
        total = ref[at, :].astype(F32)
        for o in others:
            total = total + o[at, :].astype(F32)
        into[at, :] = total.astype(BF16)
        return 0

    if rows == chunk:
        total = ref[...].astype(F32)
        for o in others:
            total = total + o[...].astype(F32)
        into[...] = total.astype(BF16)
    else:
        lax.fori_loop(0, rows // chunk, some, 0)


PARTS = 4


def chain_part(by_rows, parts):
    def part(ref, p):
        rows, cols = ref.shape[-2:]
        if by_rows:
            n = rows // parts
            return ref.at[pl.ds(pl.multiple_of(p * n, n), n)]
        n = cols // parts
        return ref.at[:, pl.ds(pl.multiple_of(p * n, n), n)]

    return part


class Chain:
    def __init__(self, pc, t, bufs, send, recv, by_rows, parts):
        self.pc, self.t, self.n = pc, t, parts
        self.part = chain_part(by_rows, parts)
        self.outer, self.swap, total = bufs
        self.total, self.other = total.at[pc.k], total.at[1 - pc.k]
        self.all = total
        self.send, self.recv = send, recv
        half = pc.nz // 2
        self.low = pc.z < half
        self.end = (pc.z == 0) | (pc.z == pc.nz - 1)
        self.mid = (pc.z == half - 1) | (pc.z == half)
        step = 1 - 2 * (pc.z // half)
        self.inner_id = (pc.d, ((pc.z + step + pc.nz) % pc.nz) * 2 + pc.k)
        self.outer_id = (pc.d, ((pc.z - step + pc.nz) % pc.nz) * 2 + pc.k)

    def up_copy(self, p):
        return remote(
            self.part(self.t, p), self.part(self.outer, p), self.send.at[0, p], self.recv.at[0, p],
            self.inner_id,
        )

    def swap_copy(self, p):
        return remote(
            self.part(self.t, p), self.part(self.swap, p), self.send.at[1, p], self.recv.at[1, p],
            self.inner_id,
        )

    def down_copy(self, p):
        at = self.part(self.total, p)
        return remote(at, at, self.send.at[2, p], self.recv.at[2, p], self.outer_id)

    def side_copy(self, p):
        at = self.part(self.total, p)
        return remote(at, at, self.send.at[3, p], self.recv.at[3, p], self.pc.sibling)

    def side_wait(self, p):
        at = self.part(self.other, p)
        remote(at, at, self.send.at[3, p], self.recv.at[3, p], self.pc.sibling).wait_recv()

    def open(self, p):
        @pl.when(self.end)
        def _():
            @pl.when(self.mid)
            def _():
                self.swap_copy(p).start()

            @pl.when(jnp.logical_not(self.mid))
            def _():
                self.up_copy(p).start()

    def up(self, p):
        @pl.when(jnp.logical_not(self.end))
        def _():
            self.up_copy(p).wait_recv()
            add(self.part(self.t, p), [self.part(self.outer, p)])

            @pl.when(self.mid)
            def _():
                self.swap_copy(p).start()

            @pl.when(jnp.logical_not(self.mid))
            def _():
                self.up_copy(p).start()

    def turn_in(self, p):
        @pl.when(self.mid)
        def _():
            self.swap_copy(p).wait_recv()
            add(self.part(self.t, p), [self.part(self.swap, p)], self.part(self.total, p))

            @pl.when(jnp.logical_not(self.end))
            def _():
                self.down_copy(p).start()

            self.side_copy(p).start()

    def turn_out(self, p):
        @pl.when(jnp.logical_not(self.mid))
        def _():
            self.down_copy(p).wait_recv()

            @pl.when(jnp.logical_not(self.end))
            def _():
                self.down_copy(p).start()

            self.side_copy(p).start()

    def both(self, p):
        self.up(p)
        self.turn_in(p - 1)

    def sent(self, p):
        @pl.when(self.mid)
        def _():
            self.swap_copy(p).wait_send()

        @pl.when(jnp.logical_not(self.mid))
        def _():
            self.up_copy(p).wait_send()

        @pl.when(jnp.logical_not(self.end))
        def _():
            self.down_copy(p).wait_send()

        self.side_copy(p).wait_send()


def head_cols(ref, c, w):
    if len(ref.shape) == 3:
        return ref.at[c]
    return ref.at[:, pl.ds(pl.multiple_of(c * w, w), w)]


def half_rows(pc, ref, core):
    rows = ref.shape[0] // pc.nd
    h = rows // 2
    return [ref.at[pl.ds(pl.multiple_of(s * rows + core * h, h), h)] for s in range(pc.nd)]


def project_kernel(
    x_ref, gains_ref, cos_ref, sin_ref, wqkv_ref, wattn_ref, win_ref,
    h1t_ref, gains_out, w1_out, w2_out, wqkv_out, wattn_out, heads_out, w1_all,
    wbuf, abuf, ibuf, h1_ref, gbuf, sendbuf,
    wsend, wrecv, asend, arecv, esend, erecv, gsend, grecv, xsend, xrecv, local,
):
    pc = Place()
    nd, nc, nz = pc.nd, pc.nc, pc.nz
    rows = wqkv_ref.shape[0]
    width = wqkv_ref.shape[1] // 3
    tok = x_ref.shape[0]
    w = width // nc
    cw = 2 * w
    own_w = [
        pltpu.make_async_copy(
            wqkv_ref.at[:, pl.ds(g * width, width)], wbuf.at[g, pc.d], local.at[g]
        )
        for g in range(3)
    ]
    for cp in own_w:
        cp.start()
    own_a = pltpu.make_async_copy(wattn_ref, abuf, local.at[3])
    own_a.start()
    own_i = pltpu.make_async_copy(win_ref, ibuf, local.at[5 + nz])
    own_i.start()
    barrier(pc)
    for cp in own_w:
        cp.wait()

    def chip_of(j):
        return (pc.z + j + 1) % nz

    def chunk(j):
        col = pl.multiple_of(chip_of(j) * cw, cw)

        def cut(shard, core, part):
            return row_cut(wbuf.at[:, shard, :, pl.ds(col, cw)], rows, core, part, lead=1)

        return Gather(pc, cut, cut, wsend.at[j], wrecv.at[j])

    def attn_cut(shard, core, part):
        return row_cut(wattn_out.at[shard], rows, core, part)

    def attn_own(shard, core, part):
        return row_cut(wattn_ref, rows, core, part)

    attn = Gather(pc, attn_cut, attn_own, asend, arecv)

    def early_cut(shard, core, part):
        return row_cut(w1_all.at[shard], e, core, part)

    def early_own(shard, core, part):
        return row_cut(w1_out, e, core, part)

    early = Gather(pc, early_cut, early_own, esend, erecv)
    e = early_rows(rows)
    extra = [attn] + [early] * (e > 0)

    gain_copies = []
    gbuf[pc.d] = gains_ref[...]
    for t in range(1, nd):
        gain_copies.append(
            remote(
                gains_ref, gbuf.at[pc.d], gsend.at[t], grecv.at[t], ((pc.d + t) % nd, pc.c)
            )
        )
        gain_copies[-1].start()
    for j in range(min(2, nz)):
        chunk(j).first()

    xf = x_ref[...].astype(F32)
    mean = jnp.mean(xf, axis=-1, keepdims=True)
    cen = xf - mean
    var = jnp.mean(cen * cen, axis=-1, keepdims=True)
    hat = cen * lax.rsqrt(var + norm_eps)
    for t in range(1, nd):
        src = gbuf.at[(pc.d + nd - t) % nd]
        remote(src, src, gsend.at[t], grecv.at[t], pc.sibling).wait_recv()
    for s in range(nd):
        cols = slice(s * rows, (s + 1) * rows)
        h1_ref[:, cols] = (hat[:, cols] * gbuf[s, 0:1, :]).astype(BF16)
    gains_out[...] = gbuf[...]
    own_a.wait()
    own_a2 = pltpu.make_async_copy(abuf, wattn_out.at[pc.d], local.at[3])
    own_a2.start()
    own_i.wait()
    ff = w1_out.shape[1]
    w1_out[...] = ibuf[:, :ff]
    w2_out[...] = ibuf[:, ff:]
    h1t_ref[...] = jnp.transpose(h1_ref[...])

    lane = lax.broadcasted_iota(jnp.int32, (1, cw), 1)
    low = (lane % HEAD) < HEAD // 2

    def out_copy(j):
        cols = pl.ds(pl.multiple_of(chip_of(j) * cw, cw), cw)
        return pltpu.make_async_copy(
            wbuf.at[:, :, :, cols], wqkv_out.at[:, :, :, cols], local.at[4 + j]
        )

    def place(ref):
        return ref.at[:, pl.ds(pl.multiple_of(pc.c * tok, tok), tok), :]

    def exchange(j, kk):
        return remote(
            sendbuf.at[j, kk], place(heads_out), xsend.at[j, kk], xrecv.at[j, pc.k],
            (pc.d, chip_of(j) * 2 + kk),
        )

    def step(j, _):
        g = chunk(j)
        g.relay()

        @pl.when(j + 2 < nz)
        def _():
            chunk(j + 2).first()

        @pl.when(j == max(nz - 2, 0))
        def _():
            attn.first()

        @pl.when(j == nz - 1)
        def _():
            for it in extra[1:]:
                it.first()

        g.cross()
        g.finish()
        out_copy(j).start()
        cols = pl.ds(pl.multiple_of(chip_of(j) * cw, cw), cw)
        for part in range(3):
            weight = wbuf[part, :, :, cols].reshape(nd * rows, cw)
            proj = jnp.dot(h1_ref[...], weight, preferred_element_type=F32)
            if part < 2:
                up = pltpu.roll(proj, cw - HEAD // 2, 1)
                down = pltpu.roll(proj, HEAD // 2, 1)
                proj = proj * cos_ref[...] + jnp.where(low, up, down) * sin_ref[...]
            proj = proj.astype(BF16)
            for kk in range(2):
                sendbuf[j, kk, part] = proj[:, kk * w : (kk + 1) * w]

        @pl.when(j < nz - 1)
        def _():
            exchange(j, 0).start()
            exchange(j, 1).start()

        return 0

    lax.fori_loop(0, nz, step, 0)
    last = nz - 1
    remote(
        sendbuf.at[last, 1 - pc.k], place(heads_out), xsend.at[last, 1 - pc.k],
        xrecv.at[last, pc.k], pc.sibling,
    ).start()
    own_x = pltpu.make_async_copy(
        sendbuf.at[last, pc.k], place(heads_out), local.at[4 + nz]
    )
    own_x.start()
    for it in extra:
        it.relay()
    for it in extra:
        it.cross()
    for it in extra:
        it.finish()

    def arrival(j, kk):
        ref = sendbuf.at[j, kk]
        return remote(ref, ref, xsend.at[j, kk], xrecv.at[j, kk], pc.sibling)

    def drain(j, _):
        arrival(j, 0).wait_recv()
        arrival(j, 1).wait_recv()
        arrival(j, 0).wait_send()
        arrival(j, 1).wait_send()
        chunk(j).sent()
        out_copy(j).wait()
        return 0

    lax.fori_loop(0, nz - 1, drain, 0)
    arrival(last, 1 - pc.k).wait_recv()
    arrival(last, 1 - pc.k).wait_send()
    chunk(last).sent()
    out_copy(last).wait()
    own_x.wait()
    own_a2.wait()
    for it in extra:
        it.sent()
    for cp in gain_copies:
        cp.wait_send()


def project(x, gains, cosine, sine, wqkv, wattn, win):
    nd, nc = lax.axis_size("dp"), lax.axis_size("ctx")
    nz = nc // 2
    tok, width = x.shape
    rows = wqkv.shape[0]
    w = width // nc
    n = Gather.count(nd)
    dma = pltpu.SemaphoreType.DMA
    return pl.pallas_call(
        project_kernel,
        out_shape=[
            S((width, tok), BF16),
            S((nd, 8, rows), F32),
            S((rows, win.shape[1] // 2), BF16),
            S((rows, win.shape[1] // 2), BF16),
            S((3, nd, rows, width), BF16),
            S((nd, rows, width), BF16),
            S((3, nc * tok, w), BF16),
            S((nd, rows, win.shape[1] // 2), BF16),
        ],
        in_specs=[VMEM, VMEM, VMEM, VMEM, ANY, ANY, ANY],
        out_specs=[VMEM, VMEM, VMEM, VMEM, ANY, ANY, ANY, ANY],
        scratch_shapes=[
            pltpu.VMEM((3, nd, rows, width), BF16),
            pltpu.VMEM((rows, width), BF16),
            pltpu.VMEM(win.shape, BF16),
            pltpu.VMEM((tok, width), BF16),
            pltpu.VMEM((nd, 8, rows), F32),
            pltpu.VMEM((nz, 2, 3, tok, w), BF16),
            dma((nz, n)), dma((nz, n)), dma((n,)), dma((n,)), dma((n,)), dma((n,)),
            dma((nd,)), dma((nd,)), dma((nz, 2)), dma((nz, 2)), dma((6 + nz,)),
        ],
        compiler_params=params(0),
        name="project",
    )(x, gains, cosine, sine, wqkv, wattn, win)


def attend_kernel(
    heads_ref, w1_ref, w2_ref, wout_ref, w1_early,
    otok_out, o_ref, lse_ref, w1_out, w2_out, wout_out,
    qkv, vext, bounce1, bounce2, bounce3,
    s1, r1, s2, r2, s3, r3, xsend, xrecv, local,
):
    pc = Place()
    nd, nc = pc.nd, pc.nc
    keys, w = heads_ref.shape[1], heads_ref.shape[2]
    tok = keys // nc
    rows = w1_ref.shape[0]
    load = pltpu.make_async_copy(heads_ref, qkv, local.at[0])
    load.start()
    pairs = [(w1_ref, bounce1, w1_out), (w2_ref, bounce2, w2_out), (wout_ref, bounce3, wout_out)]
    for i, (src, mid, _) in enumerate(pairs):
        pltpu.make_async_copy(src, mid, local.at[1 + i]).start()
    barrier(pc)
    e = early_rows(rows)
    lower = lambda ref: ref.at[pl.ds(e, rows - e)]
    cut_h, deep_h = share_rows(pc, rows - e)
    cut_r, deep_r = share_rows(pc, rows)
    cut_c, deep_c = share_cols(pc, *wout_ref.shape)

    def item(ref, out, cut, deep, send, recv):
        return Gather(
            pc,
            lambda s, k, p: cut(out.at[s], k, p),
            lambda s, k, p: cut(ref, k, p),
            send,
            recv,
            lambda s, k, mine: deep(out.at[s], k, mine),
        )

    items = [
        item(wout_ref, wout_out, cut_c, deep_c, s3, r3),
        item(w2_ref, w2_out, cut_r, deep_r, s2, r2),
        Gather(
            pc,
            lambda s, k, p: cut_h(lower(w1_out.at[s]), k, p),
            lambda s, k, p: cut_h(lower(w1_ref), k, p),
            s1,
            r1,
            lambda s, k, mine: deep_h(lower(w1_out.at[s]), k, mine),
        ),
    ]
    items[0].first()
    items[1].first()
    load.wait()
    for i, (src, mid, _) in enumerate(pairs):
        pltpu.make_async_copy(src, mid, local.at[1 + i]).wait()
    for i, (_, mid, dst) in enumerate(pairs):
        pltpu.make_async_copy(mid, dst.at[pc.d], local.at[1 + i]).start()
    nh = w // HEAD
    for h in range(nh):
        vext[h, :, :HEAD] = qkv[2, :, h * HEAD : (h + 1) * HEAD]
        vext[h, :, HEAD:] = jnp.ones((keys, HEAD), BF16)
    scale = HEAD ** (-0.5) * LOG2E

    def block_copy(i):
        to = (pc.c + i + 1) % nc
        at = pl.ds(pl.multiple_of(to * tok, tok), tok)
        return remote(
            o_ref.at[at], head_cols(otok_out, pc.c, w), xsend.at[i], xrecv.at[i], (pc.d, to)
        )

    def block(i, _):
        at = pl.ds(pl.multiple_of(((pc.c + i + 1) % nc) * tok, tok), tok)
        for h in range(nh):
            hs = slice(h * HEAD, (h + 1) * HEAD)
            s = lax.dot_general(
                qkv[0, at, hs], qkv[1, :, hs], (((1,), (1,)), ((), ())),
                preferred_element_type=F32,
            )
            m = jnp.max(s, axis=1, keepdims=True)
            p = jnp.exp2(s * scale - m * scale).astype(BF16)
            ol = jnp.dot(p, vext[h], preferred_element_type=F32)
            total = ol[:, HEAD:]
            o_ref[at, hs] = (ol[:, :HEAD] / total).astype(BF16)
            lse = m * scale + jnp.log2(total)
            lse_ref[h, :, at] = jnp.transpose(jnp.concatenate([lse, lse], axis=1))[:8]

        @pl.when(i < nc - 1)
        def _():
            block_copy(i).start()

        @pl.when(i == nc // 2)
        def _():
            items[0].relay()
            items[2].first()

        return 0

    lax.fori_loop(0, nc, block, 0)
    own = pltpu.make_async_copy(
        o_ref.at[pl.ds(pl.multiple_of(pc.c * tok, tok), tok)],
        head_cols(otok_out, pc.c, w),
        local.at[0],
    )
    own.start()
    items[1].relay()
    items[0].cross()
    items[2].relay()
    items[1].cross()
    items[0].across()
    items[2].cross()
    items[1].across()
    items[2].across()
    for it in items:
        it.finish()

    def drain(i, _):
        got = head_cols(otok_out, (pc.c + nc - i - 1) % nc, w)
        remote(got, got, xsend.at[i], xrecv.at[i], pc.sibling).wait_recv()
        block_copy(i).wait_send()
        return 0

    lax.fori_loop(0, nc - 1, drain, 0)
    own.wait()
    for i, (_, mid, dst) in enumerate(pairs):
        pltpu.make_async_copy(mid, dst.at[pc.d], local.at[1 + i]).wait()
    for it in items:
        it.sent()


def attend(heads, w1, w2, wout, w1_early):
    nd, nc = lax.axis_size("dp"), lax.axis_size("ctx")
    _, keys, w = heads.shape
    nh = w // HEAD
    n = Gather.count(nd)
    dma = pltpu.SemaphoreType.DMA
    return pl.pallas_call(
        attend_kernel,
        out_shape=[
            S((keys // nc, nc * w) if w % 128 == 0 else (nc, keys // nc, w), BF16),
            S((keys, w), BF16),
            S((nh, 8, keys), F32),
            S((nd,) + w1.shape, BF16),
            S((nd,) + w2.shape, BF16),
            S((nd,) + wout.shape, BF16),
        ],
        in_specs=[ANY] * 5,
        out_specs=[ANY, VMEM, VMEM, ANY, ANY, ANY],
        input_output_aliases={4: 3},
        scratch_shapes=[
            pltpu.VMEM((3, keys, w), BF16),
            pltpu.VMEM((nh, keys, 2 * HEAD), BF16),
            pltpu.VMEM(w1.shape, BF16),
            pltpu.VMEM(w2.shape, BF16),
            pltpu.VMEM(wout.shape, BF16),
            dma((n,)), dma((n,)), dma((n,)), dma((n,)), dma((n,)), dma((n,)),
            dma((nc,)), dma((nc,)), dma((4,)),
        ],
        compiler_params=params(1),
        name="attend",
    )(heads, w1, w2, wout, w1_early)


def attend_back_kernel(
    heads_ref, o_ref, lse_ref, dout_ref, near_ref, far_ref, h2t_ref, dl1_ref, dl2_ref,
    actt_ref, c_ref, ot_ref, dres_ref,
    dtok_out, t_ref, gout_out, gattn_out,
    qkv, dout, delta, dq, sendbuf, h2t, dl, actt, cot, ot, dres, gout, gattn,
    ga, ra0, ra1, ra2, ra3, gb, rb0, rb1, rb2, rb3,
    dsend, drecv, xsend, xrecv, ssend, srecv, asend, arecv, bsend, brecv, local,
):
    pc = Place()
    nd = pc.nd
    nc = pc.nc
    keys, w = heads_ref.shape[1], heads_ref.shape[2]
    tok = keys // nc
    nh = w // HEAD
    load = pltpu.make_async_copy(heads_ref, qkv, local.at[0])
    load.start()
    mine_t = half_rows(pc, h2t_ref, pc.k)
    hers_t = half_rows(pc, h2t_ref, 1 - pc.k)
    fetch = [pltpu.make_async_copy(mine_t[s], h2t.at[0, s], local.at[2 + s]) for s in range(nd)]
    fetch.append(pltpu.make_async_copy(dl1_ref, dl.at[0, 0], local.at[2 + nd]))
    fetch.append(pltpu.make_async_copy(dl2_ref, dl.at[1, 0], local.at[3 + nd]))
    half = cot.shape[2]
    nr = actt.shape[2]
    col = lambda core: pl.ds(pl.multiple_of(core * half, half), half)
    o_mine, o_hers = half_rows(pc, ot_ref, pc.k), half_rows(pc, ot_ref, 1 - pc.k)
    acts = [actt_ref.at[pl.ds(s * nr, nr)] for s in range(nd)]
    more = [(acts[s], actt.at[0, s]) for s in range(nd)] + [(o_mine[s], ot.at[0, s]) for s in range(nd)]
    more += [(c_ref.at[:, col(pc.k)], cot.at[0]), (dres_ref, dres.at[0])]
    first = len(fetch)
    fetch += [pltpu.make_async_copy(a, b, local.at[4 + nd + i]) for i, (a, b) in enumerate(more)]
    for cp in fetch:
        cp.start()
    barrier(pc)
    swap = [
        remote(hers_t[s], h2t.at[1, s], ssend.at[s], srecv.at[s], pc.sibling) for s in range(nd)
    ]
    more = [(acts[s], actt.at[1, s]) for s in range(nd)] + [(o_hers[s], ot.at[1, s]) for s in range(nd)]
    more += [(c_ref.at[:, col(1 - pc.k)], cot.at[1]), (dres_ref, dres.at[1])]
    late = [
        remote(a, b, ssend.at[nd + 2 + i], srecv.at[nd + 2 + i], pc.sibling)
        for i, (a, b) in enumerate(more)
    ]
    swap.append(remote(dl1_ref, dl.at[0, 1], ssend.at[nd], srecv.at[nd], pc.sibling))
    swap.append(remote(dl2_ref, dl.at[1, 1], ssend.at[nd + 1], srecv.at[nd + 1], pc.sibling))
    for cp in swap:
        cp.start()
    mine = pl.ds(pl.multiple_of(pc.c * tok, tok), tok)
    for i in range(nc - 1):
        to = (pc.c + i + 1) % nc
        remote(
            head_cols(dout_ref, to, w), dout.at[mine], dsend.at[i], drecv.at[i], (pc.d, to)
        ).start()
    own = pltpu.make_async_copy(head_cols(dout_ref, pc.c, w), dout.at[mine], local.at[1])
    own.start()
    ra = Reduce(pc, ga, (ra0, ra1, ra2, ra3), asend, arecv, True)
    rb = Reduce(pc, gb, (rb0, rb1, rb2, rb3), bsend, brecv, True)
    for cp in late:
        cp.start()
    for cp in fetch[:first]:
        cp.wait()
    for cp in swap[: nd + 1]:
        cp.wait_recv()
    weight_grad(pc, ga, h2t, dl.at[0], True)
    ra.start()
    swap[nd + 1].wait_recv()
    weight_grad(pc, gb, h2t, dl.at[1], True)
    rb.start()
    for cp in fetch[first:]:
        cp.wait()
    for cp in late:
        cp.wait_recv()
    weight_grad(pc, gout, actt, cot)
    weight_grad(pc, gattn, ot, dres)
    keep_g = [
        pltpu.make_async_copy(gout, gout_out, local.at[2]),
        pltpu.make_async_copy(gattn, gattn_out, local.at[3]),
    ]
    for cp in keep_g:
        cp.start()
    dq[...] = jnp.zeros_like(dq)
    load.wait()
    own.wait()
    for i in range(nc - 1):
        src = (pc.c + nc - i - 1) % nc
        got = dout.at[pl.ds(pl.multiple_of(src * tok, tok), tok)]
        remote(got, got, dsend.at[i], drecv.at[i], pc.sibling).wait_recv()

    def deltas(i, _):
        at = pl.ds(pl.multiple_of(i * tok, tok), tok)
        t = jnp.transpose(o_ref[at, :].astype(F32) * dout[at, :].astype(F32))
        for h in range(nh):
            row = jnp.sum(t[h * HEAD : (h + 1) * HEAD], axis=0, keepdims=True)
            delta[h, :, at] = jnp.broadcast_to(row, (8, tok))
        return 0

    lax.fori_loop(0, nc, deltas, 0)
    scale = HEAD ** (-0.5)
    lane = lax.broadcasted_iota(jnp.int32, (1, w), 1)
    low = (lane % HEAD) < HEAD // 2

    def unrotate(g, to):
        cos_n, sin_n, cos_f, sin_f = near_ref[0], near_ref[1], far_ref[0, to], far_ref[1, to]
        t = g * (sin_f * cos_n + cos_f * sin_n)
        if w == HEAD:
            up = jnp.concatenate([t[:, HEAD // 2 :], t[:, : HEAD // 2]], axis=1)
            down = up
        else:
            up = pltpu.roll(t, w - HEAD // 2, 1)
            down = pltpu.roll(t, HEAD // 2, 1)
        return g * (cos_f * cos_n - sin_f * sin_n) + jnp.where(low, up, -down)

    def kv_copy(i):
        to = (pc.c + i + 1) % nc
        return remote(
            sendbuf.at[to, pl.ds(1, 2)], dtok_out.at[pc.c, pl.ds(1, 2)],
            xsend.at[0, i], xrecv.at[0, i], (pc.d, to),
        )

    def q_copy(i):
        to = (pc.c + i + 1) % nc
        return remote(
            sendbuf.at[to, 0], dtok_out.at[pc.c, 0], xsend.at[1, i], xrecv.at[1, i], (pc.d, to)
        )

    def block(i, _):
        to = (pc.c + i + 1) % nc
        at = pl.ds(pl.multiple_of(to * tok, tok), tok)
        dks, dvs = [], []
        for h in range(nh):
            hs = slice(h * HEAD, (h + 1) * HEAD)
            kb, vb = qkv[1, at, hs], qkv[2, at, hs]
            q, do = qkv[0, :, hs], dout[:, hs]
            nt = (((1,), (1,)), ((), ()))
            st = lax.dot_general(kb, q, nt, preferred_element_type=F32)
            p = jnp.exp2(st * (scale * LOG2E) - lse_ref[h, 0:1, :])
            dvs.append(jnp.dot(p.astype(BF16), do, preferred_element_type=F32))
            dp = lax.dot_general(vb, do, nt, preferred_element_type=F32)
            ds = (p * (dp - delta[h, 0:1, :])).astype(BF16)
            dks.append(jnp.dot(ds, q, preferred_element_type=F32))
            dq[:, hs] += lax.dot_general(
                ds, kb, (((0,), (0,)), ((), ())), preferred_element_type=F32
            )
        dk = jnp.concatenate(dks, axis=1) * scale
        sendbuf[to, 1] = unrotate(dk, to).astype(BF16)
        sendbuf[to, 2] = jnp.concatenate(dvs, axis=1).astype(BF16)

        @pl.when(i < nc - 1)
        def _():
            kv_copy(i).start()

        @pl.when(i == (nc * 3) // 8)
        def _():
            ra.middle()

        @pl.when(i == (nc * 7) // 8)
        def _():
            rb.middle()

        return 0

    lax.fori_loop(0, nc, block, 0)

    def q_block(i, _):
        to = (pc.c + i + 1) % nc
        at = pl.ds(pl.multiple_of(to * tok, tok), tok)
        sendbuf[to, 0] = unrotate(dq[at, :] * scale, to).astype(BF16)

        @pl.when(i < nc - 1)
        def _():
            q_copy(i).start()

        return 0

    lax.fori_loop(0, nc, q_block, 0)
    keep = pltpu.make_async_copy(sendbuf.at[pc.c], dtok_out.at[pc.c], local.at[1])
    keep.start()
    hr = ga.shape[2]
    ra.finish(t_ref.at[pl.ds(0, hr)])
    rb.finish(t_ref.at[pl.ds(hr, hr)])

    def drain(i, _):
        got = dtok_out.at[(pc.c + nc - i - 1) % nc]
        remote(
            got.at[pl.ds(1, 2)], got.at[pl.ds(1, 2)], xsend.at[0, i], xrecv.at[0, i], pc.sibling
        ).wait_recv()
        remote(got.at[0], got.at[0], xsend.at[1, i], xrecv.at[1, i], pc.sibling).wait_recv()
        kv_copy(i).wait_send()
        q_copy(i).wait_send()
        to = (pc.c + i + 1) % nc
        remote(
            head_cols(dout_ref, to, w), dout.at[mine], dsend.at[i], drecv.at[i], (pc.d, to)
        ).wait_send()
        return 0

    lax.fori_loop(0, nc - 1, drain, 0)
    keep.wait()
    for cp in keep_g:
        cp.wait()
    for cp in swap + late:
        cp.wait_send()
    ra.sent()
    rb.sent()


def weight_grad(pc, g, lhs, rhs, flipped=False):
    dims = (((1,), (1 if flipped else 0,)), ((), ()))

    def shard(s, _):
        total = lax.dot_general(lhs[0, s], rhs[0], dims, preferred_element_type=F32)
        total = total + lax.dot_general(lhs[1, s], rhs[1], dims, preferred_element_type=F32)
        g[s // pc.nb, s % pc.nb] = total.astype(BF16)
        return 0

    lax.fori_loop(0, pc.nd, shard, 0)


def attend_back(heads, o, lse, dout, near, far, h2t, dl1, dl2, actt, cot, ot, dres):
    nc, nd = lax.axis_size("ctx"), lax.axis_size("dp")
    ff = dl1.shape[0]
    hr = h2t.shape[0] // nd // 2
    n = Reduce.count(nd)
    _, keys, w = heads.shape
    nh = w // HEAD
    tok = keys // nc
    width = w * nc
    nb = 2 if nd % 2 == 0 else 1
    vm = lambda *shape: pltpu.VMEM(shape, BF16)
    gout, gattn = (nd // nb, nb, ff // nd, width // 2), (nd // nb, nb, hr, width)
    ns = 3 * nd + 4
    dma = pltpu.SemaphoreType.DMA
    return pl.pallas_call(
        attend_back_kernel,
        out_shape=[
            S((nc, 3, tok, w), BF16), S((2 * hr, ff), BF16), S(gout, BF16), S(gattn, BF16)
        ],
        in_specs=[ANY, VMEM, VMEM, ANY, VMEM, VMEM] + [ANY] * 7,
        out_specs=[ANY, VMEM, ANY, ANY],
        scratch_shapes=[
            pltpu.VMEM((3, keys, w), BF16),
            pltpu.VMEM((keys, w), BF16),
            pltpu.VMEM((nh, 8, keys), F32),
            pltpu.VMEM((keys, w), F32),
            pltpu.VMEM((nc, 3, tok, w), BF16),
            pltpu.VMEM((2, nd, hr, tok), BF16),
            pltpu.VMEM((2, 2, ff, tok), BF16),
            vm(2, nd, ff // nd, tok), vm(2, tok, width // 2), vm(2, nd, hr, tok), vm(2, tok, width),
            vm(*gout), vm(*gattn),
            *Reduce.scratch(nd, hr, ff, True),
            *Reduce.scratch(nd, hr, ff, True),
            dma((nc,)), dma((nc,)), dma((2, nc)), dma((2, nc)), dma((ns,)), dma((ns,)),
            dma((n,)), dma((n,)), dma((n,)), dma((n,)), dma((6 + 3 * nd,)),
        ],
        compiler_params=params(2),
        name="attend_back",
    )(heads, o, lse, dout, near, far, h2t, dl1, dl2, actt, cot, ot, dres)


def each(count, *calls):
    def body(p, _):
        for call in calls:
            call(p)
        return 0

    lax.fori_loop(0, count, body, 0)


def close_kernel(
    dtok_ref, h1t_ref, wqkv_ref, x_ref, gain_ref, dres_ref, part_ref, gout_ref, gattn_ref, t_ref,
    dx_ref, gain_out, outi, outq, outo, outa,
    dtok, dproj, h1t, wqkv, dh1,
    *refs,
):
    pc = Place()
    nd, nc = pc.nd, pc.nc
    _, _, tok, w = dtok_ref.shape
    width = nc * w
    reds, refs = [refs[5 * i : 5 * i + 5] for i in range(5)], refs[25:]
    sums, refs = refs[:5], refs[5:]
    bufs, refs = [refs[3 * i : 3 * i + 3] for i in range(6)], refs[18:]
    gmine, gtotal, gctx, gdp, ssend, srecv, rsend, rrecv, isend, irecv, csend, crecv = refs[:12]
    gsend, grecv, local, outsem = refs[12:]
    third = lambda g: pl.ds(pl.multiple_of(g * width, width), width)
    h1_mine, h1_hers = half_rows(pc, h1t_ref, pc.k), half_rows(pc, h1t_ref, 1 - pc.k)
    pairs = [(dtok_ref, dtok), (gout_ref, reds[0][0])]
    pairs += [(h1_mine[s], h1t.at[0, s]) for s in range(nd)]
    pairs += [(gattn_ref, reds[4][0]), (wqkv_ref, wqkv)]
    load = [pltpu.make_async_copy(a, b, local.at[i]) for i, (a, b) in enumerate(pairs)]
    for cp in load:
        cp.start()
    barrier(pc)
    pairs = [(h1_hers[s], h1t.at[1, s]) for s in range(nd)]
    pairs += [(dproj.at[0, :, third(g)], dproj.at[1, :, third(g)]) for g in range(3)]
    swap = [
        remote(src, dst, ssend.at[i], srecv.at[i], pc.sibling) for i, (src, dst) in enumerate(pairs)
    ]
    ro, *rq, ra = [
        Reduce(pc, bs[0], bs[1:], rsend.at[i], rrecv.at[i], i > 0) for i, bs in enumerate(reds)
    ]
    to, *tq, ta = sums
    ci = Chain(pc, t_ref, bufs[0], isend, irecv, True, 2 * PARTS)
    co, *cq, ca = [
        Chain(pc, t, bs, csend.at[i], crecv.at[i], i > 0, PARTS)
        for i, (t, bs) in enumerate(zip(sums, bufs[1:]))
    ]
    for cp in swap[:nd]:
        cp.start()
    each(ci.n, ci.open)
    load[1].wait()
    ro.start()
    load[0].wait()
    for g in range(3):
        for i in range(nc):
            dproj[0, :, g * width + i * w : g * width + (i + 1) * w] = dtok[i, g]
        swap[nd + g].start()
    for cp in load[2:]:
        cp.wait()
    for cp in swap[: nd + 1]:
        cp.wait_recv()
    weight_grad(pc, reds[1][0], h1t, dproj.at[:, :, third(0)])
    rq[0].start()
    ci.up(0)
    for g in (1, 2):
        swap[nd + g].wait_recv()
        weight_grad(pc, reds[1 + g][0], h1t, dproj.at[:, :, third(g)])
    dh1[...] = jnp.zeros_like(dh1)

    def back(g, _):
        dh1[...] += lax.dot_general(
            dproj[0, :, third(g)], wqkv[g].reshape(width, width), (((1,), (1,)), ((), ())),
            preferred_element_type=F32,
        )
        ci.both(1 + g)
        return 0

    lax.fori_loop(0, 3, back, 0)
    ci.turn_out(0)
    ro.middle()
    rq[1].start()
    gain = jnp.concatenate([gain_ref[s, 0:1, :] for s in range(nd)], axis=1)
    gtotal[...] = jnp.zeros_like(gtotal)
    chunk = 32

    def norm_back(i, _):
        at = pl.ds(pl.multiple_of(i * chunk, chunk), chunk)
        xf = x_ref[at, :].astype(F32)
        mean = jnp.mean(xf, axis=-1, keepdims=True)
        cen = xf - mean
        inv = lax.rsqrt(jnp.mean(cen * cen, axis=-1, keepdims=True) + norm_eps)
        hat = cen * inv
        d = dh1[at, :]
        dhat = d * gain
        m1 = jnp.mean(dhat, axis=-1, keepdims=True)
        m2 = jnp.mean(dhat * hat, axis=-1, keepdims=True)
        dx_ref[at, :] = (dres_ref[at, :] + inv * (dhat - m1 - hat * m2)).astype(BF16)
        gtotal[...] += jnp.sum((d * hat).reshape(chunk // 8, 8, width), axis=0)
        return 0

    lax.fori_loop(0, tok // chunk, norm_back, 0)
    row = lax.broadcasted_iota(jnp.int32, (8, 1), 0)
    gmine[...] = jnp.where(row == 0, jnp.sum(gtotal[...], axis=0, keepdims=True), part_ref[...])
    rows = gain_out.shape[1]
    here = lambda d: pl.ds(pl.multiple_of(d * rows, 128), rows)
    dcopies = []
    for t in range(1, nd):
        to_d = (pc.d + t) % nd
        dcopies.append(
            remote(
                gmine.at[:, here(to_d)], gdp.at[t], gsend.at[nc + t], grecv.at[nc + t], (to_d, pc.c)
            )
        )
        dcopies[-1].start()
    ci.both(4)
    ci.turn_out(1)
    rq[0].middle()
    rq[2].start()
    ci.both(5)
    ci.turn_out(2)
    for cp in dcopies:
        cp.wait_recv()
    total = gmine[:, here(pc.d)]
    for t in range(1, nd):
        total = total + gdp[t]
    gdp[0] = total
    gcopies = []
    for t in range(1, nc):
        gcopies.append(
            remote(gdp.at[0], gctx.at[t], gsend.at[t], grecv.at[t], (pc.d, (pc.c + t) % nc))
        )
        gcopies[-1].start()
    ci.both(6)
    ci.turn_out(3)
    ro.finish(to)
    each(PARTS, co.open)
    ci.both(7)
    ci.turn_in(7)
    ci.turn_out(4)
    rq[1].middle()
    ra.start()
    ci.turn_out(5)
    co.up(0)
    rq[0].finish(tq[0])
    each(PARTS, cq[0].open)
    ci.turn_out(6)
    co.both(1)
    ci.turn_out(7)
    outs = [
        pltpu.make_async_copy(c.all, out, outsem.at[i])
        for i, (c, out) in enumerate(
            [(ci, outi), (co, outo)]
            + [(cq[g], outq.at[:, :, third(g)]) for g in range(3)]
            + [(ca, outa)]
        )
    ]
    for cp in gcopies:
        cp.wait_recv()
    total = gdp[0]
    for t in range(1, nc):
        total = total + gctx[t]
    gain_out[...] = total
    rq[2].middle()
    co.both(2)
    co.turn_out(0)
    rq[1].finish(tq[1])
    each(PARTS, cq[1].open)
    co.both(3)
    cq[0].up(0)
    co.turn_in(3)
    co.turn_out(1)
    ra.middle()
    each(PARTS - 1, lambda p: cq[0].both(p + 1))
    co.turn_out(2)
    rq[2].finish(tq[2])
    each(PARTS, cq[2].open)
    co.turn_out(3)
    cq[1].up(0)
    cq[0].turn_in(3)
    ra.finish(ta)
    each(PARTS, ca.open)
    each(PARTS - 1, lambda p: cq[1].both(p + 1), cq[0].turn_out)
    cq[2].up(0)
    cq[1].turn_in(3)
    cq[0].turn_out(3)
    each(PARTS - 1, lambda p: cq[2].both(p + 1), cq[1].turn_out)
    ca.up(0)
    cq[2].turn_in(3)
    cq[1].turn_out(3)
    each(PARTS - 1, lambda p: ca.both(p + 1), cq[2].turn_out)
    ca.turn_in(3)
    cq[2].turn_out(3)
    each(ci.n, ci.side_wait)
    outs[0].start()
    each(PARTS, co.side_wait)
    outs[1].start()
    each(PARTS, ca.turn_out)
    for i, c in enumerate(cq + [ca]):
        each(PARTS, c.side_wait)
        outs[2 + i].start()
    for cp in swap + dcopies + gcopies:
        cp.wait_send()
    for r in [ro] + rq + [ra]:
        r.sent()
    for c in [ci, co] + cq + [ca]:
        each(c.n, c.sent)
    for cp in outs:
        cp.wait()


def close(dtok, h1t, wqkv, x, gains, dres, part, gout, gattn, totals):
    nd, nc = lax.axis_size("dp"), lax.axis_size("ctx")
    tok, width = x.shape
    rows = width // nd
    hr = rows // 2
    nq, ns = Reduce.count(nd), nd + 3
    dma = pltpu.SemaphoreType.DMA
    mine = [gout.shape[2:]] + [(hr, width)] * 4
    sizes = [totals.shape] + mine
    vm = lambda *shape: pltpu.VMEM(shape, BF16)
    chain_bufs = [b for size in sizes for b in (vm(*size), vm(*size), vm(2, *size))]
    reduce_bufs = [b for i, size in enumerate(mine) for b in Reduce.scratch(nd, *size, i > 0)]
    return pl.pallas_call(
        close_kernel,
        out_shape=[S((tok, width), BF16), S((8, rows), F32)]
        + [S((2,) + size, BF16) for size in (sizes[0], (hr, 3 * width), mine[0], mine[4])],
        in_specs=[ANY, ANY, ANY, VMEM, VMEM, VMEM, VMEM, ANY, ANY, VMEM],
        out_specs=[VMEM] * 2 + [ANY] * 4,
        scratch_shapes=[
            vm(*dtok.shape), vm(2, tok, 3 * width), vm(2, nd, hr, tok), vm(*wqkv.shape),
            pltpu.VMEM((tok, width), F32),
            *reduce_bufs, *[vm(*size) for size in mine], *chain_bufs,
            pltpu.VMEM((8, width), F32), pltpu.VMEM((8, width), F32),
            pltpu.VMEM((nc, 8, rows), F32), pltpu.VMEM((nd, 8, rows), F32),
            dma((ns,)), dma((ns,)), dma((5, nq)), dma((5, nq)),
            dma((4, 2 * PARTS)), dma((4, 2 * PARTS)), dma((5, 4, PARTS)), dma((5, 4, PARTS)),
            dma((nc + nd,)), dma((nc + nd,)), dma((4 + nd,)), dma((6,)),
        ],
        compiler_params=params(3),
        name="close",
    )(dtok, h1t, wqkv, x, gains, dres, part, gout, gattn, totals)


def norm_rows(values, gain):
    row_mean = jnp.mean(values, axis=-1, keepdims=True)
    centred = values - row_mean
    row_var = jnp.mean(centred * centred, axis=-1, keepdims=True)
    return centred * lax.rsqrt(row_var + norm_eps) * gain


def gelu_exact(values):
    return 0.5 * values * (1.0 + lax.erf(values * 0.7071067811865476))


def gelu_slope(values):
    return (
        0.5 * (1.0 + lax.erf(values * 0.7071067811865476))
        + values * jnp.exp(-0.5 * values * values) * 0.3989422804014327
    )


def rope_angles(positions, lanes):
    half = HEAD // 2
    freq = rope_theta ** (-(jnp.arange(half, dtype=F32) * 2.0 / HEAD))
    freq = jnp.tile(freq, lanes // half)
    return positions.astype(F32)[:, None] * freq[None, :]


def on_device(
    tokens,
    norm1_gain,
    qkv_weight,
    attn_out_weight,
    norm2_gain,
    mlp_in_weight,
    mlp_out_weight,
    cotangent,
):
    _, tok, width = tokens.shape
    nc, nd = lax.axis_size("ctx"), lax.axis_size("dp")
    keys = tok * nc
    w = width // nc
    ff = mlp_in_weight.shape[1] // 2
    rows = norm1_gain.shape[0]
    x = tokens.reshape(tok, width)
    upstream = cotangent.reshape(tok, width)
    gains = jnp.concatenate(
        [
            norm1_gain.astype(F32)[None],
            norm2_gain.astype(F32)[None],
            jnp.zeros((6, rows), F32),
        ]
    )
    ang = rope_angles(lax.axis_index("ctx") * tok + jnp.arange(tok, dtype=jnp.int32), 2 * w)
    sign = jnp.where(jnp.arange(2 * w) % HEAD < HEAD // 2, -1.0, 1.0).astype(F32)
    h1t, gains_all, w1s, w2s, wqkv, wattn, heads, w1_early = project(
        x, gains, jnp.cos(ang), jnp.sin(ang) * sign[None], qkv_weight, attn_out_weight,
        mlp_in_weight,
    )
    otok, o_heads, lse, w1, w2, wout = attend(
        heads, w1s, w2s, mlp_out_weight, w1_early
    )
    wattn = wattn.reshape(width, width)
    w1 = w1.reshape(width, ff)
    w2 = w2.reshape(width, ff)
    wout = wout.reshape(ff, width)
    gain_one = gains_all[:, 0].reshape(width)
    gain_two = gains_all[:, 1].reshape(width)

    split = otok.ndim == 3
    attended_b = jnp.transpose(otok, (1, 0, 2)).reshape(tok, width) if split else otok
    inputs_f = x.astype(F32)
    attn_res = inputs_f + jnp.dot(attended_b, wattn, preferred_element_type=F32)
    normed_two = norm_rows(attn_res, gain_two).astype(BF16)
    gelu_in = jnp.dot(normed_two, w1, preferred_element_type=F32)
    gate_in = jnp.dot(normed_two, w2, preferred_element_type=F32)
    activated = (gelu_exact(gelu_in) * gate_in).astype(BF16)
    layer_out = (attn_res + jnp.dot(activated, wout, preferred_element_type=F32)).astype(BF16)
    grad_act = jnp.dot(upstream, wout.T, preferred_element_type=F32)
    dl1 = (grad_act * gate_in * gelu_slope(gelu_in)).astype(BF16)
    dl2 = (grad_act * gelu_exact(gelu_in)).astype(BF16)
    dl1, dl2 = lax.optimization_barrier((dl1, dl2))
    grad_normed_two = jnp.dot(dl1, w1.T, preferred_element_type=F32) + jnp.dot(
        dl2, w2.T, preferred_element_type=F32
    )
    _, pull_two = jax.vjp(norm_rows, attn_res, gain_two)
    grad_res_norm, grad_gain_two = pull_two(grad_normed_two)
    grad_res = upstream.astype(F32) + grad_res_norm
    grad_res_b = grad_res.astype(BF16)
    dout = jnp.dot(grad_res_b, wattn.T, preferred_element_type=F32).astype(BF16)
    if split:
        dout = jnp.transpose(dout.reshape(tok, nc, w), (1, 0, 2))

    near = rope_angles(jnp.arange(tok, dtype=jnp.int32), w)
    far = rope_angles(jnp.arange(nc, dtype=jnp.int32) * tok, w)[:, None]
    near, far = [jnp.stack([jnp.cos(ang), jnp.sin(ang)]) for ang in (near, far)]
    dtok, totals, gout, gattn = attend_back(
        heads, o_heads, lse, dout, near, far, normed_two.T, dl1.T, dl2.T,
        activated.T, upstream, attended_b.T, grad_res_b,
    )
    input_grad, gain_grads, gin, gqkv, gout, gattn = close(
        dtok, h1t, wqkv, x, gains_all, grad_res, grad_gain_two.reshape(1, width), gout, gattn, totals
    )
    gin = gin.reshape(2, 2, rows // 2, ff)
    grad_in = jnp.concatenate([gin[:, i].reshape(rows, ff) for i in range(2)], axis=1)
    return (
        layer_out.reshape(1, tok, width),
        input_grad.reshape(1, tok, width),
        gain_grads[0],
        gqkv.reshape(rows, 3 * width).astype(F32),
        gattn.reshape(rows, width).astype(F32),
        gain_grads[1],
        grad_in.astype(F32),
        jnp.concatenate([gout[0], gout[1]], axis=1).astype(F32),
    )


def solution(mesh):
    in_specs = (
        P("dp", "ctx", None),
        P("dp"),
        P("dp", None),
        P("dp", None),
        P("dp"),
        P("dp", None),
        P("dp", None),
        P("dp", "ctx", None),
    )
    out_specs = (
        P("dp", "ctx", None),
        P("dp", "ctx", None),
        P("dp"),
        P("dp", None),
        P("dp", None),
        P("dp"),
        P("dp", None),
        P("dp", None),
    )
    return jax.shard_map(
        on_device, mesh=mesh, in_specs=in_specs, out_specs=out_specs, check_vma=False
    )
```

```python
import functools

import jax
import jax.numpy as jnp
from jax import lax
from jax.experimental import pallas as pl
from jax.experimental.pallas import tpu as pltpu
from jax.sharding import PartitionSpec as P

HEAD = 64
norm_eps = 1e-05
rope_theta = 160000.0
F32 = jnp.float32
BF16 = jnp.bfloat16
MESH = pl.DeviceIdType.MESH
LOG2E = 1.4426950408889634
VMEM_LIMIT = 64 * 1024 * 1024 - 65536
ANY = pl.BlockSpec(memory_space=pl.ANY)
VMEM = pl.BlockSpec(memory_space=pltpu.VMEM)
S = jax.ShapeDtypeStruct


def params(cid):
    return pltpu.CompilerParams(
        collective_id=cid, has_side_effects=True, vmem_limit_bytes=VMEM_LIMIT
    )


class Place:
    def __init__(self):
        self.nd = lax.axis_size("dp")
        self.nc = lax.axis_size("ctx")
        self.d = lax.axis_index("dp")
        self.c = lax.axis_index("ctx")
        self.nb = 2 if self.nd % 2 == 0 else 1
        self.na = self.nd // self.nb
        self.a = self.d // self.nb
        self.b = self.d % self.nb
        self.nz = self.nc // 2
        self.z = self.c // 2
        self.k = self.c % 2
        self.sibling = (self.d, self.z * 2 + 1 - self.k)

    def shard(self, da, db):
        return ((self.a + da) % self.na) * self.nb + (self.b + db) % self.nb

    def at(self, da, db):
        return (self.shard(da, db), self.c)


def barrier(pc, dp=True, ctx=True):
    sem = pltpu.get_barrier_semaphore()
    count = 0
    if dp:
        for t in range(1, pc.nd):
            pl.semaphore_signal(
                sem, inc=1, device_id=((pc.d + t) % pc.nd, pc.c), device_id_type=MESH
            )
            count += 1
    if ctx:
        for t in range(1, pc.nc):
            pl.semaphore_signal(
                sem, inc=1, device_id=(pc.d, (pc.c + t) % pc.nc), device_id_type=MESH
            )
            count += 1
    pl.semaphore_wait(sem, count)


def remote(src, dst, send, recv, target):
    return pltpu.make_async_remote_copy(
        src_ref=src,
        dst_ref=dst,
        send_sem=send,
        recv_sem=recv,
        device_id=target,
        device_id_type=MESH,
    )


class Gather:
    def __init__(self, pc, cut, own, send, recv, deep=None):
        self.pc, self.cut, self.own, self.send, self.recv, self.deep = pc, cut, own, send, recv, deep
        self.lines = [(da, 0) for da in range(1, pc.na)] + [(0, db) for db in range(1, pc.nb)]
        self.cross_at = [
            (da, db, part)
            for part in (0, 1)
            for da in range(1, pc.na)
            for db in range(1, pc.nb)
        ]
        self.n = len(self.lines) + len(self.cross_at)
        self.pair = (pc.d, (pc.z + 1 - 2 * (pc.z % 2)) * 2 + pc.k)

    @staticmethod
    def count(nd):
        nb = 2 if nd % 2 == 0 else 1
        na = nd // nb
        return 2 * ((na - 1) + (nb - 1) + 2 * (na - 1) * (nb - 1)) + 2 * nd

    def _copy(self, index, shard, part, target, own=False):
        src = (self.own if own else self.cut)(shard, self.pc.k, part)
        dst = self.cut(shard, self.pc.k, part)
        return remote(src, dst, self.send.at[index], self.recv.at[index], target)

    def _arrived(self, index, shard, core, part):
        ref = self.cut(shard, core, part)
        return remote(ref, ref, self.send.at[index], self.recv.at[index], self.pc.sibling)

    def _deep(self, index, shard, core, mine, target):
        ref = self.deep(shard, core, mine)
        return remote(ref, ref, self.send.at[index], self.recv.at[index], target)

    def others(self):
        pc = self.pc
        return [(da, db) for da in range(pc.na) for db in range(pc.nb) if (da, db) != (0, 0)]

    def first(self):
        pc = self.pc
        for i, (da, db) in enumerate(self.lines):
            self._copy(i, pc.d, None, pc.at(-da, -db), own=True).start()

    def _down(self, da, db):
        if self.deep is not None:
            i = self.others().index((da, db))
            self._deep(2 * self.n + i, self.pc.shard(da, db), self.pc.k, True, self.pair).start()

    def relay(self):
        pc, nl = self.pc, len(self.lines)
        for i, (da, db) in enumerate(self.lines):
            shard = pc.shard(da, db)
            self._arrived(i, shard, pc.k, None).wait_recv()
            for j, (xa, xb, part) in enumerate(self.cross_at):
                if part == 0 and db == 0 and xa == da:
                    self._copy(nl + j, shard, part, pc.at(0, -xb)).start()
                if part == 1 and da == 0 and xb == db:
                    self._copy(nl + j, shard, part, pc.at(-xa, 0)).start()
            self._down(da, db)
            self._copy(self.n + i, shard, None, pc.sibling).start()

    def cross(self):
        pc, nl = self.pc, len(self.lines)
        for j, (xa, xb, part) in enumerate(self.cross_at):
            shard = pc.shard(xa, xb)
            self._arrived(nl + j, shard, pc.k, part).wait_recv()
            self._copy(self.n + nl + j, shard, part, pc.sibling).start()
            if part == 1:
                self._down(xa, xb)

    def across(self):
        pc = self.pc
        for i, (da, db) in enumerate(self.others()):
            shard = pc.shard(da, db)
            self._deep(2 * self.n + i, shard, pc.k, False, pc.sibling).wait_recv()
            self._deep(2 * self.n + pc.nd + i, shard, pc.k, False, pc.sibling).start()

    def finish(self):
        pc, nl = self.pc, len(self.lines)
        for i, (da, db) in enumerate(self.lines):
            self._arrived(self.n + i, pc.shard(da, db), 1 - pc.k, None).wait_recv()
        for j, (xa, xb, part) in enumerate(self.cross_at):
            self._arrived(self.n + nl + j, pc.shard(xa, xb), 1 - pc.k, part).wait_recv()
        if self.deep is not None:
            for i, (da, db) in enumerate(self.others()):
                shard = pc.shard(da, db)
                self._deep(2 * self.n + pc.nd + i, shard, 1 - pc.k, False, pc.sibling).wait_recv()

    def sent(self):
        pc, nl = self.pc, len(self.lines)
        for i, _ in enumerate(self.lines):
            self._arrived(i, pc.d, pc.k, None).wait_send()
            self._arrived(self.n + i, pc.d, pc.k, None).wait_send()
        for j, (_, _, part) in enumerate(self.cross_at):
            self._arrived(nl + j, pc.d, pc.k, part).wait_send()
            self._arrived(self.n + nl + j, pc.d, pc.k, part).wait_send()
        if self.deep is not None:
            for i, _ in enumerate(self.others()):
                self._deep(2 * self.n + i, pc.d, pc.k, True, pc.sibling).wait_send()
                self._deep(2 * self.n + pc.nd + i, pc.d, pc.k, False, pc.sibling).wait_send()


def row_cut(ref, rows, core, part, lead=0):
    start = core * (rows // 2) + (0 if part is None else part * (rows // 4))
    size = rows // 2 if part is None else rows // 4
    return ref.at[(slice(None),) * lead + (pl.ds(start, size),)]


def share_rows(pc, rows):
    q = rows // 8
    odd = pc.z % 2

    def cut(ref, core, part):
        start = core * (4 * q) + odd * q
        if part is None:
            return ref.at[pl.ds(start, 3 * q)]
        n = 3 * q // 2
        return ref.at[pl.ds(start + part * n, n)]

    def deep(ref, core, mine):
        at = odd * (3 * q) if mine else (1 - odd) * (3 * q)
        return ref.at[pl.ds(core * (4 * q) + at, q)]

    return cut, deep


def share_cols(pc, rows, cols):
    q = cols // 8
    odd = pc.z % 2
    n = rows // 2 // 16 * 16

    def cut(ref, core, part):
        start = pl.multiple_of(core * (4 * q) + odd * q, 128)
        at = slice(None) if part is None else pl.ds(0, n) if part == 0 else pl.ds(n, rows - n)
        return ref.at[at, pl.ds(start, 3 * q)]

    def deep(ref, core, mine):
        at = odd * (3 * q) if mine else (1 - odd) * (3 * q)
        return ref.at[:, pl.ds(pl.multiple_of(core * (4 * q) + at, 128), q)]

    return cut, deep


def early_rows(rows):
    return rows // 2 if rows % 256 == 0 else 0


class Reduce:
    def __init__(self, pc, g, bufs, send, recv, by_rows):
        self.pc, self.g, self.send, self.recv, self.by_rows = pc, g, send, recv, by_rows
        self.r1a, self.r1b, self.r2a, self.r2b = bufs

    @staticmethod
    def count(nd):
        nb = 2 if nd % 2 == 0 else 1
        return 2 * (nd // nb - 1 + nb - 1)

    @staticmethod
    def scratch(nd, rows, cols, by_rows):
        nb = 2 if nd % 2 == 0 else 1
        na = nd // nb
        r, c = (rows // 2, cols) if by_rows else (rows, cols // 2)
        return [
            pltpu.VMEM((na, nb, rows, cols), BF16),
            pltpu.VMEM((na - 1, nb, r, c), BF16),
            pltpu.VMEM((nb - 1, na, r, c), BF16),
            pltpu.VMEM((nb - 1, r, c), BF16),
            pltpu.VMEM((na - 1, r, c), BF16),
        ]

    def part(self, ref, p):
        lead = (slice(None),) * (len(ref.shape) - 2)
        rows, cols = ref.shape[-2:]
        if self.by_rows:
            return ref.at[lead + (pl.ds(p * (rows // 2), rows // 2),)]
        return ref.at[lead + (slice(None), pl.ds(p * (cols // 2), cols // 2))]

    def copies(self, step):
        pc = self.pc
        na, nb = pc.na, pc.nb
        out = []
        base = 0 if step == 1 else na - 1 + nb - 1
        for da in range(1, na):
            a = (pc.a + na - da) % na
            i = base + da - 1
            if step == 1:
                src, dst = self.part(self.g.at[a], 0), self.r1a.at[da - 1]
            else:
                src, dst = self.part(self.g.at[a, pc.b], 1), self.r2b.at[da - 1]
            out.append(remote(src, dst, self.send.at[i], self.recv.at[i], pc.at(-da, 0)))
        for db in range(1, nb):
            b = (pc.b + nb - db) % nb
            i = base + na - 1 + db - 1
            if step == 1:
                src, dst = self.part(self.g.at[:, b], 1), self.r1b.at[db - 1]
            else:
                src, dst = self.part(self.g.at[pc.a, b], 0), self.r2a.at[db - 1]
            out.append(remote(src, dst, self.send.at[i], self.recv.at[i], pc.at(0, -db)))
        return out

    def start(self):
        for cp in self.copies(1):
            cp.start()

    def middle(self):
        pc = self.pc
        for cp in self.copies(1):
            cp.wait_recv()
        for b in range(pc.nb):
            at = self.part(self.g.at[pc.a, b], 0)
            add(at, [self.r1a.at[i, b] for i in range(pc.na - 1)])
        for a in range(pc.na):
            at = self.part(self.g.at[a, pc.b], 1)
            add(at, [self.r1b.at[i, a] for i in range(pc.nb - 1)])
        for cp in self.copies(2):
            cp.start()

    def finish(self, total):
        pc = self.pc
        for cp in self.copies(2):
            cp.wait_recv()
        own = self.g.at[pc.a, pc.b]
        add(self.part(own, 0), [self.r2a.at[i] for i in range(pc.nb - 1)], self.part(total, 0))
        add(self.part(own, 1), [self.r2b.at[i] for i in range(pc.na - 1)], self.part(total, 1))

    def sent(self):
        for cp in self.copies(1) + self.copies(2):
            cp.wait_send()


def add(ref, others, into=None):
    into = ref if into is None else into
    rows = ref.shape[0]
    chunk = next(n for n in (32, 16, rows) if rows % n == 0)

    def some(i, _):
        at = pl.ds(pl.multiple_of(i * chunk, chunk), chunk)
        total = ref[at, :].astype(F32)
        for o in others:
            total = total + o[at, :].astype(F32)
        into[at, :] = total.astype(BF16)
        return 0

    if rows == chunk:
        total = ref[...].astype(F32)
        for o in others:
            total = total + o[...].astype(F32)
        into[...] = total.astype(BF16)
    else:
        lax.fori_loop(0, rows // chunk, some, 0)


PARTS = 4


def chain_part(by_rows, parts):
    def part(ref, p):
        rows, cols = ref.shape[-2:]
        if by_rows:
            n = rows // parts
            return ref.at[pl.ds(pl.multiple_of(p * n, n), n)]
        n = cols // parts
        return ref.at[:, pl.ds(pl.multiple_of(p * n, n), n)]

    return part


class Chain:
    def __init__(self, pc, t, bufs, send, recv, by_rows, parts):
        self.pc, self.t, self.n = pc, t, parts
        self.part = chain_part(by_rows, parts)
        self.outer, self.swap, total = bufs
        self.total, self.other = total.at[pc.k], total.at[1 - pc.k]
        self.all = total
        self.send, self.recv = send, recv
        half = pc.nz // 2
        self.low = pc.z < half
        self.end = (pc.z == 0) | (pc.z == pc.nz - 1)
        self.mid = (pc.z == half - 1) | (pc.z == half)
        step = 1 - 2 * (pc.z // half)
        self.inner_id = (pc.d, ((pc.z + step + pc.nz) % pc.nz) * 2 + pc.k)
        self.outer_id = (pc.d, ((pc.z - step + pc.nz) % pc.nz) * 2 + pc.k)

    def up_copy(self, p):
        return remote(
            self.part(self.t, p), self.part(self.outer, p), self.send.at[0, p], self.recv.at[0, p],
            self.inner_id,
        )

    def swap_copy(self, p):
        return remote(
            self.part(self.t, p), self.part(self.swap, p), self.send.at[1, p], self.recv.at[1, p],
            self.inner_id,
        )

    def down_copy(self, p):
        at = self.part(self.total, p)
        return remote(at, at, self.send.at[2, p], self.recv.at[2, p], self.outer_id)

    def side_copy(self, p):
        at = self.part(self.total, p)
        return remote(at, at, self.send.at[3, p], self.recv.at[3, p], self.pc.sibling)

    def side_wait(self, p):
        at = self.part(self.other, p)
        remote(at, at, self.send.at[3, p], self.recv.at[3, p], self.pc.sibling).wait_recv()

    def open(self, p):
        @pl.when(self.end)
        def _():
            @pl.when(self.mid)
            def _():
                self.swap_copy(p).start()

            @pl.when(jnp.logical_not(self.mid))
            def _():
                self.up_copy(p).start()

    def up(self, p):
        @pl.when(jnp.logical_not(self.end))
        def _():
            self.up_copy(p).wait_recv()
            add(self.part(self.t, p), [self.part(self.outer, p)])

            @pl.when(self.mid)
            def _():
                self.swap_copy(p).start()

            @pl.when(jnp.logical_not(self.mid))
            def _():
                self.up_copy(p).start()

    def turn_in(self, p):
        @pl.when(self.mid)
        def _():
            self.swap_copy(p).wait_recv()
            add(self.part(self.t, p), [self.part(self.swap, p)], self.part(self.total, p))

            @pl.when(jnp.logical_not(self.end))
            def _():
                self.down_copy(p).start()

            self.side_copy(p).start()

    def turn_out(self, p):
        @pl.when(jnp.logical_not(self.mid))
        def _():
            self.down_copy(p).wait_recv()

            @pl.when(jnp.logical_not(self.end))
            def _():
                self.down_copy(p).start()

            self.side_copy(p).start()

    def both(self, p):
        self.up(p)
        self.turn_in(p - 1)

    def sent(self, p):
        @pl.when(self.mid)
        def _():
            self.swap_copy(p).wait_send()

        @pl.when(jnp.logical_not(self.mid))
        def _():
            self.up_copy(p).wait_send()

        @pl.when(jnp.logical_not(self.end))
        def _():
            self.down_copy(p).wait_send()

        self.side_copy(p).wait_send()


def head_cols(ref, c, w):
    if len(ref.shape) == 3:
        return ref.at[c]
    return ref.at[:, pl.ds(pl.multiple_of(c * w, w), w)]


def half_rows(pc, ref, core):
    rows = ref.shape[0] // pc.nd
    h = rows // 2
    return [ref.at[pl.ds(pl.multiple_of(s * rows + core * h, h), h)] for s in range(pc.nd)]


def project_kernel(
    x_ref, gains_ref, cos_ref, sin_ref, wqkv_ref, wattn_ref, win_ref,
    h1t_ref, gains_out, w1_out, w2_out, wqkv_out, wattn_out, heads_out, w1_all,
    wbuf, abuf, ibuf, h1_ref, gbuf, sendbuf,
    wsend, wrecv, asend, arecv, esend, erecv, gsend, grecv, xsend, xrecv, local,
):
    pc = Place()
    nd, nc, nz = pc.nd, pc.nc, pc.nz
    rows = wqkv_ref.shape[0]
    width = wqkv_ref.shape[1] // 3
    tok = x_ref.shape[0]
    w = width // nc
    cw = 2 * w
    own_w = [
        pltpu.make_async_copy(
            wqkv_ref.at[:, pl.ds(g * width, width)], wbuf.at[g, pc.d], local.at[g]
        )
        for g in range(3)
    ]
    for cp in own_w:
        cp.start()
    own_a = pltpu.make_async_copy(wattn_ref, abuf, local.at[3])
    own_a.start()
    own_i = pltpu.make_async_copy(win_ref, ibuf, local.at[5 + nz])
    own_i.start()
    barrier(pc)
    for cp in own_w:
        cp.wait()

    def chip_of(j):
        return (pc.z + j + 1) % nz

    def chunk(j):
        col = pl.multiple_of(chip_of(j) * cw, cw)

        def cut(shard, core, part):
            return row_cut(wbuf.at[:, shard, :, pl.ds(col, cw)], rows, core, part, lead=1)

        return Gather(pc, cut, cut, wsend.at[j], wrecv.at[j])

    def attn_cut(shard, core, part):
        return row_cut(wattn_out.at[shard], rows, core, part)

    def attn_own(shard, core, part):
        return row_cut(wattn_ref, rows, core, part)

    attn = Gather(pc, attn_cut, attn_own, asend, arecv)

    def early_cut(shard, core, part):
        return row_cut(w1_all.at[shard], e, core, part)

    def early_own(shard, core, part):
        return row_cut(w1_out, e, core, part)

    early = Gather(pc, early_cut, early_own, esend, erecv)
    e = early_rows(rows)
    extra = [attn] + [early] * (e > 0)

    gain_copies = []
    gbuf[pc.d] = gains_ref[...]
    for t in range(1, nd):
        gain_copies.append(
            remote(
                gains_ref, gbuf.at[pc.d], gsend.at[t], grecv.at[t], ((pc.d + t) % nd, pc.c)
            )
        )
        gain_copies[-1].start()
    for j in range(min(2, nz)):
        chunk(j).first()

    xf = x_ref[...].astype(F32)
    mean = jnp.mean(xf, axis=-1, keepdims=True)
    cen = xf - mean
    var = jnp.mean(cen * cen, axis=-1, keepdims=True)
    hat = cen * lax.rsqrt(var + norm_eps)
    for t in range(1, nd):
        src = gbuf.at[(pc.d + nd - t) % nd]
        remote(src, src, gsend.at[t], grecv.at[t], pc.sibling).wait_recv()
    for s in range(nd):
        cols = slice(s * rows, (s + 1) * rows)
        h1_ref[:, cols] = (hat[:, cols] * gbuf[s, 0:1, :]).astype(BF16)
    gains_out[...] = gbuf[...]
    own_a.wait()
    own_a2 = pltpu.make_async_copy(abuf, wattn_out.at[pc.d], local.at[3])
    own_a2.start()
    own_i.wait()
    ff = w1_out.shape[1]
    w1_out[...] = ibuf[:, :ff]
    w2_out[...] = ibuf[:, ff:]
    h1t_ref[...] = jnp.transpose(h1_ref[...])

    lane = lax.broadcasted_iota(jnp.int32, (1, cw), 1)
    low = (lane % HEAD) < HEAD // 2

    def out_copy(j):
        cols = pl.ds(pl.multiple_of(chip_of(j) * cw, cw), cw)
        return pltpu.make_async_copy(
            wbuf.at[:, :, :, cols], wqkv_out.at[:, :, :, cols], local.at[4 + j]
        )

    def place(ref):
        return ref.at[:, pl.ds(pl.multiple_of(pc.c * tok, tok), tok), :]

    def exchange(j, kk):
        return remote(
            sendbuf.at[j, kk], place(heads_out), xsend.at[j, kk], xrecv.at[j, pc.k],
            (pc.d, chip_of(j) * 2 + kk),
        )

    def step(j, _):
        g = chunk(j)
        g.relay()

        @pl.when(j + 2 < nz)
        def _():
            chunk(j + 2).first()

        @pl.when(j == max(nz - 2, 0))
        def _():
            attn.first()

        @pl.when(j == nz - 1)
        def _():
            for it in extra[1:]:
                it.first()

        g.cross()
        g.finish()
        out_copy(j).start()
        cols = pl.ds(pl.multiple_of(chip_of(j) * cw, cw), cw)
        for part in range(3):
            weight = wbuf[part, :, :, cols].reshape(nd * rows, cw)
            proj = jnp.dot(h1_ref[...], weight, preferred_element_type=F32)
            if part < 2:
                up = pltpu.roll(proj, cw - HEAD // 2, 1)
                down = pltpu.roll(proj, HEAD // 2, 1)
                proj = proj * cos_ref[...] + jnp.where(low, up, down) * sin_ref[...]
            proj = proj.astype(BF16)
            for kk in range(2):
                sendbuf[j, kk, part] = proj[:, kk * w : (kk + 1) * w]

        @pl.when(j < nz - 1)
        def _():
            exchange(j, 0).start()
            exchange(j, 1).start()

        return 0

    lax.fori_loop(0, nz, step, 0)
    last = nz - 1
    remote(
        sendbuf.at[last, 1 - pc.k], place(heads_out), xsend.at[last, 1 - pc.k],
        xrecv.at[last, pc.k], pc.sibling,
    ).start()
    own_x = pltpu.make_async_copy(
        sendbuf.at[last, pc.k], place(heads_out), local.at[4 + nz]
    )
    own_x.start()
    for it in extra:
        it.relay()
    for it in extra:
        it.cross()
    for it in extra:
        it.finish()

    def arrival(j, kk):
        ref = sendbuf.at[j, kk]
        return remote(ref, ref, xsend.at[j, kk], xrecv.at[j, kk], pc.sibling)

    def drain(j, _):
        arrival(j, 0).wait_recv()
        arrival(j, 1).wait_recv()
        arrival(j, 0).wait_send()
        arrival(j, 1).wait_send()
        chunk(j).sent()
        out_copy(j).wait()
        return 0

    lax.fori_loop(0, nz - 1, drain, 0)
    arrival(last, 1 - pc.k).wait_recv()
    arrival(last, 1 - pc.k).wait_send()
    chunk(last).sent()
    out_copy(last).wait()
    own_x.wait()
    own_a2.wait()
    for it in extra:
        it.sent()
    for cp in gain_copies:
        cp.wait_send()


def project(x, gains, cosine, sine, wqkv, wattn, win):
    nd, nc = lax.axis_size("dp"), lax.axis_size("ctx")
    nz = nc // 2
    tok, width = x.shape
    rows = wqkv.shape[0]
    w = width // nc
    n = Gather.count(nd)
    dma = pltpu.SemaphoreType.DMA
    return pl.pallas_call(
        project_kernel,
        out_shape=[
            S((width, tok), BF16),
            S((nd, 8, rows), F32),
            S((rows, win.shape[1] // 2), BF16),
            S((rows, win.shape[1] // 2), BF16),
            S((3, nd, rows, width), BF16),
            S((nd, rows, width), BF16),
            S((3, nc * tok, w), BF16),
            S((nd, rows, win.shape[1] // 2), BF16),
        ],
        in_specs=[VMEM, VMEM, VMEM, VMEM, ANY, ANY, ANY],
        out_specs=[VMEM, VMEM, VMEM, VMEM, ANY, ANY, ANY, ANY],
        scratch_shapes=[
            pltpu.VMEM((3, nd, rows, width), BF16),
            pltpu.VMEM((rows, width), BF16),
            pltpu.VMEM(win.shape, BF16),
            pltpu.VMEM((tok, width), BF16),
            pltpu.VMEM((nd, 8, rows), F32),
            pltpu.VMEM((nz, 2, 3, tok, w), BF16),
            dma((nz, n)), dma((nz, n)), dma((n,)), dma((n,)), dma((n,)), dma((n,)),
            dma((nd,)), dma((nd,)), dma((nz, 2)), dma((nz, 2)), dma((6 + nz,)),
        ],
        compiler_params=params(0),
        name="project",
    )(x, gains, cosine, sine, wqkv, wattn, win)


def attend_kernel(
    heads_ref, w1_ref, w2_ref, wout_ref, w1_early,
    otok_out, o_ref, lse_ref, w1_out, w2_out, wout_out,
    qkv, vext, bounce1, bounce2, bounce3,
    s1, r1, s2, r2, s3, r3, xsend, xrecv, local,
):
    pc = Place()
    nd, nc = pc.nd, pc.nc
    keys, w = heads_ref.shape[1], heads_ref.shape[2]
    tok = keys // nc
    rows = w1_ref.shape[0]
    load = pltpu.make_async_copy(heads_ref, qkv, local.at[0])
    load.start()
    pairs = [(w1_ref, bounce1, w1_out), (w2_ref, bounce2, w2_out), (wout_ref, bounce3, wout_out)]
    for i, (src, mid, _) in enumerate(pairs):
        pltpu.make_async_copy(src, mid, local.at[1 + i]).start()
    barrier(pc)
    e = early_rows(rows)
    lower = lambda ref: ref.at[pl.ds(e, rows - e)]
    cut_h, deep_h = share_rows(pc, rows - e)
    cut_r, deep_r = share_rows(pc, rows)
    cut_c, deep_c = share_cols(pc, *wout_ref.shape)

    def item(ref, out, cut, deep, send, recv):
        return Gather(
            pc,
            lambda s, k, p: cut(out.at[s], k, p),
            lambda s, k, p: cut(ref, k, p),
            send,
            recv,
            lambda s, k, mine: deep(out.at[s], k, mine),
        )

    items = [
        item(wout_ref, wout_out, cut_c, deep_c, s3, r3),
        item(w2_ref, w2_out, cut_r, deep_r, s2, r2),
        Gather(
            pc,
            lambda s, k, p: cut_h(lower(w1_out.at[s]), k, p),
            lambda s, k, p: cut_h(lower(w1_ref), k, p),
            s1,
            r1,
            lambda s, k, mine: deep_h(lower(w1_out.at[s]), k, mine),
        ),
    ]
    items[0].first()
    items[1].first()
    load.wait()
    for i, (src, mid, _) in enumerate(pairs):
        pltpu.make_async_copy(src, mid, local.at[1 + i]).wait()
    for i, (_, mid, dst) in enumerate(pairs):
        pltpu.make_async_copy(mid, dst.at[pc.d], local.at[1 + i]).start()
    nh = w // HEAD
    for h in range(nh):
        vext[h, :, :HEAD] = qkv[2, :, h * HEAD : (h + 1) * HEAD]
        vext[h, :, HEAD:] = jnp.ones((keys, HEAD), BF16)
    scale = HEAD ** (-0.5) * LOG2E

    def block_copy(i):
        to = (pc.c + i + 1) % nc
        at = pl.ds(pl.multiple_of(to * tok, tok), tok)
        return remote(
            o_ref.at[at], head_cols(otok_out, pc.c, w), xsend.at[i], xrecv.at[i], (pc.d, to)
        )

    def block(i, _):
        at = pl.ds(pl.multiple_of(((pc.c + i + 1) % nc) * tok, tok), tok)
        for h in range(nh):
            hs = slice(h * HEAD, (h + 1) * HEAD)
            s = lax.dot_general(
                qkv[0, at, hs], qkv[1, :, hs], (((1,), (1,)), ((), ())),
                preferred_element_type=F32,
            )
            m = jnp.max(s, axis=1, keepdims=True)
            p = jnp.exp2(s * scale - m * scale).astype(BF16)
            ol = jnp.dot(p, vext[h], preferred_element_type=F32)
            total = ol[:, HEAD:]
            o_ref[at, hs] = (ol[:, :HEAD] / total).astype(BF16)
            lse = m * scale + jnp.log2(total)
            lse_ref[h, :, at] = jnp.transpose(jnp.concatenate([lse, lse], axis=1))[:8]

        @pl.when(i < nc - 1)
        def _():
            block_copy(i).start()

        @pl.when(i == nc // 2)
        def _():
            items[0].relay()
            items[2].first()

        return 0

    lax.fori_loop(0, nc, block, 0)
    own = pltpu.make_async_copy(
        o_ref.at[pl.ds(pl.multiple_of(pc.c * tok, tok), tok)],
        head_cols(otok_out, pc.c, w),
        local.at[0],
    )
    own.start()
    items[1].relay()
    items[0].cross()
    items[2].relay()
    items[1].cross()
    items[0].across()
    items[2].cross()
    items[1].across()
    items[2].across()
    for it in items:
        it.finish()

    def drain(i, _):
        got = head_cols(otok_out, (pc.c + nc - i - 1) % nc, w)
        remote(got, got, xsend.at[i], xrecv.at[i], pc.sibling).wait_recv()
        block_copy(i).wait_send()
        return 0

    lax.fori_loop(0, nc - 1, drain, 0)
    own.wait()
    for i, (_, mid, dst) in enumerate(pairs):
        pltpu.make_async_copy(mid, dst.at[pc.d], local.at[1 + i]).wait()
    for it in items:
        it.sent()


def attend(heads, w1, w2, wout, w1_early):
    nd, nc = lax.axis_size("dp"), lax.axis_size("ctx")
    _, keys, w = heads.shape
    nh = w // HEAD
    n = Gather.count(nd)
    dma = pltpu.SemaphoreType.DMA
    return pl.pallas_call(
        attend_kernel,
        out_shape=[
            S((keys // nc, nc * w) if w % 128 == 0 else (nc, keys // nc, w), BF16),
            S((keys, w), BF16),
            S((nh, 8, keys), F32),
            S((nd,) + w1.shape, BF16),
            S((nd,) + w2.shape, BF16),
            S((nd,) + wout.shape, BF16),
        ],
        in_specs=[ANY] * 5,
        out_specs=[ANY, VMEM, VMEM, ANY, ANY, ANY],
        input_output_aliases={4: 3},
        scratch_shapes=[
            pltpu.VMEM((3, keys, w), BF16),
            pltpu.VMEM((nh, keys, 2 * HEAD), BF16),
            pltpu.VMEM(w1.shape, BF16),
            pltpu.VMEM(w2.shape, BF16),
            pltpu.VMEM(wout.shape, BF16),
            dma((n,)), dma((n,)), dma((n,)), dma((n,)), dma((n,)), dma((n,)),
            dma((nc,)), dma((nc,)), dma((4,)),
        ],
        compiler_params=params(1),
        name="attend",
    )(heads, w1, w2, wout, w1_early)


def attend_back_kernel(
    heads_ref, o_ref, lse_ref, dout_ref, near_ref, far_ref, h2t_ref, dl1_ref, dl2_ref,
    actt_ref, c_ref, ot_ref, dres_ref,
    dtok_out, t_ref, gout_out, gattn_out,
    qkv, dout, delta, dq, sendbuf, h2t, dl, actt, cot, ot, dres, gout, gattn,
    ga, ra0, ra1, ra2, ra3, gb, rb0, rb1, rb2, rb3,
    dsend, drecv, xsend, xrecv, ssend, srecv, asend, arecv, bsend, brecv, local,
):
    pc = Place()
    nd = pc.nd
    nc = pc.nc
    keys, w = heads_ref.shape[1], heads_ref.shape[2]
    tok = keys // nc
    nh = w // HEAD
    load = pltpu.make_async_copy(heads_ref, qkv, local.at[0])
    load.start()
    mine_t = half_rows(pc, h2t_ref, pc.k)
    hers_t = half_rows(pc, h2t_ref, 1 - pc.k)
    fetch = [pltpu.make_async_copy(mine_t[s], h2t.at[0, s], local.at[2 + s]) for s in range(nd)]
    fetch.append(pltpu.make_async_copy(dl1_ref, dl.at[0, 0], local.at[2 + nd]))
    fetch.append(pltpu.make_async_copy(dl2_ref, dl.at[1, 0], local.at[3 + nd]))
    half = cot.shape[2]
    nr = actt.shape[2]
    col = lambda core: pl.ds(pl.multiple_of(core * half, half), half)
    o_mine, o_hers = half_rows(pc, ot_ref, pc.k), half_rows(pc, ot_ref, 1 - pc.k)
    acts = [actt_ref.at[pl.ds(s * nr, nr)] for s in range(nd)]
    more = [(acts[s], actt.at[0, s]) for s in range(nd)] + [(o_mine[s], ot.at[0, s]) for s in range(nd)]
    more += [(c_ref.at[:, col(pc.k)], cot.at[0]), (dres_ref, dres.at[0])]
    first = len(fetch)
    fetch += [pltpu.make_async_copy(a, b, local.at[4 + nd + i]) for i, (a, b) in enumerate(more)]
    for cp in fetch:
        cp.start()
    barrier(pc)
    swap = [
        remote(hers_t[s], h2t.at[1, s], ssend.at[s], srecv.at[s], pc.sibling) for s in range(nd)
    ]
    more = [(acts[s], actt.at[1, s]) for s in range(nd)] + [(o_hers[s], ot.at[1, s]) for s in range(nd)]
    more += [(c_ref.at[:, col(1 - pc.k)], cot.at[1]), (dres_ref, dres.at[1])]
    late = [
        remote(a, b, ssend.at[nd + 2 + i], srecv.at[nd + 2 + i], pc.sibling)
        for i, (a, b) in enumerate(more)
    ]
    swap.append(remote(dl1_ref, dl.at[0, 1], ssend.at[nd], srecv.at[nd], pc.sibling))
    swap.append(remote(dl2_ref, dl.at[1, 1], ssend.at[nd + 1], srecv.at[nd + 1], pc.sibling))
    for cp in swap:
        cp.start()
    mine = pl.ds(pl.multiple_of(pc.c * tok, tok), tok)
    for i in range(nc - 1):
        to = (pc.c + i + 1) % nc
        remote(
            head_cols(dout_ref, to, w), dout.at[mine], dsend.at[i], drecv.at[i], (pc.d, to)
        ).start()
    own = pltpu.make_async_copy(head_cols(dout_ref, pc.c, w), dout.at[mine], local.at[1])
    own.start()
    ra = Reduce(pc, ga, (ra0, ra1, ra2, ra3), asend, arecv, True)
    rb = Reduce(pc, gb, (rb0, rb1, rb2, rb3), bsend, brecv, True)
    for cp in late:
        cp.start()
    for cp in fetch[:first]:
        cp.wait()
    for cp in swap[: nd + 1]:
        cp.wait_recv()
    weight_grad(pc, ga, h2t, dl.at[0], True)
    ra.start()
    swap[nd + 1].wait_recv()
    weight_grad(pc, gb, h2t, dl.at[1], True)
    rb.start()
    for cp in fetch[first:]:
        cp.wait()
    for cp in late:
        cp.wait_recv()
    weight_grad(pc, gout, actt, cot)
    weight_grad(pc, gattn, ot, dres)
    keep_g = [
        pltpu.make_async_copy(gout, gout_out, local.at[2]),
        pltpu.make_async_copy(gattn, gattn_out, local.at[3]),
    ]
    for cp in keep_g:
        cp.start()
    dq[...] = jnp.zeros_like(dq)
    load.wait()
    own.wait()
    for i in range(nc - 1):
        src = (pc.c + nc - i - 1) % nc
        got = dout.at[pl.ds(pl.multiple_of(src * tok, tok), tok)]
        remote(got, got, dsend.at[i], drecv.at[i], pc.sibling).wait_recv()

    def deltas(i, _):
        at = pl.ds(pl.multiple_of(i * tok, tok), tok)
        t = jnp.transpose(o_ref[at, :].astype(F32) * dout[at, :].astype(F32))
        for h in range(nh):
            row = jnp.sum(t[h * HEAD : (h + 1) * HEAD], axis=0, keepdims=True)
            delta[h, :, at] = jnp.broadcast_to(row, (8, tok))
        return 0

    lax.fori_loop(0, nc, deltas, 0)
    scale = HEAD ** (-0.5)
    lane = lax.broadcasted_iota(jnp.int32, (1, w), 1)
    low = (lane % HEAD) < HEAD // 2

    def unrotate(g, to):
        cos_n, sin_n, cos_f, sin_f = near_ref[0], near_ref[1], far_ref[0, to], far_ref[1, to]
        t = g * (sin_f * cos_n + cos_f * sin_n)
        if w == HEAD:
            up = jnp.concatenate([t[:, HEAD // 2 :], t[:, : HEAD // 2]], axis=1)
            down = up
        else:
            up = pltpu.roll(t, w - HEAD // 2, 1)
            down = pltpu.roll(t, HEAD // 2, 1)
        return g * (cos_f * cos_n - sin_f * sin_n) + jnp.where(low, up, -down)

    def kv_copy(i):
        to = (pc.c + i + 1) % nc
        return remote(
            sendbuf.at[to, pl.ds(1, 2)], dtok_out.at[pc.c, pl.ds(1, 2)],
            xsend.at[0, i], xrecv.at[0, i], (pc.d, to),
        )

    def q_copy(i):
        to = (pc.c + i + 1) % nc
        return remote(
            sendbuf.at[to, 0], dtok_out.at[pc.c, 0], xsend.at[1, i], xrecv.at[1, i], (pc.d, to)
        )

    def block(i, _):
        to = (pc.c + i + 1) % nc
        at = pl.ds(pl.multiple_of(to * tok, tok), tok)
        dks, dvs = [], []
        for h in range(nh):
            hs = slice(h * HEAD, (h + 1) * HEAD)
            kb, vb = qkv[1, at, hs], qkv[2, at, hs]
            q, do = qkv[0, :, hs], dout[:, hs]
            nt = (((1,), (1,)), ((), ()))
            st = lax.dot_general(kb, q, nt, preferred_element_type=F32)
            p = jnp.exp2(st * (scale * LOG2E) - lse_ref[h, 0:1, :])
            dvs.append(jnp.dot(p.astype(BF16), do, preferred_element_type=F32))
            dp = lax.dot_general(vb, do, nt, preferred_element_type=F32)
            ds = (p * (dp - delta[h, 0:1, :])).astype(BF16)
            dks.append(jnp.dot(ds, q, preferred_element_type=F32))
            dq[:, hs] += lax.dot_general(
                ds, kb, (((0,), (0,)), ((), ())), preferred_element_type=F32
            )
        dk = jnp.concatenate(dks, axis=1) * scale
        sendbuf[to, 1] = unrotate(dk, to).astype(BF16)
        sendbuf[to, 2] = jnp.concatenate(dvs, axis=1).astype(BF16)

        @pl.when(i < nc - 1)
        def _():
            kv_copy(i).start()

        @pl.when(i == (nc * 3) // 8)
        def _():
            ra.middle()

        @pl.when(i == (nc * 7) // 8)
        def _():
            rb.middle()

        return 0

    lax.fori_loop(0, nc, block, 0)

    def q_block(i, _):
        to = (pc.c + i + 1) % nc
        at = pl.ds(pl.multiple_of(to * tok, tok), tok)
        sendbuf[to, 0] = unrotate(dq[at, :] * scale, to).astype(BF16)

        @pl.when(i < nc - 1)
        def _():
            q_copy(i).start()

        return 0

    lax.fori_loop(0, nc, q_block, 0)
    keep = pltpu.make_async_copy(sendbuf.at[pc.c], dtok_out.at[pc.c], local.at[1])
    keep.start()
    hr = ga.shape[2]
    ra.finish(t_ref.at[pl.ds(0, hr)])
    rb.finish(t_ref.at[pl.ds(hr, hr)])

    def drain(i, _):
        got = dtok_out.at[(pc.c + nc - i - 1) % nc]
        remote(
            got.at[pl.ds(1, 2)], got.at[pl.ds(1, 2)], xsend.at[0, i], xrecv.at[0, i], pc.sibling
        ).wait_recv()
        remote(got.at[0], got.at[0], xsend.at[1, i], xrecv.at[1, i], pc.sibling).wait_recv()
        kv_copy(i).wait_send()
        q_copy(i).wait_send()
        to = (pc.c + i + 1) % nc
        remote(
            head_cols(dout_ref, to, w), dout.at[mine], dsend.at[i], drecv.at[i], (pc.d, to)
        ).wait_send()
        return 0

    lax.fori_loop(0, nc - 1, drain, 0)
    keep.wait()
    for cp in keep_g:
        cp.wait()
    for cp in swap + late:
        cp.wait_send()
    ra.sent()
    rb.sent()


def weight_grad(pc, g, lhs, rhs, flipped=False):
    dims = (((1,), (1 if flipped else 0,)), ((), ()))

    def shard(s, _):
        total = lax.dot_general(lhs[0, s], rhs[0], dims, preferred_element_type=F32)
        total = total + lax.dot_general(lhs[1, s], rhs[1], dims, preferred_element_type=F32)
        g[s // pc.nb, s % pc.nb] = total.astype(BF16)
        return 0

    lax.fori_loop(0, pc.nd, shard, 0)


def attend_back(heads, o, lse, dout, near, far, h2t, dl1, dl2, actt, cot, ot, dres):
    nc, nd = lax.axis_size("ctx"), lax.axis_size("dp")
    ff = dl1.shape[0]
    hr = h2t.shape[0] // nd // 2
    n = Reduce.count(nd)
    _, keys, w = heads.shape
    nh = w // HEAD
    tok = keys // nc
    width = w * nc
    nb = 2 if nd % 2 == 0 else 1
    vm = lambda *shape: pltpu.VMEM(shape, BF16)
    gout, gattn = (nd // nb, nb, ff // nd, width // 2), (nd // nb, nb, hr, width)
    ns = 3 * nd + 4
    dma = pltpu.SemaphoreType.DMA
    return pl.pallas_call(
        attend_back_kernel,
        out_shape=[
            S((nc, 3, tok, w), BF16), S((2 * hr, ff), BF16), S(gout, BF16), S(gattn, BF16)
        ],
        in_specs=[ANY, VMEM, VMEM, ANY, VMEM, VMEM] + [ANY] * 7,
        out_specs=[ANY, VMEM, ANY, ANY],
        scratch_shapes=[
            pltpu.VMEM((3, keys, w), BF16),
            pltpu.VMEM((keys, w), BF16),
            pltpu.VMEM((nh, 8, keys), F32),
            pltpu.VMEM((keys, w), F32),
            pltpu.VMEM((nc, 3, tok, w), BF16),
            pltpu.VMEM((2, nd, hr, tok), BF16),
            pltpu.VMEM((2, 2, ff, tok), BF16),
            vm(2, nd, ff // nd, tok), vm(2, tok, width // 2), vm(2, nd, hr, tok), vm(2, tok, width),
            vm(*gout), vm(*gattn),
            *Reduce.scratch(nd, hr, ff, True),
            *Reduce.scratch(nd, hr, ff, True),
            dma((nc,)), dma((nc,)), dma((2, nc)), dma((2, nc)), dma((ns,)), dma((ns,)),
            dma((n,)), dma((n,)), dma((n,)), dma((n,)), dma((6 + 3 * nd,)),
        ],
        compiler_params=params(2),
        name="attend_back",
    )(heads, o, lse, dout, near, far, h2t, dl1, dl2, actt, cot, ot, dres)


def each(count, *calls):
    def body(p, _):
        for call in calls:
            call(p)
        return 0

    lax.fori_loop(0, count, body, 0)


def close_kernel(
    dtok_ref, h1t_ref, wqkv_ref, x_ref, gain_ref, dres_ref, part_ref, gout_ref, gattn_ref, t_ref,
    dx_ref, gain_out, outi, outq, outo, outa,
    dtok, dproj, h1t, wqkv, dh1,
    *refs,
):
    pc = Place()
    nd, nc = pc.nd, pc.nc
    _, _, tok, w = dtok_ref.shape
    width = nc * w
    reds, refs = [refs[5 * i : 5 * i + 5] for i in range(5)], refs[25:]
    sums, refs = refs[:5], refs[5:]
    bufs, refs = [refs[3 * i : 3 * i + 3] for i in range(6)], refs[18:]
    gmine, gtotal, gctx, gdp, ssend, srecv, rsend, rrecv, isend, irecv, csend, crecv = refs[:12]
    gsend, grecv, local, outsem = refs[12:]
    third = lambda g: pl.ds(pl.multiple_of(g * width, width), width)
    h1_mine, h1_hers = half_rows(pc, h1t_ref, pc.k), half_rows(pc, h1t_ref, 1 - pc.k)
    pairs = [(dtok_ref, dtok), (gout_ref, reds[0][0])]
    pairs += [(h1_mine[s], h1t.at[0, s]) for s in range(nd)]
    pairs += [(gattn_ref, reds[4][0]), (wqkv_ref, wqkv)]
    load = [pltpu.make_async_copy(a, b, local.at[i]) for i, (a, b) in enumerate(pairs)]
    for cp in load:
        cp.start()
    barrier(pc)
    pairs = [(h1_hers[s], h1t.at[1, s]) for s in range(nd)]
    pairs += [(dproj.at[0, :, third(g)], dproj.at[1, :, third(g)]) for g in range(3)]
    swap = [
        remote(src, dst, ssend.at[i], srecv.at[i], pc.sibling) for i, (src, dst) in enumerate(pairs)
    ]
    ro, *rq, ra = [
        Reduce(pc, bs[0], bs[1:], rsend.at[i], rrecv.at[i], i > 0) for i, bs in enumerate(reds)
    ]
    to, *tq, ta = sums
    ci = Chain(pc, t_ref, bufs[0], isend, irecv, True, 2 * PARTS)
    co, *cq, ca = [
        Chain(pc, t, bs, csend.at[i], crecv.at[i], i > 0, PARTS)
        for i, (t, bs) in enumerate(zip(sums, bufs[1:]))
    ]
    for cp in swap[:nd]:
        cp.start()
    each(ci.n, ci.open)
    load[1].wait()
    ro.start()
    load[0].wait()
    for g in range(3):
        for i in range(nc):
            dproj[0, :, g * width + i * w : g * width + (i + 1) * w] = dtok[i, g]
        swap[nd + g].start()
    for cp in load[2:]:
        cp.wait()
    for cp in swap[: nd + 1]:
        cp.wait_recv()
    weight_grad(pc, reds[1][0], h1t, dproj.at[:, :, third(0)])
    rq[0].start()
    ci.up(0)
    for g in (1, 2):
        swap[nd + g].wait_recv()
        weight_grad(pc, reds[1 + g][0], h1t, dproj.at[:, :, third(g)])
    dh1[...] = jnp.zeros_like(dh1)

    def back(g, _):
        dh1[...] += lax.dot_general(
            dproj[0, :, third(g)], wqkv[g].reshape(width, width), (((1,), (1,)), ((), ())),
            preferred_element_type=F32,
        )
        ci.both(1 + g)
        return 0

    lax.fori_loop(0, 3, back, 0)
    ci.turn_out(0)
    ro.middle()
    rq[1].start()
    gain = jnp.concatenate([gain_ref[s, 0:1, :] for s in range(nd)], axis=1)
    gtotal[...] = jnp.zeros_like(gtotal)
    chunk = 32

    def norm_back(i, _):
        at = pl.ds(pl.multiple_of(i * chunk, chunk), chunk)
        xf = x_ref[at, :].astype(F32)
        mean = jnp.mean(xf, axis=-1, keepdims=True)
        cen = xf - mean
        inv = lax.rsqrt(jnp.mean(cen * cen, axis=-1, keepdims=True) + norm_eps)
        hat = cen * inv
        d = dh1[at, :]
        dhat = d * gain
        m1 = jnp.mean(dhat, axis=-1, keepdims=True)
        m2 = jnp.mean(dhat * hat, axis=-1, keepdims=True)
        dx_ref[at, :] = (dres_ref[at, :] + inv * (dhat - m1 - hat * m2)).astype(BF16)
        gtotal[...] += jnp.sum((d * hat).reshape(chunk // 8, 8, width), axis=0)
        return 0

    lax.fori_loop(0, tok // chunk, norm_back, 0)
    row = lax.broadcasted_iota(jnp.int32, (8, 1), 0)
    gmine[...] = jnp.where(row == 0, jnp.sum(gtotal[...], axis=0, keepdims=True), part_ref[...])
    rows = gain_out.shape[1]
    here = lambda d: pl.ds(pl.multiple_of(d * rows, 128), rows)
    dcopies = []
    for t in range(1, nd):
        to_d = (pc.d + t) % nd
        dcopies.append(
            remote(
                gmine.at[:, here(to_d)], gdp.at[t], gsend.at[nc + t], grecv.at[nc + t], (to_d, pc.c)
            )
        )
        dcopies[-1].start()
    ci.both(4)
    ci.turn_out(1)
    rq[0].middle()
    rq[2].start()
    ci.both(5)
    ci.turn_out(2)
    for cp in dcopies:
        cp.wait_recv()
    total = gmine[:, here(pc.d)]
    for t in range(1, nd):
        total = total + gdp[t]
    gdp[0] = total
    gcopies = []
    for t in range(1, nc):
        gcopies.append(
            remote(gdp.at[0], gctx.at[t], gsend.at[t], grecv.at[t], (pc.d, (pc.c + t) % nc))
        )
        gcopies[-1].start()
    ci.both(6)
    ci.turn_out(3)
    ro.finish(to)
    each(PARTS, co.open)
    ci.both(7)
    ci.turn_in(7)
    ci.turn_out(4)
    rq[1].middle()
    ra.start()
    ci.turn_out(5)
    co.up(0)
    rq[0].finish(tq[0])
    each(PARTS, cq[0].open)
    ci.turn_out(6)
    co.both(1)
    ci.turn_out(7)
    outs = [
        pltpu.make_async_copy(c.all, out, outsem.at[i])
        for i, (c, out) in enumerate(
            [(ci, outi), (co, outo)]
            + [(cq[g], outq.at[:, :, third(g)]) for g in range(3)]
            + [(ca, outa)]
        )
    ]
    for cp in gcopies:
        cp.wait_recv()
    total = gdp[0]
    for t in range(1, nc):
        total = total + gctx[t]
    gain_out[...] = total
    rq[2].middle()
    co.both(2)
    co.turn_out(0)
    rq[1].finish(tq[1])
    each(PARTS, cq[1].open)
    co.both(3)
    cq[0].up(0)
    co.turn_in(3)
    co.turn_out(1)
    ra.middle()
    each(PARTS - 1, lambda p: cq[0].both(p + 1))
    co.turn_out(2)
    rq[2].finish(tq[2])
    each(PARTS, cq[2].open)
    co.turn_out(3)
    cq[1].up(0)
    cq[0].turn_in(3)
    ra.finish(ta)
    each(PARTS, ca.open)
    each(ci.n, ci.side_wait)
    outs[0].start()
    each(PARTS - 1, lambda p: cq[1].both(p + 1), cq[0].turn_out)
    cq[2].up(0)
    cq[1].turn_in(3)
    cq[0].turn_out(3)
    each(PARTS - 1, lambda p: cq[2].both(p + 1), cq[1].turn_out)
    ca.up(0)
    cq[2].turn_in(3)
    cq[1].turn_out(3)
    each(PARTS, co.side_wait)
    outs[1].start()
    each(PARTS - 1, lambda p: ca.both(p + 1), cq[2].turn_out)
    ca.turn_in(3)
    cq[2].turn_out(3)
    each(PARTS, ca.turn_out)
    for i, c in enumerate(cq + [ca]):
        each(PARTS, c.side_wait)
        outs[2 + i].start()
    for cp in swap + dcopies + gcopies:
        cp.wait_send()
    for r in [ro] + rq + [ra]:
        r.sent()
    for c in [ci, co] + cq + [ca]:
        each(c.n, c.sent)
    for cp in outs:
        cp.wait()


def close(dtok, h1t, wqkv, x, gains, dres, part, gout, gattn, totals):
    nd, nc = lax.axis_size("dp"), lax.axis_size("ctx")
    tok, width = x.shape
    rows = width // nd
    hr = rows // 2
    nq, ns = Reduce.count(nd), nd + 3
    dma = pltpu.SemaphoreType.DMA
    mine = [gout.shape[2:]] + [(hr, width)] * 4
    sizes = [totals.shape] + mine
    vm = lambda *shape: pltpu.VMEM(shape, BF16)
    chain_bufs = [b for size in sizes for b in (vm(*size), vm(*size), vm(2, *size))]
    reduce_bufs = [b for i, size in enumerate(mine) for b in Reduce.scratch(nd, *size, i > 0)]
    return pl.pallas_call(
        close_kernel,
        out_shape=[S((tok, width), BF16), S((8, rows), F32)]
        + [S((2,) + size, BF16) for size in (sizes[0], (hr, 3 * width), mine[0], mine[4])],
        in_specs=[ANY, ANY, ANY, VMEM, VMEM, VMEM, VMEM, ANY, ANY, VMEM],
        out_specs=[VMEM] * 2 + [ANY] * 4,
        scratch_shapes=[
            vm(*dtok.shape), vm(2, tok, 3 * width), vm(2, nd, hr, tok), vm(*wqkv.shape),
            pltpu.VMEM((tok, width), F32),
            *reduce_bufs, *[vm(*size) for size in mine], *chain_bufs,
            pltpu.VMEM((8, width), F32), pltpu.VMEM((8, width), F32),
            pltpu.VMEM((nc, 8, rows), F32), pltpu.VMEM((nd, 8, rows), F32),
            dma((ns,)), dma((ns,)), dma((5, nq)), dma((5, nq)),
            dma((4, 2 * PARTS)), dma((4, 2 * PARTS)), dma((5, 4, PARTS)), dma((5, 4, PARTS)),
            dma((nc + nd,)), dma((nc + nd,)), dma((4 + nd,)), dma((6,)),
        ],
        compiler_params=params(3),
        name="close",
    )(dtok, h1t, wqkv, x, gains, dres, part, gout, gattn, totals)


def norm_rows(values, gain):
    row_mean = jnp.mean(values, axis=-1, keepdims=True)
    centred = values - row_mean
    row_var = jnp.mean(centred * centred, axis=-1, keepdims=True)
    return centred * lax.rsqrt(row_var + norm_eps) * gain


def gelu_exact(values):
    return 0.5 * values * (1.0 + lax.erf(values * 0.7071067811865476))


def gelu_slope(values):
    return (
        0.5 * (1.0 + lax.erf(values * 0.7071067811865476))
        + values * jnp.exp(-0.5 * values * values) * 0.3989422804014327
    )


def rope_angles(positions, lanes):
    half = HEAD // 2
    freq = rope_theta ** (-(jnp.arange(half, dtype=F32) * 2.0 / HEAD))
    freq = jnp.tile(freq, lanes // half)
    return positions.astype(F32)[:, None] * freq[None, :]


def on_device(
    tokens,
    norm1_gain,
    qkv_weight,
    attn_out_weight,
    norm2_gain,
    mlp_in_weight,
    mlp_out_weight,
    cotangent,
):
    _, tok, width = tokens.shape
    nc, nd = lax.axis_size("ctx"), lax.axis_size("dp")
    keys = tok * nc
    w = width // nc
    ff = mlp_in_weight.shape[1] // 2
    rows = norm1_gain.shape[0]
    x = tokens.reshape(tok, width)
    upstream = cotangent.reshape(tok, width)
    gains = jnp.concatenate(
        [
            norm1_gain.astype(F32)[None],
            norm2_gain.astype(F32)[None],
            jnp.zeros((6, rows), F32),
        ]
    )
    ang = rope_angles(lax.axis_index("ctx") * tok + jnp.arange(tok, dtype=jnp.int32), 2 * w)
    sign = jnp.where(jnp.arange(2 * w) % HEAD < HEAD // 2, -1.0, 1.0).astype(F32)
    h1t, gains_all, w1s, w2s, wqkv, wattn, heads, w1_early = project(
        x, gains, jnp.cos(ang), jnp.sin(ang) * sign[None], qkv_weight, attn_out_weight,
        mlp_in_weight,
    )
    otok, o_heads, lse, w1, w2, wout = attend(
        heads, w1s, w2s, mlp_out_weight, w1_early
    )
    wattn = wattn.reshape(width, width)
    w1 = w1.reshape(width, ff)
    w2 = w2.reshape(width, ff)
    wout = wout.reshape(ff, width)
    gain_one = gains_all[:, 0].reshape(width)
    gain_two = gains_all[:, 1].reshape(width)

    split = otok.ndim == 3
    attended_b = jnp.transpose(otok, (1, 0, 2)).reshape(tok, width) if split else otok
    inputs_f = x.astype(F32)
    attn_res = inputs_f + jnp.dot(attended_b, wattn, preferred_element_type=F32)
    normed_two = norm_rows(attn_res, gain_two).astype(BF16)
    gelu_in = jnp.dot(normed_two, w1, preferred_element_type=F32)
    gate_in = jnp.dot(normed_two, w2, preferred_element_type=F32)
    activated = (gelu_exact(gelu_in) * gate_in).astype(BF16)
    layer_out = (attn_res + jnp.dot(activated, wout, preferred_element_type=F32)).astype(BF16)
    grad_act = jnp.dot(upstream, wout.T, preferred_element_type=F32)
    dl1 = (grad_act * gate_in * gelu_slope(gelu_in)).astype(BF16)
    dl2 = (grad_act * gelu_exact(gelu_in)).astype(BF16)
    dl1, dl2 = lax.optimization_barrier((dl1, dl2))
    grad_normed_two = jnp.dot(dl1, w1.T, preferred_element_type=F32) + jnp.dot(
        dl2, w2.T, preferred_element_type=F32
    )
    _, pull_two = jax.vjp(norm_rows, attn_res, gain_two)
    grad_res_norm, grad_gain_two = pull_two(grad_normed_two)
    grad_res = upstream.astype(F32) + grad_res_norm
    grad_res_b = grad_res.astype(BF16)
    dout = jnp.dot(grad_res_b, wattn.T, preferred_element_type=F32).astype(BF16)
    if split:
        dout = jnp.transpose(dout.reshape(tok, nc, w), (1, 0, 2))

    near = rope_angles(jnp.arange(tok, dtype=jnp.int32), w)
    far = rope_angles(jnp.arange(nc, dtype=jnp.int32) * tok, w)[:, None]
    near, far = [jnp.stack([jnp.cos(ang), jnp.sin(ang)]) for ang in (near, far)]
    dtok, totals, gout, gattn = attend_back(
        heads, o_heads, lse, dout, near, far, normed_two.T, dl1.T, dl2.T,
        activated.T, upstream, attended_b.T, grad_res_b,
    )
    input_grad, gain_grads, gin, gqkv, gout, gattn = close(
        dtok, h1t, wqkv, x, gains_all, grad_res, grad_gain_two.reshape(1, width), gout, gattn, totals
    )
    gin = gin.reshape(2, 2, rows // 2, ff)
    grad_in = jnp.concatenate([gin[:, i].reshape(rows, ff) for i in range(2)], axis=1)
    return (
        layer_out.reshape(1, tok, width),
        input_grad.reshape(1, tok, width),
        gain_grads[0],
        gqkv.reshape(rows, 3 * width).astype(F32),
        gattn.reshape(rows, width).astype(F32),
        gain_grads[1],
        grad_in.astype(F32),
        jnp.concatenate([gout[0], gout[1]], axis=1).astype(F32),
    )


def solution(mesh):
    in_specs = (
        P("dp", "ctx", None),
        P("dp"),
        P("dp", None),
        P("dp", None),
        P("dp"),
        P("dp", None),
        P("dp", None),
        P("dp", "ctx", None),
    )
    out_specs = (
        P("dp", "ctx", None),
        P("dp", "ctx", None),
        P("dp"),
        P("dp", None),
        P("dp", None),
        P("dp"),
        P("dp", None),
        P("dp", None),
    )
    return jax.shard_map(
        on_device, mesh=mesh, in_specs=in_specs, out_specs=out_specs, check_vma=False
    )
```
